32 devices in a mesh: dp: 8 (over z, y), tensor: 4 (over x, core).
Axes of the slice: x: 2, y: 2, z: 4, core: 2. Of those that a mesh axis runs over, the one named last changes fastest.
Arguments:
- tokens: bfloat16 [1024, 2, 768], P(('dp', 'tensor')), may hold values from -6 to 6
- gain_attn: bfloat16 [768], P(('dp', 'tensor')), may hold values from 0.5 to 1.5
- gain_ffn: bfloat16 [768], P(('dp', 'tensor')), may hold values from 0.5 to 1.5
- w_qkv: bfloat16 [768, 3, 768], P('dp', None, 'tensor'), may hold values from -0.21875 to 0.21875
- w_rate: bfloat16 [768, 12], P('dp', 'tensor'), may hold values from -0.21875 to 0.21875
- w_out: bfloat16 [768, 768], P('tensor', 'dp'), may hold values from -0.21875 to 0.21875
- w_gate_up: bfloat16 [768, 2, 2048], P('dp', None, 'tensor'), may hold values from -0.21875 to 0.21875
- w_down: bfloat16 [2048, 768], P('tensor', 'dp'), may hold values from -0.25 to 0.25
- w_one: bfloat16 [12, 64, 256], P('tensor', None, 'dp'), may hold values from -0.75 to 0.75
- b_one: bfloat16 [12, 256], P('tensor', 'dp'), may hold values from -3 to 3
- w_two: bfloat16 [12, 256, 64], P('tensor', 'dp'), may hold values from -0.375 to 0.375
- b_two: bfloat16 [12, 64], P('tensor', 'dp'), may hold values from -3 to 3
- norm_gain_inner: bfloat16 [12, 64], P('tensor', 'dp'), may hold values from 0.5 to 1.5
- norm_bias_inner: bfloat16 [12, 64], P('tensor', 'dp'), may hold values from -3 to 3
- cotangent: bfloat16 [1024, 2, 768], P(('dp', 'tensor')), may hold values from -6 to 6
Outputs:
- output: bfloat16 [1024, 2, 768], P(('dp', 'tensor'))
- input_grad: float32 [1024, 2, 768], P(('dp', 'tensor'))
- grad_gain_attn: float32 [768], P(('dp', 'tensor'))
- grad_gain_ffn: float32 [768], P(('dp', 'tensor'))
- grad_w_qkv: float32 [768, 3, 768], P('dp', None, 'tensor')
- grad_w_rate: float32 [768, 12], P('dp', 'tensor')
- grad_w_out: float32 [768, 768], P('tensor', 'dp')
- grad_w_gate_up: float32 [768, 2, 2048], P('dp', None, 'tensor')
- grad_w_down: float32 [2048, 768], P('tensor', 'dp')
- grad_w_one: float32 [12, 64, 256], P('tensor', None, 'dp')
- grad_b_one: float32 [12, 256], P('tensor', 'dp')
- grad_w_two: float32 [12, 256, 64], P('tensor', 'dp')
- grad_b_two: float32 [12, 64], P('tensor', 'dp')
- grad_norm_gain_inner: float32 [12, 64], P('tensor', 'dp')
- grad_norm_bias_inner: float32 [12, 64], P('tensor', 'dp')
The draws below stay inside these ranges and needn't reach their ends.
All inputs are finite; a program needn't handle non-finite values.
Results may differ from the reference program's by a relative error of at most 0.025.
Values may be sent and summed in bfloat16 or wider, within the bound.
No kernel may reach another device: no remote copies, remote signals or barrier semaphores. Data moves between devices by JAX's collectives and lax.ppermute only.
A program may use at most 64 MiB of HBM per device.

```python
import jax
import jax.numpy as jnp
from jax import lax

D = 768
HEADS = 12
HEAD_DIM = 64
INNER = 256
FF = 2048
MINI = 16
SEQS = 2
LEN = 1024


def steps_of(key, dims, cuts, smallest, high):
    level = 1.0
    for axis_at, parts in cuts:
        steps = jax.random.uniform(jax.random.fold_in(jax.random.fold_in(key, 6), axis_at), (parts,), jnp.float32, smallest / len(cuts), high / len(cuts))
        level = level * jnp.repeat(jnp.exp(steps), dims[axis_at] // parts).reshape((-1,) + (1,) * (len(dims) - 1 - axis_at))
    return level


def scatter_about(key, shape, scale, limit, cuts=(), dtype=jnp.bfloat16):
    values = jax.random.normal(key, shape, jnp.float32) * scale
    if len(cuts) > 0:
        values = steps_of(key, shape, cuts, -0.22, 0.18) * values
    return jnp.clip(values, min=-limit, max=limit).astype(dtype)


def setup_inputs(seed: int = 0) -> dict:
    seeds = jax.random.split(jax.random.key(seed), 16)
    return {
        "tokens": scatter_about(seeds[0], (LEN, SEQS, D), 1.0, 6.0, ((0, 32),)),
        "gain_attn": jnp.clip(1.0 + 0.1 * jax.random.normal(seeds[1], (D,), jnp.float32), 0.5, 1.5).astype(jnp.bfloat16),
        "gain_ffn": jnp.clip(1.0 + 0.1 * jax.random.normal(seeds[2], (D,), jnp.float32), 0.5, 1.5).astype(jnp.bfloat16),
        "w_qkv": scatter_about(seeds[3], (D, 3, D), D ** -0.5, 0.21875, ((0, 8), (2, 4))),
        "w_rate": scatter_about(seeds[4], (D, HEADS), D ** -0.5, 0.21875, ((0, 8), (1, 4))),
        "w_out": scatter_about(seeds[5], (D, D), D ** -0.5, 0.21875, ((0, 4), (1, 8))),
        "w_gate_up": scatter_about(seeds[6], (D, 2, FF), D ** -0.5, 0.21875, ((0, 8), (2, 4))),
        "w_down": scatter_about(seeds[7], (FF, D), (FF // 4) ** -0.5, 0.25, ((0, 4), (1, 8))),
        "w_one": scatter_about(seeds[8], (HEADS, HEAD_DIM, INNER), HEAD_DIM ** -0.5, 0.75, ((0, 4), (2, 8))),
        "b_one": scatter_about(seeds[9], (HEADS, INNER), 0.5, 3.0, ((0, 4), (1, 8))),
        "w_two": scatter_about(seeds[10], (HEADS, INNER, HEAD_DIM), INNER ** -0.5, 0.375, ((0, 4), (1, 8))),
        "b_two": scatter_about(seeds[11], (HEADS, HEAD_DIM), 0.5, 3.0, ((0, 4), (1, 8))),
        "norm_gain_inner": jnp.clip(1.0 + 0.1 * jax.random.normal(seeds[12], (HEADS, HEAD_DIM), jnp.float32), 0.5, 1.5).astype(jnp.bfloat16),
        "norm_bias_inner": scatter_about(seeds[13], (HEADS, HEAD_DIM), 0.5, 3.0, ((0, 4), (1, 8))),
        "cotangent": scatter_about(seeds[14], (LEN, SEQS, D), 1.0, 6.0, ((0, 32),)),
    }


@jax.custom_vjp
def low(v):
    return lax.optimization_barrier(v.astype(jnp.bfloat16)).astype(jnp.float32)

@jax.custom_vjp
def low_back(v):
    return v

def low_keep(v):
    return (low(v), None)

def low_pass(kept, grad):
    return (grad,)

def back_keep(v):
    return (v, None)

def back_low(kept, grad):
    return (low(grad),)
low.defvjp(low_keep, low_pass)
low_back.defvjp(back_keep, back_low)
epsilon = 1e-05
inner_epsilon = 1e-06
highest = lax.Precision.HIGHEST
inner_rate = 0.5
root_half = 0.7071067811865476
normal_peak = 0.3989422804014327

def gelu_exact(values):
    return 0.5 * values * (1.0 + lax.erf(values * root_half))

def gelu_slope(values):
    return 0.5 * (1.0 + lax.erf(values * root_half)) + values * jnp.exp(-0.5 * values * values) * normal_peak

def layer_norm(values, scaling):
    average = lax.optimization_barrier(jnp.mean(values, axis=-1, keepdims=True))
    centred = values - average
    spread = lax.optimization_barrier(jnp.mean(centred * centred, axis=-1, keepdims=True))
    return centred * lax.rsqrt(spread + epsilon) * scaling

def inner_norm_parts(values, norm_gain, norm_bias):
    average = lax.optimization_barrier(jnp.mean(values, axis=-1, keepdims=True))
    centred = values - average
    inverse = lax.rsqrt(lax.optimization_barrier(jnp.mean(centred * centred, axis=-1, keepdims=True)) + inner_epsilon)
    normal = centred * inverse
    return (normal, inverse, normal * norm_gain + norm_bias)

def inner_step(norm_pair, state, batch):
    first_w, first_b, second_w, second_b = state
    norm_gain, norm_bias = norm_pair
    queries, keys_in, targets, step_rates = batch
    key_pre = jnp.einsum('mhe,hei->mhi', keys_in, first_w, precision=highest) + first_b
    activity = gelu_exact(key_pre)
    key_res = jnp.einsum('mhi,hie->mhe', activity, second_w, precision=highest) + second_b
    normal, inverse, key_normed = inner_norm_parts(key_res, norm_gain, norm_bias)
    errors = keys_in + key_normed - targets
    scaled = errors * step_rates[:, :, None] * norm_gain
    back_res = inverse * (scaled - lax.optimization_barrier(jnp.mean(scaled, axis=-1, keepdims=True)) - normal * lax.optimization_barrier(jnp.mean(scaled * normal, axis=-1, keepdims=True)))
    back_act = jnp.einsum('mhe,hie->mhi', back_res, second_w, precision=highest)
    back_pre = back_act * gelu_slope(key_pre)
    count = queries.shape[0]
    causal = (lax.broadcasted_iota(jnp.int32, (count, count), 0) >= lax.broadcasted_iota(jnp.int32, (count, count), 1)).astype(jnp.float32)
    first_mix = (jnp.einsum('mhe,nhe->hmn', queries, keys_in, precision=highest) + 1.0) * causal
    query_pre = jnp.einsum('mhe,hei->mhi', queries, first_w, precision=highest) + first_b - jnp.einsum('hmn,nhi->mhi', first_mix, back_pre, precision=highest)
    hidden = gelu_exact(query_pre)
    second_mix = (jnp.einsum('mhi,nhi->hmn', hidden, activity, precision=highest) + 1.0) * causal
    query_res = jnp.einsum('mhi,hie->mhe', hidden, second_w, precision=highest) + second_b - jnp.einsum('hmn,nhe->mhe', second_mix, back_res, precision=highest)
    outputs = queries + inner_norm_parts(query_res, norm_gain, norm_bias)[2]
    grad_second = jnp.einsum('mhi,mhe->hie', activity, back_res, precision=highest)
    grad_first = jnp.einsum('mhe,mhi->hei', keys_in, back_pre, precision=highest)
    updated = (first_w - grad_first, first_b - lax.optimization_barrier(jnp.sum(back_pre, axis=0)), second_w - grad_second, second_b - lax.optimization_barrier(jnp.sum(back_res, axis=0)))
    return (updated, outputs)

def run_group(state, norm_pair, queries, keys_in, targets, step_rates):
    block_count = queries.shape[0] // MINI
    shaped = tuple((member.reshape((block_count, MINI) + member.shape[1:]) for member in (queries, keys_in, targets, step_rates)))

    def one_step(carry, batch):
        return inner_step(norm_pair, carry, batch)
    final, outputs = lax.scan(jax.checkpoint(one_step), state, shaped)
    return (final, outputs.reshape(queries.shape))

def forward(inputs, gain_attn, gain_ffn, w_qkv, w_rate, w_out, w_gate_up, w_down, w_one, b_one, w_two, b_two, norm_gain_inner, norm_bias_inner):
    length, seq_count, width = inputs.shape
    rows = inputs.reshape(length * seq_count, width)
    normed_attn = low(layer_norm(rows, gain_attn))
    projected = low_back(jnp.dot(normed_attn, w_qkv.reshape(width, 3 * width), precision=highest))
    rate_logit = low_back(jnp.dot(normed_attn, w_rate, precision=highest))
    step_rates = jax.nn.sigmoid(rate_logit) * (inner_rate / (MINI * HEAD_DIM))
    head_shape = (length, seq_count, HEADS, HEAD_DIM)
    queries = projected[:, :width].reshape(head_shape)
    keys_in = projected[:, width:2 * width].reshape(head_shape)
    targets = projected[:, 2 * width:].reshape(head_shape)
    step_rates = step_rates.reshape(length, seq_count, HEADS)
    state = (w_one, b_one, w_two, b_two)
    norm_pair = (norm_gain_inner, norm_bias_inner)

    def one_sequence(seq_query, seq_keys, seq_values, seq_rates):
        return run_group(state, norm_pair, seq_query, seq_keys, seq_values, seq_rates)[1]
    inner_out = jax.vmap(one_sequence, in_axes=1, out_axes=1)(queries, keys_in, targets, step_rates)
    head_normed = low(layer_norm(inner_out, 1.0)).reshape(length * seq_count, width)
    attn_branch = low_back(jnp.dot(head_normed, w_out, precision=highest))
    mixed = rows + attn_branch
    normed_ffn = low(layer_norm(mixed, gain_ffn))
    gate_up = low_back(jnp.einsum('rd,dgf->rgf', normed_ffn, w_gate_up, precision=highest))
    swiglu = low(jax.nn.silu(gate_up[:, 0]) * gate_up[:, 1])
    result = mixed + jnp.dot(swiglu, w_down, precision=highest)
    return result.reshape(length, seq_count, width)

def reference(tokens, gain_attn, gain_ffn, w_qkv, w_rate, w_out, w_gate_up, w_down, w_one, b_one, w_two, b_two, norm_gain_inner, norm_bias_inner, cotangent):
    primals = tuple((member.astype(jnp.float32) for member in (tokens, gain_attn, gain_ffn, w_qkv, w_rate, w_out, w_gate_up, w_down, w_one, b_one, w_two, b_two, norm_gain_inner, norm_bias_inner)))
    result, pullback = jax.vjp(forward, *primals)
    grads = pullback(cotangent.astype(jnp.float32))
    return (result.astype(jnp.bfloat16), grads[0], grads[1], grads[2], grads[3], grads[4], grads[5], grads[6], grads[7], grads[8], grads[9], grads[10], grads[11], grads[12], grads[13])
```

```python
import jax
import jax.numpy as jnp
from jax import lax
from jax.experimental import pallas as pl
from jax.experimental.pallas import tpu as pltpu
from jax.sharding import PartitionSpec as P

HEAD_DIM = 64
INNER = 256
MINI = 16
LANES = 256

epsilon = 1e-05
inner_epsilon = 1e-06
inner_rate = 0.5
rate_scale = inner_rate / (MINI * HEAD_DIM)
root_half = 0.7071067811865476
normal_peak = 0.3989422804014327

f32 = jnp.float32
bf16 = jnp.bfloat16


def dot_nn(a, b):
    return lax.dot_general(
        a.astype(bf16), b.astype(bf16), (((1,), (0,)), ((), ())), preferred_element_type=f32
    )


def dot_nt(a, b):
    return lax.dot_general(
        a.astype(bf16), b.astype(bf16), (((1,), (1,)), ((), ())), preferred_element_type=f32
    )


def dot_tn(a, b):
    return lax.dot_general(
        a.astype(bf16), b.astype(bf16), (((0,), (0,)), ((), ())), preferred_element_type=f32
    )


def row_mean(values):
    return jnp.mean(values, axis=-1, keepdims=True)


def density_and_share(values):
    density = jnp.exp(-0.5 * values * values) * normal_peak
    share = 0.5 * (1.0 + lax.erf(values * root_half))
    return density, share


def token_grid(count):
    rows = lax.broadcasted_iota(jnp.int32, (count, count), 0)
    cols = lax.broadcasted_iota(jnp.int32, (count, count), 1)
    return rows, cols


def unpack_chunk(packed, bias):
    query = packed[:, :HEAD_DIM]
    key = packed[:, HEAD_DIM : 2 * HEAD_DIM]
    value = packed[:, 2 * HEAD_DIM : 3 * HEAD_DIM]
    tail = packed[:, 3 * HEAD_DIM :].astype(f32)
    rate = jax.nn.sigmoid(tail[:, 0:1] + tail[:, 1:2]) * rate_scale
    miss = key.astype(f32) - value.astype(f32) + bias
    return query, key, rate, miss


def forward_kernel(
    packed_ref,
    first_w_in,
    first_b_in,
    second_w_in,
    second_b_in,
    gain_ref,
    bias_ref,
    normed_ref,
    act_ref,
    grad_pre_ref,
    hidden_ref,
    slope_ref,
    curve_ref,
    out_slope_ref,
    norms_ref,
    stats_ref,
    first_save,
    second_save,
    first_w,
    first_b,
    second_w,
    second_b,
    back_res_ref,
):
    @pl.when(pl.program_id(0) == 0)
    def _():
        first_w[...] = first_w_in[...]
        first_b[...] = first_b_in[...]
        second_w[...] = second_w_in[...]
        second_b[...] = second_b_in[...]

    gain = gain_ref[...]
    bias = bias_ref[...]
    chunk = packed_ref.shape[0]
    steps = chunk // MINI
    query, key, rate, miss = unpack_chunk(packed_ref[...], bias)
    base = miss * gain
    rate_base = rate * base
    rate_gain = rate * (gain * gain)
    base_mean = row_mean(rate_base)
    rows, cols = token_grid(chunk)
    before = cols // MINI + 1 < rows // MINI
    key_mix = jnp.where(before, dot_nt(key, key) + 1.0, 0.0).astype(bf16)
    first_low = first_w[...].astype(bf16)
    first_save[0] = first_low
    pre_all = dot_nn(key, first_low) + first_b[...]
    state = second_w[...]
    state_b = second_b[...]
    start_low = state.astype(bf16)
    start_b = state_b
    last_grad = None
    grads, acts, backs = [], [], []
    for step in range(steps):
        at = slice(step * MINI, (step + 1) * MINI)
        pre = pre_all[at]
        if step >= 2:
            past = (step - 1) * MINI
            older = jnp.concatenate(grads[: step - 1], axis=0) if step > 2 else grads[0]
            pre = pre - dot_nn(key_mix[at, :past], older)
        if step >= 1:
            pre = pre - dot_nn(
                dot_nt(key[at], key[(step - 1) * MINI : step * MINI]) + 1.0, last_grad
            )
        density, share = density_and_share(pre)
        act = (pre * share).astype(bf16)
        slope = share + pre * density
        state_low = state.astype(bf16)
        second_save[0, step] = state_low
        res = dot_nt(act, state_low) + state_b
        weighted = rate_gain[at] * res
        square = jnp.sum(res * res, axis=-1, keepdims=True)
        sum_gain = jnp.sum(weighted, axis=-1, keepdims=True)
        sum_base = jnp.sum(rate_base[at] * res, axis=-1, keepdims=True)
        sum_square = jnp.sum(weighted * res, axis=-1, keepdims=True)
        inverse = lax.rsqrt(square * (1.0 / HEAD_DIM) + inner_epsilon)
        scaled_mean = base_mean[at] + inverse * sum_gain * (1.0 / HEAD_DIM)
        along = inverse * (sum_base + inverse * sum_square) * (1.0 / HEAD_DIM)
        normal = res * inverse
        back_res = inverse * (rate_base[at] + rate_gain[at] * normal - scaled_mean - normal * along)
        back_low = back_res.astype(bf16)
        back_act = dot_nn(back_low, state_low)
        last_grad = (back_act * slope).astype(bf16)
        state = state - dot_tn(back_low, act)
        state_b = state_b - jnp.sum(back_res, axis=0, keepdims=True)
        grads.append(last_grad)
        acts.append(act)
        backs.append(back_low)
        slope_ref[at, :] = slope
        curve_ref[at, :] = back_act * density * (2.0 - pre * pre)
        act_ref[at, :] = act
        grad_pre_ref[at, :] = last_grad
        back_res_ref[at, :] = back_low
        norms_ref[at, :HEAD_DIM] = normal
        stats_ref[at, HEAD_DIM : HEAD_DIM + 1] = inverse
    grad_all = grad_pre_ref[...]
    act_all = act_ref[...]
    back_all = back_res_ref[...]
    start_first_b = first_b[...]
    first_w[...] = first_w[...] - dot_tn(key, grad_all)
    first_b[...] = start_first_b - jnp.sum(grad_all.astype(f32), axis=0, keepdims=True)
    second_w[...] = state
    second_b[...] = state_b

    causal = cols <= rows
    first_mix = jnp.where(causal, dot_nt(query, key) + 1.0, 0.0)
    query_pre = dot_nn(query, first_low) + start_first_b - dot_nn(first_mix, grad_all)
    density, share = density_and_share(query_pre)
    hidden = (query_pre * share).astype(bf16)
    out_slope_ref[...] = share + query_pre * density
    hidden_ref[...] = hidden
    second_mix = jnp.where(causal, dot_nt(hidden, act_all) + 1.0, 0.0)
    query_res = dot_nt(hidden, start_low) + start_b - dot_nn(second_mix, back_all)
    out_inverse = lax.rsqrt(row_mean(query_res * query_res) + inner_epsilon)
    out_normal = query_res * out_inverse
    norms_ref[:, HEAD_DIM:] = out_normal
    outputs = query.astype(f32) + out_normal * gain + bias
    centred = outputs - row_mean(outputs)
    head_inverse = lax.rsqrt(row_mean(centred * centred) + epsilon)
    head_normal = centred * head_inverse
    stats_ref[:, :HEAD_DIM] = head_normal
    stats_ref[:, HEAD_DIM + 1 : HEAD_DIM + 2] = out_inverse
    stats_ref[:, HEAD_DIM + 2 : HEAD_DIM + 3] = head_inverse
    normed_ref[...] = head_normal.astype(bf16)


def backward_kernel(
    packed_ref,
    head_grad_ref,
    act_ref,
    grad_pre_ref,
    hidden_ref,
    slope_ref,
    curve_ref,
    out_slope_ref,
    norms_ref,
    stats_ref,
    first_save,
    second_save,
    gain_ref,
    bias_ref,
    back_ref,
    first_w_out,
    first_b_out,
    second_w_out,
    second_b_out,
    gain_out,
    bias_out,
    first_w,
    first_b,
    second_w,
    second_b,
    gain_sum,
    bias_sum,
    known_ref,
    own_ref,
):
    @pl.when(pl.program_id(0) == 0)
    def _():
        first_w[...] = jnp.zeros_like(first_w)
        first_b[...] = jnp.zeros_like(first_b)
        second_w[...] = jnp.zeros_like(second_w)
        second_b[...] = jnp.zeros_like(second_b)
        gain_sum[...] = jnp.zeros_like(gain_sum)
        bias_sum[...] = jnp.zeros_like(bias_sum)
        known_ref[...] = jnp.zeros_like(known_ref)

    gain = gain_ref[...]
    bias = bias_ref[...]
    chunk = packed_ref.shape[0]
    steps = chunk // MINI
    query, key, rate, miss = unpack_chunk(packed_ref[...], bias)
    base = miss * gain
    rate_base = rate * base
    square_gain = gain * gain
    rate_gain = rate * square_gain
    normal = norms_ref[:, :HEAD_DIM]
    out_normal = norms_ref[:, HEAD_DIM:]
    head_normal = stats_ref[:, :HEAD_DIM]
    inverse = stats_ref[:, HEAD_DIM : HEAD_DIM + 1]
    out_inverse = stats_ref[:, HEAD_DIM + 1 : HEAD_DIM + 2]
    head_inverse = stats_ref[:, HEAD_DIM + 2 : HEAD_DIM + 3]
    act = act_ref[...]
    grad_pre = grad_pre_ref[...]
    hidden = hidden_ref[...]
    first_low = first_save[0]
    start_low = second_save[0, 0]
    gain_normal = rate_gain * normal
    scaled = rate_base + gain_normal
    scaled_mean = row_mean(scaled)
    along = row_mean(scaled * normal)
    back_res = (inverse * (scaled - scaled_mean - normal * along)).astype(bf16)
    coef_grad = rate_gain - along
    coef_beta = gain_normal + scaled
    gain_along = row_mean(gain_normal)
    gain_square = row_mean(gain_normal * normal)
    gain_level = row_mean(rate_gain)
    mix_cross = -(gain_along + scaled_mean)
    mix_beta = -(3.0 * along + gain_square)
    mix_alpha = -(along + gain_level)
    inverse_square = inverse * inverse

    rows, cols = token_grid(chunk)
    causal = cols <= rows
    later = rows <= cols
    head_grad = head_grad_ref[...].astype(f32)
    out_grad = head_inverse * (
        head_grad - row_mean(head_grad) - head_normal * row_mean(head_grad * head_normal)
    )
    gain_total = jnp.sum(out_grad * out_normal, axis=0, keepdims=True)
    bias_total = jnp.sum(out_grad, axis=0, keepdims=True)
    normal_grad = out_grad * gain
    res_grad = out_inverse * (
        normal_grad - row_mean(normal_grad) - out_normal * row_mean(normal_grad * out_normal)
    )
    res_grad_low = res_grad.astype(bf16)
    second_mix_grad = jnp.where(causal, -dot_nt(res_grad_low, back_res), 0.0)
    second_mix_grad_t = jnp.where(later, -dot_nt(back_res, res_grad_low), 0.0)
    hidden_grad = dot_nn(res_grad_low, start_low) + dot_nn(second_mix_grad, act)
    query_pre_grad = hidden_grad * out_slope_ref[...]
    query_pre_low = query_pre_grad.astype(bf16)
    first_mix_grad = jnp.where(causal, -dot_nt(query_pre_low, grad_pre), 0.0)
    first_mix_grad_t = jnp.where(later, -dot_nt(grad_pre, query_pre_low), 0.0)
    query_grad = out_grad + dot_nt(query_pre_low, first_low) + dot_nn(first_mix_grad, key)
    key_grad = dot_nn(first_mix_grad_t, query)
    act_grad = dot_nn(second_mix_grad_t, hidden)
    second_mix_t = jnp.where(later, dot_nt(act, hidden) + 1.0, 0.0)
    back_res_grad = -dot_nn(second_mix_t, res_grad_low)
    first_mix_t = jnp.where(later, dot_nt(key, query) + 1.0, 0.0)
    first_next = first_w[...]
    first_next_low = first_next.astype(bf16)
    pre_base = (
        -dot_nn(first_mix_t, query_pre_low) - dot_nn(key, first_next_low) - first_b[...]
    )
    after = cols // MINI > rows // MINI + 1
    near_mix = jnp.where(cols // MINI == rows // MINI + 1, dot_nt(key, key) + 1.0, 0.0).astype(bf16)
    key_mix = jnp.where(after, dot_nt(key, key) + 1.0, 0.0).astype(bf16)

    state = second_w[...]
    state_b = second_b[...]
    own_ref[...] = back_res
    pre_lows = [None] * steps
    back_grads = [None] * steps
    for step in reversed(range(steps)):
        at = slice(step * MINI, (step + 1) * MINI)
        grad = pre_base[at]
        if step + 2 < steps:
            grad = grad - dot_nn(key_mix[at], known_ref[...])
        state_low = state.astype(bf16)
        own_act = act_ref[at, :]
        own_back = own_ref[at, :]
        back_base = back_res_grad[at] - dot_nt(own_act, state_low) - state_b
        act_base = act_grad[at] - dot_nn(own_back, state_low)
        if step + 1 < steps:
            grad = grad - dot_nn(near_mix[at], known_ref[...])
        own_low = second_save[0, step]
        slope = slope_ref[at, :]
        back_act_grad = (grad * slope).astype(bf16)
        upon = back_base + dot_nt(back_act_grad, own_low)
        alpha = row_mean(upon)
        beta = row_mean(upon * normal[at])
        gamma = row_mean(upon * rate_gain[at])
        kappa = row_mean(upon * coef_beta[at])
        level = alpha * mix_alpha[at] + beta * mix_cross[at] + gamma
        tilt = alpha * mix_cross[at] + beta * mix_beta[at] + kappa
        key_res_grad = inverse_square[at] * (
            upon * coef_grad[at]
            - alpha * rate_gain[at]
            - beta * coef_beta[at]
            - level
            - normal[at] * tilt
        )
        key_res_low = key_res_grad.astype(bf16)
        pre_grad = (act_base + dot_nn(key_res_low, own_low)) * slope + grad * curve_ref[at, :]
        pre_lows[step] = pre_grad.astype(bf16)
        known_ref[at, :] = pre_lows[step]
        state = state + dot_tn(jnp.concatenate([key_res_low, own_back], axis=0), jnp.concatenate([own_act, back_act_grad], axis=0))
        state_b = state_b + jnp.sum(key_res_grad, axis=0, keepdims=True)
        back_grads[step] = upon
    pre_grad_all = known_ref[...]
    upon = jnp.concatenate(back_grads, axis=0)
    scaled_grad = inverse * (upon - row_mean(upon) - normal * row_mean(upon * normal))
    error_grad = scaled_grad * (rate * gain)
    rate_grad = jnp.sum(scaled_grad * (base + square_gain * normal), axis=-1, keepdims=True)
    error = miss + normal * gain
    gain_total += jnp.sum(scaled_grad * rate * error + error_grad * normal, axis=0, keepdims=True)
    bias_total += jnp.sum(error_grad, axis=0, keepdims=True)
    far = rows // MINI < cols // MINI
    near = rows // MINI > cols // MINI
    cross = jnp.where(far, dot_nt(grad_pre, pre_grad_all), 0.0)
    cross += jnp.where(near, dot_nt(pre_grad_all, grad_pre), 0.0)
    key_grad = (
        key_grad
        - dot_nt(grad_pre, first_next_low)
        + dot_nt(pre_grad_all, first_low)
        - dot_nn(cross, key)
        + error_grad
    )
    first_w[...] = first_next + dot_tn(key, pre_grad_all) + dot_tn(query, query_pre_low)
    first_b[...] += jnp.sum(pre_grad_all.astype(f32) + query_pre_grad, axis=0, keepdims=True)
    second_w[...] = state + dot_tn(res_grad_low, hidden)
    second_b[...] = state_b + jnp.sum(res_grad, axis=0, keepdims=True)
    gain_sum[...] += gain_total
    bias_sum[...] += bias_total
    back_rate = rate_grad * rate * (1.0 - rate * (1.0 / rate_scale))
    back_ref[:, :HEAD_DIM] = query_grad.astype(bf16)
    back_ref[:, HEAD_DIM : 2 * HEAD_DIM] = key_grad.astype(bf16)
    back_ref[:, 2 * HEAD_DIM : 3 * HEAD_DIM] = (-error_grad).astype(bf16)
    lane = lax.broadcasted_iota(jnp.int32, (chunk, HEAD_DIM), 1)
    back_ref[:, 3 * HEAD_DIM :] = jnp.where(lane == 0, back_rate, 0.0).astype(bf16)

    @pl.when(pl.program_id(0) == pl.num_programs(0) - 1)
    def _():
        first_w_out[...] = first_w[...]
        first_b_out[...] = first_b[...]
        second_w_out[...] = second_w[...]
        second_b_out[...] = second_b[...]
        gain_out[...] = gain_sum[...]
        bias_out[...] = bias_sum[...]


def whole_block(shape):
    return pl.BlockSpec(shape, lambda index: (0,) * len(shape))


STATE_SHAPES = ((HEAD_DIM, INNER), (1, INNER), (HEAD_DIM, INNER), (1, HEAD_DIM))


def saved_layout(length, chunk):
    blocks = length // chunk
    steps = chunk // MINI
    return (
        ((length, INNER), (chunk, INNER), bf16),
        ((length, INNER), (chunk, INNER), bf16),
        ((length, INNER), (chunk, INNER), bf16),
        ((length, INNER), (chunk, INNER), f32),
        ((length, INNER), (chunk, INNER), f32),
        ((length, INNER), (chunk, INNER), f32),
        ((length, 2 * HEAD_DIM), (chunk, 2 * HEAD_DIM), f32),
        ((length, 2 * HEAD_DIM), (chunk, 2 * HEAD_DIM), f32),
        ((blocks, HEAD_DIM, INNER), (1, HEAD_DIM, INNER), bf16),
        ((blocks, steps, HEAD_DIM, INNER), (1, steps, HEAD_DIM, INNER), bf16),
    )


def chain_forward(packed, state, gain, bias, chunk):
    length = packed.shape[0]
    blocks = length // chunk

    def forth(shape):
        return pl.BlockSpec(shape, lambda index: (index,) + (0,) * (len(shape) - 1))

    saved = saved_layout(length, chunk)
    row = (1, HEAD_DIM)
    return pl.pallas_call(
        forward_kernel,
        grid=(blocks,),
        in_specs=[forth((chunk, LANES))]
        + [whole_block(shape) for shape in STATE_SHAPES]
        + [whole_block(row)] * 2,
        out_specs=[forth((chunk, HEAD_DIM))] + [forth(block) for _, block, _ in saved],
        out_shape=[jax.ShapeDtypeStruct((length, HEAD_DIM), bf16)]
        + [jax.ShapeDtypeStruct(shape, dtype) for shape, _, dtype in saved],
        scratch_shapes=[pltpu.VMEM(shape, f32) for shape in STATE_SHAPES]
        + [pltpu.VMEM((chunk, HEAD_DIM), bf16)],
        compiler_params=pltpu.CompilerParams(
            dimension_semantics=("arbitrary",), vmem_limit_bytes=32 * 1024 * 1024
        ),
        name="chain_forward",
    )(packed, *state, gain, bias)


def chain_backward(packed, head_grad, saved_values, gain, bias, chunk):
    length = packed.shape[0]
    blocks = length // chunk

    def back(shape):
        return pl.BlockSpec(
            shape, lambda index: (blocks - 1 - index,) + (0,) * (len(shape) - 1)
        )

    saved = saved_layout(length, chunk)
    row = (1, HEAD_DIM)
    sums = STATE_SHAPES + (row, row)
    return pl.pallas_call(
        backward_kernel,
        grid=(blocks,),
        in_specs=[back((chunk, LANES)), back((chunk, HEAD_DIM))]
        + [back(block) for _, block, _ in saved]
        + [whole_block(row)] * 2,
        out_specs=[back((chunk, LANES))] + [whole_block(shape) for shape in sums],
        out_shape=[jax.ShapeDtypeStruct((length, LANES), bf16)]
        + [jax.ShapeDtypeStruct(shape, f32) for shape in sums],
        scratch_shapes=[pltpu.VMEM(shape, f32) for shape in sums]
        + [pltpu.VMEM((chunk, INNER), bf16), pltpu.VMEM((chunk, HEAD_DIM), bf16)],
        compiler_params=pltpu.CompilerParams(
            dimension_semantics=("arbitrary",), vmem_limit_bytes=32 * 1024 * 1024
        ),
        name="chain_backward",
    )(packed, head_grad, *saved_values, gain, bias)


def layer_norm_parts(values):
    centred = values - row_mean(values)
    inverse = lax.rsqrt(row_mean(centred * centred) + epsilon)
    return centred * inverse, inverse


def layer_norm_back(normal, inverse, scaling, grad):
    scaled = grad * scaling
    return inverse * (scaled - row_mean(scaled) - normal * row_mean(scaled * normal))


def dots(subscripts, left, right):
    return jnp.einsum(subscripts, left, right, preferred_element_type=f32)


def exchange(values, axis):
    return lax.all_to_all(values, axis, 0, 0, tiled=False)


def gather(values, axis):
    return lax.all_gather(values, axis, axis=0, tiled=True)


RATE_LANE = 3 * HEAD_DIM
VECTOR_LANE = RATE_LANE + 2
MATRIX_LANE = LANES - 32


def inner_block(matrix_one, matrix_two, vectors, rows):
    width = matrix_one.shape[-1]
    matrices = jnp.concatenate([matrix_one, matrix_two], axis=-2)
    column = jnp.concatenate(vectors, axis=-1)[..., None]
    lead = [(0, 0)] * (column.ndim - 2)
    column = jnp.pad(
        column,
        lead + [(0, rows - column.shape[-2]), (VECTOR_LANE, LANES - VECTOR_LANE - 1)],
    )
    matrices = jnp.pad(
        matrices,
        lead + [(0, rows - matrices.shape[-2]), (MATRIX_LANE, LANES - MATRIX_LANE - width)],
    )
    return column + matrices


def local(
    tokens,
    gain_attn,
    gain_ffn,
    w_qkv,
    w_rate,
    w_out,
    w_gate_up,
    w_down,
    w_one,
    b_one,
    w_two,
    b_two,
    norm_gain_inner,
    norm_bias_inner,
    cotangent,
):
    device_count = lax.axis_size("dp")
    tensor_count = lax.axis_size("tensor")
    local_rows, seq_count, width = tokens.shape
    row_count = local_rows * seq_count
    chunk = local_rows * tensor_count
    group_rows = chunk * seq_count
    head_count = w_rate.shape[1]
    local_width = head_count * HEAD_DIM
    shard = w_qkv.shape[0]
    part = gain_attn.shape[0]
    ff_local = w_down.shape[0]
    chain_count = seq_count * head_count
    inner_part = w_one.shape[2]
    feature_part = b_two.shape[1]
    assert chain_count <= device_count
    assert chunk % MINI == 0 and chunk >= 2 * HEAD_DIM and inner_part <= 32

    gain_rows = jnp.pad(
        jnp.concatenate([gain_attn, gain_ffn])[None], ((0, 0), (0, width - 2 * part))
    )
    out_rows = w_out.reshape(-1, width)
    row_pack = jnp.concatenate(
        [
            tokens.reshape(row_count, width),
            cotangent.reshape(row_count, width),
            out_rows,
            gain_rows,
        ],
        axis=0,
    )
    row_full = lax.all_gather(row_pack, "tensor", axis=0, tiled=False)
    group_tokens = row_full[:, :row_count].reshape(group_rows, width)
    group_cot = row_full[:, row_count : 2 * row_count].reshape(group_rows, width)
    out_columns = row_full[:, 2 * row_count : 2 * row_count + out_rows.shape[0]].reshape(
        tensor_count * local_width, shard
    )
    own_gains = row_full[:, -1, : 2 * part].reshape(tensor_count, 2, part)
    own_gains = own_gains.transpose(0, 2, 1).reshape(shard, 2)

    qkv_pack = jnp.concatenate([w_qkv.reshape(shard, 3 * local_width), w_rate, own_gains], axis=1)
    qkv_full = gather(qkv_pack, "dp")
    ffn_pack = jnp.concatenate(
        [w_gate_up.reshape(shard, 2 * ff_local), w_down.T, out_columns.T], axis=1
    )
    ffn_full = gather(ffn_pack, "dp")
    gate_up_full = ffn_full[:, : 2 * ff_local]
    down_full = ffn_full[:, 2 * ff_local : 3 * ff_local]
    out_full = ffn_full[:, 3 * ff_local :]
    scale_attn = qkv_full[:, -2].astype(f32)
    scale_ffn = qkv_full[:, -1].astype(f32)

    inputs = group_tokens.astype(f32)
    input_normal, _ = layer_norm_parts(inputs)
    normed_attn = (input_normal * scale_attn).astype(bf16)
    rate_columns = qkv_full[:, 3 * local_width : 3 * local_width + head_count]
    head_matrix = jnp.concatenate(
        [
            qkv_full[:, : 3 * local_width]
            .reshape(width, 3, head_count, HEAD_DIM)
            .transpose(0, 2, 1, 3)
            .reshape(width, head_count, 3 * HEAD_DIM),
            rate_columns[:, :, None],
            rate_columns[:, :, None],
            jnp.zeros((width, head_count, LANES - RATE_LANE - 2), bf16),
        ],
        axis=2,
    )
    projected = dots("rd,dhk->rhk", normed_attn, head_matrix)
    lane = lax.broadcasted_iota(jnp.int32, projected.shape, 2)
    rest = projected - lax.reduce_precision(projected, 8, 7)
    packed = jnp.where(lane == RATE_LANE + 1, rest, projected).astype(bf16)
    packed = packed.reshape(chunk, seq_count, head_count, LANES).transpose(1, 2, 0, 3)
    inner = inner_block(
        w_one,
        w_two.transpose(0, 2, 1),
        [b_one, b_two, norm_gain_inner, norm_bias_inner],
        chunk,
    )
    packed = (packed + inner[None]).reshape(chain_count, chunk, LANES)
    spare = jnp.zeros((device_count - chain_count, chunk, LANES), bf16)
    chain_in = exchange(jnp.concatenate([packed, spare], axis=0), "dp")

    normed_full = gather(normed_attn[None], "dp").reshape(
        device_count * chunk, seq_count, width
    )

    first_w = chain_in[:, :HEAD_DIM, MATRIX_LANE : MATRIX_LANE + inner_part]
    first_w = first_w.transpose(1, 0, 2).reshape(HEAD_DIM, INNER).astype(f32)
    second_w = chain_in[:, HEAD_DIM : 2 * HEAD_DIM, MATRIX_LANE : MATRIX_LANE + inner_part]
    second_w = second_w.transpose(1, 0, 2).reshape(HEAD_DIM, INNER).astype(f32)
    vectors = chain_in[:, :, VECTOR_LANE].astype(f32)
    first_b = vectors[:, :inner_part].reshape(1, INNER)
    small = vectors[:, inner_part : inner_part + 3 * feature_part]
    small = small.reshape(device_count, 3, feature_part).transpose(1, 0, 2).reshape(3, HEAD_DIM)
    second_b, inner_gain, inner_bias = small[0:1], small[1:2], small[2:3]
    second_w = second_w - jnp.mean(second_w, axis=0, keepdims=True)
    second_b = second_b - row_mean(second_b)
    chain_rows = chain_in.reshape(device_count * chunk, LANES)
    forward_out = chain_forward(
        chain_rows, (first_w, first_b, second_w, second_b), inner_gain, inner_bias, chunk
    )
    saved = forward_out[1:]
    head_send = forward_out[0].reshape(device_count, chunk, HEAD_DIM)
    head_back = exchange(head_send, "dp")[:chain_count]
    head_local = (
        head_back.reshape(seq_count, head_count, chunk, HEAD_DIM)
        .transpose(2, 0, 1, 3)
        .reshape(group_rows, local_width)
    )
    head_rows = lax.all_gather(head_local, "tensor", axis=1, tiled=True)

    mixed = inputs + dots("rk,dk->rd", head_rows, out_full)
    ffn_normal, _ = layer_norm_parts(mixed)
    normed_ffn = (ffn_normal * scale_ffn).astype(bf16)
    gate_up = dots("rd,df->rf", normed_ffn, gate_up_full)
    gate, up = gate_up[:, :ff_local], gate_up[:, ff_local:]
    share = jax.nn.sigmoid(gate)
    silu = gate * share
    swiglu = (silu * up).astype(bf16)
    back_swiglu = dots("rd,df->rf", group_cot, down_full)
    back_gate_up = jnp.concatenate(
        [back_swiglu * up * (share * (1.0 + gate * (1.0 - share))), back_swiglu * silu], axis=1
    ).astype(bf16)
    down_term = dots("rf,df->rd", swiglu, down_full).astype(bf16)
    ffn_term = dots("rf,df->rd", back_gate_up, gate_up_full).astype(bf16)
    terms = jnp.stack(
        [
            down_term.reshape(tensor_count, row_count, width),
            ffn_term.reshape(tensor_count, row_count, width),
        ],
        axis=1,
    )
    sums = exchange(terms, "tensor").astype(f32).sum(axis=0)
    rank = lax.axis_index("tensor")
    own_mixed = lax.dynamic_slice_in_dim(mixed, rank * row_count, row_count, 0)
    result = (own_mixed + sums[0]).astype(bf16)
    own_normal, own_inverse = layer_norm_parts(own_mixed)
    back_mixed = cotangent.reshape(row_count, width).astype(f32) + layer_norm_back(
        own_normal, own_inverse, scale_ffn, sums[1]
    )
    attn_grads = gather(back_mixed.astype(bf16), "tensor")
    own_out = lax.dynamic_slice_in_dim(out_full, rank * local_width, local_width, 1)
    back_head = dots("rd,dk->rk", attn_grads, own_out).astype(bf16)
    back_head = (
        back_head.reshape(chunk, seq_count, head_count, HEAD_DIM)
        .transpose(1, 2, 0, 3)
        .reshape(chain_count, chunk, HEAD_DIM)
    )
    spare = jnp.zeros((device_count - chain_count, chunk, HEAD_DIM), bf16)
    head_grad = exchange(jnp.concatenate([back_head, spare], axis=0), "dp")
    head_grad = head_grad.reshape(device_count * chunk, HEAD_DIM)

    matrix_grads = jnp.concatenate(
        [
            dots("rd,rf->df", normed_ffn, back_gate_up),
            dots("rd,rf->df", group_cot, swiglu),
            dots("rd,rk->dk", attn_grads, head_local),
        ],
        axis=1,
    ).astype(bf16)
    matrix_sums = lax.psum_scatter(matrix_grads, "dp", scatter_dimension=0, tiled=True)
    matrix_sums = matrix_sums.astype(f32)

    backward_out = chain_backward(chain_rows, head_grad, saved, inner_gain, inner_bias, chunk)
    back_packed, state_grads = backward_out[0], backward_out[1:]
    sequence = jnp.minimum(lax.axis_index("dp") // head_count, seq_count - 1)
    chain_normed = lax.dynamic_index_in_dim(normed_full, sequence, 1, keepdims=False)
    grad_packed = dots("rd,rk->dk", chain_normed, back_packed).astype(bf16)
    by_part = lambda values: (
        values.reshape(HEAD_DIM, device_count, inner_part).transpose(1, 0, 2).astype(bf16)
    )
    split = lambda values, size: values.reshape(device_count, size).astype(bf16)
    inner_grads = inner_block(
        by_part(state_grads[0]),
        by_part(state_grads[2]),
        [
            split(state_grads[1], inner_part),
            split(state_grads[3], feature_part),
            split(state_grads[4], feature_part),
            split(state_grads[5], feature_part),
        ],
        chunk,
    )
    send = jnp.concatenate(
        [
            back_packed.reshape(device_count, chunk, LANES) + inner_grads,
            grad_packed.reshape(device_count, shard, LANES),
        ],
        axis=1,
    )
    received = exchange(send, "dp")[:chain_count]
    back_rows = received[:, :chunk].reshape(seq_count, head_count, chunk, LANES)
    attn_term = dots("shck,dhk->csd", back_rows, head_matrix_back(head_matrix))
    attn_term = attn_term.reshape(tensor_count, row_count, width).astype(bf16)

    by_head = received.astype(f32).reshape(seq_count, head_count, chunk + shard, LANES).sum(axis=0)
    grad_block = by_head[:, chunk:]
    grad_qkv = (
        grad_block[:, :, :RATE_LANE]
        .reshape(head_count, shard, 3, HEAD_DIM)
        .transpose(1, 2, 0, 3)
        .reshape(shard, 3, local_width)
    )
    grad_rate = grad_block[:, :, RATE_LANE].T
    grad_one = by_head[:, :HEAD_DIM, MATRIX_LANE : MATRIX_LANE + inner_part]
    grad_two = by_head[:, HEAD_DIM : 2 * HEAD_DIM, MATRIX_LANE : MATRIX_LANE + inner_part]
    grad_two = grad_two.transpose(0, 2, 1)
    columns = by_head[:, :, VECTOR_LANE]
    ends = [inner_part + index * feature_part for index in range(4)]
    grad_b_one = columns[:, : ends[0]]
    grad_b_two, grad_gain_inner, grad_bias_inner = (
        columns[:, ends[index] : ends[index + 1]] for index in range(3)
    )

    gain_one = (
        jnp.sum(grad_qkv * w_qkv.astype(f32), axis=(1, 2))
        + jnp.sum(grad_rate * w_rate.astype(f32), axis=1)
    ) / own_gains[:, 0].astype(f32)
    grad_gate_up = matrix_sums[:, : 2 * ff_local].reshape(shard, 2, ff_local)
    gain_two = jnp.sum(grad_gate_up * w_gate_up.astype(f32), axis=(1, 2)) / own_gains[:, 1].astype(
        f32
    )
    gain_terms = jnp.stack([gain_one, gain_two]).reshape(2, tensor_count, part).transpose(1, 0, 2)
    gain_terms = gain_terms.reshape(tensor_count, 1, 2 * part)
    gain_high = gain_terms.astype(bf16)
    gain_low = (gain_terms - lax.reduce_precision(gain_terms, 8, 7)).astype(bf16)
    gain_send = jnp.pad(
        jnp.concatenate([gain_high, gain_low], axis=1), ((0, 0), (0, 0), (0, width - 2 * part))
    )
    tail = exchange(jnp.concatenate([attn_term, gain_send], axis=1), "tensor")
    tail = tail.astype(f32).sum(axis=0)
    gain_sums = tail[row_count, : 2 * part] + tail[row_count + 1, : 2 * part]
    own_inputs = tokens.reshape(row_count, width).astype(f32)
    own_normal, own_inverse = layer_norm_parts(own_inputs)
    input_grad = back_mixed + layer_norm_back(own_normal, own_inverse, scale_attn, tail[:row_count])

    return (
        result.reshape(tokens.shape),
        input_grad.reshape(tokens.shape),
        gain_sums[:part],
        gain_sums[part:],
        grad_qkv,
        grad_rate,
        matrix_sums[:, 3 * ff_local :].T,
        grad_gate_up,
        matrix_sums[:, 2 * ff_local : 3 * ff_local].T,
        grad_one,
        grad_b_one,
        grad_two,
        grad_b_two,
        grad_gain_inner,
        grad_bias_inner,
    )


def head_matrix_back(head_matrix):
    lane = lax.broadcasted_iota(jnp.int32, head_matrix.shape, 2)
    return jnp.where(lane <= RATE_LANE, head_matrix, jnp.zeros_like(head_matrix))


def solution(mesh):
    rows = P(("dp", "tensor"), None, None)
    gains = P(("dp", "tensor"))
    placed = (
        rows,
        gains,
        gains,
        P("dp", None, "tensor"),
        P("dp", "tensor"),
        P("tensor", "dp"),
        P("dp", None, "tensor"),
        P("tensor", "dp"),
        P("tensor", None, "dp"),
        P("tensor", "dp"),
        P("tensor", "dp", None),
        P("tensor", "dp"),
        P("tensor", "dp"),
        P("tensor", "dp"),
    )
    return jax.shard_map(
        local,
        mesh=mesh,
        in_specs=placed + (rows,),
        out_specs=(rows,) + placed,
        check_vma=False,
    )
```

```python
import functools


import jax
import jax.numpy as jnp
from jax import lax
from jax.experimental import pallas as pl
from jax.experimental.pallas import tpu as pltpu
from jax.sharding import PartitionSpec as P

HEAD_DIM = 64
INNER = 256
MINI = 16
LANES = 256
RATE_LANE = 3 * HEAD_DIM
VECTOR_LANE = RATE_LANE + 2
MATRIX_LANE = LANES - 32
VMEM_BYTES = 56 * 1024 * 1024
GLUE_BYTES = 32 * 1024 * 1024

epsilon = 1e-05
inner_epsilon = 1e-06
inner_rate = 0.5
rate_scale = inner_rate / (MINI * HEAD_DIM)
root_half = 0.7071067811865476
normal_peak = 0.3989422804014327

f32 = jnp.float32
bf16 = jnp.bfloat16


def dot_nn(a, b):
    return lax.dot_general(
        a.astype(bf16), b.astype(bf16), (((1,), (0,)), ((), ())), preferred_element_type=f32
    )


def dot_nt(a, b):
    return lax.dot_general(
        a.astype(bf16), b.astype(bf16), (((1,), (1,)), ((), ())), preferred_element_type=f32
    )


def dot_tn(a, b):
    return lax.dot_general(
        a.astype(bf16), b.astype(bf16), (((0,), (0,)), ((), ())), preferred_element_type=f32
    )


def row_mean(values):
    return jnp.mean(values, axis=-1, keepdims=True)


def density_and_share(values):
    density = jnp.exp(-0.5 * values * values) * normal_peak
    share = 0.5 * (1.0 + lax.erf(values * root_half))
    return density, share


def token_grid(count):
    rows = lax.broadcasted_iota(jnp.int32, (count, count), 0)
    cols = lax.broadcasted_iota(jnp.int32, (count, count), 1)
    return rows, cols


def unpack_chunk(packed, bias):
    query = packed[:, :HEAD_DIM]
    key = packed[:, HEAD_DIM : 2 * HEAD_DIM]
    value = packed[:, 2 * HEAD_DIM : 3 * HEAD_DIM]
    tail = packed[:, 3 * HEAD_DIM :].astype(f32)
    rate = jax.nn.sigmoid(tail[:, 0:1] + tail[:, 1:2]) * rate_scale
    miss = key.astype(f32) - value.astype(f32) + bias
    return query, key, rate, miss


def forward_kernel(
    inner_part,
    feature_part,
    packed_ref,
    normed_ref,
    act_ref,
    grad_pre_ref,
    hidden_ref,
    slope_ref,
    curve_ref,
    out_slope_ref,
    norms_ref,
    stats_ref,
    first_save,
    second_save,
    gain_ref,
    bias_ref,
    first_w,
    first_b,
    second_w,
    second_b,
    back_res_ref,
):
    devices, chunk, _ = packed_ref.shape

    @pl.when(pl.program_id(0) == 0)
    def _():
        for index in range(devices):
            block = packed_ref[index, :, LANES - 128 :].astype(f32)
            first = slice(index * inner_part, (index + 1) * inner_part)
            lanes = slice(MATRIX_LANE - LANES + 128, MATRIX_LANE - LANES + 128 + inner_part)
            first_w[:, first] = block[:HEAD_DIM, lanes]
            second_w[:, first] = block[HEAD_DIM : 2 * HEAD_DIM, lanes]
            at = VECTOR_LANE - LANES + 128
            vector = jnp.transpose(block)[at : at + 1]
            first_b[:, first] = vector[:, :inner_part]
            small = slice(index * feature_part, (index + 1) * feature_part)
            for number, target in enumerate((second_b, gain_ref, bias_ref)):
                start = inner_part + number * feature_part
                target[:, small] = vector[:, start : start + feature_part]
        centred = second_w[...]
        second_w[...] = centred - jnp.mean(centred, axis=0, keepdims=True)
        second_b[...] = second_b[...] - row_mean(second_b[...])

    gain = gain_ref[...]
    bias = bias_ref[...]
    steps = chunk // MINI
    query, key, rate, miss = unpack_chunk(packed_ref[pl.program_id(0)], bias)
    base = miss * gain
    rate_base = rate * base
    rate_gain = rate * (gain * gain)
    base_mean = row_mean(rate_base)
    rows, cols = token_grid(chunk)
    before = cols // MINI + 1 < rows // MINI
    key_mix = jnp.where(before, dot_nt(key, key) + 1.0, 0.0).astype(bf16)
    first_low = first_w[...].astype(bf16)
    first_save[0] = first_low
    pre_all = dot_nn(key, first_low) + first_b[...]
    state = second_w[...]
    state_b = second_b[...]
    start_low = state.astype(bf16)
    start_b = state_b
    last_grad = None
    grads, acts, backs = [], [], []
    for step in range(steps):
        at = slice(step * MINI, (step + 1) * MINI)
        pre = pre_all[at]
        if step >= 2:
            past = (step - 1) * MINI
            older = jnp.concatenate(grads[: step - 1], axis=0) if step > 2 else grads[0]
            pre = pre - dot_nn(key_mix[at, :past], older)
        if step >= 1:
            pre = pre - dot_nn(
                dot_nt(key[at], key[(step - 1) * MINI : step * MINI]) + 1.0, last_grad
            )
        density, share = density_and_share(pre)
        act = (pre * share).astype(bf16)
        slope = share + pre * density
        state_low = state.astype(bf16)
        second_save[0, step] = state_low
        res = dot_nt(act, state_low) + state_b
        weighted = rate_gain[at] * res
        square = jnp.sum(res * res, axis=-1, keepdims=True)
        sum_gain = jnp.sum(weighted, axis=-1, keepdims=True)
        sum_base = jnp.sum(rate_base[at] * res, axis=-1, keepdims=True)
        sum_square = jnp.sum(weighted * res, axis=-1, keepdims=True)
        inverse = lax.rsqrt(square * (1.0 / HEAD_DIM) + inner_epsilon)
        scaled_mean = base_mean[at] + inverse * sum_gain * (1.0 / HEAD_DIM)
        along = inverse * (sum_base + inverse * sum_square) * (1.0 / HEAD_DIM)
        normal = res * inverse
        back_res = inverse * (rate_base[at] + rate_gain[at] * normal - scaled_mean - normal * along)
        back_low = back_res.astype(bf16)
        back_act = dot_nn(back_low, state_low)
        last_grad = (back_act * slope).astype(bf16)
        state = state - dot_tn(back_low, act)
        state_b = state_b - jnp.sum(back_res, axis=0, keepdims=True)
        grads.append(last_grad)
        acts.append(act)
        backs.append(back_low)
        slope_ref[at, :] = slope
        curve_ref[at, :] = back_act * density * (2.0 - pre * pre)
        act_ref[at, :] = act
        grad_pre_ref[at, :] = last_grad
        back_res_ref[at, :] = back_low
        norms_ref[at, :HEAD_DIM] = normal
        stats_ref[at, HEAD_DIM : HEAD_DIM + 1] = inverse
    grad_all = grad_pre_ref[...]
    act_all = act_ref[...]
    back_all = back_res_ref[...]
    start_first_b = first_b[...]
    first_w[...] = first_w[...] - dot_tn(key, grad_all)
    first_b[...] = start_first_b - jnp.sum(grad_all.astype(f32), axis=0, keepdims=True)
    second_w[...] = state
    second_b[...] = state_b

    causal = cols <= rows
    first_mix = jnp.where(causal, dot_nt(query, key) + 1.0, 0.0)
    query_pre = dot_nn(query, first_low) + start_first_b - dot_nn(first_mix, grad_all)
    density, share = density_and_share(query_pre)
    hidden = (query_pre * share).astype(bf16)
    out_slope_ref[...] = share + query_pre * density
    hidden_ref[...] = hidden
    second_mix = jnp.where(causal, dot_nt(hidden, act_all) + 1.0, 0.0)
    query_res = dot_nt(hidden, start_low) + start_b - dot_nn(second_mix, back_all)
    out_inverse = lax.rsqrt(row_mean(query_res * query_res) + inner_epsilon)
    out_normal = query_res * out_inverse
    norms_ref[:, HEAD_DIM:] = out_normal
    outputs = query.astype(f32) + out_normal * gain + bias
    centred = outputs - row_mean(outputs)
    head_inverse = lax.rsqrt(row_mean(centred * centred) + epsilon)
    head_normal = centred * head_inverse
    stats_ref[:, :HEAD_DIM] = head_normal
    stats_ref[:, HEAD_DIM + 1 : HEAD_DIM + 2] = out_inverse
    stats_ref[:, HEAD_DIM + 2 : HEAD_DIM + 3] = head_inverse
    normed_ref[0] = jnp.transpose(head_normal).astype(bf16)


def backward_kernel(
    inner_part,
    feature_part,
    packed_ref,
    head_grad_ref,
    act_ref,
    grad_pre_ref,
    hidden_ref,
    slope_ref,
    curve_ref,
    out_slope_ref,
    norms_ref,
    stats_ref,
    first_save,
    second_save,
    gain_ref,
    bias_ref,
    back_ref,
    first_w,
    first_b,
    second_w,
    second_b,
    gain_sum,
    bias_sum,
    known_ref,
    own_ref,
    vector_ref,
):
    @pl.when(pl.program_id(0) == 0)
    def _():
        first_w[...] = jnp.zeros_like(first_w)
        first_b[...] = jnp.zeros_like(first_b)
        second_w[...] = jnp.zeros_like(second_w)
        second_b[...] = jnp.zeros_like(second_b)
        gain_sum[...] = jnp.zeros_like(gain_sum)
        bias_sum[...] = jnp.zeros_like(bias_sum)
        known_ref[...] = jnp.zeros_like(known_ref)

    gain = gain_ref[...]
    bias = bias_ref[...]
    devices, chunk, _ = packed_ref.shape
    steps = chunk // MINI
    place = devices - 1 - pl.program_id(0)
    query, key, rate, miss = unpack_chunk(packed_ref[place], bias)
    base = miss * gain
    rate_base = rate * base
    square_gain = gain * gain
    rate_gain = rate * square_gain
    normal = norms_ref[:, :HEAD_DIM]
    out_normal = norms_ref[:, HEAD_DIM:]
    head_normal = stats_ref[:, :HEAD_DIM]
    inverse = stats_ref[:, HEAD_DIM : HEAD_DIM + 1]
    out_inverse = stats_ref[:, HEAD_DIM + 1 : HEAD_DIM + 2]
    head_inverse = stats_ref[:, HEAD_DIM + 2 : HEAD_DIM + 3]
    act = act_ref[...]
    grad_pre = grad_pre_ref[...]
    hidden = hidden_ref[...]
    first_low = first_save[0]
    start_low = second_save[0, 0]
    gain_normal = rate_gain * normal
    scaled = rate_base + gain_normal
    scaled_mean = row_mean(scaled)
    along = row_mean(scaled * normal)
    back_res = (inverse * (scaled - scaled_mean - normal * along)).astype(bf16)
    coef_grad = rate_gain - along
    coef_beta = gain_normal + scaled
    gain_along = row_mean(gain_normal)
    gain_square = row_mean(gain_normal * normal)
    gain_level = row_mean(rate_gain)
    mix_cross = -(gain_along + scaled_mean)
    mix_beta = -(3.0 * along + gain_square)
    mix_alpha = -(along + gain_level)
    inverse_square = inverse * inverse

    rows, cols = token_grid(chunk)
    causal = cols <= rows
    later = rows <= cols
    head_grad = jnp.transpose(head_grad_ref[0].astype(f32))
    out_grad = head_inverse * (
        head_grad - row_mean(head_grad) - head_normal * row_mean(head_grad * head_normal)
    )
    gain_total = jnp.sum(out_grad * out_normal, axis=0, keepdims=True)
    bias_total = jnp.sum(out_grad, axis=0, keepdims=True)
    normal_grad = out_grad * gain
    res_grad = out_inverse * (
        normal_grad - row_mean(normal_grad) - out_normal * row_mean(normal_grad * out_normal)
    )
    res_grad_low = res_grad.astype(bf16)
    second_mix_grad = jnp.where(causal, -dot_nt(res_grad_low, back_res), 0.0)
    second_mix_grad_t = jnp.where(later, -dot_nt(back_res, res_grad_low), 0.0)
    hidden_grad = dot_nn(res_grad_low, start_low) + dot_nn(second_mix_grad, act)
    query_pre_grad = hidden_grad * out_slope_ref[...]
    query_pre_low = query_pre_grad.astype(bf16)
    first_mix_grad = jnp.where(causal, -dot_nt(query_pre_low, grad_pre), 0.0)
    first_mix_grad_t = jnp.where(later, -dot_nt(grad_pre, query_pre_low), 0.0)
    query_grad = out_grad + dot_nt(query_pre_low, first_low) + dot_nn(first_mix_grad, key)
    key_grad = dot_nn(first_mix_grad_t, query)
    act_grad = dot_nn(second_mix_grad_t, hidden)
    second_mix_t = jnp.where(later, dot_nt(act, hidden) + 1.0, 0.0)
    back_res_grad = -dot_nn(second_mix_t, res_grad_low)
    first_mix_t = jnp.where(later, dot_nt(key, query) + 1.0, 0.0)
    first_next = first_w[...]
    first_next_low = first_next.astype(bf16)
    pre_base = (
        -dot_nn(first_mix_t, query_pre_low) - dot_nn(key, first_next_low) - first_b[...]
    )
    after = cols // MINI > rows // MINI + 1
    near_mix = jnp.where(cols // MINI == rows // MINI + 1, dot_nt(key, key) + 1.0, 0.0).astype(bf16)
    key_mix = jnp.where(after, dot_nt(key, key) + 1.0, 0.0).astype(bf16)

    state = second_w[...]
    state_b = second_b[...]
    own_ref[...] = back_res
    pre_lows = [None] * steps
    back_grads = [None] * steps
    for step in reversed(range(steps)):
        at = slice(step * MINI, (step + 1) * MINI)
        grad = pre_base[at]
        if step + 2 < steps:
            grad = grad - dot_nn(key_mix[at], known_ref[...])
        state_low = state.astype(bf16)
        own_act = act_ref[at, :]
        own_back = own_ref[at, :]
        back_base = back_res_grad[at] - dot_nt(own_act, state_low) - state_b
        act_base = act_grad[at] - dot_nn(own_back, state_low)
        if step + 1 < steps:
            grad = grad - dot_nn(near_mix[at], known_ref[...])
        own_low = second_save[0, step]
        slope = slope_ref[at, :]
        back_act_grad = (grad * slope).astype(bf16)
        upon = back_base + dot_nt(back_act_grad, own_low)
        alpha = row_mean(upon)
        beta = row_mean(upon * normal[at])
        gamma = row_mean(upon * rate_gain[at])
        kappa = row_mean(upon * coef_beta[at])
        level = alpha * mix_alpha[at] + beta * mix_cross[at] + gamma
        tilt = alpha * mix_cross[at] + beta * mix_beta[at] + kappa
        key_res_grad = inverse_square[at] * (
            upon * coef_grad[at]
            - alpha * rate_gain[at]
            - beta * coef_beta[at]
            - level
            - normal[at] * tilt
        )
        key_res_low = key_res_grad.astype(bf16)
        pre_grad = (act_base + dot_nn(key_res_low, own_low)) * slope + grad * curve_ref[at, :]
        pre_lows[step] = pre_grad.astype(bf16)
        known_ref[at, :] = pre_lows[step]
        state = state + dot_tn(jnp.concatenate([key_res_low, own_back], axis=0), jnp.concatenate([own_act, back_act_grad], axis=0))
        state_b = state_b + jnp.sum(key_res_grad, axis=0, keepdims=True)
        back_grads[step] = upon
    pre_grad_all = known_ref[...]
    upon = jnp.concatenate(back_grads, axis=0)
    scaled_grad = inverse * (upon - row_mean(upon) - normal * row_mean(upon * normal))
    error_grad = scaled_grad * (rate * gain)
    rate_grad = jnp.sum(scaled_grad * (base + square_gain * normal), axis=-1, keepdims=True)
    error = miss + normal * gain
    gain_total += jnp.sum(scaled_grad * rate * error + error_grad * normal, axis=0, keepdims=True)
    bias_total += jnp.sum(error_grad, axis=0, keepdims=True)
    far = rows // MINI < cols // MINI
    near = rows // MINI > cols // MINI
    cross = jnp.where(far, dot_nt(grad_pre, pre_grad_all), 0.0)
    cross += jnp.where(near, dot_nt(pre_grad_all, grad_pre), 0.0)
    key_grad = (
        key_grad
        - dot_nt(grad_pre, first_next_low)
        + dot_nt(pre_grad_all, first_low)
        - dot_nn(cross, key)
        + error_grad
    )
    first_w[...] = first_next + dot_tn(key, pre_grad_all) + dot_tn(query, query_pre_low)
    first_b[...] += jnp.sum(pre_grad_all.astype(f32) + query_pre_grad, axis=0, keepdims=True)
    second_w[...] = state + dot_tn(res_grad_low, hidden)
    second_b[...] = state_b + jnp.sum(res_grad, axis=0, keepdims=True)
    gain_sum[...] += gain_total
    bias_sum[...] += bias_total
    back_rate = rate_grad * rate * (1.0 - rate * (1.0 / rate_scale))
    back_ref[place, :, :HEAD_DIM] = query_grad.astype(bf16)
    back_ref[place, :, HEAD_DIM : 2 * HEAD_DIM] = key_grad.astype(bf16)
    back_ref[place, :, 2 * HEAD_DIM : 3 * HEAD_DIM] = (-error_grad).astype(bf16)
    lane = lax.broadcasted_iota(jnp.int32, (chunk, HEAD_DIM), 1)
    back_ref[place, :, 3 * HEAD_DIM :] = jnp.where(lane == 0, back_rate, 0.0).astype(bf16)

    @pl.when(pl.program_id(0) == devices - 1)
    def _():
        vector_ref[...] = jnp.zeros_like(vector_ref)
        for index in range(devices):
            first = slice(index * inner_part, (index + 1) * inner_part)
            small = slice(index * feature_part, (index + 1) * feature_part)
            vector_ref[index : index + 1, :inner_part] = first_b[:, first]
            for number, source in enumerate((second_b, gain_sum, bias_sum)):
                start = inner_part + number * feature_part
                vector_ref[index : index + 1, start : start + feature_part] = source[:, small]
        columns = jnp.transpose(vector_ref[...]).astype(bf16)
        lanes = slice(MATRIX_LANE, MATRIX_LANE + inner_part)
        for index in range(devices):
            first = slice(index * inner_part, (index + 1) * inner_part)
            back_ref[index, :HEAD_DIM, lanes] = first_w[:, first].astype(bf16)
            back_ref[index, HEAD_DIM : 2 * HEAD_DIM, lanes] = second_w[:, first].astype(bf16)
            back_ref[index, :, VECTOR_LANE : VECTOR_LANE + 1] = columns[:, index : index + 1]


def whole_block(shape):
    return pl.BlockSpec(shape, lambda index: (0,) * len(shape))


STATE_SHAPES = ((HEAD_DIM, INNER), (1, INNER), (HEAD_DIM, INNER), (1, HEAD_DIM))


def saved_layout(length, chunk):
    blocks = length // chunk
    steps = chunk // MINI
    return (
        ((length, INNER), (chunk, INNER), bf16),
        ((length, INNER), (chunk, INNER), bf16),
        ((length, INNER), (chunk, INNER), bf16),
        ((length, INNER), (chunk, INNER), f32),
        ((length, INNER), (chunk, INNER), f32),
        ((length, INNER), (chunk, INNER), f32),
        ((length, 2 * HEAD_DIM), (chunk, 2 * HEAD_DIM), f32),
        ((length, 2 * HEAD_DIM), (chunk, 2 * HEAD_DIM), f32),
        ((blocks, HEAD_DIM, INNER), (1, HEAD_DIM, INNER), bf16),
        ((blocks, steps, HEAD_DIM, INNER), (1, steps, HEAD_DIM, INNER), bf16),
    )


def chain_forward(packed, inner_part, feature_part):
    blocks, chunk, _ = packed.shape

    def forth(shape):
        return pl.BlockSpec(shape, lambda index: (index,) + (0,) * (len(shape) - 1))

    saved = saved_layout(blocks * chunk, chunk)
    row = (1, HEAD_DIM)
    return pl.pallas_call(
        functools.partial(forward_kernel, inner_part, feature_part),
        grid=(blocks,),
        in_specs=[whole_block(packed.shape)],
        out_specs=[forth((1, HEAD_DIM, chunk))]
        + [forth(block) for _, block, _ in saved]
        + [whole_block(row)] * 2,
        out_shape=[jax.ShapeDtypeStruct((blocks, HEAD_DIM, chunk), bf16)]
        + [jax.ShapeDtypeStruct(shape, dtype) for shape, _, dtype in saved]
        + [jax.ShapeDtypeStruct(row, f32)] * 2,
        scratch_shapes=[pltpu.VMEM(shape, f32) for shape in STATE_SHAPES]
        + [pltpu.VMEM((chunk, HEAD_DIM), bf16)],
        compiler_params=pltpu.CompilerParams(
            dimension_semantics=("arbitrary",), vmem_limit_bytes=VMEM_BYTES
        ),
        name="chain_forward",
    )(packed)


def chain_backward(packed, head_grad, saved_values, inner_part, feature_part):
    blocks, chunk, _ = packed.shape

    def back(shape):
        return pl.BlockSpec(
            shape, lambda index: (blocks - 1 - index,) + (0,) * (len(shape) - 1)
        )

    saved = saved_layout(blocks * chunk, chunk)
    row = (1, HEAD_DIM)
    return pl.pallas_call(
        functools.partial(backward_kernel, inner_part, feature_part),
        grid=(blocks,),
        in_specs=[whole_block(packed.shape), back((1, HEAD_DIM, chunk))]
        + [back(block) for _, block, _ in saved]
        + [whole_block(row)] * 2,
        out_specs=whole_block(packed.shape),
        out_shape=jax.ShapeDtypeStruct(packed.shape, bf16),
        scratch_shapes=[pltpu.VMEM(shape, f32) for shape in STATE_SHAPES + (row, row)]
        + [
            pltpu.VMEM((chunk, INNER), bf16),
            pltpu.VMEM((chunk, HEAD_DIM), bf16),
            pltpu.VMEM((chunk, 128), f32),
        ],
        compiler_params=pltpu.CompilerParams(
            dimension_semantics=("arbitrary",), vmem_limit_bytes=VMEM_BYTES
        ),
        name="chain_backward",
    )(packed, head_grad, *saved_values)


def layer_norm_parts(values):
    centred = values - row_mean(values)
    inverse = lax.rsqrt(row_mean(centred * centred) + epsilon)
    return centred * inverse, inverse


def layer_norm_back(normal, inverse, scaling, grad):
    scaled = grad * scaling
    return inverse * (scaled - row_mean(scaled) - normal * row_mean(scaled * normal))


def start_kernel(
    head_count,
    rows_ref,
    weights_ref,
    gain_ref,
    inner_ref,
    packed_ref,
    normed_ref,
    matrix_ref,
):
    tensor_count = rows_ref.shape[0]
    seq_count, chunk, _ = normed_ref.shape
    rows = chunk // tensor_count
    matrix_ref[...] = jnp.zeros_like(matrix_ref)
    for head in range(head_count):
        first = head * 3 * HEAD_DIM
        rate = head_count * 3 * HEAD_DIM + head
        column = weights_ref[:, rate : rate + 1]
        matrix_ref[head, :, : 3 * HEAD_DIM] = weights_ref[:, first : first + 3 * HEAD_DIM]
        matrix_ref[head, :, RATE_LANE : RATE_LANE + 1] = column
        matrix_ref[head, :, RATE_LANE + 1 : RATE_LANE + 2] = column
    lane = lax.broadcasted_iota(jnp.int32, (chunk, LANES), 1)
    for sequence in range(seq_count):
        part = slice(sequence * rows, (sequence + 1) * rows)
        values = jnp.concatenate([rows_ref[index, part] for index in range(tensor_count)], axis=0)
        normal, _ = layer_norm_parts(values.astype(f32))
        normed = (normal * gain_ref[...]).astype(bf16)
        normed_ref[sequence] = normed
        for head in range(head_count):
            projected = dot_nn(normed, matrix_ref[head])
            rest = projected - projected.astype(bf16).astype(f32)
            projected = jnp.where(lane == RATE_LANE + 1, rest, projected).astype(bf16)
            packed_ref[head * seq_count + sequence] = jnp.where(
                lane >= VECTOR_LANE, inner_ref[head], projected
            )
    for index in range(head_count * seq_count, packed_ref.shape[0]):
        packed_ref[index] = jnp.zeros((chunk, LANES), bf16)


def feed_forward_kernel(
    heads_ref,
    rows_ref,
    weights_ref,
    out_ref,
    gain_ref,
    terms_ref,
    mixed_ref,
    normed_ref,
    back_ref,
    swiglu_ref,
    cot_ref,
):
    tensor_count, head_count, seq_count, _, chunk = heads_ref.shape
    ff_local = swiglu_ref.shape[1]
    rows = chunk // tensor_count
    total = seq_count * chunk
    for sequence in range(seq_count):
        part = slice(sequence * rows, (sequence + 1) * rows)
        other = slice((seq_count + sequence) * rows, (seq_count + sequence + 1) * rows)
        values = jnp.concatenate([rows_ref[index, part] for index in range(tensor_count)], axis=0)
        mixed = values.astype(f32)
        for index in range(tensor_count):
            heads = [heads_ref[index, head, sequence] for head in range(head_count)]
            heads = jnp.transpose(jnp.concatenate(heads, axis=0).astype(f32))
            mixed = mixed + dot_nt(heads, out_ref[index])
        for index in range(tensor_count):
            mixed_ref[index, sequence] = mixed[index * rows : (index + 1) * rows]
        normal, _ = layer_norm_parts(mixed)
        at = slice(sequence * chunk, (sequence + 1) * chunk)
        normed_ref[at] = (normal * gain_ref[...]).astype(bf16)
        for index in range(tensor_count):
            first = sequence * chunk + index * rows
            cot_ref[first : first + rows] = rows_ref[index, other]
    normed = normed_ref[...]
    cot = cot_ref[...]
    for first in range(0, ff_local, 256):
        at = slice(first, first + 256)
        beyond = slice(ff_local + first, ff_local + first + 256)
        gate = dot_nn(normed, weights_ref[:, at])
        up = dot_nn(normed, weights_ref[:, beyond])
        back = dot_nn(cot, weights_ref[:, 2 * ff_local + first : 2 * ff_local + first + 256])
        share = jax.nn.sigmoid(gate)
        silu = gate * share
        swiglu_ref[:, at] = (silu * up).astype(bf16)
        back_ref[:, at] = (back * up * (share * (1.0 + gate * (1.0 - share)))).astype(bf16)
        back_ref[:, beyond] = (back * silu).astype(bf16)
    ffn_term = dot_nt(back_ref[...], weights_ref[:, : 2 * ff_local]).astype(bf16)
    down_term = dot_nt(swiglu_ref[...], weights_ref[:, 2 * ff_local : 3 * ff_local]).astype(bf16)
    for sequence in range(seq_count):
        for index in range(tensor_count):
            first = sequence * chunk + index * rows
            terms_ref[index, sequence] = ffn_term[first : first + rows]
            terms_ref[index, seq_count + sequence] = down_term[first : first + rows]


def feed_forward_grad_kernel(normed_ref, back_ref, swiglu_ref, cot_ref, grads_ref):
    normed = jnp.transpose(normed_ref[...].astype(f32)).astype(bf16)
    cot = jnp.transpose(cot_ref[...].astype(f32)).astype(bf16)
    width = back_ref.shape[1]
    for first in range(0, width, 256):
        at = slice(first, first + 256)
        grads_ref[:, at] = dot_nn(normed, back_ref[:, at]).astype(bf16)
    for first in range(0, swiglu_ref.shape[1], 256):
        at = slice(width + first, width + first + 256)
        grads_ref[:, at] = dot_nn(cot, swiglu_ref[:, first : first + 256]).astype(bf16)


def head_back_kernel(grads_ref, out_ref, heads_ref, back_ref, out_grad_ref):
    head_count, seq_count, _, chunk = heads_ref.shape
    devices, shard, _ = out_grad_ref.shape
    total = None
    for sequence in range(seq_count):
        grads = grads_ref[sequence]
        back = jnp.transpose(dot_nn(grads, out_ref[...])).astype(bf16)
        for head in range(head_count):
            back_ref[head * seq_count + sequence] = back[head * HEAD_DIM : (head + 1) * HEAD_DIM]
        heads = [heads_ref[head, sequence] for head in range(head_count)]
        term = dot_nt(jnp.transpose(grads.astype(f32)), jnp.concatenate(heads, axis=0))
        total = term if total is None else total + term
    for index in range(head_count * seq_count, devices):
        back_ref[index] = jnp.zeros((HEAD_DIM, chunk), bf16)
    for index in range(devices):
        out_grad_ref[index] = total[index * shard : (index + 1) * shard].astype(bf16)


def attention_term_kernel(rows_ref, matrix_ref, terms_ref):
    head_count = matrix_ref.shape[0]
    tensor_count, seq_count, rows, _ = terms_ref.shape
    chunk = tensor_count * rows
    lane = lax.broadcasted_iota(jnp.int32, (chunk, LANES), 1)
    for sequence in range(seq_count):
        total = None
        for head in range(head_count):
            values = rows_ref[head * seq_count + sequence]
            values = jnp.where(lane <= RATE_LANE, values, jnp.zeros_like(values))
            term = dot_nt(values, matrix_ref[head])
            total = term if total is None else total + term
        for index in range(tensor_count):
            part = total[index * rows : (index + 1) * rows]
            terms_ref[index, sequence] = part.astype(bf16)


def whole_call(kernel, name, operands, results, vmem_bytes=GLUE_BYTES):
    def spec(shape):
        return pl.BlockSpec(shape, lambda: (0,) * len(shape))

    return pl.pallas_call(
        kernel,
        in_specs=[spec(operand.shape) for operand in operands],
        out_specs=[spec(result.shape) for result in results],
        out_shape=results,
        compiler_params=pltpu.CompilerParams(vmem_limit_bytes=vmem_bytes),
        name=name,
    )(*operands)


def dots(subscripts, left, right):
    return jnp.einsum(subscripts, left, right, preferred_element_type=f32)


def exchange(values, axis):
    return lax.all_to_all(values, axis, 0, 0, tiled=False)


def share_out(values, axis):
    count = lax.axis_size(axis)
    return exchange(jnp.broadcast_to(values[None], (count,) + values.shape), axis)


def ordered(first, then):
    return lax.optimization_barrier((first, then))


def inner_block(matrix_one, matrix_two, vectors, rows):
    width = matrix_one.shape[-1]
    matrices = jnp.concatenate([matrix_one, matrix_two], axis=-2)
    column = jnp.concatenate(vectors, axis=-1)[..., None]
    lead = [(0, 0)] * (column.ndim - 2)
    column = jnp.pad(
        column,
        lead + [(0, rows - column.shape[-2]), (VECTOR_LANE, LANES - VECTOR_LANE - 1)],
    )
    matrices = jnp.pad(
        matrices,
        lead + [(0, rows - matrices.shape[-2]), (MATRIX_LANE, LANES - MATRIX_LANE - width)],
    )
    return column + matrices


def local(
    tokens,
    gain_attn,
    gain_ffn,
    w_qkv,
    w_rate,
    w_out,
    w_gate_up,
    w_down,
    w_one,
    b_one,
    w_two,
    b_two,
    norm_gain_inner,
    norm_bias_inner,
    cotangent,
):
    device_count = lax.axis_size("dp")
    tensor_count = lax.axis_size("tensor")
    local_rows, seq_count, width = tokens.shape
    row_count = local_rows * seq_count
    chunk = local_rows * tensor_count
    head_count = w_rate.shape[1]
    local_width = head_count * HEAD_DIM
    shard = w_qkv.shape[0]
    part = gain_attn.shape[0]
    ff_local = w_down.shape[0]
    chain_count = seq_count * head_count
    inner_part = w_one.shape[2]
    feature_part = b_two.shape[1]
    assert chain_count <= device_count
    assert chunk == 2 * HEAD_DIM and inner_part <= 32 and part <= shard
    rank = lax.axis_index("tensor")
    place = lax.axis_index("dp")

    own_tokens = tokens.transpose(1, 0, 2).reshape(row_count, width)
    own_cot = cotangent.transpose(1, 0, 2).reshape(row_count, width)
    row_full = share_out(jnp.concatenate([own_tokens, own_cot], axis=0), "tensor")
    head_columns = w_qkv.reshape(shard, 3, head_count, HEAD_DIM).transpose(0, 2, 1, 3)
    gain_columns = jnp.pad(jnp.stack([gain_attn, gain_ffn], axis=1), ((0, shard - part), (0, 0)))
    qkv_pack = jnp.concatenate(
        [head_columns.reshape(shard, 3 * local_width), w_rate, gain_columns], axis=1
    )
    qkv_full = lax.all_gather(qkv_pack, "dp", axis=0, tiled=True)
    qkv_full, row_full = ordered(qkv_full, row_full)
    some_gains = qkv_full[:, 3 * local_width + head_count :]
    some_gains = some_gains.reshape(device_count, shard, 2)[:, :part].transpose(2, 0, 1)
    gains = lax.all_gather(some_gains.reshape(2, device_count * part), "tensor", axis=0)
    gains = gains.reshape(tensor_count, 2, device_count, part).transpose(1, 2, 0, 3)
    gains = gains.reshape(2, width).astype(f32)
    scale_attn, scale_ffn = gains[0:1], gains[1:2]

    ffn_pack = jnp.concatenate(
        [w_gate_up.reshape(shard, 2 * ff_local), w_down.T, w_out.T], axis=1
    )
    ffn_full = lax.all_gather(ffn_pack, "dp", axis=0, tiled=True)
    own_out = ffn_full[:, 3 * ff_local :]

    inner = inner_block(
        w_one,
        w_two.transpose(0, 2, 1),
        [b_one, b_two, norm_gain_inner, norm_bias_inner],
        chunk,
    )
    shape = jax.ShapeDtypeStruct
    packed, normed_attn, head_matrix = whole_call(
        functools.partial(start_kernel, head_count),
        "projections",
        (row_full, qkv_full, scale_attn, inner),
        (
            shape((device_count, chunk, LANES), bf16),
            shape((seq_count, chunk, width), bf16),
            shape((head_count, width, LANES), bf16),
        ),
    )
    chain_in = exchange(packed, "dp")
    chain_in, own_out = ordered(chain_in, own_out)
    out_full = lax.all_gather(own_out, "tensor", axis=0)

    normed_full = lax.all_gather(normed_attn, "dp", axis=1, tiled=False)

    forward_out = chain_forward(chain_in, inner_part, feature_part)
    saved = forward_out[1:]
    head_local = exchange(forward_out[0], "dp")[:chain_count]
    head_local = head_local.reshape(head_count, seq_count, HEAD_DIM, chunk)
    head_rows = lax.all_gather(head_local, "tensor", axis=0, tiled=False)

    group_rows = seq_count * chunk
    terms, mixed, normed_ffn, back_gate_up, swiglu, group_cot = whole_call(
        feed_forward_kernel,
        "feed_forward",
        (head_rows, row_full, ffn_full, out_full, scale_ffn),
        (
            shape((tensor_count, 2 * seq_count, local_rows, width), bf16),
            shape((tensor_count, seq_count, local_rows, width), f32),
            shape((group_rows, width), bf16),
            shape((group_rows, 2 * ff_local), bf16),
            shape((group_rows, ff_local), bf16),
            shape((group_rows, width), bf16),
        ),
        VMEM_BYTES,
    )
    ffn_sums = exchange(terms, "tensor")
    (ffn_grads,) = whole_call(
        feed_forward_grad_kernel,
        "feed_forward_grads",
        (normed_ffn, back_gate_up, swiglu, group_cot),
        (shape((width, 3 * ff_local), bf16),),
        VMEM_BYTES,
    )
    ffn_grad_sums = lax.psum_scatter(ffn_grads, "dp", scatter_dimension=0, tiled=True).astype(f32)
    ffn_sums, normed_full = ordered(ffn_sums, normed_full)
    ffn_sums = ffn_sums.astype(f32).sum(axis=0)
    own_mixed = lax.dynamic_index_in_dim(mixed, rank, 0, keepdims=False)
    own_normal, own_inverse = layer_norm_parts(own_mixed)
    back_mixed = own_cot.astype(f32).reshape(own_mixed.shape) + layer_norm_back(
        own_normal, own_inverse, scale_ffn, ffn_sums[:seq_count]
    )
    result = (own_mixed + ffn_sums[seq_count:]).astype(bf16)
    attn_grads = lax.all_gather(back_mixed.astype(bf16), "tensor", axis=1, tiled=True)
    back_head, out_terms = whole_call(
        head_back_kernel,
        "head_back",
        (attn_grads, own_out, head_local),
        (
            shape((device_count, HEAD_DIM, chunk), bf16),
            shape((device_count, shard, local_width), bf16),
        ),
    )
    head_grad = exchange(back_head, "dp")
    out_sums = exchange(out_terms, "dp")

    back_packed = chain_backward(chain_in, head_grad, saved, inner_part, feature_part)
    back_rows = exchange(back_packed, "dp")
    sequence = place % seq_count
    chain_normed = lax.dynamic_index_in_dim(normed_full, sequence, 0, keepdims=False)
    grad_packed = dots("pnd,pnk->dk", chain_normed, back_packed)
    grad_packed = grad_packed.astype(bf16).reshape(device_count, shard, LANES)
    back_rows, grad_packed = ordered(back_rows, grad_packed)
    grad_block = exchange(grad_packed, "dp")

    (attn_term,) = whole_call(
        attention_term_kernel,
        "attention_term",
        (back_rows, head_matrix),
        (shape((tensor_count, seq_count, local_rows, width), bf16),),
    )
    attn_sums = exchange(attn_term, "tensor").astype(f32).sum(axis=0)
    back_rows = back_rows[:chain_count].reshape(head_count, seq_count, chunk, LANES)
    own_inputs = tokens.transpose(1, 0, 2).astype(f32)
    own_normal, own_inverse = layer_norm_parts(own_inputs)
    input_grad = back_mixed + layer_norm_back(
        own_normal, own_inverse, scale_attn, attn_sums
    )

    grad_block = grad_block[:chain_count].astype(f32)
    grad_block = grad_block.reshape(head_count, seq_count, shard, LANES).sum(axis=1)
    grad_qkv = (
        grad_block[:, :, :RATE_LANE]
        .reshape(head_count, shard, 3, HEAD_DIM)
        .transpose(1, 2, 0, 3)
        .reshape(shard, 3, local_width)
    )
    grad_rate = grad_block[:, :, RATE_LANE].T
    state_block = back_rows[..., VECTOR_LANE:].astype(f32).sum(axis=1)
    matrices = state_block[..., MATRIX_LANE - VECTOR_LANE :][..., :inner_part]
    grad_one = matrices[:, :HEAD_DIM]
    grad_two = matrices[:, HEAD_DIM : 2 * HEAD_DIM].transpose(0, 2, 1)
    columns = state_block[:, :, 0]
    ends = [inner_part + index * feature_part for index in range(4)]
    grad_b_one = columns[:, : ends[0]]
    grad_b_two, grad_gain_inner, grad_bias_inner = (
        columns[:, ends[index] : ends[index + 1]] for index in range(3)
    )

    own_gains = lax.dynamic_slice_in_dim(gains, place * shard, shard, 1)
    gain_one = jnp.sum(grad_qkv * w_qkv.astype(f32), axis=(1, 2)) + jnp.sum(
        grad_rate * w_rate.astype(f32), axis=1
    )
    grad_gate_up = ffn_grad_sums[:, : 2 * ff_local].reshape(shard, 2, ff_local)
    gain_two = jnp.sum(grad_gate_up * w_gate_up.astype(f32), axis=(1, 2))
    gain_terms = jnp.stack([gain_one, gain_two]) / own_gains
    gain_terms = gain_terms.reshape(2, tensor_count, part).transpose(1, 0, 2)
    gain_terms = jnp.pad(
        gain_terms.reshape(tensor_count, 1, 2 * part), ((0, 0), (0, 0), (0, 128 - 2 * part))
    )
    gain_sums = exchange(gain_terms, "tensor").sum(axis=0)[0]

    def by_token(values):
        return values.reshape(seq_count, local_rows, width).transpose(1, 0, 2)

    return (
        by_token(result),
        by_token(input_grad),
        gain_sums[:part],
        gain_sums[part : 2 * part],
        grad_qkv,
        grad_rate,
        out_sums.astype(f32).sum(axis=0).T,
        grad_gate_up,
        ffn_grad_sums[:, 2 * ff_local : 3 * ff_local].T,
        grad_one,
        grad_b_one,
        grad_two,
        grad_b_two,
        grad_gain_inner,
        grad_bias_inner,
    )


def solution(mesh):
    rows = P(("dp", "tensor"), None, None)
    gains = P(("dp", "tensor"))
    placed = (
        rows,
        gains,
        gains,
        P("dp", None, "tensor"),
        P("dp", "tensor"),
        P("tensor", "dp"),
        P("dp", None, "tensor"),
        P("tensor", "dp"),
        P("tensor", None, "dp"),
        P("tensor", "dp"),
        P("tensor", "dp", None),
        P("tensor", "dp"),
        P("tensor", "dp"),
        P("tensor", "dp"),
    )
    return jax.shard_map(
        local,
        mesh=mesh,
        in_specs=placed + (rows,),
        out_specs=(rows,) + placed,
        check_vma=False,
    )
```

```python
import functools


import jax
import jax.numpy as jnp
from jax import lax
from jax.experimental import pallas as pl
from jax.experimental.pallas import tpu as pltpu
from jax.sharding import PartitionSpec as P

HEAD_DIM = 64
INNER = 256
MINI = 16
LANES = 256
RATE_LANE = 3 * HEAD_DIM
VECTOR_LANE = RATE_LANE + 2
MATRIX_LANE = LANES - 32
VMEM_BYTES = 56 * 1024 * 1024
GLUE_BYTES = 32 * 1024 * 1024

epsilon = 1e-05
inner_epsilon = 1e-06
inner_rate = 0.5
rate_scale = inner_rate / (MINI * HEAD_DIM)
root_half = 0.7071067811865476
normal_peak = 0.3989422804014327

f32 = jnp.float32
bf16 = jnp.bfloat16


def dot_nn(a, b):
    return lax.dot_general(
        a.astype(bf16), b.astype(bf16), (((1,), (0,)), ((), ())), preferred_element_type=f32
    )


def dot_nt(a, b):
    return lax.dot_general(
        a.astype(bf16), b.astype(bf16), (((1,), (1,)), ((), ())), preferred_element_type=f32
    )


def dot_tn(a, b):
    return lax.dot_general(
        a.astype(bf16), b.astype(bf16), (((0,), (0,)), ((), ())), preferred_element_type=f32
    )


def row_mean(values):
    return jnp.mean(values, axis=-1, keepdims=True)


def density_and_share(values):
    density = jnp.exp(-0.5 * values * values) * normal_peak
    share = 0.5 * (1.0 + lax.erf(values * root_half))
    return density, share


def token_grid(count):
    rows = lax.broadcasted_iota(jnp.int32, (count, count), 0)
    cols = lax.broadcasted_iota(jnp.int32, (count, count), 1)
    return rows, cols


def wide_mean(values):
    high = values.astype(bf16)
    low = (values - high.astype(f32)).astype(bf16)
    ones = jnp.full((values.shape[1], 128), 1.0 / values.shape[1], bf16)
    return dot_nn(high, ones) + dot_nn(low, ones)


def mean_of(values):
    return wide_mean(values)[:, :HEAD_DIM]


def two_parts(packed):
    return packed[:, :HEAD_DIM], packed[:, HEAD_DIM : 2 * HEAD_DIM]


def rate_logit(packed):
    source = lax.broadcasted_iota(jnp.int32, (2 * HEAD_DIM, 128), 0)
    spread = jnp.where((source >= HEAD_DIM) & (source < HEAD_DIM + 2), 1.0, 0.0)
    return dot_nn(packed[:, 2 * HEAD_DIM :], spread)


def alternate(*generators):
    left = list(generators)
    while left:
        for generator in list(left):
            if next(generator, generator) is generator:
                left.remove(generator)
            else:
                yield


def interleave(generator, count):
    for _ in range(count):
        if next(generator, generator) is generator:
            return


def forward_kernel(
    inner_part,
    feature_part,
    packed_ref,
    normed_ref,
    act_ref,
    grad_pre_ref,
    slope_ref,
    curve_ref,
    norms_ref,
    first_save,
    second_save,
    hidden_ref,
    out_slope_ref,
    out_norms_ref,
    gain_ref,
    bias_ref,
    first_w,
    first_b,
    second_w,
    second_b,
    known_ref,
    back_res_ref,
    pre_ref,
    to_rows,
    to_level,
    to_mix,
    row_ref,
    level_ref,
    mix_ref,
    done_act,
    done_grad,
    done_back,
    done_first,
    done_second,
    done_first_b,
    done_second_b,
):
    devices, chunk, _ = packed_ref.shape
    steps = chunk // MINI
    turn = pl.program_id(0)

    @pl.when(turn == 0)
    def _():
        for index in range(devices):
            block = packed_ref[index, :, LANES - 128 :].astype(f32)
            first = slice(index * inner_part, (index + 1) * inner_part)
            lanes = slice(MATRIX_LANE - LANES + 128, MATRIX_LANE - LANES + 128 + inner_part)
            first_w[:, first] = block[:HEAD_DIM, lanes]
            second_w[:, first] = block[HEAD_DIM : 2 * HEAD_DIM, lanes]
            at = VECTOR_LANE - LANES + 128
            vector = jnp.transpose(block)[at : at + 1]
            first_b[:, first] = vector[:, :inner_part]
            small = slice(index * feature_part, (index + 1) * feature_part)
            for number, target in enumerate((second_b, gain_ref, bias_ref)):
                start = inner_part + number * feature_part
                target[:, small] = vector[:, start : start + feature_part]
        known_ref[...] = jnp.zeros_like(known_ref)
        centred = second_w[...]
        second_w[...] = centred - jnp.mean(centred, axis=0, keepdims=True)
        second_b[...] = second_b[...] - row_mean(second_b[...])

    gain = gain_ref[...]
    bias = bias_ref[...]
    rows, cols = token_grid(chunk)

    def finish():
        query, key = two_parts(packed_ref[jnp.maximum(turn - 1, 0)])
        causal = cols <= rows
        mix = dot_nt(query, key)
        query_base = dot_nn(query, done_first[...])
        yield
        first_mix = jnp.where(causal, mix + 1.0, 0.0)
        taken = dot_nn(first_mix, done_grad[...])
        yield
        query_pre = query_base + done_first_b[...] - taken
        density, share = density_and_share(query_pre)
        hidden = (query_pre * share).astype(bf16)
        hidden_ref[...] = hidden
        out_slope_ref[...] = share + query_pre * density
        yield
        mix = dot_nt(hidden, done_act[...])
        res_base = dot_nt(hidden, done_second[...])
        yield
        second_mix = jnp.where(causal, mix + 1.0, 0.0)
        taken = dot_nn(second_mix, done_back[...])
        yield
        query_res = res_base + done_second_b[...] - taken
        square = mean_of(query_res * query_res)
        yield
        out_inverse = lax.rsqrt(square + inner_epsilon)
        out_normal = query_res * out_inverse
        outputs = query.astype(f32) + out_normal * gain + bias
        middle = mean_of(outputs)
        out_norms_ref[:, :HEAD_DIM] = out_normal
        out_norms_ref[:, 2 * HEAD_DIM : 3 * HEAD_DIM] = out_inverse
        yield
        centred = outputs - middle
        square = mean_of(centred * centred)
        yield
        head_inverse = lax.rsqrt(square + epsilon)
        head_normal = centred * head_inverse
        out_norms_ref[:, HEAD_DIM : 2 * HEAD_DIM] = head_normal
        out_norms_ref[:, 3 * HEAD_DIM :] = head_inverse
        normed_ref[0] = jnp.transpose(head_normal).astype(bf16)

    def ahead(place):
        packed = packed_ref[place]
        _, key = two_parts(packed)
        value = packed[:, 2 * HEAD_DIM : 3 * HEAD_DIM]
        logit = rate_logit(packed)
        mix = dot_nt(key, key)
        yield
        rate = jax.nn.sigmoid(logit) * rate_scale
        square_gain = gain * gain
        level_gain = rate * row_mean(square_gain)
        rate_base = rate[:, :HEAD_DIM] * (
            (key.astype(f32) - value.astype(f32) + bias) * gain
        )
        middle = mean_of(rate_base)
        to_rows[0] = rate_base
        to_rows[1] = rate[:, :HEAD_DIM] * square_gain - level_gain[:, :HEAD_DIM]
        to_level[...] = level_gain * inner_epsilon
        to_mix[...] = jnp.where(cols // MINI < rows // MINI, mix + 1.0, 0.0).astype(bf16)
        yield
        to_rows[2] = middle

    def chain(others):
        _, key = two_parts(packed_ref[jnp.minimum(turn, devices - 1)])
        row_ref[...] = to_rows[...]
        level_ref[...] = to_level[...]
        mix_ref[...] = to_mix[...]
        first_low = first_w[...].astype(bf16)
        first_save[0] = first_low
        start_first_b = first_b[...]
        start_b = second_b[...]
        pre_ref[...] = dot_nn(key, first_low) + start_first_b
        state = second_w[...]
        start_low = state.astype(bf16)
        state_b = start_b
        for step in range(steps):
            at = slice(step * MINI, (step + 1) * MINI)
            own_base = row_ref[0, at, :]
            own_gain = row_ref[1, at, :]
            pre = pre_ref[at, :]
            if step >= 1:
                taken = dot_nn(mix_ref[at, :], known_ref[...])
                interleave(others, 1)
                pre = pre - taken
            density, share = density_and_share(pre)
            act = (pre * share).astype(bf16)
            state_low = state.astype(bf16)
            res = dot_nt(act, state_low)
            slope = share + pre * density
            second_save[0, step] = state_low
            interleave(others, 1)
            res = res + state_b
            weighted = own_gain * res
            parts = dot_nn(jnp.concatenate([res, weighted], axis=0), state_low)
            base_act = dot_nn(own_base, state_low)
            interleave(others, 1)
            square = jnp.sum(res * res, axis=-1, keepdims=True)
            sum_gain = jnp.sum(weighted, axis=-1, keepdims=True)
            sum_base = jnp.sum(own_base * res, axis=-1, keepdims=True)
            sum_square = jnp.sum(weighted * res, axis=-1, keepdims=True)
            inverse = lax.rsqrt(square * (1.0 / HEAD_DIM) + inner_epsilon)
            scaled_mean = row_ref[2, at, :] + inverse * sum_gain * (1.0 / HEAD_DIM)
            along = inverse * (sum_base + inverse * sum_square) * (1.0 / HEAD_DIM)
            square_inverse = inverse * inverse
            along_half = along - square_inverse * level_ref[at, :]
            along_wide = jnp.concatenate([along_half, along_half], axis=1)
            normal = res * inverse
            back_res = inverse * (
                own_base + own_gain * normal - scaled_mean - normal * along_half[:, :HEAD_DIM]
            )
            back_low = back_res.astype(bf16)
            back_act = inverse * base_act + square_inverse * (
                parts[MINI:] - along_wide * parts[:MINI]
            )
            grad = (back_act * slope).astype(bf16)
            known_ref[at, :] = grad
            state = state - dot_tn(back_low, act)
            state_b = state_b - jnp.sum(back_res, axis=0, keepdims=True)
            slope_ref[at, :] = slope
            curve_ref[at, :] = back_act * density * (2.0 - pre * pre)
            act_ref[at, :] = act
            grad_pre_ref[at, :] = grad
            back_res_ref[at, :] = back_low
            norms_ref[at, :HEAD_DIM] = normal
            norms_ref[at, HEAD_DIM:] = jnp.broadcast_to(inverse, (MINI, HEAD_DIM))
        for _ in others:
            pass
        grad_all = known_ref[...]
        first_w[...] = first_w[...] - dot_tn(key, grad_all)
        first_b[...] = start_first_b - jnp.sum(grad_all.astype(f32), axis=0, keepdims=True)
        second_w[...] = state
        second_b[...] = state_b
        done_act[...] = act_ref[...]
        done_grad[...] = grad_all
        done_back[...] = back_res_ref[...]
        done_first[...] = first_low
        done_second[...] = start_low
        done_first_b[...] = start_first_b
        done_second_b[...] = start_b

    @pl.when(turn == 0)
    def _():
        for _ in ahead(0):
            pass
        chain(ahead(1))

    @pl.when((turn > 0) & (turn < devices))
    def _():
        chain(alternate(finish(), ahead(jnp.minimum(turn + 1, devices - 1))))

    @pl.when(turn == devices)
    def _():
        for _ in finish():
            pass


def backward_kernel(
    inner_part,
    feature_part,
    sequence_ref,
    packed_ref,
    rows_ref,
    head_grad_ref,
    next_act,
    next_grad,
    next_hidden,
    next_out_slope,
    next_norms,
    next_out_norms,
    next_first,
    next_second,
    now_act,
    now_slope,
    now_curve,
    now_second,
    last_grad,
    last_norms,
    last_first,
    gain_ref,
    bias_ref,
    back_ref,
    first_w,
    first_b,
    second_w,
    second_b,
    gain_sum,
    bias_sum,
    known_ref,
    vector_ref,
    grad_sum,
    to_wide,
    to_rows,
    to_spread,
    to_low,
    to_mix,
    to_state,
    to_sums,
    wide_ref,
    row_ref,
    spread_ref,
    low_ref,
    mix_ref,
    state_ref,
    sums_ref,
    end_known,
    end_rows,
    end_first,
):
    devices, chunk, _ = packed_ref.shape
    steps = chunk // MINI
    turn = pl.program_id(0)
    shard = back_ref.shape[1] - chunk
    gain = gain_ref[...]
    bias = bias_ref[...]
    square_gain = gain * gain
    rows, cols = token_grid(chunk)

    @pl.when(turn == 0)
    def _():
        for ref in (
            first_w,
            first_b,
            second_w,
            second_b,
            gain_sum,
            bias_sum,
            known_ref,
            grad_sum,
            end_known,
            end_rows,
            end_first,
        ):
            ref[...] = jnp.zeros_like(ref)

    def unpack(place):
        packed = packed_ref[place]
        query, key = two_parts(packed)
        miss = key.astype(f32) - packed[:, 2 * HEAD_DIM : 3 * HEAD_DIM].astype(f32) + bias
        return query, key, miss, rate_logit(packed)

    def rate_of(logit):
        return jax.nn.sigmoid(logit[:, :HEAD_DIM]) * rate_scale

    def prepare():
        query, key, miss, logit = unpack(jnp.maximum(devices - 1 - turn, 0))
        head_grad = jnp.transpose(head_grad_ref[0].astype(f32))
        head_normal = next_out_norms[:, HEAD_DIM : 2 * HEAD_DIM]
        head_mean = mean_of(head_grad)
        head_tilt = mean_of(head_grad * head_normal)
        yield
        rate = rate_of(logit)
        normal = next_norms[:, :HEAD_DIM]
        rate_gain = rate * square_gain
        gain_normal = rate_gain * normal
        scaled = rate * (miss * gain) + gain_normal
        scaled_mean = mean_of(scaled)
        along = mean_of(scaled * normal)
        yield
        out_grad = next_out_norms[:, 3 * HEAD_DIM :] * (
            head_grad - head_mean - head_normal * head_tilt
        )
        out_normal = next_out_norms[:, :HEAD_DIM]
        normal_grad = out_grad * gain
        out_mean = mean_of(normal_grad)
        out_tilt = mean_of(normal_grad * out_normal)
        yield
        inverse = next_norms[:, HEAD_DIM:]
        back_res = (inverse * (scaled - scaled_mean - normal * along)).astype(bf16)
        gain_along = mean_of(gain_normal)
        gain_square = mean_of(gain_normal * normal)
        to_low[0] = back_res
        to_low[1] = key
        to_sums[2:3, :HEAD_DIM] = jnp.sum(out_grad * out_normal, axis=0, keepdims=True)
        to_sums[3:4, :HEAD_DIM] = jnp.sum(out_grad, axis=0, keepdims=True)
        yield
        res_grad = next_out_norms[:, 2 * HEAD_DIM : 3 * HEAD_DIM] * (
            normal_grad - out_mean - out_normal * out_tilt
        )
        to_sums[1:2, :HEAD_DIM] = jnp.sum(res_grad, axis=0, keepdims=True)
        res_grad_low = res_grad.astype(bf16)
        hidden_base = dot_nn(res_grad_low, next_second[0, 0])
        mix = dot_nt(res_grad_low, back_res)
        yield
        mix_t = dot_nt(back_res, res_grad_low)
        causal = cols <= rows
        later = rows <= cols
        second_grad = jnp.where(causal, -mix, 0.0)
        hidden_more = dot_nn(second_grad, next_act[...])
        yield
        second_grad_t = jnp.where(later, -mix_t, 0.0)
        to_rows[1] = normal
        to_rows[2] = rate_gain
        to_rows[3] = rate_gain - along
        to_rows[4] = gain_normal + scaled
        to_rows[5] = -(along + rate * row_mean(square_gain))
        yield
        for index, value in enumerate(
            (-(gain_along + scaled_mean), -(3.0 * along + gain_square), inverse * inverse)
        ):
            to_spread[index] = jnp.concatenate([value, value], axis=1)
        mix = dot_nt(next_act[...], next_hidden[...])
        yield
        query_pre_grad = (hidden_base + hidden_more) * next_out_slope[...]
        query_pre_low = query_pre_grad.astype(bf16)
        to_sums[0:1] = jnp.sum(query_pre_grad, axis=0, keepdims=True)
        first = dot_nt(query_pre_low, next_grad[...])
        yield
        second_mix_t = jnp.where(later, mix + 1.0, 0.0)
        to_rows[0] = -dot_nn(second_mix_t, res_grad_low)
        first_t = dot_nt(next_grad[...], query_pre_low)
        yield
        first_grad = jnp.where(causal, -first, 0.0)
        mix = dot_nt(key, query)
        query_grad = dot_nt(query_pre_low, next_first[0])
        query_more = dot_nn(first_grad, key)
        yield
        first_grad_t = jnp.where(later, -first_t, 0.0)
        to_rows[6] = dot_nn(first_grad_t, query)
        first_mix_t = jnp.where(later, mix + 1.0, 0.0).astype(bf16)
        yield
        to_rows[7] = out_grad + query_grad + query_more
        to_wide[1] = dot_nn(second_grad_t, next_hidden[...])
        yield
        to_wide[0] = -dot_nn(first_mix_t, query_pre_low)
        mix = dot_nt(key, key)
        yield
        to_mix[...] = jnp.where(cols // MINI > rows // MINI, mix + 1.0, 0.0).astype(bf16)
        to_state[0] = dot_tn(query, query_pre_low)
        yield
        to_state[1] = dot_tn(res_grad_low, next_hidden[...])

    def conclude():
        place = jnp.minimum(devices + 1 - turn, devices - 1)
        _, key, miss, logit = unpack(place)
        normal = last_norms[:, :HEAD_DIM]
        upon = end_rows[0]
        upon_mean = mean_of(upon)
        upon_tilt = mean_of(upon * normal)
        yield
        pre_grad = end_known[...]
        mix = dot_nt(last_grad[...], pre_grad)
        mix_t = dot_nt(pre_grad, last_grad[...])
        yield
        rate = rate_of(logit)
        scaled_grad = last_norms[:, HEAD_DIM:] * (upon - upon_mean - normal * upon_tilt)
        error_grad = scaled_grad * (rate * gain)
        rate_grad = mean_of(scaled_grad * (miss * gain + square_gain * normal))
        yield
        error = miss + normal * gain
        gain_sum[...] += jnp.sum(
            scaled_grad * rate * error + error_grad * normal, axis=0, keepdims=True
        )
        bias_sum[...] += jnp.sum(error_grad, axis=0, keepdims=True)
        from_grad = dot_nt(last_grad[...], end_first[...])
        yield
        far = rows // MINI < cols // MINI
        near = rows // MINI > cols // MINI
        cross = jnp.where(far, mix, 0.0) + jnp.where(near, mix_t, 0.0)
        from_pre = dot_nt(pre_grad, last_first[0])
        from_cross = dot_nn(cross, key)
        yield
        key_grad = end_rows[1] + error_grad - from_grad + from_pre - from_cross
        back_rate = rate_grad * float(HEAD_DIM) * rate * (1.0 - rate * (1.0 / rate_scale))
        lane = lax.broadcasted_iota(jnp.int32, (chunk, HEAD_DIM), 1)
        tail = jnp.where(lane == 0, back_rate, 0.0)
        packed = jnp.concatenate([end_rows[2], key_grad, -error_grad, tail], axis=1).astype(bf16)
        back_ref[place, :chunk] = packed
        yield
        count = 6
        size = grad_sum.shape[0] // count
        for index in range(count):
            at = slice(index * size, (index + 1) * size)
            grad_sum[at] = grad_sum[at] + dot_tn(rows_ref[0, 0, :, at], packed)
            yield

    def chain(following, previous):
        wide_ref[...] = to_wide[...]
        row_ref[...] = to_rows[...]
        spread_ref[...] = to_spread[...]
        low_ref[...] = to_low[...]
        mix_ref[...] = to_mix[...]
        state_ref[...] = to_state[...]
        sums_ref[...] = to_sums[...]
        first_next = first_w[...]
        first_next_low = first_next.astype(bf16)
        first_next_b = first_b[...]
        state = second_w[...]
        state_b = second_b[...]
        for step in reversed(range(steps)):
            at = slice(step * MINI, (step + 1) * MINI)
            grad = wide_ref[0, at, :] - dot_nn(low_ref[1, at, :], first_next_low) - first_next_b
            if step + 1 < steps:
                grad = grad - dot_nn(mix_ref[at, :], known_ref[...])
            state_low = state.astype(bf16)
            own_act = now_act[at, :]
            own_back = low_ref[0, at, :]
            back_base = row_ref[0, at, :] - dot_nt(own_act, state_low) - state_b
            act_base = wide_ref[1, at, :] - dot_nn(own_back, state_low)
            interleave(following, 1)
            own_low = now_second[0, step]
            slope = now_slope[at, :]
            back_act_grad = (grad * slope).astype(bf16)
            upon = dot_nt(back_act_grad, own_low)
            interleave(following, 1)
            upon = back_base + upon
            own_normal, own_gain, own_grad, own_beta, own_alpha = (
                row_ref[index, at, :] for index in range(1, 6)
            )
            cross, cross_beta, square_inverse = (spread_ref[index, at, :] for index in range(3))
            main = dot_nn(upon * own_grad, own_low)
            sides = dot_nn(jnp.concatenate([own_normal, own_gain, own_beta], axis=0), own_low)
            interleave(previous, 1)
            alpha = row_mean(upon)
            beta = row_mean(upon * own_normal)
            gamma = row_mean(upon * own_gain)
            kappa = row_mean(upon * own_beta)
            level = alpha * own_alpha + beta * cross[:, :HEAD_DIM] + gamma
            tilt = alpha * cross + beta * cross_beta + kappa
            key_res_grad = square_inverse[:, :HEAD_DIM] * (
                upon * own_grad
                - alpha * own_gain
                - beta * own_beta
                - level
                - own_normal * tilt[:, :HEAD_DIM]
            )
            key_res_low = key_res_grad.astype(bf16)
            from_res = (
                main
                - alpha * sides[MINI : 2 * MINI]
                - beta * sides[2 * MINI :]
                - jnp.concatenate([tilt, tilt], axis=1) * sides[:MINI]
            )
            factor = jnp.concatenate([square_inverse, square_inverse], axis=1)
            pre_grad = (act_base + factor * from_res) * slope + grad * now_curve[at, :]
            known_ref[at, :] = pre_grad.astype(bf16)
            state = state + dot_tn(
                jnp.concatenate([key_res_low, own_back], axis=0),
                jnp.concatenate([own_act, back_act_grad], axis=0),
            )
            state_b = state_b + jnp.sum(key_res_grad, axis=0, keepdims=True)
            row_ref[0, at, :] = upon
            interleave(following, 1)
            interleave(previous, 1)
        for generator in (following, previous):
            for _ in generator:
                pass
        pre_grad_all = known_ref[...]
        first_w[...] = first_next + dot_tn(low_ref[1], pre_grad_all) + state_ref[0]
        first_b[...] = (
            first_next_b
            + jnp.sum(pre_grad_all.astype(f32), axis=0, keepdims=True)
            + sums_ref[0:1]
        )
        second_w[...] = state + state_ref[1]
        second_b[...] = state_b + sums_ref[1:2, :HEAD_DIM]
        gain_sum[...] += sums_ref[2:3, :HEAD_DIM]
        bias_sum[...] += sums_ref[3:4, :HEAD_DIM]
        end_known[...] = pre_grad_all
        end_rows[0] = row_ref[0]
        end_rows[1] = row_ref[6]
        end_rows[2] = row_ref[7]
        end_first[...] = first_next_low

    @pl.when(turn == 0)
    def _():
        for _ in prepare():
            pass

    @pl.when((turn > 0) & (turn <= devices))
    def _():
        chain(prepare(), conclude())

    @pl.when(turn == devices + 1)
    def _():
        for _ in conclude():
            pass
        vector_ref[...] = jnp.zeros_like(vector_ref)
        for index in range(devices):
            first = slice(index * inner_part, (index + 1) * inner_part)
            small = slice(index * feature_part, (index + 1) * feature_part)
            vector_ref[index : index + 1, :inner_part] = first_b[:, first]
            for number, source in enumerate((second_b, gain_sum, bias_sum)):
                start = inner_part + number * feature_part
                vector_ref[index : index + 1, start : start + feature_part] = source[:, small]
        columns = jnp.transpose(vector_ref[...]).astype(bf16)
        lanes = slice(MATRIX_LANE, MATRIX_LANE + inner_part)
        for index in range(devices):
            first = slice(index * inner_part, (index + 1) * inner_part)
            back_ref[index, :HEAD_DIM, lanes] = first_w[:, first].astype(bf16)
            back_ref[index, HEAD_DIM : 2 * HEAD_DIM, lanes] = second_w[:, first].astype(bf16)
            back_ref[index, :chunk, VECTOR_LANE : VECTOR_LANE + 1] = columns[:, index : index + 1]
            back_ref[index, chunk:] = grad_sum[index * shard : (index + 1) * shard].astype(bf16)


def whole_block(shape):
    return pl.BlockSpec(shape, lambda index, *_: (0,) * len(shape))


STATE_SHAPES = ((HEAD_DIM, INNER), (1, INNER), (HEAD_DIM, INNER), (1, HEAD_DIM))


def chain_forward(packed, inner_part, feature_part):
    blocks, chunk, _ = packed.shape
    length = blocks * chunk
    steps = chunk // MINI
    row = (1, HEAD_DIM)

    def forth(shape):
        return pl.BlockSpec(
            shape, lambda turn: (jnp.minimum(turn, blocks - 1),) + (0,) * (len(shape) - 1)
        )

    def behind(shape):
        return pl.BlockSpec(
            shape, lambda turn: (jnp.maximum(turn - 1, 0),) + (0,) * (len(shape) - 1)
        )

    def of_length(width, dtype):
        return jax.ShapeDtypeStruct((length, width), dtype)

    wide = (chunk, INNER)
    return pl.pallas_call(
        functools.partial(forward_kernel, inner_part, feature_part),
        grid=(blocks + 1,),
        in_specs=[whole_block(packed.shape)],
        out_specs=[behind((1, HEAD_DIM, chunk))]
        + [forth(wide)] * 4
        + [
            forth((chunk, 2 * HEAD_DIM)),
            forth((1, HEAD_DIM, INNER)),
            forth((1, steps, HEAD_DIM, INNER)),
        ]
        + [behind(wide)] * 3
        + [whole_block(row)] * 2,
        out_shape=[jax.ShapeDtypeStruct((blocks, HEAD_DIM, chunk), bf16)]
        + [of_length(INNER, dtype) for dtype in (bf16, bf16, f32, f32)]
        + [
            of_length(2 * HEAD_DIM, f32),
            jax.ShapeDtypeStruct((blocks, HEAD_DIM, INNER), bf16),
            jax.ShapeDtypeStruct((blocks, steps, HEAD_DIM, INNER), bf16),
        ]
        + [of_length(INNER, dtype) for dtype in (bf16, f32, f32)]
        + [jax.ShapeDtypeStruct(row, f32)] * 2,
        scratch_shapes=[pltpu.VMEM(shape, f32) for shape in STATE_SHAPES]
        + [
            pltpu.VMEM(wide, bf16),
            pltpu.VMEM((chunk, HEAD_DIM), bf16),
            pltpu.VMEM(wide, f32),
        ]
        + [
            pltpu.VMEM((3, chunk, HEAD_DIM), f32),
            pltpu.VMEM((chunk, 2 * HEAD_DIM), f32),
            pltpu.VMEM((chunk, chunk), bf16),
        ]
        * 2
        + [
            pltpu.VMEM(wide, bf16),
            pltpu.VMEM(wide, bf16),
            pltpu.VMEM((chunk, HEAD_DIM), bf16),
            pltpu.VMEM((HEAD_DIM, INNER), bf16),
            pltpu.VMEM((HEAD_DIM, INNER), bf16),
            pltpu.VMEM((1, INNER), f32),
            pltpu.VMEM(row, f32),
        ],
        compiler_params=pltpu.CompilerParams(
            dimension_semantics=("arbitrary",), vmem_limit_bytes=VMEM_BYTES
        ),
        name="chain_forward",
    )(packed)


def chain_backward(packed, rows, sequence, head_grad, saved, inner_part, feature_part):
    act, grad_pre, slope, curve, norms, first_save, second_save = saved[:7]
    hidden, out_slope, out_norms, gain, bias = saved[7:]
    blocks, chunk, _ = packed.shape
    width = rows.shape[-1]
    shard = width // blocks
    steps = chunk // MINI
    row = (1, HEAD_DIM)
    wide = (chunk, INNER)
    narrow = (chunk, 2 * HEAD_DIM)

    def at(shape, delay):
        def index_map(turn, _):
            place = jnp.clip(blocks - 1 - turn + delay, 0, blocks - 1)
            return (place,) + (0,) * (len(shape) - 1)

        return pl.BlockSpec(shape, index_map)

    def rows_map(turn, chosen):
        return (chosen[0], jnp.clip(blocks + 1 - turn, 0, blocks - 1), 0, 0)

    state = (HEAD_DIM, INNER)
    carried = [
        pltpu.VMEM((2,) + wide, f32),
        pltpu.VMEM((8, chunk, HEAD_DIM), f32),
        pltpu.VMEM((3,) + narrow, f32),
        pltpu.VMEM((2, chunk, HEAD_DIM), bf16),
        pltpu.VMEM((chunk, chunk), bf16),
        pltpu.VMEM((2,) + state, f32),
        pltpu.VMEM((8, INNER), f32),
    ]
    return pl.pallas_call(
        functools.partial(backward_kernel, inner_part, feature_part),
        grid_spec=pltpu.PrefetchScalarGridSpec(
            num_scalar_prefetch=1,
            grid=(blocks + 2,),
            in_specs=[
                whole_block(packed.shape),
                pl.BlockSpec((1, 1, chunk, width), rows_map),
                at((1, HEAD_DIM, chunk), 0),
                at(wide, 0),
                at(wide, 0),
                at(wide, 0),
                at(wide, 0),
                at(narrow, 0),
                at(wide, 0),
                at((1,) + state, 0),
                at((1, 1) + state, 0),
                at(wide, 1),
                at(wide, 1),
                at(wide, 1),
                at((1, steps) + state, 1),
                at(wide, 2),
                at(narrow, 2),
                at((1,) + state, 2),
                whole_block(row),
                whole_block(row),
            ],
            out_specs=whole_block((blocks, chunk + shard, LANES)),
            scratch_shapes=[pltpu.VMEM(shape, f32) for shape in STATE_SHAPES + (row, row)]
            + [
                pltpu.VMEM(wide, bf16),
                pltpu.VMEM((chunk, 128), f32),
                pltpu.VMEM((width, LANES), f32),
            ]
            + carried
            + carried
            + [
                pltpu.VMEM(wide, bf16),
                pltpu.VMEM((3, chunk, HEAD_DIM), f32),
                pltpu.VMEM(state, bf16),
            ],
        ),
        out_shape=jax.ShapeDtypeStruct((blocks, chunk + shard, LANES), bf16),
        compiler_params=pltpu.CompilerParams(
            dimension_semantics=("arbitrary",), vmem_limit_bytes=VMEM_BYTES
        ),
        name="chain_backward",
    )(
        sequence,
        packed,
        rows,
        head_grad,
        act,
        grad_pre,
        hidden,
        out_slope,
        norms,
        out_norms,
        first_save,
        second_save,
        act,
        slope,
        curve,
        second_save,
        grad_pre,
        norms,
        first_save,
        gain,
        bias,
    )


def layer_norm_parts(values):
    centred = values - row_mean(values)
    inverse = lax.rsqrt(row_mean(centred * centred) + epsilon)
    return centred * inverse, inverse


def layer_norm_back(normal, inverse, scaling, grad):
    scaled = grad * scaling
    return inverse * (scaled - row_mean(scaled) - normal * row_mean(scaled * normal))


def start_kernel(
    head_count,
    rows_ref,
    weights_ref,
    gain_ref,
    inner_ref,
    packed_ref,
    normed_ref,
    matrix_ref,
):
    tensor_count = rows_ref.shape[0]
    seq_count, chunk, _ = normed_ref.shape
    rows = chunk // tensor_count
    matrix_ref[...] = jnp.zeros_like(matrix_ref)
    for head in range(head_count):
        first = head * 3 * HEAD_DIM
        rate = head_count * 3 * HEAD_DIM + head
        column = weights_ref[:, rate : rate + 1]
        matrix_ref[head, :, : 3 * HEAD_DIM] = weights_ref[:, first : first + 3 * HEAD_DIM]
        matrix_ref[head, :, RATE_LANE : RATE_LANE + 1] = column
        matrix_ref[head, :, RATE_LANE + 1 : RATE_LANE + 2] = column
    lane = lax.broadcasted_iota(jnp.int32, (chunk, LANES), 1)
    for sequence in range(seq_count):
        part = slice(sequence * rows, (sequence + 1) * rows)
        values = jnp.concatenate([rows_ref[index, part] for index in range(tensor_count)], axis=0)
        normal, _ = layer_norm_parts(values.astype(f32))
        normed = (normal * gain_ref[...]).astype(bf16)
        normed_ref[sequence] = normed
        for head in range(head_count):
            projected = dot_nn(normed, matrix_ref[head])
            rest = projected - projected.astype(bf16).astype(f32)
            projected = jnp.where(lane == RATE_LANE + 1, rest, projected).astype(bf16)
            packed_ref[head * seq_count + sequence] = jnp.where(
                lane >= VECTOR_LANE, inner_ref[head], projected
            )
    for index in range(head_count * seq_count, packed_ref.shape[0]):
        packed_ref[index] = jnp.zeros((chunk, LANES), bf16)


def feed_forward_kernel(
    heads_ref,
    rows_ref,
    weights_ref,
    out_ref,
    gain_ref,
    terms_ref,
    mixed_ref,
    normed_ref,
    back_ref,
    swiglu_ref,
    cot_ref,
):
    tensor_count, head_count, seq_count, _, chunk = heads_ref.shape
    ff_local = swiglu_ref.shape[1]
    rows = chunk // tensor_count
    total = seq_count * chunk
    for sequence in range(seq_count):
        part = slice(sequence * rows, (sequence + 1) * rows)
        other = slice((seq_count + sequence) * rows, (seq_count + sequence + 1) * rows)
        values = jnp.concatenate([rows_ref[index, part] for index in range(tensor_count)], axis=0)
        mixed = values.astype(f32)
        for index in range(tensor_count):
            heads = [heads_ref[index, head, sequence] for head in range(head_count)]
            heads = jnp.transpose(jnp.concatenate(heads, axis=0).astype(f32))
            mixed = mixed + dot_nt(heads, out_ref[index])
        for index in range(tensor_count):
            mixed_ref[index, sequence] = mixed[index * rows : (index + 1) * rows]
        normal, _ = layer_norm_parts(mixed)
        at = slice(sequence * chunk, (sequence + 1) * chunk)
        normed_ref[at] = (normal * gain_ref[...]).astype(bf16)
        for index in range(tensor_count):
            first = sequence * chunk + index * rows
            cot_ref[first : first + rows] = rows_ref[index, other]
    normed = normed_ref[...]
    cot = cot_ref[...]
    for first in range(0, ff_local, 256):
        at = slice(first, first + 256)
        beyond = slice(ff_local + first, ff_local + first + 256)
        gate = dot_nn(normed, weights_ref[:, at])
        up = dot_nn(normed, weights_ref[:, beyond])
        back = dot_nn(cot, weights_ref[:, 2 * ff_local + first : 2 * ff_local + first + 256])
        share = jax.nn.sigmoid(gate)
        silu = gate * share
        swiglu_ref[:, at] = (silu * up).astype(bf16)
        back_ref[:, at] = (back * up * (share * (1.0 + gate * (1.0 - share)))).astype(bf16)
        back_ref[:, beyond] = (back * silu).astype(bf16)
    ffn_term = dot_nt(back_ref[...], weights_ref[:, : 2 * ff_local]).astype(bf16)
    down_term = dot_nt(swiglu_ref[...], weights_ref[:, 2 * ff_local : 3 * ff_local]).astype(bf16)
    for sequence in range(seq_count):
        for index in range(tensor_count):
            first = sequence * chunk + index * rows
            terms_ref[index, sequence] = ffn_term[first : first + rows]
            terms_ref[index, seq_count + sequence] = down_term[first : first + rows]


def feed_forward_grad_kernel(normed_ref, back_ref, swiglu_ref, cot_ref, grads_ref):
    normed = jnp.transpose(normed_ref[...].astype(f32)).astype(bf16)
    cot = jnp.transpose(cot_ref[...].astype(f32)).astype(bf16)
    width = back_ref.shape[1]
    for first in range(0, width, 256):
        at = slice(first, first + 256)
        grads_ref[:, at] = dot_nn(normed, back_ref[:, at]).astype(bf16)
    for first in range(0, swiglu_ref.shape[1], 256):
        at = slice(width + first, width + first + 256)
        grads_ref[:, at] = dot_nn(cot, swiglu_ref[:, first : first + 256]).astype(bf16)


def head_back_kernel(grads_ref, out_ref, heads_ref, back_ref, out_grad_ref):
    head_count, seq_count, _, chunk = heads_ref.shape
    devices, shard, _ = out_grad_ref.shape
    total = None
    for sequence in range(seq_count):
        grads = grads_ref[sequence]
        back = jnp.transpose(dot_nn(grads, out_ref[...])).astype(bf16)
        for head in range(head_count):
            back_ref[head * seq_count + sequence] = back[head * HEAD_DIM : (head + 1) * HEAD_DIM]
        heads = [heads_ref[head, sequence] for head in range(head_count)]
        term = dot_nt(jnp.transpose(grads.astype(f32)), jnp.concatenate(heads, axis=0))
        total = term if total is None else total + term
    for index in range(head_count * seq_count, devices):
        back_ref[index] = jnp.zeros((HEAD_DIM, chunk), bf16)
    for index in range(devices):
        out_grad_ref[index] = total[index * shard : (index + 1) * shard].astype(bf16)


def matrix_output_kernel(sums_ref, out_ref, weights_ref, gate_up_ref, down_ref, out_grad_ref, gain_ref):
    ff_local = down_ref.shape[1]
    sums = sums_ref[...].astype(f32)
    for index in range(2):
        gate_up_ref[:, index, :] = sums[:, index * ff_local : (index + 1) * ff_local]
    down_ref[...] = sums[:, 2 * ff_local :]
    total = out_ref[0].astype(f32)
    for index in range(1, out_ref.shape[0]):
        total = total + out_ref[index].astype(f32)
    out_grad_ref[...] = jnp.transpose(total)
    products = sums[:, : 2 * ff_local] * weights_ref[:, : 2 * ff_local].astype(f32)
    gain = jnp.sum(products, axis=-1, keepdims=True)
    gain_ref[...] = jnp.broadcast_to(gain, gain_ref.shape)


def tail_kernel(
    received_ref,
    matrix_ref,
    own_ref,
    gain_two_ref,
    gains_ref,
    terms_ref,
    qkv_ref,
    small_ref,
    state_ref,
):
    head_count = matrix_ref.shape[0]
    shard = own_ref.shape[1]
    tensor_count, term_rows, width = terms_ref.shape
    chunk = received_ref.shape[1] - shard
    seq_count = (term_rows - 16) * tensor_count // chunk
    rows = chunk // tensor_count
    lane = lax.broadcasted_iota(jnp.int32, (chunk, LANES), 1)
    for sequence in range(seq_count):
        total = None
        for head in range(head_count):
            values = received_ref[head * seq_count + sequence, :chunk]
            values = jnp.where(lane <= RATE_LANE, values, jnp.zeros_like(values))
            term = dot_nt(values, matrix_ref[head])
            total = term if total is None else total + term
        for index in range(tensor_count):
            part = total[index * rows : (index + 1) * rows]
            terms_ref[index, sequence * rows : (sequence + 1) * rows] = part.astype(bf16)
    lane = lax.broadcasted_iota(jnp.int32, (shard, LANES), 1)
    column = lax.broadcasted_iota(jnp.int32, (shard, 128), 1)
    gain = None
    small = jnp.where(column == 1, gain_two_ref[...], 0.0)
    for head in range(head_count):
        grads = received_ref[head * seq_count, chunk:].astype(f32)
        state = received_ref[head * seq_count, :chunk, RATE_LANE:].astype(f32)
        for sequence in range(1, seq_count):
            grads = grads + received_ref[head * seq_count + sequence, chunk:].astype(f32)
            state = state + received_ref[
                head * seq_count + sequence, :chunk, RATE_LANE:
            ].astype(f32)
        state_ref[head] = state
        for index in range(3):
            at = slice(index * HEAD_DIM, (index + 1) * HEAD_DIM)
            qkv_ref[index, :, head * HEAD_DIM : (head + 1) * HEAD_DIM] = grads[:, at]
        products = jnp.where(lane <= RATE_LANE, grads * own_ref[head].astype(f32), 0.0)
        products = jnp.sum(products, axis=-1, keepdims=True)
        gain = products if gain is None else gain + products
        small = jnp.where(column == 2 + head, grads[:, RATE_LANE : RATE_LANE + 1], small)
    small = jnp.transpose(jnp.where(column == 0, gain, small))[: small_ref.shape[0]]
    small_ref[...] = small
    gain = small[:2] / gains_ref[...]
    high = gain.astype(bf16)
    low = (gain - high.astype(f32)).astype(bf16)
    block = jnp.concatenate([high.astype(f32), low.astype(f32), jnp.zeros((12, shard), f32)], axis=0)
    for index in range(tensor_count):
        first = seq_count * rows
        terms_ref[index, first:, :] = jnp.zeros((16, width), bf16)
        terms_ref[index, first:, :shard] = block.astype(bf16)


def whole_call(kernel, name, operands, results, vmem_bytes=GLUE_BYTES):
    def spec(shape):
        return pl.BlockSpec(shape, lambda: (0,) * len(shape))

    return pl.pallas_call(
        kernel,
        in_specs=[spec(operand.shape) for operand in operands],
        out_specs=[spec(result.shape) for result in results],
        out_shape=results,
        compiler_params=pltpu.CompilerParams(vmem_limit_bytes=vmem_bytes),
        name=name,
    )(*operands)


def dots(subscripts, left, right):
    return jnp.einsum(subscripts, left, right, preferred_element_type=f32)


def exchange(values, axis):
    return lax.all_to_all(values, axis, 0, 0, tiled=False)


def share_out(values, axis):
    count = lax.axis_size(axis)
    return exchange(jnp.broadcast_to(values[None], (count,) + values.shape), axis)


def ordered(first, then):
    return lax.optimization_barrier((first, then))


def inner_block(matrix_one, matrix_two, vectors, rows):
    width = matrix_one.shape[-1]
    matrices = jnp.concatenate([matrix_one, matrix_two], axis=-2)
    column = jnp.concatenate(vectors, axis=-1)[..., None]
    lead = [(0, 0)] * (column.ndim - 2)
    column = jnp.pad(
        column,
        lead + [(0, rows - column.shape[-2]), (VECTOR_LANE, LANES - VECTOR_LANE - 1)],
    )
    matrices = jnp.pad(
        matrices,
        lead + [(0, rows - matrices.shape[-2]), (MATRIX_LANE, LANES - MATRIX_LANE - width)],
    )
    return column + matrices


def local(
    tokens,
    gain_attn,
    gain_ffn,
    w_qkv,
    w_rate,
    w_out,
    w_gate_up,
    w_down,
    w_one,
    b_one,
    w_two,
    b_two,
    norm_gain_inner,
    norm_bias_inner,
    cotangent,
):
    device_count = lax.axis_size("dp")
    tensor_count = lax.axis_size("tensor")
    local_rows, seq_count, width = tokens.shape
    row_count = local_rows * seq_count
    chunk = local_rows * tensor_count
    head_count = w_rate.shape[1]
    local_width = head_count * HEAD_DIM
    shard = w_qkv.shape[0]
    part = gain_attn.shape[0]
    ff_local = w_down.shape[0]
    chain_count = seq_count * head_count
    inner_part = w_one.shape[2]
    feature_part = b_two.shape[1]
    assert chain_count <= device_count
    assert chunk == 2 * HEAD_DIM and inner_part <= 32 and part <= shard
    rank = lax.axis_index("tensor")
    place = lax.axis_index("dp")

    own_tokens = tokens.transpose(1, 0, 2).reshape(row_count, width)
    own_cot = cotangent.transpose(1, 0, 2).reshape(row_count, width)
    row_full = share_out(jnp.concatenate([own_tokens, own_cot], axis=0), "tensor")
    head_columns = w_qkv.reshape(shard, 3, head_count, HEAD_DIM).transpose(0, 2, 1, 3)
    gain_columns = jnp.pad(jnp.stack([gain_attn, gain_ffn], axis=1), ((0, shard - part), (0, 0)))
    qkv_pack = jnp.concatenate(
        [head_columns.reshape(shard, 3 * local_width), w_rate, gain_columns], axis=1
    )
    qkv_full = lax.all_gather(qkv_pack, "dp", axis=0, tiled=True)
    qkv_full, row_full = ordered(qkv_full, row_full)
    some_gains = qkv_full[:, 3 * local_width + head_count :]
    some_gains = some_gains.reshape(device_count, shard, 2)[:, :part].transpose(2, 0, 1)
    gains = lax.all_gather(some_gains.reshape(2, device_count * part), "tensor", axis=0)
    gains = gains.reshape(tensor_count, 2, device_count, part).transpose(1, 2, 0, 3)
    gains = gains.reshape(2, width).astype(f32)
    scale_attn, scale_ffn = gains[0:1], gains[1:2]

    ffn_pack = jnp.concatenate(
        [w_gate_up.reshape(shard, 2 * ff_local), w_down.T, w_out.T], axis=1
    )
    ffn_full = lax.all_gather(ffn_pack, "dp", axis=0, tiled=True)
    own_out = ffn_full[:, 3 * ff_local :]

    inner = inner_block(
        w_one,
        w_two.transpose(0, 2, 1),
        [b_one, b_two, norm_gain_inner, norm_bias_inner],
        chunk,
    )
    shape = jax.ShapeDtypeStruct
    packed, normed_attn, head_matrix = whole_call(
        functools.partial(start_kernel, head_count),
        "projections",
        (row_full, qkv_full, scale_attn, inner),
        (
            shape((device_count, chunk, LANES), bf16),
            shape((seq_count, chunk, width), bf16),
            shape((head_count, width, LANES), bf16),
        ),
    )
    chain_in = exchange(packed, "dp")
    chain_in, own_out = ordered(chain_in, own_out)
    out_full = lax.all_gather(own_out, "tensor", axis=0)

    normed_full = lax.all_gather(normed_attn, "dp", axis=1, tiled=False)

    forward_out = chain_forward(chain_in, inner_part, feature_part)
    saved = forward_out[1:]
    head_local = exchange(forward_out[0], "dp")[:chain_count]
    head_local = head_local.reshape(head_count, seq_count, HEAD_DIM, chunk)
    head_rows = lax.all_gather(head_local, "tensor", axis=0, tiled=False)

    group_rows = seq_count * chunk
    terms, mixed, normed_ffn, back_gate_up, swiglu, group_cot = whole_call(
        feed_forward_kernel,
        "feed_forward",
        (head_rows, row_full, ffn_full, out_full, scale_ffn),
        (
            shape((tensor_count, 2 * seq_count, local_rows, width), bf16),
            shape((tensor_count, seq_count, local_rows, width), f32),
            shape((group_rows, width), bf16),
            shape((group_rows, 2 * ff_local), bf16),
            shape((group_rows, ff_local), bf16),
            shape((group_rows, width), bf16),
        ),
        VMEM_BYTES,
    )
    ffn_sums = exchange(terms, "tensor")
    (ffn_grads,) = whole_call(
        feed_forward_grad_kernel,
        "feed_forward_grads",
        (normed_ffn, back_gate_up, swiglu, group_cot),
        (shape((width, 3 * ff_local), bf16),),
        VMEM_BYTES,
    )
    ffn_grad_sums = lax.psum_scatter(ffn_grads, "dp", scatter_dimension=0, tiled=True)
    ffn_sums, normed_full = ordered(ffn_sums, normed_full)
    ffn_sums = ffn_sums.astype(f32).sum(axis=0)
    own_mixed = lax.dynamic_index_in_dim(mixed, rank, 0, keepdims=False)
    own_normal, own_inverse = layer_norm_parts(own_mixed)
    back_mixed = own_cot.astype(f32).reshape(own_mixed.shape) + layer_norm_back(
        own_normal, own_inverse, scale_ffn, ffn_sums[:seq_count]
    )
    result = (own_mixed + ffn_sums[seq_count:]).astype(bf16)
    attn_grads = lax.all_gather(back_mixed.astype(bf16), "tensor", axis=1, tiled=True)
    back_head, out_terms = whole_call(
        head_back_kernel,
        "head_back",
        (attn_grads, own_out, head_local),
        (
            shape((device_count, HEAD_DIM, chunk), bf16),
            shape((device_count, shard, local_width), bf16),
        ),
    )
    head_grad = exchange(back_head, "dp")
    out_sums = exchange(out_terms, "dp")

    chosen = jnp.reshape(place % seq_count, (1,)).astype(jnp.int32)
    back_packed = chain_backward(
        chain_in, normed_full, chosen, head_grad, saved, inner_part, feature_part
    )
    received = exchange(back_packed, "dp")
    grad_gate_up, grad_down, grad_out, gain_two = whole_call(
        matrix_output_kernel,
        "matrix_outputs",
        (ffn_grad_sums, out_sums, ffn_pack),
        (
            shape((shard, 2, ff_local), f32),
            shape((shard, ff_local), f32),
            shape((local_width, shard), f32),
            shape((shard, 128), f32),
        ),
    )
    own_matrix = lax.dynamic_slice_in_dim(head_matrix, place * shard, shard, 1)
    own_gains = lax.dynamic_slice_in_dim(gains, place * shard, shard, 1)
    terms, grad_qkv, small, state_block = whole_call(
        tail_kernel,
        "tail",
        (received, head_matrix, own_matrix, gain_two, own_gains),
        (
            shape((tensor_count, row_count + 16, width), bf16),
            shape((3, shard, local_width), f32),
            shape((8, shard), f32),
            shape((head_count, chunk, LANES - RATE_LANE), f32),
        ),
    )
    tail = exchange(terms, "tensor").astype(f32).sum(axis=0)
    own_inputs = tokens.transpose(1, 0, 2).astype(f32)
    own_normal, own_inverse = layer_norm_parts(own_inputs)
    attn_sums = tail[:row_count].reshape(own_inputs.shape)
    input_grad = back_mixed + layer_norm_back(own_normal, own_inverse, scale_attn, attn_sums)
    gain_sums = tail[row_count : row_count + 2, :shard] + tail[row_count + 2 : row_count + 4, :shard]
    gain_sums = lax.dynamic_slice_in_dim(gain_sums, rank * part, part, 1)

    matrices = state_block[..., MATRIX_LANE - RATE_LANE :][..., :inner_part]
    grad_one = matrices[:, :HEAD_DIM]
    grad_two = matrices[:, HEAD_DIM : 2 * HEAD_DIM].transpose(0, 2, 1)
    columns = state_block[:, :, VECTOR_LANE - RATE_LANE]
    ends = [inner_part + index * feature_part for index in range(4)]
    grad_b_one = columns[:, : ends[0]]
    grad_b_two, grad_gain_inner, grad_bias_inner = (
        columns[:, ends[index] : ends[index + 1]] for index in range(3)
    )

    def by_token(values):
        return values.reshape(seq_count, local_rows, width).transpose(1, 0, 2)

    return (
        by_token(result),
        by_token(input_grad),
        gain_sums[0],
        gain_sums[1],
        grad_qkv.transpose(1, 0, 2),
        small[2 : 2 + head_count].T,
        grad_out,
        grad_gate_up,
        grad_down.T,
        grad_one,
        grad_b_one,
        grad_two,
        grad_b_two,
        grad_gain_inner,
        grad_bias_inner,
    )


def solution(mesh):
    rows = P(("dp", "tensor"), None, None)
    gains = P(("dp", "tensor"))
    placed = (
        rows,
        gains,
        gains,
        P("dp", None, "tensor"),
        P("dp", "tensor"),
        P("tensor", "dp"),
        P("dp", None, "tensor"),
        P("tensor", "dp"),
        P("tensor", None, "dp"),
        P("tensor", "dp"),
        P("tensor", "dp", None),
        P("tensor", "dp"),
        P("tensor", "dp"),
        P("tensor", "dp"),
    )
    return jax.shard_map(
        local,
        mesh=mesh,
        in_specs=placed + (rows,),
        out_specs=(rows,) + placed,
        check_vma=False,
    )
```

```python
import functools


import jax
import jax.numpy as jnp
from jax import lax
from jax.experimental import pallas as pl
from jax.experimental.pallas import tpu as pltpu
from jax.sharding import PartitionSpec as P

HEAD_DIM = 64
INNER = 256
MINI = 16
SEQS = 2
LANES = 256
RATE_LANE = 3 * HEAD_DIM
VECTOR_LANE = RATE_LANE + 2
MATRIX_LANE = LANES - 32
VMEM_BYTES = 56 * 1024 * 1024
DP = ("outer", "inner")
CHAIN_FLOPS = 20_000_000_000
GLUE_BYTES = 32 * 1024 * 1024

epsilon = 1e-05
inner_epsilon = 1e-06
inner_rate = 0.5
rate_scale = inner_rate / (MINI * HEAD_DIM)
root_half = 0.7071067811865476
normal_peak = 0.3989422804014327

f32 = jnp.float32
bf16 = jnp.bfloat16


def dot_nn(a, b):
    return lax.dot_general(
        a.astype(bf16), b.astype(bf16), (((1,), (0,)), ((), ())), preferred_element_type=f32
    )


def dot_nt(a, b):
    return lax.dot_general(
        a.astype(bf16), b.astype(bf16), (((1,), (1,)), ((), ())), preferred_element_type=f32
    )


def dot_tn(a, b):
    return lax.dot_general(
        a.astype(bf16), b.astype(bf16), (((0,), (0,)), ((), ())), preferred_element_type=f32
    )


def row_mean(values):
    return jnp.mean(values, axis=-1, keepdims=True)


def density_and_share(values):
    density = jnp.exp(-0.5 * values * values) * normal_peak
    share = 0.5 * (1.0 + lax.erf(values * root_half))
    return density, share


def token_grid(count):
    rows = lax.broadcasted_iota(jnp.int32, (count, count), 0)
    cols = lax.broadcasted_iota(jnp.int32, (count, count), 1)
    return rows, cols


def wide_mean(values):
    high = values.astype(bf16)
    low = (values - high.astype(f32)).astype(bf16)
    ones = jnp.full((values.shape[1], 128), 1.0 / values.shape[1], bf16)
    return dot_nn(high, ones) + dot_nn(low, ones)


def mean_of(values):
    return wide_mean(values)[:, :HEAD_DIM]


def two_parts(packed):
    return packed[:, :HEAD_DIM], packed[:, HEAD_DIM : 2 * HEAD_DIM]


def rate_logit(packed):
    source = lax.broadcasted_iota(jnp.int32, (2 * HEAD_DIM, 128), 0)
    spread = jnp.where((source >= HEAD_DIM) & (source < HEAD_DIM + 2), 1.0, 0.0)
    return dot_nn(packed[:, 2 * HEAD_DIM :], spread)


def alternate(*generators):
    left = list(generators)
    while left:
        for generator in list(left):
            if next(generator, generator) is generator:
                left.remove(generator)
            else:
                yield


def interleave(generator, count):
    for _ in range(count):
        if next(generator, generator) is generator:
            return


def forward_kernel(
    inner_part,
    feature_part,
    packed_ref,
    normed_ref,
    act_ref,
    grad_pre_ref,
    slope_ref,
    curve_ref,
    norms_ref,
    first_save,
    second_save,
    hidden_ref,
    out_slope_ref,
    out_norms_ref,
    gain_ref,
    bias_ref,
    first_w,
    first_b,
    second_w,
    second_b,
    known_ref,
    back_res_ref,
    pre_ref,
    to_rows,
    to_level,
    to_mix,
    row_ref,
    level_ref,
    mix_ref,
    done_act,
    done_grad,
    done_back,
    done_first,
    done_second,
    done_first_b,
    done_second_b,
):
    devices, chunk, _ = packed_ref.shape
    steps = chunk // MINI
    turn = pl.program_id(0)

    @pl.when(turn == 0)
    def _():
        for index in range(devices):
            block = packed_ref[index, :, LANES - 128 :].astype(f32)
            first = slice(index * inner_part, (index + 1) * inner_part)
            lanes = slice(MATRIX_LANE - LANES + 128, MATRIX_LANE - LANES + 128 + inner_part)
            first_w[:, first] = block[:HEAD_DIM, lanes]
            second_w[:, first] = block[HEAD_DIM : 2 * HEAD_DIM, lanes]
            at = VECTOR_LANE - LANES + 128
            vector = jnp.transpose(block)[at : at + 1]
            first_b[:, first] = vector[:, :inner_part]
            small = slice(index * feature_part, (index + 1) * feature_part)
            for number, target in enumerate((second_b, gain_ref, bias_ref)):
                start = inner_part + number * feature_part
                target[:, small] = vector[:, start : start + feature_part]
        known_ref[...] = jnp.zeros_like(known_ref)
        centred = second_w[...]
        second_w[...] = centred - jnp.mean(centred, axis=0, keepdims=True)
        second_b[...] = second_b[...] - row_mean(second_b[...])

    gain = gain_ref[...]
    bias = bias_ref[...]
    rows, cols = token_grid(chunk)

    def finish():
        query, key = two_parts(packed_ref[jnp.maximum(turn - 1, 0)])
        causal = cols <= rows
        mix = dot_nt(query, key)
        query_base = dot_nn(query, done_first[...])
        yield
        first_mix = jnp.where(causal, mix + 1.0, 0.0)
        taken = dot_nn(first_mix, done_grad[...])
        yield
        query_pre = query_base + done_first_b[...] - taken
        density, share = density_and_share(query_pre)
        hidden = (query_pre * share).astype(bf16)
        hidden_ref[...] = hidden
        out_slope_ref[...] = share + query_pre * density
        yield
        mix = dot_nt(hidden, done_act[...])
        res_base = dot_nt(hidden, done_second[...])
        yield
        second_mix = jnp.where(causal, mix + 1.0, 0.0)
        taken = dot_nn(second_mix, done_back[...])
        yield
        query_res = res_base + done_second_b[...] - taken
        square = mean_of(query_res * query_res)
        yield
        out_inverse = lax.rsqrt(square + inner_epsilon)
        out_normal = query_res * out_inverse
        outputs = query.astype(f32) + out_normal * gain + bias
        middle = mean_of(outputs)
        out_norms_ref[:, :HEAD_DIM] = out_normal
        out_norms_ref[:, 2 * HEAD_DIM : 3 * HEAD_DIM] = out_inverse
        yield
        centred = outputs - middle
        square = mean_of(centred * centred)
        yield
        head_inverse = lax.rsqrt(square + epsilon)
        head_normal = centred * head_inverse
        out_norms_ref[:, HEAD_DIM : 2 * HEAD_DIM] = head_normal
        out_norms_ref[:, 3 * HEAD_DIM :] = head_inverse
        normed_ref[0] = jnp.transpose(head_normal).astype(bf16)

    def ahead(place):
        packed = packed_ref[place]
        _, key = two_parts(packed)
        value = packed[:, 2 * HEAD_DIM : 3 * HEAD_DIM]
        logit = rate_logit(packed)
        mix = dot_nt(key, key)
        yield
        rate = jax.nn.sigmoid(logit) * rate_scale
        square_gain = gain * gain
        level_gain = rate * row_mean(square_gain)
        rate_base = rate[:, :HEAD_DIM] * (
            (key.astype(f32) - value.astype(f32) + bias) * gain
        )
        middle = mean_of(rate_base)
        to_rows[0] = rate_base
        to_rows[1] = rate[:, :HEAD_DIM] * square_gain - level_gain[:, :HEAD_DIM]
        to_level[...] = level_gain * inner_epsilon
        to_mix[...] = jnp.where(cols // MINI < rows // MINI, mix + 1.0, 0.0).astype(bf16)
        yield
        to_rows[2] = middle

    def chain(others):
        _, key = two_parts(packed_ref[jnp.minimum(turn, devices - 1)])
        row_ref[...] = to_rows[...]
        level_ref[...] = to_level[...]
        mix_ref[...] = to_mix[...]
        first_low = first_w[...].astype(bf16)
        first_save[0] = first_low
        start_first_b = first_b[...]
        start_b = second_b[...]
        pre_ref[...] = dot_nn(key, first_low) + start_first_b
        state = second_w[...]
        start_low = state.astype(bf16)
        state_b = start_b
        for step in range(steps):
            at = slice(step * MINI, (step + 1) * MINI)
            own_base = row_ref[0, at, :]
            own_gain = row_ref[1, at, :]
            pre = pre_ref[at, :]
            if step >= 1:
                taken = dot_nn(mix_ref[at, :], known_ref[...])
                interleave(others, 1)
                pre = pre - taken
            density, share = density_and_share(pre)
            act = (pre * share).astype(bf16)
            state_low = state.astype(bf16)
            res = dot_nt(act, state_low)
            slope = share + pre * density
            second_save[0, step] = state_low
            interleave(others, 1)
            res = res + state_b
            weighted = own_gain * res
            parts = dot_nn(jnp.concatenate([res, weighted], axis=0), state_low)
            base_act = dot_nn(own_base, state_low)
            interleave(others, 1)
            square = jnp.sum(res * res, axis=-1, keepdims=True)
            sum_gain = jnp.sum(weighted, axis=-1, keepdims=True)
            sum_base = jnp.sum(own_base * res, axis=-1, keepdims=True)
            sum_square = jnp.sum(weighted * res, axis=-1, keepdims=True)
            inverse = lax.rsqrt(square * (1.0 / HEAD_DIM) + inner_epsilon)
            scaled_mean = row_ref[2, at, :] + inverse * sum_gain * (1.0 / HEAD_DIM)
            along = inverse * (sum_base + inverse * sum_square) * (1.0 / HEAD_DIM)
            square_inverse = inverse * inverse
            along_half = along - square_inverse * level_ref[at, :]
            along_wide = jnp.concatenate([along_half, along_half], axis=1)
            normal = res * inverse
            back_res = inverse * (
                own_base + own_gain * normal - scaled_mean - normal * along_half[:, :HEAD_DIM]
            )
            back_low = back_res.astype(bf16)
            with_base = inverse * slope * base_act
            with_part = square_inverse * slope
            with_res = with_part * along_wide
            grad_full = with_base + (with_part * parts[MINI:] - with_res * parts[:MINI])
            grad = grad_full.astype(bf16)
            known_ref[at, :] = grad
            state = state - dot_tn(back_low, act)
            state_b = state_b - jnp.sum(back_res, axis=0, keepdims=True)
            slope_ref[at, :] = slope
            back_act = inverse * base_act + square_inverse * (
                parts[MINI:] - along_wide * parts[:MINI]
            )
            curve_ref[at, :] = back_act * density * (2.0 - pre * pre)
            act_ref[at, :] = act
            grad_pre_ref[at, :] = grad
            back_res_ref[at, :] = back_low
            norms_ref[at, :HEAD_DIM] = normal
            norms_ref[at, HEAD_DIM:] = jnp.broadcast_to(inverse, (MINI, HEAD_DIM))
        for _ in others:
            pass
        grad_all = known_ref[...]
        first_w[...] = first_w[...] - dot_tn(key, grad_all)
        first_b[...] = start_first_b - jnp.sum(grad_all.astype(f32), axis=0, keepdims=True)
        second_w[...] = state
        second_b[...] = state_b
        done_act[...] = act_ref[...]
        done_grad[...] = grad_all
        done_back[...] = back_res_ref[...]
        done_first[...] = first_low
        done_second[...] = start_low
        done_first_b[...] = start_first_b
        done_second_b[...] = start_b

    @pl.when(turn == 0)
    def _():
        for _ in ahead(0):
            pass
        chain(ahead(1))

    @pl.when((turn > 0) & (turn < devices))
    def _():
        chain(alternate(finish(), ahead(jnp.minimum(turn + 1, devices - 1))))

    @pl.when(turn == devices)
    def _():
        for _ in finish():
            pass


def backward_kernel(
    inner_part,
    feature_part,
    sequence_ref,
    packed_ref,
    rows_ref,
    head_grad_ref,
    next_act,
    next_grad,
    next_hidden,
    next_out_slope,
    next_norms,
    next_out_norms,
    next_first,
    next_second,
    now_act,
    now_slope,
    now_curve,
    now_second,
    last_grad,
    last_norms,
    last_first,
    gain_ref,
    bias_ref,
    back_ref,
    first_w,
    first_b,
    second_w,
    second_b,
    gain_sum,
    bias_sum,
    known_ref,
    vector_ref,
    grad_sum,
    to_wide,
    to_rows,
    to_spread,
    to_low,
    to_mix,
    to_state,
    to_sums,
    wide_ref,
    row_ref,
    spread_ref,
    low_ref,
    mix_ref,
    state_ref,
    sums_ref,
    end_known,
    end_rows,
    end_first,
):
    devices, chunk, _ = packed_ref.shape
    steps = chunk // MINI
    turn = pl.program_id(0)
    shard = back_ref.shape[1] - chunk
    gain = gain_ref[...]
    bias = bias_ref[...]
    square_gain = gain * gain
    rows, cols = token_grid(chunk)

    @pl.when(turn == 0)
    def _():
        for ref in (
            first_w,
            first_b,
            second_w,
            second_b,
            gain_sum,
            bias_sum,
            known_ref,
            grad_sum,
            end_known,
            end_rows,
            end_first,
        ):
            ref[...] = jnp.zeros_like(ref)

    def unpack(place):
        packed = packed_ref[place]
        query, key = two_parts(packed)
        miss = key.astype(f32) - packed[:, 2 * HEAD_DIM : 3 * HEAD_DIM].astype(f32) + bias
        return query, key, miss, rate_logit(packed)

    def rate_of(logit):
        return jax.nn.sigmoid(logit[:, :HEAD_DIM]) * rate_scale

    def prepare():
        query, key, miss, logit = unpack(jnp.maximum(devices - 1 - turn, 0))
        head_grad = jnp.transpose(head_grad_ref[0].astype(f32))
        head_normal = next_out_norms[:, HEAD_DIM : 2 * HEAD_DIM]
        head_mean = mean_of(head_grad)
        head_tilt = mean_of(head_grad * head_normal)
        yield
        rate = rate_of(logit)
        normal = next_norms[:, :HEAD_DIM]
        rate_gain = rate * square_gain
        gain_normal = rate_gain * normal
        scaled = rate * (miss * gain) + gain_normal
        scaled_mean = mean_of(scaled)
        along = mean_of(scaled * normal)
        yield
        out_grad = next_out_norms[:, 3 * HEAD_DIM :] * (
            head_grad - head_mean - head_normal * head_tilt
        )
        out_normal = next_out_norms[:, :HEAD_DIM]
        normal_grad = out_grad * gain
        out_mean = mean_of(normal_grad)
        out_tilt = mean_of(normal_grad * out_normal)
        yield
        inverse = next_norms[:, HEAD_DIM:]
        back_res = (inverse * (scaled - scaled_mean - normal * along)).astype(bf16)
        gain_along = mean_of(gain_normal)
        gain_square = mean_of(gain_normal * normal)
        to_low[0] = back_res
        to_low[1] = key
        to_sums[2:3, :HEAD_DIM] = jnp.sum(out_grad * out_normal, axis=0, keepdims=True)
        to_sums[3:4, :HEAD_DIM] = jnp.sum(out_grad, axis=0, keepdims=True)
        yield
        res_grad = next_out_norms[:, 2 * HEAD_DIM : 3 * HEAD_DIM] * (
            normal_grad - out_mean - out_normal * out_tilt
        )
        to_sums[1:2, :HEAD_DIM] = jnp.sum(res_grad, axis=0, keepdims=True)
        res_grad_low = res_grad.astype(bf16)
        hidden_base = dot_nn(res_grad_low, next_second[0, 0])
        mix = dot_nt(res_grad_low, back_res)
        yield
        mix_t = dot_nt(back_res, res_grad_low)
        causal = cols <= rows
        later = rows <= cols
        second_grad = jnp.where(causal, -mix, 0.0)
        hidden_more = dot_nn(second_grad, next_act[...])
        yield
        second_grad_t = jnp.where(later, -mix_t, 0.0)
        to_rows[1] = normal
        to_rows[2] = rate_gain
        to_rows[3] = rate_gain - along
        to_rows[4] = gain_normal + scaled
        to_rows[5] = -(along + rate * row_mean(square_gain))
        yield
        for index, value in enumerate(
            (-(gain_along + scaled_mean), -(3.0 * along + gain_square), inverse * inverse)
        ):
            to_spread[index] = jnp.concatenate([value, value], axis=1)
        mix = dot_nt(next_act[...], next_hidden[...])
        yield
        query_pre_grad = (hidden_base + hidden_more) * next_out_slope[...]
        query_pre_low = query_pre_grad.astype(bf16)
        to_sums[0:1] = jnp.sum(query_pre_grad, axis=0, keepdims=True)
        first = dot_nt(query_pre_low, next_grad[...])
        yield
        second_mix_t = jnp.where(later, mix + 1.0, 0.0)
        to_rows[0] = -dot_nn(second_mix_t, res_grad_low)
        first_t = dot_nt(next_grad[...], query_pre_low)
        yield
        first_grad = jnp.where(causal, -first, 0.0)
        mix = dot_nt(key, query)
        query_grad = dot_nt(query_pre_low, next_first[0])
        query_more = dot_nn(first_grad, key)
        yield
        first_grad_t = jnp.where(later, -first_t, 0.0)
        to_rows[6] = dot_nn(first_grad_t, query)
        first_mix_t = jnp.where(later, mix + 1.0, 0.0).astype(bf16)
        yield
        to_rows[7] = out_grad + query_grad + query_more
        to_wide[1] = dot_nn(second_grad_t, next_hidden[...])
        yield
        to_wide[0] = -dot_nn(first_mix_t, query_pre_low)
        mix = dot_nt(key, key)
        yield
        to_mix[...] = jnp.where(cols // MINI > rows // MINI, mix + 1.0, 0.0).astype(bf16)
        to_state[0] = dot_tn(query, query_pre_low)
        yield
        to_state[1] = dot_tn(res_grad_low, next_hidden[...])

    def conclude():
        place = jnp.minimum(devices + 1 - turn, devices - 1)
        _, key, miss, logit = unpack(place)
        normal = last_norms[:, :HEAD_DIM]
        upon = end_rows[0]
        upon_mean = mean_of(upon)
        upon_tilt = mean_of(upon * normal)
        yield
        pre_grad = end_known[...]
        mix = dot_nt(last_grad[...], pre_grad)
        mix_t = dot_nt(pre_grad, last_grad[...])
        yield
        rate = rate_of(logit)
        scaled_grad = last_norms[:, HEAD_DIM:] * (upon - upon_mean - normal * upon_tilt)
        error_grad = scaled_grad * (rate * gain)
        rate_grad = mean_of(scaled_grad * (miss * gain + square_gain * normal))
        yield
        error = miss + normal * gain
        gain_sum[...] += jnp.sum(
            scaled_grad * rate * error + error_grad * normal, axis=0, keepdims=True
        )
        bias_sum[...] += jnp.sum(error_grad, axis=0, keepdims=True)
        from_grad = dot_nt(last_grad[...], end_first[...])
        yield
        far = rows // MINI < cols // MINI
        near = rows // MINI > cols // MINI
        cross = jnp.where(far, mix, 0.0) + jnp.where(near, mix_t, 0.0)
        from_pre = dot_nt(pre_grad, last_first[0])
        from_cross = dot_nn(cross, key)
        yield
        key_grad = end_rows[1] + error_grad - from_grad + from_pre - from_cross
        back_rate = rate_grad * float(HEAD_DIM) * rate * (1.0 - rate * (1.0 / rate_scale))
        lane = lax.broadcasted_iota(jnp.int32, (chunk, HEAD_DIM), 1)
        tail = jnp.where(lane == 0, back_rate, 0.0)
        packed = jnp.concatenate([end_rows[2], key_grad, -error_grad, tail], axis=1).astype(bf16)
        back_ref[place, :chunk] = packed
        yield
        count = 6
        size = grad_sum.shape[0] // count
        for index in range(count):
            at = slice(index * size, (index + 1) * size)
            grad_sum[at] = grad_sum[at] + dot_tn(rows_ref[0, 0, :, at], packed)
            yield

    def chain(following, previous):
        wide_ref[...] = to_wide[...]
        row_ref[...] = to_rows[...]
        spread_ref[...] = to_spread[...]
        low_ref[...] = to_low[...]
        mix_ref[...] = to_mix[...]
        state_ref[...] = to_state[...]
        sums_ref[...] = to_sums[...]
        first_next = first_w[...]
        first_next_low = first_next.astype(bf16)
        first_next_b = first_b[...]
        state = second_w[...]
        state_b = second_b[...]
        for step in reversed(range(steps)):
            at = slice(step * MINI, (step + 1) * MINI)
            grad = wide_ref[0, at, :] - dot_nn(low_ref[1, at, :], first_next_low) - first_next_b
            if step + 1 < steps:
                grad = grad - dot_nn(mix_ref[at, :], known_ref[...])
            state_low = state.astype(bf16)
            own_act = now_act[at, :]
            own_back = low_ref[0, at, :]
            back_base = row_ref[0, at, :] - dot_nt(own_act, state_low) - state_b
            act_base = wide_ref[1, at, :] - dot_nn(own_back, state_low)
            interleave(following, 1)
            own_low = now_second[0, step]
            slope = now_slope[at, :]
            back_act_grad = (grad * slope).astype(bf16)
            upon = dot_nt(back_act_grad, own_low)
            interleave(following, 1)
            upon = back_base + upon
            own_normal, own_gain, own_grad, own_beta, own_alpha = (
                row_ref[index, at, :] for index in range(1, 6)
            )
            cross, cross_beta, square_inverse = (spread_ref[index, at, :] for index in range(3))
            main = dot_nn(upon * own_grad, own_low)
            sides = dot_nn(jnp.concatenate([own_normal, own_gain, own_beta], axis=0), own_low)
            interleave(previous, 1)
            alpha = row_mean(upon)
            beta = row_mean(upon * own_normal)
            gamma = row_mean(upon * own_gain)
            kappa = row_mean(upon * own_beta)
            level = alpha * own_alpha + beta * cross[:, :HEAD_DIM] + gamma
            tilt = alpha * cross + beta * cross_beta + kappa
            key_res_grad = square_inverse[:, :HEAD_DIM] * (
                upon * own_grad
                - alpha * own_gain
                - beta * own_beta
                - level
                - own_normal * tilt[:, :HEAD_DIM]
            )
            key_res_low = key_res_grad.astype(bf16)
            from_sides = (
                alpha * sides[MINI : 2 * MINI]
                + beta * sides[2 * MINI :]
                + jnp.concatenate([tilt, tilt], axis=1) * sides[:MINI]
            )
            factor = jnp.concatenate([square_inverse, square_inverse], axis=1) * slope
            known = act_base * slope + grad * now_curve[at, :] - factor * from_sides
            pre_grad = known + factor * main
            known_ref[at, :] = pre_grad.astype(bf16)
            state = state + dot_tn(
                jnp.concatenate([key_res_low, own_back], axis=0),
                jnp.concatenate([own_act, back_act_grad], axis=0),
            )
            state_b = state_b + jnp.sum(key_res_grad, axis=0, keepdims=True)
            row_ref[0, at, :] = upon
            interleave(following, 1)
            interleave(previous, 1)
        for generator in (following, previous):
            for _ in generator:
                pass
        pre_grad_all = known_ref[...]
        first_w[...] = first_next + dot_tn(low_ref[1], pre_grad_all) + state_ref[0]
        first_b[...] = (
            first_next_b
            + jnp.sum(pre_grad_all.astype(f32), axis=0, keepdims=True)
            + sums_ref[0:1]
        )
        second_w[...] = state + state_ref[1]
        second_b[...] = state_b + sums_ref[1:2, :HEAD_DIM]
        gain_sum[...] += sums_ref[2:3, :HEAD_DIM]
        bias_sum[...] += sums_ref[3:4, :HEAD_DIM]
        end_known[...] = pre_grad_all
        end_rows[0] = row_ref[0]
        end_rows[1] = row_ref[6]
        end_rows[2] = row_ref[7]
        end_first[...] = first_next_low

    @pl.when(turn == 0)
    def _():
        for _ in prepare():
            pass

    @pl.when((turn > 0) & (turn <= devices))
    def _():
        chain(prepare(), conclude())

    @pl.when(turn == devices + 1)
    def _():
        for _ in conclude():
            pass
        vector_ref[...] = jnp.zeros_like(vector_ref)
        for index in range(devices):
            first = slice(index * inner_part, (index + 1) * inner_part)
            small = slice(index * feature_part, (index + 1) * feature_part)
            vector_ref[index : index + 1, :inner_part] = first_b[:, first]
            for number, source in enumerate((second_b, gain_sum, bias_sum)):
                start = inner_part + number * feature_part
                vector_ref[index : index + 1, start : start + feature_part] = source[:, small]
        columns = jnp.transpose(vector_ref[...]).astype(bf16)
        lanes = slice(MATRIX_LANE, MATRIX_LANE + inner_part)
        for index in range(devices):
            first = slice(index * inner_part, (index + 1) * inner_part)
            back_ref[index, :HEAD_DIM, lanes] = first_w[:, first].astype(bf16)
            back_ref[index, HEAD_DIM : 2 * HEAD_DIM, lanes] = second_w[:, first].astype(bf16)
            back_ref[index, :chunk, VECTOR_LANE : VECTOR_LANE + 1] = columns[:, index : index + 1]
            back_ref[index, chunk:] = grad_sum[index * shard : (index + 1) * shard].astype(bf16)


def whole_block(shape):
    return pl.BlockSpec(shape, lambda index, *_: (0,) * len(shape))


STATE_SHAPES = ((HEAD_DIM, INNER), (1, INNER), (HEAD_DIM, INNER), (1, HEAD_DIM))


def chain_forward(packed, inner_part, feature_part):
    blocks, chunk, _ = packed.shape
    length = blocks * chunk
    steps = chunk // MINI
    row = (1, HEAD_DIM)

    def forth(shape):
        return pl.BlockSpec(
            shape, lambda turn: (jnp.minimum(turn, blocks - 1),) + (0,) * (len(shape) - 1)
        )

    def behind(shape):
        return pl.BlockSpec(
            shape, lambda turn: (jnp.maximum(turn - 1, 0),) + (0,) * (len(shape) - 1)
        )

    def of_length(width, dtype):
        return jax.ShapeDtypeStruct((length, width), dtype)

    wide = (chunk, INNER)
    return pl.pallas_call(
        functools.partial(forward_kernel, inner_part, feature_part),
        grid=(blocks + 1,),
        in_specs=[whole_block(packed.shape)],
        out_specs=[behind((1, HEAD_DIM, chunk))]
        + [forth(wide)] * 4
        + [
            forth((chunk, 2 * HEAD_DIM)),
            forth((1, HEAD_DIM, INNER)),
            forth((1, steps, HEAD_DIM, INNER)),
        ]
        + [behind(wide)] * 3
        + [whole_block(row)] * 2,
        out_shape=[jax.ShapeDtypeStruct((blocks, HEAD_DIM, chunk), bf16)]
        + [of_length(INNER, dtype) for dtype in (bf16, bf16, f32, f32)]
        + [
            of_length(2 * HEAD_DIM, f32),
            jax.ShapeDtypeStruct((blocks, HEAD_DIM, INNER), bf16),
            jax.ShapeDtypeStruct((blocks, steps, HEAD_DIM, INNER), bf16),
        ]
        + [of_length(INNER, dtype) for dtype in (bf16, f32, f32)]
        + [jax.ShapeDtypeStruct(row, f32)] * 2,
        scratch_shapes=[pltpu.VMEM(shape, f32) for shape in STATE_SHAPES]
        + [
            pltpu.VMEM(wide, bf16),
            pltpu.VMEM((chunk, HEAD_DIM), bf16),
            pltpu.VMEM(wide, f32),
        ]
        + [
            pltpu.VMEM((3, chunk, HEAD_DIM), f32),
            pltpu.VMEM((chunk, 2 * HEAD_DIM), f32),
            pltpu.VMEM((chunk, chunk), bf16),
        ]
        * 2
        + [
            pltpu.VMEM(wide, bf16),
            pltpu.VMEM(wide, bf16),
            pltpu.VMEM((chunk, HEAD_DIM), bf16),
            pltpu.VMEM((HEAD_DIM, INNER), bf16),
            pltpu.VMEM((HEAD_DIM, INNER), bf16),
            pltpu.VMEM((1, INNER), f32),
            pltpu.VMEM(row, f32),
        ],
        compiler_params=pltpu.CompilerParams(
            dimension_semantics=("arbitrary",), vmem_limit_bytes=VMEM_BYTES
        ),
        cost_estimate=pl.CostEstimate(
            flops=CHAIN_FLOPS, transcendentals=0, bytes_accessed=16 * length * INNER
        ),
        name="chain_forward",
    )(packed)


def chain_backward(packed, rows, sequence, head_grad, saved, inner_part, feature_part):
    act, grad_pre, slope, curve, norms, first_save, second_save = saved[:7]
    hidden, out_slope, out_norms, gain, bias = saved[7:]
    blocks, chunk, _ = packed.shape
    width = rows.shape[-1]
    shard = width // blocks
    steps = chunk // MINI
    row = (1, HEAD_DIM)
    wide = (chunk, INNER)
    narrow = (chunk, 2 * HEAD_DIM)

    def at(shape, delay):
        def index_map(turn, _):
            place = jnp.clip(blocks - 1 - turn + delay, 0, blocks - 1)
            return (place,) + (0,) * (len(shape) - 1)

        return pl.BlockSpec(shape, index_map)

    def rows_map(turn, chosen):
        place = jnp.clip(blocks + 1 - turn, 0, blocks - 1)
        return (place // SEQS, (place + chosen[0]) % SEQS, 0, 0)

    state = (HEAD_DIM, INNER)
    carried = [
        pltpu.VMEM((2,) + wide, f32),
        pltpu.VMEM((8, chunk, HEAD_DIM), f32),
        pltpu.VMEM((3,) + narrow, f32),
        pltpu.VMEM((2, chunk, HEAD_DIM), bf16),
        pltpu.VMEM((chunk, chunk), bf16),
        pltpu.VMEM((2,) + state, f32),
        pltpu.VMEM((8, INNER), f32),
    ]
    return pl.pallas_call(
        functools.partial(backward_kernel, inner_part, feature_part),
        grid_spec=pltpu.PrefetchScalarGridSpec(
            num_scalar_prefetch=1,
            grid=(blocks + 2,),
            in_specs=[
                whole_block(packed.shape),
                pl.BlockSpec((1, 1, chunk, width), rows_map),
                at((1, HEAD_DIM, chunk), 0),
                at(wide, 0),
                at(wide, 0),
                at(wide, 0),
                at(wide, 0),
                at(narrow, 0),
                at(wide, 0),
                at((1,) + state, 0),
                at((1, 1) + state, 0),
                at(wide, 1),
                at(wide, 1),
                at(wide, 1),
                at((1, steps) + state, 1),
                at(wide, 2),
                at(narrow, 2),
                at((1,) + state, 2),
                whole_block(row),
                whole_block(row),
            ],
            out_specs=whole_block((blocks, chunk + shard, LANES)),
            scratch_shapes=[pltpu.VMEM(shape, f32) for shape in STATE_SHAPES + (row, row)]
            + [
                pltpu.VMEM(wide, bf16),
                pltpu.VMEM((chunk, 128), f32),
                pltpu.VMEM((width, LANES), f32),
            ]
            + carried
            + carried
            + [
                pltpu.VMEM(wide, bf16),
                pltpu.VMEM((3, chunk, HEAD_DIM), f32),
                pltpu.VMEM(state, bf16),
            ],
        ),
        out_shape=jax.ShapeDtypeStruct((blocks, chunk + shard, LANES), bf16),
        compiler_params=pltpu.CompilerParams(
            dimension_semantics=("arbitrary",), vmem_limit_bytes=VMEM_BYTES
        ),
        cost_estimate=pl.CostEstimate(
            flops=CHAIN_FLOPS, transcendentals=0, bytes_accessed=16 * blocks * chunk * INNER
        ),
        name="chain_backward",
    )(
        sequence,
        packed,
        rows,
        head_grad,
        act,
        grad_pre,
        hidden,
        out_slope,
        norms,
        out_norms,
        first_save,
        second_save,
        act,
        slope,
        curve,
        second_save,
        grad_pre,
        norms,
        first_save,
        gain,
        bias,
    )


def layer_norm_parts(values):
    centred = values - row_mean(values)
    inverse = lax.rsqrt(row_mean(centred * centred) + epsilon)
    return centred * inverse, inverse


def layer_norm_back(normal, inverse, scaling, grad):
    scaled = grad * scaling
    return inverse * (scaled - row_mean(scaled) - normal * row_mean(scaled * normal))


def start_kernel(
    head_count,
    rows_ref,
    weights_ref,
    gain_ref,
    inner_ref,
    packed_ref,
    normed_ref,
    matrix_ref,
):
    tensor_count = rows_ref.shape[0]
    seq_count, chunk, _ = normed_ref.shape
    rows = chunk // tensor_count
    matrix_ref[...] = jnp.zeros_like(matrix_ref)
    for head in range(head_count):
        first = head * 3 * HEAD_DIM
        rate = head_count * 3 * HEAD_DIM + head
        column = weights_ref[:, rate : rate + 1]
        matrix_ref[head, :, : 3 * HEAD_DIM] = weights_ref[:, first : first + 3 * HEAD_DIM]
        matrix_ref[head, :, RATE_LANE : RATE_LANE + 1] = column
        matrix_ref[head, :, RATE_LANE + 1 : RATE_LANE + 2] = column
    lane = lax.broadcasted_iota(jnp.int32, (chunk, LANES), 1)
    for sequence in range(seq_count):
        part = slice(sequence * rows, (sequence + 1) * rows)
        values = jnp.concatenate([rows_ref[index, part] for index in range(tensor_count)], axis=0)
        normal, _ = layer_norm_parts(values.astype(f32))
        normed = (normal * gain_ref[...]).astype(bf16)
        normed_ref[sequence] = normed
        for head in range(head_count):
            projected = dot_nn(normed, matrix_ref[head])
            rest = projected - projected.astype(bf16).astype(f32)
            projected = jnp.where(lane == RATE_LANE + 1, rest, projected).astype(bf16)
            packed_ref[head * seq_count + sequence] = jnp.where(
                lane >= VECTOR_LANE, inner_ref[head], projected
            )
    for index in range(head_count * seq_count, packed_ref.shape[0]):
        packed_ref[index] = jnp.zeros((chunk, LANES), bf16)


def feed_forward_kernel(
    heads_ref,
    rows_ref,
    weights_ref,
    out_ref,
    gain_ref,
    terms_ref,
    mixed_ref,
    normed_ref,
    back_ref,
    swiglu_ref,
    cot_ref,
):
    tensor_count, head_count, seq_count, _, chunk = heads_ref.shape
    ff_local = swiglu_ref.shape[1]
    rows = chunk // tensor_count
    total = seq_count * chunk
    for sequence in range(seq_count):
        part = slice(sequence * rows, (sequence + 1) * rows)
        other = slice((seq_count + sequence) * rows, (seq_count + sequence + 1) * rows)
        values = jnp.concatenate([rows_ref[index, part] for index in range(tensor_count)], axis=0)
        mixed = values.astype(f32)
        for index in range(tensor_count):
            heads = [heads_ref[index, head, sequence] for head in range(head_count)]
            heads = jnp.transpose(jnp.concatenate(heads, axis=0).astype(f32))
            mixed = mixed + dot_nt(heads, out_ref[index])
        for index in range(tensor_count):
            mixed_ref[index, sequence] = mixed[index * rows : (index + 1) * rows]
        normal, _ = layer_norm_parts(mixed)
        at = slice(sequence * chunk, (sequence + 1) * chunk)
        normed_ref[at] = (normal * gain_ref[...]).astype(bf16)
        for index in range(tensor_count):
            first = sequence * chunk + index * rows
            cot_ref[first : first + rows] = rows_ref[index, other]
    normed = normed_ref[...]
    cot = cot_ref[...]
    for first in range(0, ff_local, 256):
        at = slice(first, first + 256)
        beyond = slice(ff_local + first, ff_local + first + 256)
        gate = dot_nn(normed, weights_ref[:, at])
        up = dot_nn(normed, weights_ref[:, beyond])
        back = dot_nn(cot, weights_ref[:, 2 * ff_local + first : 2 * ff_local + first + 256])
        share = jax.nn.sigmoid(gate)
        silu = gate * share
        swiglu_ref[:, at] = (silu * up).astype(bf16)
        back_ref[:, at] = (back * up * (share * (1.0 + gate * (1.0 - share)))).astype(bf16)
        back_ref[:, beyond] = (back * silu).astype(bf16)
    ffn_term = dot_nt(back_ref[...], weights_ref[:, : 2 * ff_local]).astype(bf16)
    down_term = dot_nt(swiglu_ref[...], weights_ref[:, 2 * ff_local : 3 * ff_local]).astype(bf16)
    for sequence in range(seq_count):
        for index in range(tensor_count):
            first = sequence * chunk + index * rows
            terms_ref[index, sequence] = ffn_term[first : first + rows]
            terms_ref[index, seq_count + sequence] = down_term[first : first + rows]


def feed_forward_grad_kernel(normed_ref, back_ref, swiglu_ref, cot_ref, grads_ref):
    normed = jnp.transpose(normed_ref[...].astype(f32)).astype(bf16)
    cot = jnp.transpose(cot_ref[...].astype(f32)).astype(bf16)
    width = back_ref.shape[1]
    for first in range(0, width, 256):
        at = slice(first, first + 256)
        grads_ref[:, at] = dot_nn(normed, back_ref[:, at]).astype(bf16)
    for first in range(0, swiglu_ref.shape[1], 256):
        at = slice(width + first, width + first + 256)
        grads_ref[:, at] = dot_nn(cot, swiglu_ref[:, first : first + 256]).astype(bf16)


def head_back_kernel(grads_ref, out_ref, heads_ref, back_ref, out_grad_ref):
    head_count, seq_count, _, chunk = heads_ref.shape
    devices, shard, _ = out_grad_ref.shape
    total = None
    for sequence in range(seq_count):
        grads = grads_ref[sequence]
        back = jnp.transpose(dot_nn(grads, out_ref[...])).astype(bf16)
        for head in range(head_count):
            back_ref[head * seq_count + sequence] = back[head * HEAD_DIM : (head + 1) * HEAD_DIM]
        heads = [heads_ref[head, sequence] for head in range(head_count)]
        term = dot_nt(jnp.transpose(grads.astype(f32)), jnp.concatenate(heads, axis=0))
        total = term if total is None else total + term
    for index in range(head_count * seq_count, devices):
        back_ref[index] = jnp.zeros((HEAD_DIM, chunk), bf16)
    for index in range(devices):
        out_grad_ref[index] = total[index * shard : (index + 1) * shard].astype(bf16)


def matrix_output_kernel(sums_ref, out_ref, weights_ref, gate_up_ref, down_ref, out_grad_ref, gain_ref):
    ff_local = down_ref.shape[1]
    sums = sums_ref[...].astype(f32)
    for index in range(2):
        gate_up_ref[:, index, :] = sums[:, index * ff_local : (index + 1) * ff_local]
    down_ref[...] = sums[:, 2 * ff_local :]
    total = out_ref[0].astype(f32)
    for index in range(1, out_ref.shape[0]):
        total = total + out_ref[index].astype(f32)
    out_grad_ref[...] = jnp.transpose(total)
    products = sums[:, : 2 * ff_local] * weights_ref[:, : 2 * ff_local].astype(f32)
    gain = jnp.sum(products, axis=-1, keepdims=True)
    gain_ref[...] = jnp.broadcast_to(gain, gain_ref.shape)


def tail_kernel(
    received_ref,
    matrix_ref,
    own_ref,
    gain_two_ref,
    gains_ref,
    terms_ref,
    qkv_ref,
    small_ref,
    state_ref,
):
    head_count = matrix_ref.shape[0]
    shard = own_ref.shape[1]
    tensor_count, term_rows, width = terms_ref.shape
    chunk = received_ref.shape[1] - shard
    seq_count = (term_rows - 16) * tensor_count // chunk
    rows = chunk // tensor_count
    lane = lax.broadcasted_iota(jnp.int32, (chunk, LANES), 1)
    for sequence in range(seq_count):
        total = None
        for head in range(head_count):
            values = received_ref[head * seq_count + sequence, :chunk]
            values = jnp.where(lane <= RATE_LANE, values, jnp.zeros_like(values))
            term = dot_nt(values, matrix_ref[head])
            total = term if total is None else total + term
        for index in range(tensor_count):
            part = total[index * rows : (index + 1) * rows]
            terms_ref[index, sequence * rows : (sequence + 1) * rows] = part.astype(bf16)
    lane = lax.broadcasted_iota(jnp.int32, (shard, LANES), 1)
    column = lax.broadcasted_iota(jnp.int32, (shard, 128), 1)
    gain = None
    small = jnp.where(column == 1, gain_two_ref[...], 0.0)
    for head in range(head_count):
        grads = received_ref[head * seq_count, chunk:].astype(f32)
        state = received_ref[head * seq_count, :chunk, RATE_LANE:].astype(f32)
        for sequence in range(1, seq_count):
            grads = grads + received_ref[head * seq_count + sequence, chunk:].astype(f32)
            state = state + received_ref[
                head * seq_count + sequence, :chunk, RATE_LANE:
            ].astype(f32)
        state_ref[head] = state
        for index in range(3):
            at = slice(index * HEAD_DIM, (index + 1) * HEAD_DIM)
            qkv_ref[index, :, head * HEAD_DIM : (head + 1) * HEAD_DIM] = grads[:, at]
        products = jnp.where(lane <= RATE_LANE, grads * own_ref[head].astype(f32), 0.0)
        products = jnp.sum(products, axis=-1, keepdims=True)
        gain = products if gain is None else gain + products
        small = jnp.where(column == 2 + head, grads[:, RATE_LANE : RATE_LANE + 1], small)
    small = jnp.transpose(jnp.where(column == 0, gain, small))[: small_ref.shape[0]]
    small_ref[...] = small
    gain = small[:2] / gains_ref[...]
    high = gain.astype(bf16)
    low = (gain - high.astype(f32)).astype(bf16)
    block = jnp.concatenate([high.astype(f32), low.astype(f32), jnp.zeros((12, shard), f32)], axis=0)
    for index in range(tensor_count):
        first = seq_count * rows
        terms_ref[index, first:, :] = jnp.zeros((16, width), bf16)
        terms_ref[index, first:, :shard] = block.astype(bf16)


def whole_call(kernel, name, operands, results, vmem_bytes=GLUE_BYTES):
    def spec(shape):
        return pl.BlockSpec(shape, lambda: (0,) * len(shape))

    return pl.pallas_call(
        kernel,
        in_specs=[spec(operand.shape) for operand in operands],
        out_specs=[spec(result.shape) for result in results],
        out_shape=results,
        compiler_params=pltpu.CompilerParams(vmem_limit_bytes=vmem_bytes),
        name=name,
    )(*operands)


def dots(subscripts, left, right):
    return jnp.einsum(subscripts, left, right, preferred_element_type=f32)


def exchange(values, axis):
    return lax.all_to_all(values, axis, 0, 0, tiled=False)


def share_out(values, axis):
    count = lax.axis_size(axis)
    return exchange(jnp.broadcast_to(values[None], (count,) + values.shape), axis)


def ordered(*values):
    return lax.optimization_barrier(values)


def inner_block(matrix_one, matrix_two, vectors, rows):
    width = matrix_one.shape[-1]
    matrices = jnp.concatenate([matrix_one, matrix_two], axis=-2)
    column = jnp.concatenate(vectors, axis=-1)[..., None]
    lead = [(0, 0)] * (column.ndim - 2)
    column = jnp.pad(
        column,
        lead + [(0, rows - column.shape[-2]), (VECTOR_LANE, LANES - VECTOR_LANE - 1)],
    )
    matrices = jnp.pad(
        matrices,
        lead + [(0, rows - matrices.shape[-2]), (MATRIX_LANE, LANES - MATRIX_LANE - width)],
    )
    return column + matrices


def local(
    tokens,
    gain_attn,
    gain_ffn,
    w_qkv,
    w_rate,
    w_out,
    w_gate_up,
    w_down,
    w_one,
    b_one,
    w_two,
    b_two,
    norm_gain_inner,
    norm_bias_inner,
    cotangent,
):
    device_count = lax.axis_size(DP)
    tensor_count = lax.axis_size("tensor")
    local_rows, seq_count, width = tokens.shape
    row_count = local_rows * seq_count
    chunk = local_rows * tensor_count
    head_count = w_rate.shape[1]
    local_width = head_count * HEAD_DIM
    shard = w_qkv.shape[0]
    part = gain_attn.shape[0]
    ff_local = w_down.shape[0]
    chain_count = seq_count * head_count
    inner_part = w_one.shape[2]
    feature_part = b_two.shape[1]
    assert chain_count <= device_count and seq_count == SEQS
    assert chunk == 2 * HEAD_DIM and inner_part <= 32 and part <= shard
    rank = lax.axis_index("tensor")
    place = lax.axis_index(DP)

    own_tokens = tokens.transpose(1, 0, 2).reshape(row_count, width)
    own_cot = cotangent.transpose(1, 0, 2).reshape(row_count, width)
    row_full = share_out(jnp.concatenate([own_tokens, own_cot], axis=0), "tensor")
    head_columns = w_qkv.reshape(shard, 3, head_count, HEAD_DIM).transpose(0, 2, 1, 3)
    gain_columns = jnp.pad(jnp.stack([gain_attn, gain_ffn], axis=1), ((0, shard - part), (0, 0)))
    qkv_pack = jnp.concatenate(
        [head_columns.reshape(shard, 3 * local_width), w_rate, gain_columns], axis=1
    )
    qkv_half = lax.all_gather(qkv_pack, "inner", axis=0, tiled=True)
    qkv_full = lax.all_gather(qkv_half, "outer", axis=0, tiled=True)
    qkv_full, row_full = ordered(qkv_full, row_full)
    some_gains = qkv_full[:, 3 * local_width + head_count :]
    some_gains = some_gains.reshape(device_count, shard, 2)[:, :part].transpose(2, 0, 1)
    gains = lax.all_gather(some_gains.reshape(2, device_count * part), "tensor", axis=0)
    gains = gains.reshape(tensor_count, 2, device_count, part).transpose(1, 2, 0, 3)
    gains = gains.reshape(2, width).astype(f32)
    scale_attn, scale_ffn = gains[0:1], gains[1:2]

    ffn_pack = jnp.concatenate(
        [w_gate_up.reshape(shard, 2 * ff_local), w_down.T, w_out.T], axis=1
    )
    ffn_full = lax.all_gather(ffn_pack, DP, axis=0, tiled=True)
    own_out = ffn_full[:, 3 * ff_local :]

    inner = inner_block(
        w_one,
        w_two.transpose(0, 2, 1),
        [b_one, b_two, norm_gain_inner, norm_bias_inner],
        chunk,
    )
    shape = jax.ShapeDtypeStruct
    packed, normed_attn, head_matrix = whole_call(
        functools.partial(start_kernel, head_count),
        "projections",
        (row_full, qkv_full, scale_attn, inner),
        (
            shape((device_count, chunk, LANES), bf16),
            shape((seq_count, chunk, width), bf16),
            shape((head_count, width, LANES), bf16),
        ),
    )
    chain_in = exchange(packed, DP)

    side = lax.axis_index("inner")
    kept = lax.dynamic_index_in_dim(normed_attn, side, 0)
    given = lax.dynamic_index_in_dim(normed_attn, 1 - side, 0)
    taken = lax.ppermute(given, "inner", [(0, 1), (1, 0)])
    pair = jnp.concatenate([kept, taken], axis=0)
    chain_in, own_out, pair = ordered(chain_in, own_out, pair)
    chain_rows = lax.all_gather(pair, "outer", axis=0)
    out_full = lax.all_gather(own_out, "tensor", axis=0)

    forward_out = chain_forward(chain_in, inner_part, feature_part)
    saved = forward_out[1:]
    head_local = exchange(forward_out[0], DP)[:chain_count]
    head_local = head_local.reshape(head_count, seq_count, HEAD_DIM, chunk)
    head_rows = lax.all_gather(head_local, "tensor", axis=0, tiled=False)

    group_rows = seq_count * chunk
    terms, mixed, normed_ffn, back_gate_up, swiglu, group_cot = whole_call(
        feed_forward_kernel,
        "feed_forward",
        (head_rows, row_full, ffn_full, out_full, scale_ffn),
        (
            shape((tensor_count, 2 * seq_count, local_rows, width), bf16),
            shape((tensor_count, seq_count, local_rows, width), f32),
            shape((group_rows, width), bf16),
            shape((group_rows, 2 * ff_local), bf16),
            shape((group_rows, ff_local), bf16),
            shape((group_rows, width), bf16),
        ),
        VMEM_BYTES,
    )
    ffn_sums = exchange(terms, "tensor")
    (ffn_grads,) = whole_call(
        feed_forward_grad_kernel,
        "feed_forward_grads",
        (normed_ffn, back_gate_up, swiglu, group_cot),
        (shape((width, 3 * ff_local), bf16),),
        VMEM_BYTES,
    )
    ffn_grad_sums = lax.psum_scatter(ffn_grads, DP, scatter_dimension=0, tiled=True)
    ffn_sums, chain_rows, _ = ordered(ffn_sums, chain_rows, ffn_grads)
    ffn_sums = ffn_sums.astype(f32).sum(axis=0)
    own_mixed = lax.dynamic_index_in_dim(mixed, rank, 0, keepdims=False)
    own_normal, own_inverse = layer_norm_parts(own_mixed)
    back_mixed = own_cot.astype(f32).reshape(own_mixed.shape) + layer_norm_back(
        own_normal, own_inverse, scale_ffn, ffn_sums[:seq_count]
    )
    result = (own_mixed + ffn_sums[seq_count:]).astype(bf16)
    attn_grads = lax.all_gather(back_mixed.astype(bf16), "tensor", axis=1, tiled=True)
    back_head, out_terms = whole_call(
        head_back_kernel,
        "head_back",
        (attn_grads, own_out, head_local),
        (
            shape((device_count, HEAD_DIM, chunk), bf16),
            shape((device_count, shard, local_width), bf16),
        ),
    )
    head_grad = exchange(back_head, DP)
    out_sums = exchange(out_terms, DP)

    chosen = jnp.reshape(side, (1,)).astype(jnp.int32)
    back_packed = chain_backward(
        chain_in, chain_rows, chosen, head_grad, saved, inner_part, feature_part
    )
    received = exchange(back_packed, DP)
    grad_gate_up, grad_down, grad_out, gain_two = whole_call(
        matrix_output_kernel,
        "matrix_outputs",
        (ffn_grad_sums, out_sums, ffn_pack),
        (
            shape((shard, 2, ff_local), f32),
            shape((shard, ff_local), f32),
            shape((local_width, shard), f32),
            shape((shard, 128), f32),
        ),
    )
    own_matrix = lax.dynamic_slice_in_dim(head_matrix, place * shard, shard, 1)
    own_gains = lax.dynamic_slice_in_dim(gains, place * shard, shard, 1)
    terms, grad_qkv, small, state_block = whole_call(
        tail_kernel,
        "tail",
        (received, head_matrix, own_matrix, gain_two, own_gains),
        (
            shape((tensor_count, row_count + 16, width), bf16),
            shape((3, shard, local_width), f32),
            shape((8, shard), f32),
            shape((head_count, chunk, LANES - RATE_LANE), f32),
        ),
    )
    tail = exchange(terms, "tensor").astype(f32).sum(axis=0)
    own_inputs = tokens.transpose(1, 0, 2).astype(f32)
    own_normal, own_inverse = layer_norm_parts(own_inputs)
    attn_sums = tail[:row_count].reshape(own_inputs.shape)
    input_grad = back_mixed + layer_norm_back(own_normal, own_inverse, scale_attn, attn_sums)
    gain_sums = tail[row_count : row_count + 2, :shard] + tail[row_count + 2 : row_count + 4, :shard]
    gain_sums = lax.dynamic_slice_in_dim(gain_sums, rank * part, part, 1)

    matrices = state_block[..., MATRIX_LANE - RATE_LANE :][..., :inner_part]
    grad_one = matrices[:, :HEAD_DIM]
    grad_two = matrices[:, HEAD_DIM : 2 * HEAD_DIM].transpose(0, 2, 1)
    columns = state_block[:, :, VECTOR_LANE - RATE_LANE]
    ends = [inner_part + index * feature_part for index in range(4)]
    grad_b_one = columns[:, : ends[0]]
    grad_b_two, grad_gain_inner, grad_bias_inner = (
        columns[:, ends[index] : ends[index + 1]] for index in range(3)
    )

    def by_token(values):
        return values.reshape(seq_count, local_rows, width).transpose(1, 0, 2)

    return (
        by_token(result),
        by_token(input_grad),
        gain_sums[0],
        gain_sums[1],
        grad_qkv.transpose(1, 0, 2),
        small[2 : 2 + head_count].T,
        grad_out,
        grad_gate_up,
        grad_down.T,
        grad_one,
        grad_b_one,
        grad_two,
        grad_b_two,
        grad_gain_inner,
        grad_bias_inner,
    )


def solution(mesh):
    devices = mesh.devices
    dp_count, tensor_count = mesh.shape["dp"], mesh.shape["tensor"]
    devices = devices.reshape(dp_count // SEQS, SEQS, tensor_count)
    split = jax.sharding.Mesh(devices, DP + ("tensor",))
    rows = P(DP + ("tensor",), None, None)
    gains = P(DP + ("tensor",))
    placed = (
        rows,
        gains,
        gains,
        P(DP, None, "tensor"),
        P(DP, "tensor"),
        P("tensor", DP),
        P(DP, None, "tensor"),
        P("tensor", DP),
        P("tensor", None, DP),
        P("tensor", DP),
        P("tensor", DP, None),
        P("tensor", DP),
        P("tensor", DP),
        P("tensor", DP),
    )
    return jax.shard_map(
        local,
        mesh=split,
        in_specs=placed + (rows,),
        out_specs=(rows,) + placed,
        check_vma=False,
    )
```

```python
import functools


import jax
import jax.numpy as jnp
from jax import lax
from jax.experimental import pallas as pl
from jax.experimental.pallas import tpu as pltpu
from jax.sharding import PartitionSpec as P

HEAD_DIM = 64
INNER = 256
MINI = 16
SEQS = 2
LANES = 256
RATE_LANE = 3 * HEAD_DIM
VECTOR_LANE = RATE_LANE + 2
MATRIX_LANE = LANES - 32
VMEM_BYTES = 56 * 1024 * 1024
DP = ("outer", "inner")
CHAIN_FLOPS = 27_000_000_000
GLUE_BYTES = 32 * 1024 * 1024

epsilon = 1e-05
inner_epsilon = 1e-06
inner_rate = 0.5
rate_scale = inner_rate / (MINI * HEAD_DIM)
root_half = 0.7071067811865476
normal_peak = 0.3989422804014327

f32 = jnp.float32
bf16 = jnp.bfloat16


def dot_nn(a, b):
    return lax.dot_general(
        a.astype(bf16), b.astype(bf16), (((1,), (0,)), ((), ())), preferred_element_type=f32
    )


def dot_nt(a, b):
    return lax.dot_general(
        a.astype(bf16), b.astype(bf16), (((1,), (1,)), ((), ())), preferred_element_type=f32
    )


def dot_tn(a, b):
    return lax.dot_general(
        a.astype(bf16), b.astype(bf16), (((0,), (0,)), ((), ())), preferred_element_type=f32
    )


def row_mean(values):
    return jnp.mean(values, axis=-1, keepdims=True)


def density_and_share(values):
    density = jnp.exp(-0.5 * values * values) * normal_peak
    share = 0.5 * (1.0 + lax.erf(values * root_half))
    return density, share


def token_grid(count):
    rows = lax.broadcasted_iota(jnp.int32, (count, count), 0)
    cols = lax.broadcasted_iota(jnp.int32, (count, count), 1)
    return rows, cols


def wide_mean(values):
    high = values.astype(bf16)
    low = (values - high.astype(f32)).astype(bf16)
    ones = jnp.full((values.shape[1], 128), 1.0 / values.shape[1], bf16)
    return dot_nn(high, ones) + dot_nn(low, ones)


def mean_of(values):
    return wide_mean(values)[:, :HEAD_DIM]


def two_parts(packed):
    return packed[:, :HEAD_DIM], packed[:, HEAD_DIM : 2 * HEAD_DIM]


def rate_logit(packed):
    source = lax.broadcasted_iota(jnp.int32, (2 * HEAD_DIM, 128), 0)
    spread = jnp.where((source >= HEAD_DIM) & (source < HEAD_DIM + 2), 1.0, 0.0)
    return dot_nn(packed[:, 2 * HEAD_DIM :], spread)


def alternate(*generators):
    left = list(generators)
    while left:
        for generator in list(left):
            if next(generator, generator) is generator:
                left.remove(generator)
            else:
                yield


def interleave(generator, count):
    for _ in range(count):
        if next(generator, generator) is generator:
            return


def forward_kernel(
    inner_part,
    feature_part,
    packed_ref,
    normed_ref,
    act_ref,
    grad_pre_ref,
    slope_ref,
    curve_ref,
    norms_ref,
    first_save,
    second_save,
    hidden_ref,
    out_slope_ref,
    out_norms_ref,
    gain_ref,
    bias_ref,
    first_w,
    first_b,
    second_w,
    second_b,
    known_ref,
    back_res_ref,
    pre_ref,
    to_rows,
    to_level,
    to_mix,
    row_ref,
    level_ref,
    mix_ref,
    done_act,
    done_grad,
    done_back,
    done_first,
    done_second,
    done_first_b,
    done_second_b,
):
    devices, chunk, _ = packed_ref.shape
    steps = chunk // MINI
    turn = pl.program_id(0)

    @pl.when(turn == 0)
    def _():
        for index in range(devices):
            block = packed_ref[index, :, LANES - 128 :].astype(f32)
            first = slice(index * inner_part, (index + 1) * inner_part)
            lanes = slice(MATRIX_LANE - LANES + 128, MATRIX_LANE - LANES + 128 + inner_part)
            first_w[:, first] = block[:HEAD_DIM, lanes]
            second_w[:, first] = block[HEAD_DIM : 2 * HEAD_DIM, lanes]
            at = VECTOR_LANE - LANES + 128
            vector = jnp.transpose(block)[at : at + 1]
            first_b[:, first] = vector[:, :inner_part]
            small = slice(index * feature_part, (index + 1) * feature_part)
            for number, target in enumerate((second_b, gain_ref, bias_ref)):
                start = inner_part + number * feature_part
                target[:, small] = vector[:, start : start + feature_part]
        known_ref[...] = jnp.zeros_like(known_ref)
        centred = second_w[...]
        second_w[...] = centred - jnp.mean(centred, axis=0, keepdims=True)
        second_b[...] = second_b[...] - row_mean(second_b[...])

    gain = gain_ref[...]
    bias = bias_ref[...]
    rows, cols = token_grid(chunk)

    def finish():
        query, key = two_parts(packed_ref[jnp.maximum(turn - 1, 0)])
        causal = cols <= rows
        mix = dot_nt(query, key)
        query_base = dot_nn(query, done_first[...])
        yield
        first_mix = jnp.where(causal, mix + 1.0, 0.0)
        taken = dot_nn(first_mix, done_grad[...])
        yield
        query_pre = query_base + done_first_b[...] - taken
        density, share = density_and_share(query_pre)
        hidden = (query_pre * share).astype(bf16)
        hidden_ref[...] = hidden
        out_slope_ref[...] = share + query_pre * density
        yield
        mix = dot_nt(hidden, done_act[...])
        res_base = dot_nt(hidden, done_second[...])
        yield
        second_mix = jnp.where(causal, mix + 1.0, 0.0)
        taken = dot_nn(second_mix, done_back[...])
        yield
        query_res = res_base + done_second_b[...] - taken
        square = mean_of(query_res * query_res)
        yield
        out_inverse = lax.rsqrt(square + inner_epsilon)
        out_normal = query_res * out_inverse
        outputs = query.astype(f32) + out_normal * gain + bias
        middle = mean_of(outputs)
        out_norms_ref[:, :HEAD_DIM] = out_normal
        out_norms_ref[:, 2 * HEAD_DIM : 3 * HEAD_DIM] = out_inverse
        yield
        centred = outputs - middle
        square = mean_of(centred * centred)
        yield
        head_inverse = lax.rsqrt(square + epsilon)
        head_normal = centred * head_inverse
        out_norms_ref[:, HEAD_DIM : 2 * HEAD_DIM] = head_normal
        out_norms_ref[:, 3 * HEAD_DIM :] = head_inverse
        normed_ref[0] = jnp.transpose(head_normal).astype(bf16)

    def ahead(place):
        packed = packed_ref[place]
        _, key = two_parts(packed)
        value = packed[:, 2 * HEAD_DIM : 3 * HEAD_DIM]
        logit = rate_logit(packed)
        mix = dot_nt(key, key)
        yield
        rate = jax.nn.sigmoid(logit) * rate_scale
        square_gain = gain * gain
        level_gain = rate * row_mean(square_gain)
        rate_base = rate[:, :HEAD_DIM] * (
            (key.astype(f32) - value.astype(f32) + bias) * gain
        )
        middle = mean_of(rate_base)
        to_rows[0] = rate_base
        to_rows[1] = rate[:, :HEAD_DIM] * square_gain - level_gain[:, :HEAD_DIM]
        to_level[...] = level_gain * inner_epsilon
        to_mix[...] = jnp.where(cols // MINI < rows // MINI, mix + 1.0, 0.0).astype(bf16)
        yield
        to_rows[2] = middle

    def chain(others):
        _, key = two_parts(packed_ref[jnp.minimum(turn, devices - 1)])
        row_ref[...] = to_rows[...]
        level_ref[...] = to_level[...]
        mix_ref[...] = to_mix[...]
        first_low = first_w[...].astype(bf16)
        first_save[0] = first_low
        start_first_b = first_b[...]
        start_b = second_b[...]
        pre_ref[...] = dot_nn(key, first_low) + start_first_b
        state = second_w[...]
        start_low = state.astype(bf16)
        state_b = start_b
        for step in range(steps):
            at = slice(step * MINI, (step + 1) * MINI)
            own_base = row_ref[0, at, :]
            own_gain = row_ref[1, at, :]
            pre = pre_ref[at, :]
            if step >= 1:
                taken = dot_nn(mix_ref[at, :], known_ref[...])
                pre = pre - taken
            density, share = density_and_share(pre)
            act = (pre * share).astype(bf16)
            state_low = state.astype(bf16)
            res = dot_nt(act, state_low)
            slope = share + pre * density
            second_save[0, step] = state_low
            interleave(others, 1)
            res = res + state_b
            weighted = own_gain * res
            parts = dot_nn(jnp.concatenate([res, weighted], axis=0), state_low)
            base_act = dot_nn(own_base, state_low)
            interleave(others, 1)
            square = jnp.sum(res * res, axis=-1, keepdims=True)
            sum_gain = jnp.sum(weighted, axis=-1, keepdims=True)
            sum_base = jnp.sum(own_base * res, axis=-1, keepdims=True)
            sum_square = jnp.sum(weighted * res, axis=-1, keepdims=True)
            inverse = lax.rsqrt(square * (1.0 / HEAD_DIM) + inner_epsilon)
            scaled_mean = row_ref[2, at, :] + inverse * sum_gain * (1.0 / HEAD_DIM)
            along = inverse * (sum_base + inverse * sum_square) * (1.0 / HEAD_DIM)
            square_inverse = inverse * inverse
            along_half = along - square_inverse * level_ref[at, :]
            along_wide = jnp.concatenate([along_half, along_half], axis=1)
            normal = res * inverse
            back_res = inverse * (
                own_base + own_gain * normal - scaled_mean - normal * along_half[:, :HEAD_DIM]
            )
            back_low = back_res.astype(bf16)
            with_base = inverse * slope * base_act
            with_part = square_inverse * slope
            with_res = with_part * along_wide
            grad_full = with_base + (with_part * parts[MINI:] - with_res * parts[:MINI])
            grad = grad_full.astype(bf16)
            known_ref[at, :] = grad
            state = state - dot_tn(back_low, act)
            state_b = state_b - jnp.sum(back_res, axis=0, keepdims=True)
            slope_ref[at, :] = slope
            back_act = inverse * base_act + square_inverse * (
                parts[MINI:] - along_wide * parts[:MINI]
            )
            curve_ref[at, :] = back_act * density * (2.0 - pre * pre)
            act_ref[at, :] = act
            grad_pre_ref[at, :] = grad
            back_res_ref[at, :] = back_low
            norms_ref[at, :HEAD_DIM] = normal
            norms_ref[at, HEAD_DIM:] = jnp.broadcast_to(inverse, (MINI, HEAD_DIM))
        for _ in others:
            pass
        grad_all = known_ref[...]
        first_w[...] = first_w[...] - dot_tn(key, grad_all)
        first_b[...] = start_first_b - jnp.sum(grad_all.astype(f32), axis=0, keepdims=True)
        second_w[...] = state
        second_b[...] = state_b
        done_act[...] = act_ref[...]
        done_grad[...] = grad_all
        done_back[...] = back_res_ref[...]
        done_first[...] = first_low
        done_second[...] = start_low
        done_first_b[...] = start_first_b
        done_second_b[...] = start_b

    @pl.when(turn == 0)
    def _():
        for _ in ahead(0):
            pass
        chain(ahead(1))

    @pl.when((turn > 0) & (turn < devices))
    def _():
        chain(alternate(finish(), ahead(jnp.minimum(turn + 1, devices - 1))))

    @pl.when(turn == devices)
    def _():
        for _ in finish():
            pass


def backward_kernel(
    inner_part,
    feature_part,
    sequence_ref,
    packed_ref,
    rows_ref,
    head_grad_ref,
    next_act,
    next_grad,
    next_hidden,
    next_out_slope,
    next_norms,
    next_out_norms,
    next_first,
    next_second,
    now_act,
    now_slope,
    now_curve,
    now_second,
    last_grad,
    last_norms,
    last_first,
    gain_ref,
    bias_ref,
    back_ref,
    first_w,
    first_b,
    second_w,
    second_b,
    gain_sum,
    bias_sum,
    known_ref,
    vector_ref,
    grad_sum,
    to_wide,
    to_rows,
    to_spread,
    to_low,
    to_mix,
    to_state,
    to_sums,
    wide_ref,
    row_ref,
    spread_ref,
    low_ref,
    mix_ref,
    state_ref,
    sums_ref,
    end_known,
    end_rows,
    end_first,
):
    devices, chunk, _ = packed_ref.shape
    steps = chunk // MINI
    turn = pl.program_id(0)
    shard = back_ref.shape[1] - chunk
    gain = gain_ref[...]
    bias = bias_ref[...]
    square_gain = gain * gain
    rows, cols = token_grid(chunk)

    @pl.when(turn == 0)
    def _():
        for ref in (
            first_w,
            first_b,
            second_w,
            second_b,
            gain_sum,
            bias_sum,
            known_ref,
            grad_sum,
            end_known,
            end_rows,
            end_first,
        ):
            ref[...] = jnp.zeros_like(ref)

    def unpack(place):
        packed = packed_ref[place]
        query, key = two_parts(packed)
        miss = key.astype(f32) - packed[:, 2 * HEAD_DIM : 3 * HEAD_DIM].astype(f32) + bias
        return query, key, miss, rate_logit(packed)

    def rate_of(logit):
        return jax.nn.sigmoid(logit[:, :HEAD_DIM]) * rate_scale

    def prepare():
        query, key, miss, logit = unpack(jnp.maximum(devices - 1 - turn, 0))
        head_grad = jnp.transpose(head_grad_ref[0].astype(f32))
        head_normal = next_out_norms[:, HEAD_DIM : 2 * HEAD_DIM]
        head_mean = mean_of(head_grad)
        head_tilt = mean_of(head_grad * head_normal)
        yield
        rate = rate_of(logit)
        normal = next_norms[:, :HEAD_DIM]
        rate_gain = rate * square_gain
        gain_normal = rate_gain * normal
        scaled = rate * (miss * gain) + gain_normal
        scaled_mean = mean_of(scaled)
        along = mean_of(scaled * normal)
        yield
        out_grad = next_out_norms[:, 3 * HEAD_DIM :] * (
            head_grad - head_mean - head_normal * head_tilt
        )
        out_normal = next_out_norms[:, :HEAD_DIM]
        normal_grad = out_grad * gain
        out_mean = mean_of(normal_grad)
        out_tilt = mean_of(normal_grad * out_normal)
        yield
        inverse = next_norms[:, HEAD_DIM:]
        back_res = (inverse * (scaled - scaled_mean - normal * along)).astype(bf16)
        gain_along = mean_of(gain_normal)
        gain_square = mean_of(gain_normal * normal)
        to_low[0] = back_res
        to_low[1] = key
        to_sums[2:3, :HEAD_DIM] = jnp.sum(out_grad * out_normal, axis=0, keepdims=True)
        to_sums[3:4, :HEAD_DIM] = jnp.sum(out_grad, axis=0, keepdims=True)
        yield
        res_grad = next_out_norms[:, 2 * HEAD_DIM : 3 * HEAD_DIM] * (
            normal_grad - out_mean - out_normal * out_tilt
        )
        to_sums[1:2, :HEAD_DIM] = jnp.sum(res_grad, axis=0, keepdims=True)
        res_grad_low = res_grad.astype(bf16)
        hidden_base = dot_nn(res_grad_low, next_second[0, 0])
        mix = dot_nt(res_grad_low, back_res)
        yield
        mix_t = dot_nt(back_res, res_grad_low)
        causal = cols <= rows
        later = rows <= cols
        second_grad = jnp.where(causal, -mix, 0.0)
        hidden_more = dot_nn(second_grad, next_act[...])
        yield
        second_grad_t = jnp.where(later, -mix_t, 0.0)
        to_rows[1] = normal
        to_rows[2] = rate_gain
        to_rows[3] = rate_gain - along
        to_rows[4] = gain_normal + scaled
        to_rows[5] = -(along + rate * row_mean(square_gain))
        yield
        for index, value in enumerate(
            (-(gain_along + scaled_mean), -(3.0 * along + gain_square), inverse * inverse)
        ):
            to_spread[index] = jnp.concatenate([value, value], axis=1)
        mix = dot_nt(next_act[...], next_hidden[...])
        yield
        query_pre_grad = (hidden_base + hidden_more) * next_out_slope[...]
        query_pre_low = query_pre_grad.astype(bf16)
        to_sums[0:1] = jnp.sum(query_pre_grad, axis=0, keepdims=True)
        first = dot_nt(query_pre_low, next_grad[...])
        yield
        second_mix_t = jnp.where(later, mix + 1.0, 0.0)
        to_rows[0] = -dot_nn(second_mix_t, res_grad_low)
        first_t = dot_nt(next_grad[...], query_pre_low)
        yield
        first_grad = jnp.where(causal, -first, 0.0)
        mix = dot_nt(key, query)
        query_grad = dot_nt(query_pre_low, next_first[0])
        query_more = dot_nn(first_grad, key)
        yield
        first_grad_t = jnp.where(later, -first_t, 0.0)
        to_rows[6] = dot_nn(first_grad_t, query)
        first_mix_t = jnp.where(later, mix + 1.0, 0.0).astype(bf16)
        yield
        to_rows[7] = out_grad + query_grad + query_more
        to_wide[1] = dot_nn(second_grad_t, next_hidden[...])
        yield
        to_wide[0] = -dot_nn(first_mix_t, query_pre_low)
        mix = dot_nt(key, key)
        yield
        to_mix[...] = jnp.where(cols // MINI > rows // MINI, mix + 1.0, 0.0).astype(bf16)
        to_state[0] = dot_tn(query, query_pre_low)
        yield
        to_state[1] = dot_tn(res_grad_low, next_hidden[...])

    def conclude():
        place = jnp.minimum(devices + 1 - turn, devices - 1)
        _, key, miss, logit = unpack(place)
        normal = last_norms[:, :HEAD_DIM]
        upon = end_rows[0]
        upon_mean = mean_of(upon)
        upon_tilt = mean_of(upon * normal)
        yield
        pre_grad = end_known[...]
        mix = dot_nt(last_grad[...], pre_grad)
        mix_t = dot_nt(pre_grad, last_grad[...])
        yield
        rate = rate_of(logit)
        scaled_grad = last_norms[:, HEAD_DIM:] * (upon - upon_mean - normal * upon_tilt)
        error_grad = scaled_grad * (rate * gain)
        rate_grad = mean_of(scaled_grad * (miss * gain + square_gain * normal))
        yield
        error = miss + normal * gain
        gain_sum[...] += jnp.sum(
            scaled_grad * rate * error + error_grad * normal, axis=0, keepdims=True
        )
        bias_sum[...] += jnp.sum(error_grad, axis=0, keepdims=True)
        from_grad = dot_nt(last_grad[...], end_first[...])
        yield
        far = rows // MINI < cols // MINI
        near = rows // MINI > cols // MINI
        cross = jnp.where(far, mix, 0.0) + jnp.where(near, mix_t, 0.0)
        from_pre = dot_nt(pre_grad, last_first[0])
        from_cross = dot_nn(cross, key)
        yield
        key_grad = end_rows[1] + error_grad - from_grad + from_pre - from_cross
        back_rate = rate_grad * float(HEAD_DIM) * rate * (1.0 - rate * (1.0 / rate_scale))
        lane = lax.broadcasted_iota(jnp.int32, (chunk, HEAD_DIM), 1)
        tail = jnp.where(lane == 0, back_rate, 0.0)
        packed = jnp.concatenate([end_rows[2], key_grad, -error_grad, tail], axis=1).astype(bf16)
        back_ref[place, :chunk] = packed
        yield
        count = 6
        size = grad_sum.shape[0] // count
        for index in range(count):
            at = slice(index * size, (index + 1) * size)
            grad_sum[at] = grad_sum[at] + dot_tn(rows_ref[0, 0, :, at], packed)
            yield

    def chain(following, previous):
        wide_ref[...] = to_wide[...]
        row_ref[...] = to_rows[...]
        spread_ref[...] = to_spread[...]
        low_ref[...] = to_low[...]
        mix_ref[...] = to_mix[...]
        state_ref[...] = to_state[...]
        sums_ref[...] = to_sums[...]
        first_next = first_w[...]
        first_next_low = first_next.astype(bf16)
        first_next_b = first_b[...]
        state = second_w[...]
        state_b = second_b[...]

        def base_of(step):
            at = slice(step * MINI, (step + 1) * MINI)
            return wide_ref[0, at, :] - dot_nn(low_ref[1, at, :], first_next_low) - first_next_b

        base = base_of(steps - 1)
        for step in reversed(range(steps)):
            at = slice(step * MINI, (step + 1) * MINI)
            grad = base
            if step + 1 < steps:
                grad = grad - taken
            state_low = state.astype(bf16)
            own_act = now_act[at, :]
            own_back = low_ref[0, at, :]
            back_base = row_ref[0, at, :] - dot_nt(own_act, state_low) - state_b
            own_low = now_second[0, step]
            slope = now_slope[at, :]
            back_act_grad = (grad * slope).astype(bf16)
            upon = dot_nt(back_act_grad, own_low)
            upon = back_base + upon
            own_normal, own_gain, own_grad, own_beta, own_alpha = (
                row_ref[index, at, :] for index in range(1, 6)
            )
            cross, cross_beta, square_inverse = (spread_ref[index, at, :] for index in range(3))
            main = dot_nn(upon * own_grad, own_low)
            act_base = wide_ref[1, at, :] - dot_nn(own_back, state_low)
            sides = dot_nn(jnp.concatenate([own_normal, own_gain, own_beta], axis=0), own_low)
            interleave(following, 2)
            interleave(previous, 1)
            alpha = row_mean(upon)
            beta = row_mean(upon * own_normal)
            gamma = row_mean(upon * own_gain)
            kappa = row_mean(upon * own_beta)
            level = alpha * own_alpha + beta * cross[:, :HEAD_DIM] + gamma
            tilt = alpha * cross + beta * cross_beta + kappa
            key_res_grad = square_inverse[:, :HEAD_DIM] * (
                upon * own_grad
                - alpha * own_gain
                - beta * own_beta
                - level
                - own_normal * tilt[:, :HEAD_DIM]
            )
            key_res_low = key_res_grad.astype(bf16)
            from_sides = (
                alpha * sides[MINI : 2 * MINI]
                + beta * sides[2 * MINI :]
                + jnp.concatenate([tilt, tilt], axis=1) * sides[:MINI]
            )
            factor = jnp.concatenate([square_inverse, square_inverse], axis=1) * slope
            known = act_base * slope + grad * now_curve[at, :] - factor * from_sides
            pre_grad = known + factor * main
            known_ref[at, :] = pre_grad.astype(bf16)
            if step > 0:
                taken = dot_nn(mix_ref[(step - 1) * MINI : step * MINI, :], known_ref[...])
                base = base_of(step - 1)
            state = state + dot_tn(
                jnp.concatenate([key_res_low, own_back], axis=0),
                jnp.concatenate([own_act, back_act_grad], axis=0),
            )
            state_b = state_b + jnp.sum(key_res_grad, axis=0, keepdims=True)
            row_ref[0, at, :] = upon
        for generator in (following, previous):
            for _ in generator:
                pass
        pre_grad_all = known_ref[...]
        first_w[...] = first_next + dot_tn(low_ref[1], pre_grad_all) + state_ref[0]
        first_b[...] = (
            first_next_b
            + jnp.sum(pre_grad_all.astype(f32), axis=0, keepdims=True)
            + sums_ref[0:1]
        )
        second_w[...] = state + state_ref[1]
        second_b[...] = state_b + sums_ref[1:2, :HEAD_DIM]
        gain_sum[...] += sums_ref[2:3, :HEAD_DIM]
        bias_sum[...] += sums_ref[3:4, :HEAD_DIM]
        end_known[...] = pre_grad_all
        end_rows[0] = row_ref[0]
        end_rows[1] = row_ref[6]
        end_rows[2] = row_ref[7]
        end_first[...] = first_next_low

    @pl.when(turn == 0)
    def _():
        for _ in prepare():
            pass

    @pl.when((turn > 0) & (turn <= devices))
    def _():
        chain(prepare(), conclude())

    @pl.when(turn == devices + 1)
    def _():
        for _ in conclude():
            pass
        vector_ref[...] = jnp.zeros_like(vector_ref)
        for index in range(devices):
            first = slice(index * inner_part, (index + 1) * inner_part)
            small = slice(index * feature_part, (index + 1) * feature_part)
            vector_ref[index : index + 1, :inner_part] = first_b[:, first]
            for number, source in enumerate((second_b, gain_sum, bias_sum)):
                start = inner_part + number * feature_part
                vector_ref[index : index + 1, start : start + feature_part] = source[:, small]
        columns = jnp.transpose(vector_ref[...]).astype(bf16)
        lanes = slice(MATRIX_LANE, MATRIX_LANE + inner_part)
        for index in range(devices):
            first = slice(index * inner_part, (index + 1) * inner_part)
            back_ref[index, :HEAD_DIM, lanes] = first_w[:, first].astype(bf16)
            back_ref[index, HEAD_DIM : 2 * HEAD_DIM, lanes] = second_w[:, first].astype(bf16)
            back_ref[index, :chunk, VECTOR_LANE : VECTOR_LANE + 1] = columns[:, index : index + 1]
            back_ref[index, chunk:] = grad_sum[index * shard : (index + 1) * shard].astype(bf16)


def whole_block(shape):
    return pl.BlockSpec(shape, lambda index, *_: (0,) * len(shape))


STATE_SHAPES = ((HEAD_DIM, INNER), (1, INNER), (HEAD_DIM, INNER), (1, HEAD_DIM))


def chain_forward(packed, inner_part, feature_part):
    blocks, chunk, _ = packed.shape
    length = blocks * chunk
    steps = chunk // MINI
    row = (1, HEAD_DIM)

    def forth(shape):
        return pl.BlockSpec(
            shape, lambda turn: (jnp.minimum(turn, blocks - 1),) + (0,) * (len(shape) - 1)
        )

    def behind(shape):
        return pl.BlockSpec(
            shape, lambda turn: (jnp.maximum(turn - 1, 0),) + (0,) * (len(shape) - 1)
        )

    def of_length(width, dtype):
        return jax.ShapeDtypeStruct((length, width), dtype)

    wide = (chunk, INNER)
    return pl.pallas_call(
        functools.partial(forward_kernel, inner_part, feature_part),
        grid=(blocks + 1,),
        in_specs=[whole_block(packed.shape)],
        out_specs=[behind((1, HEAD_DIM, chunk))]
        + [forth(wide)] * 4
        + [
            forth((chunk, 2 * HEAD_DIM)),
            forth((1, HEAD_DIM, INNER)),
            forth((1, steps, HEAD_DIM, INNER)),
        ]
        + [behind(wide)] * 3
        + [whole_block(row)] * 2,
        out_shape=[jax.ShapeDtypeStruct((blocks, HEAD_DIM, chunk), bf16)]
        + [of_length(INNER, dtype) for dtype in (bf16, bf16, f32, f32)]
        + [
            of_length(2 * HEAD_DIM, f32),
            jax.ShapeDtypeStruct((blocks, HEAD_DIM, INNER), bf16),
            jax.ShapeDtypeStruct((blocks, steps, HEAD_DIM, INNER), bf16),
        ]
        + [of_length(INNER, dtype) for dtype in (bf16, f32, f32)]
        + [jax.ShapeDtypeStruct(row, f32)] * 2,
        scratch_shapes=[pltpu.VMEM(shape, f32) for shape in STATE_SHAPES]
        + [
            pltpu.VMEM(wide, bf16),
            pltpu.VMEM((chunk, HEAD_DIM), bf16),
            pltpu.VMEM(wide, f32),
        ]
        + [
            pltpu.VMEM((3, chunk, HEAD_DIM), f32),
            pltpu.VMEM((chunk, 2 * HEAD_DIM), f32),
            pltpu.VMEM((chunk, chunk), bf16),
        ]
        * 2
        + [
            pltpu.VMEM(wide, bf16),
            pltpu.VMEM(wide, bf16),
            pltpu.VMEM((chunk, HEAD_DIM), bf16),
            pltpu.VMEM((HEAD_DIM, INNER), bf16),
            pltpu.VMEM((HEAD_DIM, INNER), bf16),
            pltpu.VMEM((1, INNER), f32),
            pltpu.VMEM(row, f32),
        ],
        compiler_params=pltpu.CompilerParams(
            dimension_semantics=("arbitrary",), vmem_limit_bytes=VMEM_BYTES
        ),
        cost_estimate=pl.CostEstimate(
            flops=CHAIN_FLOPS, transcendentals=0, bytes_accessed=16 * length * INNER
        ),
        name="chain_forward",
    )(packed)


def chain_backward(packed, rows, sequence, head_grad, saved, inner_part, feature_part):
    act, grad_pre, slope, curve, norms, first_save, second_save = saved[:7]
    hidden, out_slope, out_norms, gain, bias = saved[7:]
    blocks, chunk, _ = packed.shape
    width = rows.shape[-1]
    shard = width // blocks
    steps = chunk // MINI
    row = (1, HEAD_DIM)
    wide = (chunk, INNER)
    narrow = (chunk, 2 * HEAD_DIM)

    def at(shape, delay):
        def index_map(turn, _):
            place = jnp.clip(blocks - 1 - turn + delay, 0, blocks - 1)
            return (place,) + (0,) * (len(shape) - 1)

        return pl.BlockSpec(shape, index_map)

    def rows_map(turn, chosen):
        place = jnp.clip(blocks + 1 - turn, 0, blocks - 1)
        return (place // SEQS, (place + chosen[0]) % SEQS, 0, 0)

    state = (HEAD_DIM, INNER)
    carried = [
        pltpu.VMEM((2,) + wide, f32),
        pltpu.VMEM((8, chunk, HEAD_DIM), f32),
        pltpu.VMEM((3,) + narrow, f32),
        pltpu.VMEM((2, chunk, HEAD_DIM), bf16),
        pltpu.VMEM((chunk, chunk), bf16),
        pltpu.VMEM((2,) + state, f32),
        pltpu.VMEM((8, INNER), f32),
    ]
    return pl.pallas_call(
        functools.partial(backward_kernel, inner_part, feature_part),
        grid_spec=pltpu.PrefetchScalarGridSpec(
            num_scalar_prefetch=1,
            grid=(blocks + 2,),
            in_specs=[
                whole_block(packed.shape),
                pl.BlockSpec((1, 1, chunk, width), rows_map),
                at((1, HEAD_DIM, chunk), 0),
                at(wide, 0),
                at(wide, 0),
                at(wide, 0),
                at(wide, 0),
                at(narrow, 0),
                at(wide, 0),
                at((1,) + state, 0),
                at((1, 1) + state, 0),
                at(wide, 1),
                at(wide, 1),
                at(wide, 1),
                at((1, steps) + state, 1),
                at(wide, 2),
                at(narrow, 2),
                at((1,) + state, 2),
                whole_block(row),
                whole_block(row),
            ],
            out_specs=whole_block((blocks, chunk + shard, LANES)),
            scratch_shapes=[pltpu.VMEM(shape, f32) for shape in STATE_SHAPES + (row, row)]
            + [
                pltpu.VMEM(wide, bf16),
                pltpu.VMEM((chunk, 128), f32),
                pltpu.VMEM((width, LANES), f32),
            ]
            + carried
            + carried
            + [
                pltpu.VMEM(wide, bf16),
                pltpu.VMEM((3, chunk, HEAD_DIM), f32),
                pltpu.VMEM(state, bf16),
            ],
        ),
        out_shape=jax.ShapeDtypeStruct((blocks, chunk + shard, LANES), bf16),
        compiler_params=pltpu.CompilerParams(
            dimension_semantics=("arbitrary",), vmem_limit_bytes=VMEM_BYTES
        ),
        cost_estimate=pl.CostEstimate(
            flops=CHAIN_FLOPS, transcendentals=0, bytes_accessed=16 * blocks * chunk * INNER
        ),
        name="chain_backward",
    )(
        sequence,
        packed,
        rows,
        head_grad,
        act,
        grad_pre,
        hidden,
        out_slope,
        norms,
        out_norms,
        first_save,
        second_save,
        act,
        slope,
        curve,
        second_save,
        grad_pre,
        norms,
        first_save,
        gain,
        bias,
    )


def layer_norm_parts(values):
    centred = values - row_mean(values)
    inverse = lax.rsqrt(row_mean(centred * centred) + epsilon)
    return centred * inverse, inverse


def layer_norm_back(normal, inverse, scaling, grad):
    scaled = grad * scaling
    return inverse * (scaled - row_mean(scaled) - normal * row_mean(scaled * normal))


def start_kernel(
    head_count,
    rows_ref,
    weights_ref,
    gain_ref,
    inner_ref,
    packed_ref,
    normed_ref,
    matrix_ref,
):
    tensor_count = rows_ref.shape[0]
    seq_count, chunk, _ = normed_ref.shape
    rows = chunk // tensor_count
    matrix_ref[...] = jnp.zeros_like(matrix_ref)
    for head in range(head_count):
        first = head * 3 * HEAD_DIM
        rate = head_count * 3 * HEAD_DIM + head
        column = weights_ref[:, rate : rate + 1]
        matrix_ref[head, :, : 3 * HEAD_DIM] = weights_ref[:, first : first + 3 * HEAD_DIM]
        matrix_ref[head, :, RATE_LANE : RATE_LANE + 1] = column
        matrix_ref[head, :, RATE_LANE + 1 : RATE_LANE + 2] = column
    lane = lax.broadcasted_iota(jnp.int32, (chunk, LANES), 1)
    for sequence in range(seq_count):
        part = slice(sequence * rows, (sequence + 1) * rows)
        values = jnp.concatenate([rows_ref[index, part] for index in range(tensor_count)], axis=0)
        normal, _ = layer_norm_parts(values.astype(f32))
        normed = (normal * gain_ref[...]).astype(bf16)
        normed_ref[sequence] = normed
        for head in range(head_count):
            projected = dot_nn(normed, matrix_ref[head])
            rest = projected - projected.astype(bf16).astype(f32)
            projected = jnp.where(lane == RATE_LANE + 1, rest, projected).astype(bf16)
            packed_ref[head * seq_count + sequence] = jnp.where(
                lane >= VECTOR_LANE, inner_ref[head], projected
            )
    for index in range(head_count * seq_count, packed_ref.shape[0]):
        packed_ref[index] = jnp.zeros((chunk, LANES), bf16)


def feed_forward_kernel(
    heads_ref,
    rows_ref,
    weights_ref,
    out_ref,
    gain_ref,
    terms_ref,
    mixed_ref,
    normed_ref,
    back_ref,
    swiglu_ref,
    cot_ref,
):
    tensor_count, head_count, seq_count, _, chunk = heads_ref.shape
    ff_local = swiglu_ref.shape[1]
    rows = chunk // tensor_count
    total = seq_count * chunk
    for sequence in range(seq_count):
        part = slice(sequence * rows, (sequence + 1) * rows)
        other = slice((seq_count + sequence) * rows, (seq_count + sequence + 1) * rows)
        values = jnp.concatenate([rows_ref[index, part] for index in range(tensor_count)], axis=0)
        mixed = values.astype(f32)
        for index in range(tensor_count):
            heads = [heads_ref[index, head, sequence] for head in range(head_count)]
            heads = jnp.transpose(jnp.concatenate(heads, axis=0).astype(f32))
            mixed = mixed + dot_nt(heads, out_ref[index])
        for index in range(tensor_count):
            mixed_ref[index, sequence] = mixed[index * rows : (index + 1) * rows]
        normal, _ = layer_norm_parts(mixed)
        at = slice(sequence * chunk, (sequence + 1) * chunk)
        normed_ref[at] = (normal * gain_ref[...]).astype(bf16)
        for index in range(tensor_count):
            first = sequence * chunk + index * rows
            cot_ref[first : first + rows] = rows_ref[index, other]
    normed = normed_ref[...]
    cot = cot_ref[...]
    for first in range(0, ff_local, 256):
        at = slice(first, first + 256)
        beyond = slice(ff_local + first, ff_local + first + 256)
        gate = dot_nn(normed, weights_ref[:, at])
        up = dot_nn(normed, weights_ref[:, beyond])
        back = dot_nn(cot, weights_ref[:, 2 * ff_local + first : 2 * ff_local + first + 256])
        share = jax.nn.sigmoid(gate)
        silu = gate * share
        swiglu_ref[:, at] = (silu * up).astype(bf16)
        back_ref[:, at] = (back * up * (share * (1.0 + gate * (1.0 - share)))).astype(bf16)
        back_ref[:, beyond] = (back * silu).astype(bf16)
    ffn_term = dot_nt(back_ref[...], weights_ref[:, : 2 * ff_local]).astype(bf16)
    down_term = dot_nt(swiglu_ref[...], weights_ref[:, 2 * ff_local : 3 * ff_local]).astype(bf16)
    for sequence in range(seq_count):
        for index in range(tensor_count):
            first = sequence * chunk + index * rows
            terms_ref[index, sequence] = ffn_term[first : first + rows]
            terms_ref[index, seq_count + sequence] = down_term[first : first + rows]


def feed_forward_grad_kernel(normed_ref, back_ref, swiglu_ref, cot_ref, grads_ref):
    normed = jnp.transpose(normed_ref[...].astype(f32)).astype(bf16)
    cot = jnp.transpose(cot_ref[...].astype(f32)).astype(bf16)
    width = back_ref.shape[1]
    for first in range(0, width, 256):
        at = slice(first, first + 256)
        grads_ref[:, at] = dot_nn(normed, back_ref[:, at]).astype(bf16)
    for first in range(0, swiglu_ref.shape[1], 256):
        at = slice(width + first, width + first + 256)
        grads_ref[:, at] = dot_nn(cot, swiglu_ref[:, first : first + 256]).astype(bf16)


def head_back_kernel(grads_ref, out_ref, heads_ref, back_ref, out_grad_ref):
    head_count, seq_count, _, chunk = heads_ref.shape
    devices, shard, _ = out_grad_ref.shape
    total = None
    for sequence in range(seq_count):
        grads = grads_ref[sequence]
        back = jnp.transpose(dot_nn(grads, out_ref[...])).astype(bf16)
        for head in range(head_count):
            back_ref[head * seq_count + sequence] = back[head * HEAD_DIM : (head + 1) * HEAD_DIM]
        heads = [heads_ref[head, sequence] for head in range(head_count)]
        term = dot_nt(jnp.transpose(grads.astype(f32)), jnp.concatenate(heads, axis=0))
        total = term if total is None else total + term
    for index in range(head_count * seq_count, devices):
        back_ref[index] = jnp.zeros((HEAD_DIM, chunk), bf16)
    for index in range(devices):
        out_grad_ref[index] = total[index * shard : (index + 1) * shard].astype(bf16)


def matrix_output_kernel(sums_ref, out_ref, weights_ref, gate_up_ref, down_ref, out_grad_ref, gain_ref):
    ff_local = down_ref.shape[1]
    sums = sums_ref[...].astype(f32)
    for index in range(2):
        gate_up_ref[:, index, :] = sums[:, index * ff_local : (index + 1) * ff_local]
    down_ref[...] = sums[:, 2 * ff_local :]
    total = out_ref[0].astype(f32)
    for index in range(1, out_ref.shape[0]):
        total = total + out_ref[index].astype(f32)
    out_grad_ref[...] = jnp.transpose(total)
    products = sums[:, : 2 * ff_local] * weights_ref[:, : 2 * ff_local].astype(f32)
    gain = jnp.sum(products, axis=-1, keepdims=True)
    gain_ref[...] = jnp.broadcast_to(gain, gain_ref.shape)


def feed_forward_back_kernel(
    rank_ref, terms_ref, mixed_ref, cot_ref, gain_ref, back_ref, low_ref, result_ref
):
    seq_count = mixed_ref.shape[1]
    for sequence in range(seq_count):
        grad = terms_ref[0, sequence].astype(f32)
        down = terms_ref[0, seq_count + sequence].astype(f32)
        for index in range(1, terms_ref.shape[0]):
            grad = grad + terms_ref[index, sequence].astype(f32)
            down = down + terms_ref[index, seq_count + sequence].astype(f32)
        mixed = mixed_ref[0, sequence]
        normal, inverse = layer_norm_parts(mixed)
        back = cot_ref[sequence].astype(f32)
        back = back + layer_norm_back(normal, inverse, gain_ref[...], grad)
        back_ref[sequence] = back
        low_ref[sequence] = back.astype(bf16)
        result_ref[sequence] = (mixed + down).astype(bf16)


def input_grad_kernel(terms_ref, tokens_ref, back_ref, gain_ref, grad_ref, gains_ref):
    seq_count, rows, _ = tokens_ref.shape
    for sequence in range(seq_count):
        at = slice(sequence * rows, (sequence + 1) * rows)
        total = terms_ref[0, at].astype(f32)
        for index in range(1, terms_ref.shape[0]):
            total = total + terms_ref[index, at].astype(f32)
        normal, inverse = layer_norm_parts(tokens_ref[sequence].astype(f32))
        total = layer_norm_back(normal, inverse, gain_ref[...], total)
        grad_ref[:, sequence, :] = back_ref[sequence] + total
    total = terms_ref[0, seq_count * rows :].astype(f32)
    for index in range(1, terms_ref.shape[0]):
        total = total + terms_ref[index, seq_count * rows :].astype(f32)
    width = gains_ref.shape[1]
    gains_ref[...] = (total[:2] + total[2:4])[:, :width]


def tail_kernel(
    received_ref,
    matrix_ref,
    own_ref,
    gain_two_ref,
    gains_ref,
    terms_ref,
    qkv_ref,
    small_ref,
    state_ref,
):
    head_count = matrix_ref.shape[0]
    shard = own_ref.shape[1]
    tensor_count, term_rows, width = terms_ref.shape
    chunk = received_ref.shape[1] - shard
    seq_count = (term_rows - 16) * tensor_count // chunk
    rows = chunk // tensor_count
    lane = lax.broadcasted_iota(jnp.int32, (chunk, LANES), 1)
    for sequence in range(seq_count):
        total = None
        for head in range(head_count):
            values = received_ref[head * seq_count + sequence, :chunk]
            values = jnp.where(lane <= RATE_LANE, values, jnp.zeros_like(values))
            term = dot_nt(values, matrix_ref[head])
            total = term if total is None else total + term
        for index in range(tensor_count):
            part = total[index * rows : (index + 1) * rows]
            terms_ref[index, sequence * rows : (sequence + 1) * rows] = part.astype(bf16)
    lane = lax.broadcasted_iota(jnp.int32, (shard, LANES), 1)
    column = lax.broadcasted_iota(jnp.int32, (shard, 128), 1)
    gain = None
    small = jnp.where(column == 1, gain_two_ref[...], 0.0)
    for head in range(head_count):
        grads = received_ref[head * seq_count, chunk:].astype(f32)
        state = received_ref[head * seq_count, :chunk, RATE_LANE:].astype(f32)
        for sequence in range(1, seq_count):
            grads = grads + received_ref[head * seq_count + sequence, chunk:].astype(f32)
            state = state + received_ref[
                head * seq_count + sequence, :chunk, RATE_LANE:
            ].astype(f32)
        state_ref[head] = state
        for index in range(3):
            at = slice(index * HEAD_DIM, (index + 1) * HEAD_DIM)
            qkv_ref[index, :, head * HEAD_DIM : (head + 1) * HEAD_DIM] = grads[:, at]
        products = jnp.where(lane <= RATE_LANE, grads * own_ref[head].astype(f32), 0.0)
        products = jnp.sum(products, axis=-1, keepdims=True)
        gain = products if gain is None else gain + products
        small = jnp.where(column == 2 + head, grads[:, RATE_LANE : RATE_LANE + 1], small)
    small = jnp.transpose(jnp.where(column == 0, gain, small))[: small_ref.shape[0]]
    small_ref[...] = small
    gain = small[:2] / gains_ref[...]
    high = gain.astype(bf16)
    low = (gain - high.astype(f32)).astype(bf16)
    block = jnp.concatenate([high.astype(f32), low.astype(f32), jnp.zeros((12, shard), f32)], axis=0)
    for index in range(tensor_count):
        first = seq_count * rows
        terms_ref[index, first:, :] = jnp.zeros((16, width), bf16)
        terms_ref[index, first:, :shard] = block.astype(bf16)


def whole_call(kernel, name, operands, results, vmem_bytes=GLUE_BYTES):
    def spec(shape):
        return pl.BlockSpec(shape, lambda: (0,) * len(shape))

    return pl.pallas_call(
        kernel,
        in_specs=[spec(operand.shape) for operand in operands],
        out_specs=[spec(result.shape) for result in results],
        out_shape=results,
        compiler_params=pltpu.CompilerParams(vmem_limit_bytes=vmem_bytes),
        name=name,
    )(*operands)


def dots(subscripts, left, right):
    return jnp.einsum(subscripts, left, right, preferred_element_type=f32)


def exchange(values, axis):
    return lax.all_to_all(values, axis, 0, 0, tiled=False)


def share_out(values, axis):
    count = lax.axis_size(axis)
    return exchange(jnp.broadcast_to(values[None], (count,) + values.shape), axis)


def ordered(*values):
    return lax.optimization_barrier(values)


def inner_block(matrix_one, matrix_two, vectors, rows):
    width = matrix_one.shape[-1]
    matrices = jnp.concatenate([matrix_one, matrix_two], axis=-2)
    column = jnp.concatenate(vectors, axis=-1)[..., None]
    lead = [(0, 0)] * (column.ndim - 2)
    column = jnp.pad(
        column,
        lead + [(0, rows - column.shape[-2]), (VECTOR_LANE, LANES - VECTOR_LANE - 1)],
    )
    matrices = jnp.pad(
        matrices,
        lead + [(0, rows - matrices.shape[-2]), (MATRIX_LANE, LANES - MATRIX_LANE - width)],
    )
    return column + matrices


def local(
    tokens,
    gain_attn,
    gain_ffn,
    w_qkv,
    w_rate,
    w_out,
    w_gate_up,
    w_down,
    w_one,
    b_one,
    w_two,
    b_two,
    norm_gain_inner,
    norm_bias_inner,
    cotangent,
):
    device_count = lax.axis_size(DP)
    tensor_count = lax.axis_size("tensor")
    local_rows, seq_count, width = tokens.shape
    row_count = local_rows * seq_count
    chunk = local_rows * tensor_count
    head_count = w_rate.shape[1]
    local_width = head_count * HEAD_DIM
    shard = w_qkv.shape[0]
    part = gain_attn.shape[0]
    ff_local = w_down.shape[0]
    chain_count = seq_count * head_count
    inner_part = w_one.shape[2]
    feature_part = b_two.shape[1]
    assert chain_count <= device_count and seq_count == SEQS
    assert chunk == 2 * HEAD_DIM and inner_part <= 32 and part <= shard
    rank = lax.axis_index("tensor")
    place = lax.axis_index(DP)

    own_tokens = tokens.transpose(1, 0, 2).reshape(row_count, width)
    own_cot = cotangent.transpose(1, 0, 2).reshape(row_count, width)
    row_full = share_out(jnp.concatenate([own_tokens, own_cot], axis=0), "tensor")
    head_columns = w_qkv.reshape(shard, 3, head_count, HEAD_DIM).transpose(0, 2, 1, 3)
    gain_columns = jnp.pad(jnp.stack([gain_attn, gain_ffn], axis=1), ((0, shard - part), (0, 0)))
    qkv_pack = jnp.concatenate(
        [head_columns.reshape(shard, 3 * local_width), w_rate, gain_columns], axis=1
    )
    qkv_half = lax.all_gather(qkv_pack, "inner", axis=0, tiled=True)
    qkv_full = lax.all_gather(qkv_half, "outer", axis=0, tiled=True)
    qkv_full, row_full = ordered(qkv_full, row_full)
    some_gains = qkv_full[:, 3 * local_width + head_count :]
    some_gains = some_gains.reshape(device_count, shard, 2)[:, :part].transpose(2, 0, 1)
    gains = lax.all_gather(some_gains.reshape(2, device_count * part), "tensor", axis=0)
    gains = gains.reshape(tensor_count, 2, device_count, part).transpose(1, 2, 0, 3)
    gains = gains.reshape(2, width).astype(f32)
    scale_attn, scale_ffn = gains[0:1], gains[1:2]

    ffn_pack = jnp.concatenate(
        [w_gate_up.reshape(shard, 2 * ff_local), w_down.T, w_out.T], axis=1
    )
    ffn_full = lax.all_gather(ffn_pack, DP, axis=0, tiled=True)
    own_out = ffn_full[:, 3 * ff_local :]

    inner = inner_block(
        w_one,
        w_two.transpose(0, 2, 1),
        [b_one, b_two, norm_gain_inner, norm_bias_inner],
        chunk,
    )
    shape = jax.ShapeDtypeStruct
    packed, normed_attn, head_matrix = whole_call(
        functools.partial(start_kernel, head_count),
        "projections",
        (row_full, qkv_full, scale_attn, inner),
        (
            shape((device_count, chunk, LANES), bf16),
            shape((seq_count, chunk, width), bf16),
            shape((head_count, width, LANES), bf16),
        ),
    )
    chain_in = exchange(packed, DP)

    side = lax.axis_index("inner")
    kept = lax.dynamic_index_in_dim(normed_attn, side, 0)
    given = lax.dynamic_index_in_dim(normed_attn, 1 - side, 0)
    taken = lax.ppermute(given, "inner", [(0, 1), (1, 0)])
    pair = jnp.concatenate([kept, taken], axis=0)
    chain_in, own_out, pair = ordered(chain_in, own_out, pair)
    chain_rows = lax.all_gather(pair, "outer", axis=0)
    out_full = lax.all_gather(own_out, "tensor", axis=0)

    forward_out = chain_forward(chain_in, inner_part, feature_part)
    saved = forward_out[1:]
    head_local = exchange(forward_out[0], DP)[:chain_count]
    head_local = head_local.reshape(head_count, seq_count, HEAD_DIM, chunk)
    head_rows = lax.all_gather(head_local, "tensor", axis=0, tiled=False)

    group_rows = seq_count * chunk
    terms, mixed, normed_ffn, back_gate_up, swiglu, group_cot = whole_call(
        feed_forward_kernel,
        "feed_forward",
        (head_rows, row_full, ffn_full, out_full, scale_ffn),
        (
            shape((tensor_count, 2 * seq_count, local_rows, width), bf16),
            shape((tensor_count, seq_count, local_rows, width), f32),
            shape((group_rows, width), bf16),
            shape((group_rows, 2 * ff_local), bf16),
            shape((group_rows, ff_local), bf16),
            shape((group_rows, width), bf16),
        ),
        VMEM_BYTES,
    )
    ffn_sums = exchange(terms, "tensor")
    (ffn_grads,) = whole_call(
        feed_forward_grad_kernel,
        "feed_forward_grads",
        (normed_ffn, back_gate_up, swiglu, group_cot),
        (shape((width, 3 * ff_local), bf16),),
        VMEM_BYTES,
    )
    ffn_grad_sums = lax.psum_scatter(ffn_grads, DP, scatter_dimension=0, tiled=True)
    ffn_sums, chain_rows, _ = ordered(ffn_sums, chain_rows, ffn_grads)
    own_shape = (seq_count, local_rows, width)
    own_cot = own_cot.reshape(own_shape)

    def fixed(operand):
        return pl.BlockSpec(operand.shape, lambda turn, _: (0,) * operand.ndim)

    chosen_mixed = pl.BlockSpec((1,) + own_shape, lambda turn, chosen: (chosen[0], 0, 0, 0))
    own_block = pl.BlockSpec(own_shape, lambda turn, _: (0, 0, 0))
    back_mixed, back_low, result = pl.pallas_call(
        feed_forward_back_kernel,
        grid_spec=pltpu.PrefetchScalarGridSpec(
            num_scalar_prefetch=1,
            grid=(1,),
            in_specs=[fixed(ffn_sums), chosen_mixed, own_block, fixed(scale_ffn)],
            out_specs=[own_block] * 3,
        ),
        out_shape=[shape(own_shape, dtype) for dtype in (f32, bf16, bf16)],
        compiler_params=pltpu.CompilerParams(vmem_limit_bytes=GLUE_BYTES),
        name="feed_forward_back",
    )(jnp.reshape(rank, (1,)).astype(jnp.int32), ffn_sums, mixed, own_cot, scale_ffn)
    result = result.transpose(1, 0, 2)
    attn_grads = lax.all_gather(back_low, "tensor", axis=1, tiled=True)
    back_head, out_terms = whole_call(
        head_back_kernel,
        "head_back",
        (attn_grads, own_out, head_local),
        (
            shape((device_count, HEAD_DIM, chunk), bf16),
            shape((device_count, shard, local_width), bf16),
        ),
    )
    head_grad = exchange(back_head, DP)
    out_sums = exchange(out_terms, DP)

    chosen = jnp.reshape(side, (1,)).astype(jnp.int32)
    back_packed = chain_backward(
        chain_in, chain_rows, chosen, head_grad, saved, inner_part, feature_part
    )
    received = exchange(back_packed, DP)
    grad_gate_up, grad_down, grad_out, gain_two = whole_call(
        matrix_output_kernel,
        "matrix_outputs",
        (ffn_grad_sums, out_sums, ffn_pack),
        (
            shape((shard, 2, ff_local), f32),
            shape((shard, ff_local), f32),
            shape((local_width, shard), f32),
            shape((shard, 128), f32),
        ),
    )
    own_matrix = lax.dynamic_slice_in_dim(head_matrix, place * shard, shard, 1)
    own_gains = lax.dynamic_slice_in_dim(gains, place * shard, shard, 1)
    terms, grad_qkv, small, state_block = whole_call(
        tail_kernel,
        "tail",
        (received, head_matrix, own_matrix, gain_two, own_gains),
        (
            shape((tensor_count, row_count + 16, width), bf16),
            shape((3, shard, local_width), f32),
            shape((8, shard), f32),
            shape((head_count, chunk, LANES - RATE_LANE), f32),
        ),
    )
    input_grad, gain_sums = whole_call(
        input_grad_kernel,
        "input_grad",
        (exchange(terms, "tensor"), own_tokens.reshape(own_shape), back_mixed, scale_attn),
        (shape(tokens.shape, f32), shape((2, shard), f32)),
    )
    gain_sums = lax.dynamic_slice_in_dim(gain_sums, rank * part, part, 1)

    matrices = state_block[..., MATRIX_LANE - RATE_LANE :][..., :inner_part]
    grad_one = matrices[:, :HEAD_DIM]
    grad_two = matrices[:, HEAD_DIM : 2 * HEAD_DIM].transpose(0, 2, 1)
    columns = state_block[:, :, VECTOR_LANE - RATE_LANE]
    ends = [inner_part + index * feature_part for index in range(4)]
    grad_b_one = columns[:, : ends[0]]
    grad_b_two, grad_gain_inner, grad_bias_inner = (
        columns[:, ends[index] : ends[index + 1]] for index in range(3)
    )

    return (
        result,
        input_grad,
        gain_sums[0],
        gain_sums[1],
        grad_qkv.transpose(1, 0, 2),
        small[2 : 2 + head_count].T,
        grad_out,
        grad_gate_up,
        grad_down.T,
        grad_one,
        grad_b_one,
        grad_two,
        grad_b_two,
        grad_gain_inner,
        grad_bias_inner,
    )


def solution(mesh):
    devices = mesh.devices
    dp_count, tensor_count = mesh.shape["dp"], mesh.shape["tensor"]
    devices = devices.reshape(dp_count // SEQS, SEQS, tensor_count)
    split = jax.sharding.Mesh(devices, DP + ("tensor",))
    rows = P(DP + ("tensor",), None, None)
    gains = P(DP + ("tensor",))
    placed = (
        rows,
        gains,
        gains,
        P(DP, None, "tensor"),
        P(DP, "tensor"),
        P("tensor", DP),
        P(DP, None, "tensor"),
        P("tensor", DP),
        P("tensor", None, DP),
        P("tensor", DP),
        P("tensor", DP, None),
        P("tensor", DP),
        P("tensor", DP),
        P("tensor", DP),
    )
    return jax.shard_map(
        local,
        mesh=split,
        in_specs=placed + (rows,),
        out_specs=(rows,) + placed,
        check_vma=False,
    )
```

```python
import functools


import jax
import jax.numpy as jnp
from jax import lax
from jax.experimental import pallas as pl
from jax.experimental.pallas import tpu as pltpu
from jax.sharding import PartitionSpec as P

HEAD_DIM = 64
INNER = 256
MINI = 16
SEQS = 2
LANES = 256
RATE_LANE = 3 * HEAD_DIM
VECTOR_LANE = RATE_LANE + 2
MATRIX_LANE = LANES - 32
VMEM_BYTES = 56 * 1024 * 1024
DP = ("outer", "inner")
CHAIN_FLOPS = 27_000_000_000
GLUE_BYTES = 32 * 1024 * 1024

epsilon = 1e-05
inner_epsilon = 1e-06
inner_rate = 0.5
rate_scale = inner_rate / (MINI * HEAD_DIM)
root_half = 0.7071067811865476
normal_peak = 0.3989422804014327

f32 = jnp.float32
bf16 = jnp.bfloat16


def dot_nn(a, b):
    return lax.dot_general(
        a.astype(bf16), b.astype(bf16), (((1,), (0,)), ((), ())), preferred_element_type=f32
    )


def dot_nt(a, b):
    return lax.dot_general(
        a.astype(bf16), b.astype(bf16), (((1,), (1,)), ((), ())), preferred_element_type=f32
    )


def dot_tn(a, b):
    return lax.dot_general(
        a.astype(bf16), b.astype(bf16), (((0,), (0,)), ((), ())), preferred_element_type=f32
    )


def row_mean(values):
    return jnp.mean(values, axis=-1, keepdims=True)


def density_and_share(values):
    density = jnp.exp(-0.5 * values * values) * normal_peak
    share = 0.5 * (1.0 + lax.erf(values * root_half))
    return density, share


def token_grid(count):
    rows = lax.broadcasted_iota(jnp.int32, (count, count), 0)
    cols = lax.broadcasted_iota(jnp.int32, (count, count), 1)
    return rows, cols


def wide_mean(values):
    high = values.astype(bf16)
    low = (values - high.astype(f32)).astype(bf16)
    ones = jnp.full((values.shape[1], 128), 1.0 / values.shape[1], bf16)
    return dot_nn(high, ones) + dot_nn(low, ones)


def mean_of(values):
    return wide_mean(values)[:, :HEAD_DIM]


def two_parts(packed):
    return packed[:, :HEAD_DIM], packed[:, HEAD_DIM : 2 * HEAD_DIM]


def rate_logit(packed):
    source = lax.broadcasted_iota(jnp.int32, (2 * HEAD_DIM, 128), 0)
    spread = jnp.where((source >= HEAD_DIM) & (source < HEAD_DIM + 2), 1.0, 0.0)
    return dot_nn(packed[:, 2 * HEAD_DIM :], spread)


def alternate(*generators):
    left = list(generators)
    while left:
        for generator in list(left):
            if next(generator, generator) is generator:
                left.remove(generator)
            else:
                yield


def interleave(generator, count):
    for _ in range(count):
        if next(generator, generator) is generator:
            return


def forward_kernel(
    inner_part,
    feature_part,
    packed_ref,
    normed_ref,
    act_ref,
    grad_pre_ref,
    slope_ref,
    curve_ref,
    norms_ref,
    first_save,
    second_save,
    hidden_ref,
    out_slope_ref,
    out_norms_ref,
    gain_ref,
    bias_ref,
    first_w,
    first_b,
    second_w,
    second_b,
    known_ref,
    back_res_ref,
    pre_ref,
    to_rows,
    to_level,
    to_mix,
    row_ref,
    level_ref,
    mix_ref,
    done_act,
    done_grad,
    done_back,
    done_first,
    done_second,
    done_first_b,
    done_second_b,
):
    devices, chunk, _ = packed_ref.shape
    steps = chunk // MINI
    turn = pl.program_id(0)

    @pl.when(turn == 0)
    def _():
        for index in range(devices):
            block = packed_ref[index, :, LANES - 128 :].astype(f32)
            first = slice(index * inner_part, (index + 1) * inner_part)
            lanes = slice(MATRIX_LANE - LANES + 128, MATRIX_LANE - LANES + 128 + inner_part)
            first_w[:, first] = block[:HEAD_DIM, lanes]
            second_w[:, first] = block[HEAD_DIM : 2 * HEAD_DIM, lanes]
            at = VECTOR_LANE - LANES + 128
            vector = jnp.transpose(block)[at : at + 1]
            first_b[:, first] = vector[:, :inner_part]
            small = slice(index * feature_part, (index + 1) * feature_part)
            for number, target in enumerate((second_b, gain_ref, bias_ref)):
                start = inner_part + number * feature_part
                target[:, small] = vector[:, start : start + feature_part]
        known_ref[...] = jnp.zeros_like(known_ref)
        centred = second_w[...]
        second_w[...] = centred - jnp.mean(centred, axis=0, keepdims=True)
        second_b[...] = second_b[...] - row_mean(second_b[...])

    gain = gain_ref[...]
    bias = bias_ref[...]
    rows, cols = token_grid(chunk)

    def finish():
        query, key = two_parts(packed_ref[jnp.maximum(turn - 1, 0)])
        causal = cols <= rows
        mix = dot_nt(query, key)
        query_base = dot_nn(query, done_first[...])
        yield
        first_mix = jnp.where(causal, mix + 1.0, 0.0)
        taken = dot_nn(first_mix, done_grad[...])
        yield
        query_pre = query_base + done_first_b[...] - taken
        density, share = density_and_share(query_pre)
        hidden = (query_pre * share).astype(bf16)
        hidden_ref[...] = hidden
        out_slope_ref[...] = share + query_pre * density
        yield
        mix = dot_nt(hidden, done_act[...])
        res_base = dot_nt(hidden, done_second[...])
        yield
        second_mix = jnp.where(causal, mix + 1.0, 0.0)
        taken = dot_nn(second_mix, done_back[...])
        yield
        query_res = res_base + done_second_b[...] - taken
        square = mean_of(query_res * query_res)
        yield
        out_inverse = lax.rsqrt(square + inner_epsilon)
        out_normal = query_res * out_inverse
        outputs = query.astype(f32) + out_normal * gain + bias
        middle = mean_of(outputs)
        out_norms_ref[:, :HEAD_DIM] = out_normal
        out_norms_ref[:, 2 * HEAD_DIM : 3 * HEAD_DIM] = out_inverse
        yield
        centred = outputs - middle
        square = mean_of(centred * centred)
        yield
        head_inverse = lax.rsqrt(square + epsilon)
        head_normal = centred * head_inverse
        out_norms_ref[:, HEAD_DIM : 2 * HEAD_DIM] = head_normal
        out_norms_ref[:, 3 * HEAD_DIM :] = head_inverse
        normed_ref[0] = jnp.transpose(head_normal).astype(bf16)

    def ahead(place):
        packed = packed_ref[place]
        _, key = two_parts(packed)
        value = packed[:, 2 * HEAD_DIM : 3 * HEAD_DIM]
        logit = rate_logit(packed)
        mix = dot_nt(key, key)
        yield
        rate = jax.nn.sigmoid(logit) * rate_scale
        square_gain = gain * gain
        level_gain = rate * row_mean(square_gain)
        rate_base = rate[:, :HEAD_DIM] * (
            (key.astype(f32) - value.astype(f32) + bias) * gain
        )
        middle = mean_of(rate_base)
        to_rows[0] = rate_base
        to_rows[1] = rate[:, :HEAD_DIM] * square_gain - level_gain[:, :HEAD_DIM]
        to_level[...] = level_gain * inner_epsilon
        to_mix[...] = jnp.where(cols // MINI < rows // MINI, mix + 1.0, 0.0).astype(bf16)
        yield
        to_rows[2] = middle

    def chain(others):
        _, key = two_parts(packed_ref[jnp.minimum(turn, devices - 1)])
        row_ref[...] = to_rows[...]
        level_ref[...] = to_level[...]
        mix_ref[...] = to_mix[...]
        first_low = first_w[...].astype(bf16)
        first_save[0] = first_low
        start_first_b = first_b[...]
        start_b = second_b[...]
        pre_ref[...] = dot_nn(key, first_low) + start_first_b
        state = second_w[...]
        start_low = state.astype(bf16)
        state_b = start_b
        for step in range(steps):
            at = slice(step * MINI, (step + 1) * MINI)
            own_base = row_ref[0, at, :]
            own_gain = row_ref[1, at, :]
            pre = pre_ref[at, :]
            if step >= 1:
                taken = dot_nn(mix_ref[at, :], known_ref[...])
                pre = pre - taken
            density, share = density_and_share(pre)
            act = (pre * share).astype(bf16)
            state_low = state.astype(bf16)
            res = dot_nt(act, state_low)
            slope = share + pre * density
            second_save[0, step] = state_low
            interleave(others, 1)
            res = res + state_b
            weighted = own_gain * res
            parts = dot_nn(jnp.concatenate([res, weighted], axis=0), state_low)
            base_act = dot_nn(own_base, state_low)
            interleave(others, 1)
            square = jnp.sum(res * res, axis=-1, keepdims=True)
            sum_gain = jnp.sum(weighted, axis=-1, keepdims=True)
            sum_base = jnp.sum(own_base * res, axis=-1, keepdims=True)
            sum_square = jnp.sum(weighted * res, axis=-1, keepdims=True)
            inverse = lax.rsqrt(square * (1.0 / HEAD_DIM) + inner_epsilon)
            scaled_mean = row_ref[2, at, :] + inverse * sum_gain * (1.0 / HEAD_DIM)
            along = inverse * (sum_base + inverse * sum_square) * (1.0 / HEAD_DIM)
            square_inverse = inverse * inverse
            along_half = along - square_inverse * level_ref[at, :]
            along_wide = jnp.concatenate([along_half, along_half], axis=1)
            normal = res * inverse
            back_res = inverse * (
                own_base + own_gain * normal - scaled_mean - normal * along_half[:, :HEAD_DIM]
            )
            back_low = back_res.astype(bf16)
            with_base = inverse * slope * base_act
            with_part = square_inverse * slope
            with_res = with_part * along_wide
            grad_full = with_base + (with_part * parts[MINI:] - with_res * parts[:MINI])
            grad = grad_full.astype(bf16)
            known_ref[at, :] = grad
            state = state - dot_tn(back_low, act)
            state_b = state_b - jnp.sum(back_res, axis=0, keepdims=True)
            slope_ref[at, :] = slope
            back_act = inverse * base_act + square_inverse * (
                parts[MINI:] - along_wide * parts[:MINI]
            )
            curve_ref[at, :] = back_act * density * (2.0 - pre * pre)
            act_ref[at, :] = act
            grad_pre_ref[at, :] = grad
            back_res_ref[at, :] = back_low
            norms_ref[at, :HEAD_DIM] = normal
            norms_ref[at, HEAD_DIM:] = jnp.broadcast_to(inverse, (MINI, HEAD_DIM))
        for _ in others:
            pass
        grad_all = known_ref[...]
        first_w[...] = first_w[...] - dot_tn(key, grad_all)
        first_b[...] = start_first_b - jnp.sum(grad_all.astype(f32), axis=0, keepdims=True)
        second_w[...] = state
        second_b[...] = state_b
        done_act[...] = act_ref[...]
        done_grad[...] = grad_all
        done_back[...] = back_res_ref[...]
        done_first[...] = first_low
        done_second[...] = start_low
        done_first_b[...] = start_first_b
        done_second_b[...] = start_b

    @pl.when(turn == 0)
    def _():
        for _ in ahead(0):
            pass
        chain(ahead(1))

    @pl.when((turn > 0) & (turn < devices))
    def _():
        chain(alternate(finish(), ahead(jnp.minimum(turn + 1, devices - 1))))

    @pl.when(turn == devices)
    def _():
        for _ in finish():
            pass


def backward_kernel(
    inner_part,
    feature_part,
    sequence_ref,
    packed_ref,
    rows_ref,
    head_grad_ref,
    next_act,
    next_grad,
    next_hidden,
    next_out_slope,
    next_norms,
    next_out_norms,
    next_first,
    next_second,
    now_act,
    now_slope,
    now_curve,
    now_second,
    last_grad,
    last_norms,
    last_first,
    gain_ref,
    bias_ref,
    back_ref,
    first_w,
    first_b,
    second_w,
    second_b,
    gain_sum,
    bias_sum,
    known_ref,
    vector_ref,
    grad_sum,
    to_wide,
    to_rows,
    to_spread,
    to_low,
    to_mix,
    to_state,
    to_sums,
    wide_ref,
    row_ref,
    spread_ref,
    low_ref,
    mix_ref,
    state_ref,
    sums_ref,
    end_known,
    end_rows,
    end_first,
):
    devices, chunk, _ = packed_ref.shape
    steps = chunk // MINI
    turn = pl.program_id(0)
    shard = back_ref.shape[1] - chunk
    gain = gain_ref[...]
    bias = bias_ref[...]
    square_gain = gain * gain
    rows, cols = token_grid(chunk)

    @pl.when(turn == 0)
    def _():
        for ref in (
            first_w,
            first_b,
            second_w,
            second_b,
            gain_sum,
            bias_sum,
            known_ref,
            grad_sum,
            end_known,
            end_rows,
            end_first,
        ):
            ref[...] = jnp.zeros_like(ref)

    def unpack(place):
        packed = packed_ref[place]
        query, key = two_parts(packed)
        miss = key.astype(f32) - packed[:, 2 * HEAD_DIM : 3 * HEAD_DIM].astype(f32) + bias
        return query, key, miss, rate_logit(packed)

    def rate_of(logit):
        return jax.nn.sigmoid(logit[:, :HEAD_DIM]) * rate_scale

    def prepare():
        query, key, miss, logit = unpack(jnp.maximum(devices - 1 - turn, 0))
        halves = []
        for index in range(head_grad_ref.shape[1]):
            values = head_grad_ref[0, index].astype(f32)
            halves += [values[:, :HEAD_DIM], values[:, HEAD_DIM:]]
        head_grad = jnp.concatenate(halves, axis=0)
        head_normal = next_out_norms[:, HEAD_DIM : 2 * HEAD_DIM]
        head_mean = mean_of(head_grad)
        head_tilt = mean_of(head_grad * head_normal)
        yield
        rate = rate_of(logit)
        normal = next_norms[:, :HEAD_DIM]
        rate_gain = rate * square_gain
        gain_normal = rate_gain * normal
        scaled = rate * (miss * gain) + gain_normal
        scaled_mean = mean_of(scaled)
        along = mean_of(scaled * normal)
        yield
        out_grad = next_out_norms[:, 3 * HEAD_DIM :] * (
            head_grad - head_mean - head_normal * head_tilt
        )
        out_normal = next_out_norms[:, :HEAD_DIM]
        normal_grad = out_grad * gain
        out_mean = mean_of(normal_grad)
        out_tilt = mean_of(normal_grad * out_normal)
        yield
        inverse = next_norms[:, HEAD_DIM:]
        back_res = (inverse * (scaled - scaled_mean - normal * along)).astype(bf16)
        gain_along = mean_of(gain_normal)
        gain_square = mean_of(gain_normal * normal)
        to_low[0] = back_res
        to_low[1] = key
        to_sums[2:3, :HEAD_DIM] = jnp.sum(out_grad * out_normal, axis=0, keepdims=True)
        to_sums[3:4, :HEAD_DIM] = jnp.sum(out_grad, axis=0, keepdims=True)
        yield
        res_grad = next_out_norms[:, 2 * HEAD_DIM : 3 * HEAD_DIM] * (
            normal_grad - out_mean - out_normal * out_tilt
        )
        to_sums[1:2, :HEAD_DIM] = jnp.sum(res_grad, axis=0, keepdims=True)
        res_grad_low = res_grad.astype(bf16)
        hidden_base = dot_nn(res_grad_low, next_second[0, 0])
        mix = dot_nt(res_grad_low, back_res)
        yield
        mix_t = dot_nt(back_res, res_grad_low)
        causal = cols <= rows
        later = rows <= cols
        second_grad = jnp.where(causal, -mix, 0.0)
        hidden_more = dot_nn(second_grad, next_act[...])
        yield
        second_grad_t = jnp.where(later, -mix_t, 0.0)
        to_rows[1] = normal
        to_rows[2] = rate_gain
        to_rows[3] = rate_gain - along
        to_rows[4] = gain_normal + scaled
        to_rows[5] = -(along + rate * row_mean(square_gain))
        yield
        for index, value in enumerate(
            (-(gain_along + scaled_mean), -(3.0 * along + gain_square), inverse * inverse)
        ):
            to_spread[index] = jnp.concatenate([value, value], axis=1)
        mix = dot_nt(next_act[...], next_hidden[...])
        yield
        query_pre_grad = (hidden_base + hidden_more) * next_out_slope[...]
        query_pre_low = query_pre_grad.astype(bf16)
        to_sums[0:1] = jnp.sum(query_pre_grad, axis=0, keepdims=True)
        first = dot_nt(query_pre_low, next_grad[...])
        yield
        second_mix_t = jnp.where(later, mix + 1.0, 0.0)
        to_rows[0] = -dot_nn(second_mix_t, res_grad_low)
        first_t = dot_nt(next_grad[...], query_pre_low)
        yield
        first_grad = jnp.where(causal, -first, 0.0)
        mix = dot_nt(key, query)
        query_grad = dot_nt(query_pre_low, next_first[0])
        query_more = dot_nn(first_grad, key)
        yield
        first_grad_t = jnp.where(later, -first_t, 0.0)
        to_rows[6] = dot_nn(first_grad_t, query)
        first_mix_t = jnp.where(later, mix + 1.0, 0.0).astype(bf16)
        yield
        to_rows[7] = out_grad + query_grad + query_more
        to_wide[1] = dot_nn(second_grad_t, next_hidden[...])
        yield
        to_wide[0] = -dot_nn(first_mix_t, query_pre_low)
        mix = dot_nt(key, key)
        yield
        to_mix[...] = jnp.where(cols // MINI > rows // MINI, mix + 1.0, 0.0).astype(bf16)
        to_state[0] = dot_tn(query, query_pre_low)
        yield
        to_state[1] = dot_tn(res_grad_low, next_hidden[...])

    def conclude():
        place = jnp.minimum(devices + 1 - turn, devices - 1)
        _, key, miss, logit = unpack(place)
        normal = last_norms[:, :HEAD_DIM]
        upon = end_rows[0]
        upon_mean = mean_of(upon)
        upon_tilt = mean_of(upon * normal)
        yield
        pre_grad = end_known[...]
        mix = dot_nt(last_grad[...], pre_grad)
        mix_t = dot_nt(pre_grad, last_grad[...])
        yield
        rate = rate_of(logit)
        scaled_grad = last_norms[:, HEAD_DIM:] * (upon - upon_mean - normal * upon_tilt)
        error_grad = scaled_grad * (rate * gain)
        rate_grad = mean_of(scaled_grad * (miss * gain + square_gain * normal))
        yield
        error = miss + normal * gain
        gain_sum[...] += jnp.sum(
            scaled_grad * rate * error + error_grad * normal, axis=0, keepdims=True
        )
        bias_sum[...] += jnp.sum(error_grad, axis=0, keepdims=True)
        from_grad = dot_nt(last_grad[...], end_first[...])
        yield
        far = rows // MINI < cols // MINI
        near = rows // MINI > cols // MINI
        cross = jnp.where(far, mix, 0.0) + jnp.where(near, mix_t, 0.0)
        from_pre = dot_nt(pre_grad, last_first[0])
        from_cross = dot_nn(cross, key)
        yield
        key_grad = end_rows[1] + error_grad - from_grad + from_pre - from_cross
        back_rate = rate_grad * float(HEAD_DIM) * rate * (1.0 - rate * (1.0 / rate_scale))
        lane = lax.broadcasted_iota(jnp.int32, (chunk, HEAD_DIM), 1)
        tail = jnp.where(lane == 0, back_rate, 0.0)
        packed = jnp.concatenate([end_rows[2], key_grad, -error_grad, tail], axis=1).astype(bf16)
        back_ref[place, :chunk] = packed
        yield
        count = 6
        size = grad_sum.shape[0] // count
        for index in range(count):
            at = slice(index * size, (index + 1) * size)
            grad_sum[at] = grad_sum[at] + dot_tn(rows_ref[0, 0, :, at], packed)
            yield

    def chain(following, previous):
        wide_ref[...] = to_wide[...]
        row_ref[...] = to_rows[...]
        spread_ref[...] = to_spread[...]
        low_ref[...] = to_low[...]
        mix_ref[...] = to_mix[...]
        state_ref[...] = to_state[...]
        sums_ref[...] = to_sums[...]
        first_next = first_w[...]
        first_next_low = first_next.astype(bf16)
        first_next_b = first_b[...]
        state = second_w[...]
        state_b = second_b[...]

        def base_of(step):
            at = slice(step * MINI, (step + 1) * MINI)
            return wide_ref[0, at, :] - dot_nn(low_ref[1, at, :], first_next_low) - first_next_b

        base = base_of(steps - 1)
        for step in reversed(range(steps)):
            at = slice(step * MINI, (step + 1) * MINI)
            grad = base
            if step + 1 < steps:
                grad = grad - taken
            state_low = state.astype(bf16)
            own_act = now_act[at, :]
            own_back = low_ref[0, at, :]
            back_base = row_ref[0, at, :] - dot_nt(own_act, state_low) - state_b
            own_low = now_second[0, step]
            slope = now_slope[at, :]
            back_act_grad = (grad * slope).astype(bf16)
            upon = dot_nt(back_act_grad, own_low)
            upon = back_base + upon
            own_normal, own_gain, own_grad, own_beta, own_alpha = (
                row_ref[index, at, :] for index in range(1, 6)
            )
            cross, cross_beta, square_inverse = (spread_ref[index, at, :] for index in range(3))
            main = dot_nn(upon * own_grad, own_low)
            act_base = wide_ref[1, at, :] - dot_nn(own_back, state_low)
            sides = dot_nn(jnp.concatenate([own_normal, own_gain, own_beta], axis=0), own_low)
            interleave(following, 2)
            interleave(previous, 1)
            alpha = row_mean(upon)
            beta = row_mean(upon * own_normal)
            gamma = row_mean(upon * own_gain)
            kappa = row_mean(upon * own_beta)
            level = alpha * own_alpha + beta * cross[:, :HEAD_DIM] + gamma
            tilt = alpha * cross + beta * cross_beta + kappa
            key_res_grad = square_inverse[:, :HEAD_DIM] * (
                upon * own_grad
                - alpha * own_gain
                - beta * own_beta
                - level
                - own_normal * tilt[:, :HEAD_DIM]
            )
            key_res_low = key_res_grad.astype(bf16)
            from_sides = (
                alpha * sides[MINI : 2 * MINI]
                + beta * sides[2 * MINI :]
                + jnp.concatenate([tilt, tilt], axis=1) * sides[:MINI]
            )
            factor = jnp.concatenate([square_inverse, square_inverse], axis=1) * slope
            known = act_base * slope + grad * now_curve[at, :] - factor * from_sides
            pre_grad = known + factor * main
            known_ref[at, :] = pre_grad.astype(bf16)
            if step > 0:
                taken = dot_nn(mix_ref[(step - 1) * MINI : step * MINI, :], known_ref[...])
                base = base_of(step - 1)
            state = state + dot_tn(
                jnp.concatenate([key_res_low, own_back], axis=0),
                jnp.concatenate([own_act, back_act_grad], axis=0),
            )
            state_b = state_b + jnp.sum(key_res_grad, axis=0, keepdims=True)
            row_ref[0, at, :] = upon
        for generator in (following, previous):
            for _ in generator:
                pass
        pre_grad_all = known_ref[...]
        first_w[...] = first_next + dot_tn(low_ref[1], pre_grad_all) + state_ref[0]
        first_b[...] = (
            first_next_b
            + jnp.sum(pre_grad_all.astype(f32), axis=0, keepdims=True)
            + sums_ref[0:1]
        )
        second_w[...] = state + state_ref[1]
        second_b[...] = state_b + sums_ref[1:2, :HEAD_DIM]
        gain_sum[...] += sums_ref[2:3, :HEAD_DIM]
        bias_sum[...] += sums_ref[3:4, :HEAD_DIM]
        end_known[...] = pre_grad_all
        end_rows[0] = row_ref[0]
        end_rows[1] = row_ref[6]
        end_rows[2] = row_ref[7]
        end_first[...] = first_next_low

    @pl.when(turn == 0)
    def _():
        for _ in prepare():
            pass

    @pl.when((turn > 0) & (turn <= devices))
    def _():
        chain(prepare(), conclude())

    @pl.when(turn == devices + 1)
    def _():
        for _ in conclude():
            pass
        vector_ref[...] = jnp.zeros_like(vector_ref)
        for index in range(devices):
            first = slice(index * inner_part, (index + 1) * inner_part)
            small = slice(index * feature_part, (index + 1) * feature_part)
            vector_ref[index : index + 1, :inner_part] = first_b[:, first]
            for number, source in enumerate((second_b, gain_sum, bias_sum)):
                start = inner_part + number * feature_part
                vector_ref[index : index + 1, start : start + feature_part] = source[:, small]
        columns = jnp.transpose(vector_ref[...]).astype(bf16)
        lanes = slice(MATRIX_LANE, MATRIX_LANE + inner_part)
        for index in range(devices):
            first = slice(index * inner_part, (index + 1) * inner_part)
            back_ref[index, :HEAD_DIM, lanes] = first_w[:, first].astype(bf16)
            back_ref[index, HEAD_DIM : 2 * HEAD_DIM, lanes] = second_w[:, first].astype(bf16)
            back_ref[index, :chunk, VECTOR_LANE : VECTOR_LANE + 1] = columns[:, index : index + 1]
            back_ref[index, chunk:] = grad_sum[index * shard : (index + 1) * shard].astype(bf16)


def whole_block(shape):
    return pl.BlockSpec(shape, lambda index, *_: (0,) * len(shape))


STATE_SHAPES = ((HEAD_DIM, INNER), (1, INNER), (HEAD_DIM, INNER), (1, HEAD_DIM))


def chain_forward(packed, inner_part, feature_part):
    blocks, chunk, _ = packed.shape
    length = blocks * chunk
    steps = chunk // MINI
    row = (1, HEAD_DIM)

    def forth(shape):
        return pl.BlockSpec(
            shape, lambda turn: (jnp.minimum(turn, blocks - 1),) + (0,) * (len(shape) - 1)
        )

    def behind(shape):
        return pl.BlockSpec(
            shape, lambda turn: (jnp.maximum(turn - 1, 0),) + (0,) * (len(shape) - 1)
        )

    def of_length(width, dtype):
        return jax.ShapeDtypeStruct((length, width), dtype)

    wide = (chunk, INNER)
    return pl.pallas_call(
        functools.partial(forward_kernel, inner_part, feature_part),
        grid=(blocks + 1,),
        in_specs=[whole_block(packed.shape)],
        out_specs=[behind((1, HEAD_DIM, chunk))]
        + [forth(wide)] * 4
        + [
            forth((chunk, 2 * HEAD_DIM)),
            forth((1, HEAD_DIM, INNER)),
            forth((1, steps, HEAD_DIM, INNER)),
        ]
        + [behind(wide)] * 3
        + [whole_block(row)] * 2,
        out_shape=[jax.ShapeDtypeStruct((blocks, HEAD_DIM, chunk), bf16)]
        + [of_length(INNER, dtype) for dtype in (bf16, bf16, f32, f32)]
        + [
            of_length(2 * HEAD_DIM, f32),
            jax.ShapeDtypeStruct((blocks, HEAD_DIM, INNER), bf16),
            jax.ShapeDtypeStruct((blocks, steps, HEAD_DIM, INNER), bf16),
        ]
        + [of_length(INNER, dtype) for dtype in (bf16, f32, f32)]
        + [jax.ShapeDtypeStruct(row, f32)] * 2,
        scratch_shapes=[pltpu.VMEM(shape, f32) for shape in STATE_SHAPES]
        + [
            pltpu.VMEM(wide, bf16),
            pltpu.VMEM((chunk, HEAD_DIM), bf16),
            pltpu.VMEM(wide, f32),
        ]
        + [
            pltpu.VMEM((3, chunk, HEAD_DIM), f32),
            pltpu.VMEM((chunk, 2 * HEAD_DIM), f32),
            pltpu.VMEM((chunk, chunk), bf16),
        ]
        * 2
        + [
            pltpu.VMEM(wide, bf16),
            pltpu.VMEM(wide, bf16),
            pltpu.VMEM((chunk, HEAD_DIM), bf16),
            pltpu.VMEM((HEAD_DIM, INNER), bf16),
            pltpu.VMEM((HEAD_DIM, INNER), bf16),
            pltpu.VMEM((1, INNER), f32),
            pltpu.VMEM(row, f32),
        ],
        compiler_params=pltpu.CompilerParams(
            dimension_semantics=("arbitrary",), vmem_limit_bytes=VMEM_BYTES
        ),
        cost_estimate=pl.CostEstimate(
            flops=CHAIN_FLOPS, transcendentals=0, bytes_accessed=16 * length * INNER
        ),
        name="chain_forward",
    )(packed)


def chain_backward(packed, rows, sequence, head_grad, saved, inner_part, feature_part):
    act, grad_pre, slope, curve, norms, first_save, second_save = saved[:7]
    hidden, out_slope, out_norms, gain, bias = saved[7:]
    blocks, chunk, _ = packed.shape
    width = rows.shape[-1]
    shard = width // blocks
    steps = chunk // MINI
    row = (1, HEAD_DIM)
    wide = (chunk, INNER)
    narrow = (chunk, 2 * HEAD_DIM)

    def at(shape, delay):
        def index_map(turn, _):
            place = jnp.clip(blocks - 1 - turn + delay, 0, blocks - 1)
            return (place,) + (0,) * (len(shape) - 1)

        return pl.BlockSpec(shape, index_map)

    def rows_map(turn, chosen):
        place = jnp.clip(blocks + 1 - turn, 0, blocks - 1)
        return (place // SEQS, (place + chosen[0]) % SEQS, 0, 0)

    state = (HEAD_DIM, INNER)
    carried = [
        pltpu.VMEM((2,) + wide, f32),
        pltpu.VMEM((8, chunk, HEAD_DIM), f32),
        pltpu.VMEM((3,) + narrow, f32),
        pltpu.VMEM((2, chunk, HEAD_DIM), bf16),
        pltpu.VMEM((chunk, chunk), bf16),
        pltpu.VMEM((2,) + state, f32),
        pltpu.VMEM((8, INNER), f32),
    ]
    return pl.pallas_call(
        functools.partial(backward_kernel, inner_part, feature_part),
        grid_spec=pltpu.PrefetchScalarGridSpec(
            num_scalar_prefetch=1,
            grid=(blocks + 2,),
            in_specs=[
                whole_block(packed.shape),
                pl.BlockSpec((1, 1, chunk, width), rows_map),
                at((1,) + head_grad.shape[1:], 0),
                at(wide, 0),
                at(wide, 0),
                at(wide, 0),
                at(wide, 0),
                at(narrow, 0),
                at(wide, 0),
                at((1,) + state, 0),
                at((1, 1) + state, 0),
                at(wide, 1),
                at(wide, 1),
                at(wide, 1),
                at((1, steps) + state, 1),
                at(wide, 2),
                at(narrow, 2),
                at((1,) + state, 2),
                whole_block(row),
                whole_block(row),
            ],
            out_specs=whole_block((blocks, chunk + shard, LANES)),
            scratch_shapes=[pltpu.VMEM(shape, f32) for shape in STATE_SHAPES + (row, row)]
            + [
                pltpu.VMEM(wide, bf16),
                pltpu.VMEM((chunk, 128), f32),
                pltpu.VMEM((width, LANES), f32),
            ]
            + carried
            + carried
            + [
                pltpu.VMEM(wide, bf16),
                pltpu.VMEM((3, chunk, HEAD_DIM), f32),
                pltpu.VMEM(state, bf16),
            ],
        ),
        out_shape=jax.ShapeDtypeStruct((blocks, chunk + shard, LANES), bf16),
        compiler_params=pltpu.CompilerParams(
            dimension_semantics=("arbitrary",), vmem_limit_bytes=VMEM_BYTES
        ),
        cost_estimate=pl.CostEstimate(
            flops=CHAIN_FLOPS, transcendentals=0, bytes_accessed=16 * blocks * chunk * INNER
        ),
        name="chain_backward",
    )(
        sequence,
        packed,
        rows,
        head_grad,
        act,
        grad_pre,
        hidden,
        out_slope,
        norms,
        out_norms,
        first_save,
        second_save,
        act,
        slope,
        curve,
        second_save,
        grad_pre,
        norms,
        first_save,
        gain,
        bias,
    )


def layer_norm_parts(values):
    centred = values - row_mean(values)
    inverse = lax.rsqrt(row_mean(centred * centred) + epsilon)
    return centred * inverse, inverse


def layer_norm_back(normal, inverse, scaling, grad):
    scaled = grad * scaling
    return inverse * (scaled - row_mean(scaled) - normal * row_mean(scaled * normal))


def start_kernel(
    head_count,
    rows_ref,
    weights_ref,
    gain_ref,
    inner_ref,
    packed_ref,
    normed_ref,
    matrix_ref,
):
    tensor_count = rows_ref.shape[0]
    seq_count, chunk, _ = normed_ref.shape
    rows = chunk // tensor_count
    matrix_ref[...] = jnp.zeros_like(matrix_ref)
    for head in range(head_count):
        first = head * 3 * HEAD_DIM
        rate = head_count * 3 * HEAD_DIM + head
        column = weights_ref[:, rate : rate + 1]
        matrix_ref[head, :, : 3 * HEAD_DIM] = weights_ref[:, first : first + 3 * HEAD_DIM]
        matrix_ref[head, :, RATE_LANE : RATE_LANE + 1] = column
        matrix_ref[head, :, RATE_LANE + 1 : RATE_LANE + 2] = column
    lane = lax.broadcasted_iota(jnp.int32, (chunk, LANES), 1)
    for sequence in range(seq_count):
        part = slice(sequence * rows, (sequence + 1) * rows)
        values = jnp.concatenate([rows_ref[index, part] for index in range(tensor_count)], axis=0)
        normal, _ = layer_norm_parts(values.astype(f32))
        normed = (normal * gain_ref[...]).astype(bf16)
        normed_ref[sequence] = normed
        for head in range(head_count):
            projected = dot_nn(normed, matrix_ref[head])
            rest = projected - projected.astype(bf16).astype(f32)
            projected = jnp.where(lane == RATE_LANE + 1, rest, projected).astype(bf16)
            packed_ref[head * seq_count + sequence] = jnp.where(
                lane >= VECTOR_LANE, inner_ref[head], projected
            )
    for index in range(head_count * seq_count, packed_ref.shape[0]):
        packed_ref[index] = jnp.zeros((chunk, LANES), bf16)


def feed_forward_kernel(
    heads_ref,
    rows_ref,
    weights_ref,
    out_ref,
    gain_ref,
    terms_ref,
    mixed_ref,
    normed_ref,
    back_ref,
    swiglu_ref,
    cot_ref,
):
    tensor_count, head_count, seq_count, _, chunk = heads_ref.shape
    ff_local = swiglu_ref.shape[1]
    rows = chunk // tensor_count
    total = seq_count * chunk
    for sequence in range(seq_count):
        part = slice(sequence * rows, (sequence + 1) * rows)
        other = slice((seq_count + sequence) * rows, (seq_count + sequence + 1) * rows)
        values = jnp.concatenate([rows_ref[index, part] for index in range(tensor_count)], axis=0)
        mixed = values.astype(f32)
        for index in range(tensor_count):
            heads = [heads_ref[index, head, sequence] for head in range(head_count)]
            heads = jnp.transpose(jnp.concatenate(heads, axis=0).astype(f32))
            mixed = mixed + dot_nt(heads, out_ref[index])
        for index in range(tensor_count):
            mixed_ref[index, sequence] = mixed[index * rows : (index + 1) * rows]
        normal, _ = layer_norm_parts(mixed)
        at = slice(sequence * chunk, (sequence + 1) * chunk)
        normed_ref[at] = (normal * gain_ref[...]).astype(bf16)
        for index in range(tensor_count):
            first = sequence * chunk + index * rows
            cot_ref[first : first + rows] = rows_ref[index, other]
    normed = normed_ref[...]
    cot = cot_ref[...]
    for first in range(0, ff_local, 256):
        at = slice(first, first + 256)
        beyond = slice(ff_local + first, ff_local + first + 256)
        gate = dot_nn(normed, weights_ref[:, at])
        up = dot_nn(normed, weights_ref[:, beyond])
        back = dot_nn(cot, weights_ref[:, 2 * ff_local + first : 2 * ff_local + first + 256])
        share = jax.nn.sigmoid(gate)
        silu = gate * share
        swiglu_ref[:, at] = (silu * up).astype(bf16)
        back_ref[:, at] = (back * up * (share * (1.0 + gate * (1.0 - share)))).astype(bf16)
        back_ref[:, beyond] = (back * silu).astype(bf16)
    ffn_term = dot_nt(back_ref[...], weights_ref[:, : 2 * ff_local]).astype(bf16)
    down_term = dot_nt(swiglu_ref[...], weights_ref[:, 2 * ff_local : 3 * ff_local]).astype(bf16)
    for sequence in range(seq_count):
        for index in range(tensor_count):
            first = sequence * chunk + index * rows
            terms_ref[index, sequence] = ffn_term[first : first + rows]
            terms_ref[index, seq_count + sequence] = down_term[first : first + rows]


def feed_forward_grad_kernel(normed_ref, back_ref, swiglu_ref, cot_ref, grads_ref):
    normed = jnp.transpose(normed_ref[...].astype(f32)).astype(bf16)
    cot = jnp.transpose(cot_ref[...].astype(f32)).astype(bf16)
    width = back_ref.shape[1]
    for first in range(0, width, 256):
        at = slice(first, first + 256)
        grads_ref[:, at] = dot_nn(normed, back_ref[:, at]).astype(bf16)
    for first in range(0, swiglu_ref.shape[1], 256):
        at = slice(width + first, width + first + 256)
        grads_ref[:, at] = dot_nn(cot, swiglu_ref[:, first : first + 256]).astype(bf16)


def head_back_kernel(grads_ref, out_ref, back_ref):
    tensor_count = out_ref.shape[0]
    seq_count, rows, _ = grads_ref.shape
    head_count = out_ref.shape[2] // HEAD_DIM
    for index in range(tensor_count):
        for sequence in range(seq_count):
            back = dot_nn(grads_ref[sequence], out_ref[index]).astype(bf16)
            for head in range(head_count):
                place = (head * seq_count + sequence) * tensor_count + index
                values = back[:, head * HEAD_DIM : (head + 1) * HEAD_DIM]
                back_ref[place, :, :HEAD_DIM] = values[: rows // 2]
                back_ref[place, :, HEAD_DIM:] = values[rows // 2 :]
    for place in range(head_count * seq_count * tensor_count, back_ref.shape[0]):
        back_ref[place] = jnp.zeros((rows // 2, 2 * HEAD_DIM), bf16)


def out_grad_kernel(grads_ref, heads_ref, out_grad_ref):
    head_count, seq_count, _, _ = heads_ref.shape
    devices, shard, _ = out_grad_ref.shape
    total = None
    for sequence in range(seq_count):
        heads = [heads_ref[head, sequence] for head in range(head_count)]
        grads = jnp.transpose(grads_ref[sequence].astype(f32))
        term = dot_nt(grads, jnp.concatenate(heads, axis=0))
        total = term if total is None else total + term
    for index in range(devices):
        out_grad_ref[index] = total[index * shard : (index + 1) * shard].astype(bf16)


def matrix_output_kernel(sums_ref, out_ref, weights_ref, gate_up_ref, down_ref, out_grad_ref, gain_ref):
    ff_local = down_ref.shape[1]
    sums = sums_ref[...].astype(f32)
    for index in range(2):
        gate_up_ref[:, index, :] = sums[:, index * ff_local : (index + 1) * ff_local]
    down_ref[...] = sums[:, 2 * ff_local :]
    total = out_ref[0].astype(f32)
    for index in range(1, out_ref.shape[0]):
        total = total + out_ref[index].astype(f32)
    out_grad_ref[...] = jnp.transpose(total)
    products = sums[:, : 2 * ff_local] * weights_ref[:, : 2 * ff_local].astype(f32)
    gain = jnp.sum(products, axis=-1, keepdims=True)
    gain_ref[...] = jnp.broadcast_to(gain, gain_ref.shape)


def feed_forward_back_kernel(
    rank_ref, terms_ref, mixed_ref, cot_ref, gain_ref, back_ref, low_ref, result_ref
):
    seq_count = mixed_ref.shape[1]
    for sequence in range(seq_count):
        grad = terms_ref[0, sequence].astype(f32)
        down = terms_ref[0, seq_count + sequence].astype(f32)
        for index in range(1, terms_ref.shape[0]):
            grad = grad + terms_ref[index, sequence].astype(f32)
            down = down + terms_ref[index, seq_count + sequence].astype(f32)
        mixed = mixed_ref[0, sequence]
        normal, inverse = layer_norm_parts(mixed)
        back = cot_ref[sequence].astype(f32)
        back = back + layer_norm_back(normal, inverse, gain_ref[...], grad)
        back_ref[sequence] = back
        low_ref[sequence] = back.astype(bf16)
        result_ref[sequence] = (mixed + down).astype(bf16)


def input_grad_kernel(terms_ref, tokens_ref, back_ref, gain_ref, grad_ref, gains_ref):
    seq_count, rows, _ = tokens_ref.shape
    for sequence in range(seq_count):
        at = slice(sequence * rows, (sequence + 1) * rows)
        total = terms_ref[0, at].astype(f32)
        for index in range(1, terms_ref.shape[0]):
            total = total + terms_ref[index, at].astype(f32)
        normal, inverse = layer_norm_parts(tokens_ref[sequence].astype(f32))
        total = layer_norm_back(normal, inverse, gain_ref[...], total)
        grad_ref[:, sequence, :] = back_ref[sequence] + total
    total = terms_ref[0, seq_count * rows :].astype(f32)
    for index in range(1, terms_ref.shape[0]):
        total = total + terms_ref[index, seq_count * rows :].astype(f32)
    width = gains_ref.shape[1]
    gains_ref[...] = (total[:2] + total[2:4])[:, :width]


def tail_kernel(
    received_ref,
    matrix_ref,
    own_ref,
    gain_two_ref,
    gains_ref,
    terms_ref,
    qkv_ref,
    small_ref,
    state_ref,
):
    head_count = matrix_ref.shape[0]
    shard = own_ref.shape[1]
    tensor_count, term_rows, width = terms_ref.shape
    chunk = received_ref.shape[1] - shard
    seq_count = (term_rows - 16) * tensor_count // chunk
    rows = chunk // tensor_count
    lane = lax.broadcasted_iota(jnp.int32, (chunk, LANES), 1)
    for sequence in range(seq_count):
        total = None
        for head in range(head_count):
            values = received_ref[head * seq_count + sequence, :chunk]
            values = jnp.where(lane <= RATE_LANE, values, jnp.zeros_like(values))
            term = dot_nt(values, matrix_ref[head])
            total = term if total is None else total + term
        for index in range(tensor_count):
            part = total[index * rows : (index + 1) * rows]
            terms_ref[index, sequence * rows : (sequence + 1) * rows] = part.astype(bf16)
    lane = lax.broadcasted_iota(jnp.int32, (shard, LANES), 1)
    column = lax.broadcasted_iota(jnp.int32, (shard, 128), 1)
    gain = None
    small = jnp.where(column == 1, gain_two_ref[...], 0.0)
    for head in range(head_count):
        grads = received_ref[head * seq_count, chunk:].astype(f32)
        state = received_ref[head * seq_count, :chunk, RATE_LANE:].astype(f32)
        for sequence in range(1, seq_count):
            grads = grads + received_ref[head * seq_count + sequence, chunk:].astype(f32)
            state = state + received_ref[
                head * seq_count + sequence, :chunk, RATE_LANE:
            ].astype(f32)
        state_ref[head] = state
        for index in range(3):
            at = slice(index * HEAD_DIM, (index + 1) * HEAD_DIM)
            qkv_ref[index, :, head * HEAD_DIM : (head + 1) * HEAD_DIM] = grads[:, at]
        products = jnp.where(lane <= RATE_LANE, grads * own_ref[head].astype(f32), 0.0)
        products = jnp.sum(products, axis=-1, keepdims=True)
        gain = products if gain is None else gain + products
        small = jnp.where(column == 2 + head, grads[:, RATE_LANE : RATE_LANE + 1], small)
    small = jnp.transpose(jnp.where(column == 0, gain, small))[: small_ref.shape[0]]
    small_ref[...] = small
    gain = small[:2] / gains_ref[...]
    high = gain.astype(bf16)
    low = (gain - high.astype(f32)).astype(bf16)
    block = jnp.concatenate([high.astype(f32), low.astype(f32), jnp.zeros((12, shard), f32)], axis=0)
    for index in range(tensor_count):
        first = seq_count * rows
        terms_ref[index, first:, :] = jnp.zeros((16, width), bf16)
        terms_ref[index, first:, :shard] = block.astype(bf16)


def whole_call(kernel, name, operands, results, vmem_bytes=GLUE_BYTES):
    def spec(shape):
        return pl.BlockSpec(shape, lambda: (0,) * len(shape))

    return pl.pallas_call(
        kernel,
        in_specs=[spec(operand.shape) for operand in operands],
        out_specs=[spec(result.shape) for result in results],
        out_shape=results,
        compiler_params=pltpu.CompilerParams(vmem_limit_bytes=vmem_bytes),
        name=name,
    )(*operands)


def dots(subscripts, left, right):
    return jnp.einsum(subscripts, left, right, preferred_element_type=f32)


def exchange(values, axis):
    return lax.all_to_all(values, axis, 0, 0, tiled=False)


def share_out(values, axis):
    count = lax.axis_size(axis)
    return exchange(jnp.broadcast_to(values[None], (count,) + values.shape), axis)


def ordered(*values):
    return lax.optimization_barrier(values)


def inner_block(matrix_one, matrix_two, vectors, rows):
    width = matrix_one.shape[-1]
    matrices = jnp.concatenate([matrix_one, matrix_two], axis=-2)
    column = jnp.concatenate(vectors, axis=-1)[..., None]
    lead = [(0, 0)] * (column.ndim - 2)
    column = jnp.pad(
        column,
        lead + [(0, rows - column.shape[-2]), (VECTOR_LANE, LANES - VECTOR_LANE - 1)],
    )
    matrices = jnp.pad(
        matrices,
        lead + [(0, rows - matrices.shape[-2]), (MATRIX_LANE, LANES - MATRIX_LANE - width)],
    )
    return column + matrices


def local(
    tokens,
    gain_attn,
    gain_ffn,
    w_qkv,
    w_rate,
    w_out,
    w_gate_up,
    w_down,
    w_one,
    b_one,
    w_two,
    b_two,
    norm_gain_inner,
    norm_bias_inner,
    cotangent,
):
    device_count = lax.axis_size(DP)
    tensor_count = lax.axis_size("tensor")
    local_rows, seq_count, width = tokens.shape
    row_count = local_rows * seq_count
    chunk = local_rows * tensor_count
    head_count = w_rate.shape[1]
    local_width = head_count * HEAD_DIM
    shard = w_qkv.shape[0]
    part = gain_attn.shape[0]
    ff_local = w_down.shape[0]
    chain_count = seq_count * head_count
    inner_part = w_one.shape[2]
    feature_part = b_two.shape[1]
    assert chain_count <= device_count and seq_count == SEQS
    assert chunk == 2 * HEAD_DIM and inner_part <= 32 and part <= shard
    rank = lax.axis_index("tensor")
    place = lax.axis_index(DP)

    own_tokens = tokens.transpose(1, 0, 2).reshape(row_count, width)
    own_cot = cotangent.transpose(1, 0, 2).reshape(row_count, width)
    row_full = share_out(jnp.concatenate([own_tokens, own_cot], axis=0), "tensor")
    head_columns = w_qkv.reshape(shard, 3, head_count, HEAD_DIM).transpose(0, 2, 1, 3)
    gain_columns = jnp.pad(jnp.stack([gain_attn, gain_ffn], axis=1), ((0, shard - part), (0, 0)))
    qkv_pack = jnp.concatenate(
        [head_columns.reshape(shard, 3 * local_width), w_rate, gain_columns], axis=1
    )
    qkv_half = lax.all_gather(qkv_pack, "inner", axis=0, tiled=True)
    qkv_full = lax.all_gather(qkv_half, "outer", axis=0, tiled=True)
    qkv_full, row_full = ordered(qkv_full, row_full)
    some_gains = qkv_full[:, 3 * local_width + head_count :]
    some_gains = some_gains.reshape(device_count, shard, 2)[:, :part].transpose(2, 0, 1)
    gains = lax.all_gather(some_gains.reshape(2, device_count * part), "tensor", axis=0)
    gains = gains.reshape(tensor_count, 2, device_count, part).transpose(1, 2, 0, 3)
    gains = gains.reshape(2, width).astype(f32)
    scale_attn, scale_ffn = gains[0:1], gains[1:2]

    ffn_pack = jnp.concatenate(
        [w_gate_up.reshape(shard, 2 * ff_local), w_down.T, w_out.T], axis=1
    )
    ffn_full = lax.all_gather(ffn_pack, DP, axis=0, tiled=True)
    own_out = ffn_full[:, 3 * ff_local :]

    inner = inner_block(
        w_one,
        w_two.transpose(0, 2, 1),
        [b_one, b_two, norm_gain_inner, norm_bias_inner],
        chunk,
    )
    shape = jax.ShapeDtypeStruct
    packed, normed_attn, head_matrix = whole_call(
        functools.partial(start_kernel, head_count),
        "projections",
        (row_full, qkv_full, scale_attn, inner),
        (
            shape((device_count, chunk, LANES), bf16),
            shape((seq_count, chunk, width), bf16),
            shape((head_count, width, LANES), bf16),
        ),
    )
    chain_in = exchange(packed, DP)

    side = lax.axis_index("inner")
    kept = lax.dynamic_index_in_dim(normed_attn, side, 0)
    given = lax.dynamic_index_in_dim(normed_attn, 1 - side, 0)
    taken = lax.ppermute(given, "inner", [(0, 1), (1, 0)])
    pair = jnp.concatenate([kept, taken], axis=0)
    chain_in, own_out, pair = ordered(chain_in, own_out, pair)
    chain_rows = lax.all_gather(pair, "outer", axis=0)
    out_full = lax.all_gather(own_out, "tensor", axis=0)

    forward_out = chain_forward(chain_in, inner_part, feature_part)
    saved = forward_out[1:]
    head_local = exchange(forward_out[0], DP)[:chain_count]
    head_local = head_local.reshape(head_count, seq_count, HEAD_DIM, chunk)
    head_rows = lax.all_gather(head_local, "tensor", axis=0, tiled=False)

    group_rows = seq_count * chunk
    terms, mixed, normed_ffn, back_gate_up, swiglu, group_cot = whole_call(
        feed_forward_kernel,
        "feed_forward",
        (head_rows, row_full, ffn_full, out_full, scale_ffn),
        (
            shape((tensor_count, 2 * seq_count, local_rows, width), bf16),
            shape((tensor_count, seq_count, local_rows, width), f32),
            shape((group_rows, width), bf16),
            shape((group_rows, 2 * ff_local), bf16),
            shape((group_rows, ff_local), bf16),
            shape((group_rows, width), bf16),
        ),
        VMEM_BYTES,
    )
    ffn_sums = exchange(terms, "tensor")
    (ffn_grads,) = whole_call(
        feed_forward_grad_kernel,
        "feed_forward_grads",
        (normed_ffn, back_gate_up, swiglu, group_cot),
        (shape((width, 3 * ff_local), bf16),),
        VMEM_BYTES,
    )
    ffn_grad_sums = lax.psum_scatter(ffn_grads, DP, scatter_dimension=0, tiled=True)
    ffn_sums, chain_rows, _ = ordered(ffn_sums, chain_rows, ffn_grads)
    own_shape = (seq_count, local_rows, width)
    own_cot = own_cot.reshape(own_shape)

    def fixed(operand):
        return pl.BlockSpec(operand.shape, lambda turn, _: (0,) * operand.ndim)

    chosen_mixed = pl.BlockSpec((1,) + own_shape, lambda turn, chosen: (chosen[0], 0, 0, 0))
    own_block = pl.BlockSpec(own_shape, lambda turn, _: (0, 0, 0))
    back_mixed, back_low, result = pl.pallas_call(
        feed_forward_back_kernel,
        grid_spec=pltpu.PrefetchScalarGridSpec(
            num_scalar_prefetch=1,
            grid=(1,),
            in_specs=[fixed(ffn_sums), chosen_mixed, own_block, fixed(scale_ffn)],
            out_specs=[own_block] * 3,
        ),
        out_shape=[shape(own_shape, dtype) for dtype in (f32, bf16, bf16)],
        compiler_params=pltpu.CompilerParams(vmem_limit_bytes=VMEM_BYTES),
        name="feed_forward_back",
    )(jnp.reshape(rank, (1,)).astype(jnp.int32), ffn_sums, mixed, own_cot, scale_ffn)
    result = result.transpose(1, 0, 2)
    (back_head,) = whole_call(
        head_back_kernel,
        "head_back",
        (back_low, out_full),
        (shape((device_count * tensor_count, local_rows // 2, 2 * HEAD_DIM), bf16),),
        VMEM_BYTES,
    )
    back_head, back_low = ordered(back_head, back_low)
    head_grad = exchange(back_head, DP + ("tensor",))
    head_grad = head_grad.reshape(device_count, tensor_count, local_rows // 2, 2 * HEAD_DIM)
    attn_grads = lax.all_gather(back_low, "tensor", axis=1, tiled=True)
    (out_terms,) = whole_call(
        out_grad_kernel,
        "out_grads",
        (attn_grads, head_local),
        (shape((device_count, shard, local_width), bf16),),
    )
    head_grad, out_terms = ordered(head_grad, out_terms)
    out_sums = exchange(out_terms, DP)

    chosen = jnp.reshape(side, (1,)).astype(jnp.int32)
    back_packed = chain_backward(
        chain_in, chain_rows, chosen, head_grad, saved, inner_part, feature_part
    )
    received = exchange(back_packed, DP)
    grad_gate_up, grad_down, grad_out, gain_two = whole_call(
        matrix_output_kernel,
        "matrix_outputs",
        (ffn_grad_sums, out_sums, ffn_pack),
        (
            shape((shard, 2, ff_local), f32),
            shape((shard, ff_local), f32),
            shape((local_width, shard), f32),
            shape((shard, 128), f32),
        ),
    )
    own_matrix = lax.dynamic_slice_in_dim(head_matrix, place * shard, shard, 1)
    own_gains = lax.dynamic_slice_in_dim(gains, place * shard, shard, 1)
    terms, grad_qkv, small, state_block = whole_call(
        tail_kernel,
        "tail",
        (received, head_matrix, own_matrix, gain_two, own_gains),
        (
            shape((tensor_count, row_count + 16, width), bf16),
            shape((3, shard, local_width), f32),
            shape((8, shard), f32),
            shape((head_count, chunk, LANES - RATE_LANE), f32),
        ),
    )
    input_grad, gain_sums = whole_call(
        input_grad_kernel,
        "input_grad",
        (exchange(terms, "tensor"), own_tokens.reshape(own_shape), back_mixed, scale_attn),
        (shape(tokens.shape, f32), shape((2, shard), f32)),
    )
    gain_sums = lax.dynamic_slice_in_dim(gain_sums, rank * part, part, 1)

    matrices = state_block[..., MATRIX_LANE - RATE_LANE :][..., :inner_part]
    grad_one = matrices[:, :HEAD_DIM]
    grad_two = matrices[:, HEAD_DIM : 2 * HEAD_DIM].transpose(0, 2, 1)
    columns = state_block[:, :, VECTOR_LANE - RATE_LANE]
    ends = [inner_part + index * feature_part for index in range(4)]
    grad_b_one = columns[:, : ends[0]]
    grad_b_two, grad_gain_inner, grad_bias_inner = (
        columns[:, ends[index] : ends[index + 1]] for index in range(3)
    )

    return (
        result,
        input_grad,
        gain_sums[0],
        gain_sums[1],
        grad_qkv.transpose(1, 0, 2),
        small[2 : 2 + head_count].T,
        grad_out,
        grad_gate_up,
        grad_down.T,
        grad_one,
        grad_b_one,
        grad_two,
        grad_b_two,
        grad_gain_inner,
        grad_bias_inner,
    )


def solution(mesh):
    devices = mesh.devices
    dp_count, tensor_count = mesh.shape["dp"], mesh.shape["tensor"]
    devices = devices.reshape(dp_count // SEQS, SEQS, tensor_count)
    split = jax.sharding.Mesh(devices, DP + ("tensor",))
    rows = P(DP + ("tensor",), None, None)
    gains = P(DP + ("tensor",))
    placed = (
        rows,
        gains,
        gains,
        P(DP, None, "tensor"),
        P(DP, "tensor"),
        P("tensor", DP),
        P(DP, None, "tensor"),
        P("tensor", DP),
        P("tensor", None, DP),
        P("tensor", DP),
        P("tensor", DP, None),
        P("tensor", DP),
        P("tensor", DP),
        P("tensor", DP),
    )
    return jax.shard_map(
        local,
        mesh=split,
        in_specs=placed + (rows,),
        out_specs=(rows,) + placed,
        check_vma=False,
    )
```

```python
import functools


import jax
import jax.numpy as jnp
from jax import lax
from jax.experimental import pallas as pl
from jax.experimental.pallas import tpu as pltpu
from jax.sharding import PartitionSpec as P

HEAD_DIM = 64
INNER = 256
MINI = 16
SEQS = 2
LANES = 256
RATE_LANE = 3 * HEAD_DIM
VECTOR_LANE = RATE_LANE + 2
MATRIX_LANE = LANES - 32
VMEM_BYTES = 56 * 1024 * 1024
DP = ("outer", "inner")
CHAIN_FLOPS = 27_000_000_000
GLUE_BYTES = 32 * 1024 * 1024

epsilon = 1e-05
inner_epsilon = 1e-06
inner_rate = 0.5
rate_scale = inner_rate / (MINI * HEAD_DIM)
root_half = 0.7071067811865476
normal_peak = 0.3989422804014327

f32 = jnp.float32
bf16 = jnp.bfloat16


def dot_nn(a, b):
    return lax.dot_general(
        a.astype(bf16), b.astype(bf16), (((1,), (0,)), ((), ())), preferred_element_type=f32
    )


def dot_nt(a, b):
    return lax.dot_general(
        a.astype(bf16), b.astype(bf16), (((1,), (1,)), ((), ())), preferred_element_type=f32
    )


def dot_tn(a, b):
    return lax.dot_general(
        a.astype(bf16), b.astype(bf16), (((0,), (0,)), ((), ())), preferred_element_type=f32
    )


def row_mean(values):
    return jnp.mean(values, axis=-1, keepdims=True)


def density_and_share(values):
    density = jnp.exp(-0.5 * values * values) * normal_peak
    share = 0.5 * (1.0 + lax.erf(values * root_half))
    return density, share


def token_grid(count):
    rows = lax.broadcasted_iota(jnp.int32, (count, count), 0)
    cols = lax.broadcasted_iota(jnp.int32, (count, count), 1)
    return rows, cols


def wide_mean(values):
    high = values.astype(bf16)
    low = (values - high.astype(f32)).astype(bf16)
    ones = jnp.full((values.shape[1], 128), 1.0 / values.shape[1], bf16)
    return dot_nn(high, ones) + dot_nn(low, ones)


def mean_of(values):
    return wide_mean(values)[:, :HEAD_DIM]


def two_parts(packed):
    return packed[:, :HEAD_DIM], packed[:, HEAD_DIM : 2 * HEAD_DIM]


def rate_logit(packed):
    source = lax.broadcasted_iota(jnp.int32, (2 * HEAD_DIM, 128), 0)
    spread = jnp.where((source >= HEAD_DIM) & (source < HEAD_DIM + 2), 1.0, 0.0)
    return dot_nn(packed[:, 2 * HEAD_DIM :], spread)


def alternate(*generators):
    left = list(generators)
    while left:
        for generator in list(left):
            if next(generator, generator) is generator:
                left.remove(generator)
            else:
                yield


def interleave(generator, count):
    for _ in range(count):
        if next(generator, generator) is generator:
            return


def forward_kernel(
    inner_part,
    feature_part,
    packed_ref,
    normed_ref,
    act_ref,
    grad_pre_ref,
    slope_ref,
    curve_ref,
    norms_ref,
    first_save,
    second_save,
    hidden_ref,
    out_slope_ref,
    out_norms_ref,
    gain_ref,
    bias_ref,
    first_w,
    first_b,
    second_w,
    second_b,
    known_ref,
    back_res_ref,
    pre_ref,
    to_rows,
    to_level,
    to_mix,
    row_ref,
    level_ref,
    mix_ref,
    done_act,
    done_grad,
    done_back,
    done_first,
    done_second,
    done_first_b,
    done_second_b,
):
    devices, chunk, _ = packed_ref.shape
    steps = chunk // MINI
    turn = pl.program_id(0)

    @pl.when(turn == 0)
    def _():
        for index in range(devices):
            block = packed_ref[index, :, LANES - 128 :].astype(f32)
            first = slice(index * inner_part, (index + 1) * inner_part)
            lanes = slice(MATRIX_LANE - LANES + 128, MATRIX_LANE - LANES + 128 + inner_part)
            first_w[:, first] = block[:HEAD_DIM, lanes]
            second_w[:, first] = block[HEAD_DIM : 2 * HEAD_DIM, lanes]
            at = VECTOR_LANE - LANES + 128
            vector = jnp.transpose(block)[at : at + 1]
            first_b[:, first] = vector[:, :inner_part]
            small = slice(index * feature_part, (index + 1) * feature_part)
            for number, target in enumerate((second_b, gain_ref, bias_ref)):
                start = inner_part + number * feature_part
                target[:, small] = vector[:, start : start + feature_part]
        known_ref[...] = jnp.zeros_like(known_ref)
        centred = second_w[...]
        second_w[...] = centred - jnp.mean(centred, axis=0, keepdims=True)
        second_b[...] = second_b[...] - row_mean(second_b[...])

    gain = gain_ref[...]
    bias = bias_ref[...]
    rows, cols = token_grid(chunk)

    def finish():
        query, key = two_parts(packed_ref[jnp.maximum(turn - 1, 0)])
        causal = cols <= rows
        mix = dot_nt(query, key)
        query_base = dot_nn(query, done_first[...])
        yield
        first_mix = jnp.where(causal, mix + 1.0, 0.0)
        taken = dot_nn(first_mix, done_grad[...])
        yield
        query_pre = query_base + done_first_b[...] - taken
        density, share = density_and_share(query_pre)
        hidden = (query_pre * share).astype(bf16)
        hidden_ref[...] = hidden
        out_slope_ref[...] = share + query_pre * density
        yield
        mix = dot_nt(hidden, done_act[...])
        res_base = dot_nt(hidden, done_second[...])
        yield
        second_mix = jnp.where(causal, mix + 1.0, 0.0)
        taken = dot_nn(second_mix, done_back[...])
        yield
        query_res = res_base + done_second_b[...] - taken
        square = mean_of(query_res * query_res)
        yield
        out_inverse = lax.rsqrt(square + inner_epsilon)
        out_normal = query_res * out_inverse
        outputs = query.astype(f32) + out_normal * gain + bias
        middle = mean_of(outputs)
        out_norms_ref[:, :HEAD_DIM] = out_normal
        out_norms_ref[:, 2 * HEAD_DIM : 3 * HEAD_DIM] = out_inverse
        yield
        centred = outputs - middle
        square = mean_of(centred * centred)
        yield
        head_inverse = lax.rsqrt(square + epsilon)
        head_normal = centred * head_inverse
        out_norms_ref[:, HEAD_DIM : 2 * HEAD_DIM] = head_normal
        out_norms_ref[:, 3 * HEAD_DIM :] = head_inverse
        normed_ref[0] = jnp.transpose(head_normal).astype(bf16)

    def ahead(place):
        packed = packed_ref[place]
        _, key = two_parts(packed)
        value = packed[:, 2 * HEAD_DIM : 3 * HEAD_DIM]
        logit = rate_logit(packed)
        mix = dot_nt(key, key)
        yield
        rate = jax.nn.sigmoid(logit) * rate_scale
        square_gain = gain * gain
        level_gain = rate * row_mean(square_gain)
        rate_base = rate[:, :HEAD_DIM] * (
            (key.astype(f32) - value.astype(f32) + bias) * gain
        )
        middle = mean_of(rate_base)
        to_rows[0] = rate_base
        to_rows[1] = rate[:, :HEAD_DIM] * square_gain - level_gain[:, :HEAD_DIM]
        to_level[...] = level_gain * inner_epsilon
        to_mix[...] = jnp.where(cols // MINI < rows // MINI, mix + 1.0, 0.0).astype(bf16)
        yield
        to_rows[2] = middle

    def chain(others):
        _, key = two_parts(packed_ref[jnp.minimum(turn, devices - 1)])
        row_ref[...] = to_rows[...]
        level_ref[...] = to_level[...]
        mix_ref[...] = to_mix[...]
        first_low = first_w[...].astype(bf16)
        first_save[0] = first_low
        start_first_b = first_b[...]
        start_b = second_b[...]
        pre_ref[...] = dot_nn(key, first_low) + start_first_b
        state = second_w[...]
        start_low = state.astype(bf16)
        state_b = start_b
        for step in range(steps):
            at = slice(step * MINI, (step + 1) * MINI)
            own_base = row_ref[0, at, :]
            own_gain = row_ref[1, at, :]
            pre = pre_ref[at, :]
            if step >= 1:
                taken = dot_nn(mix_ref[at, :], known_ref[...])
                pre = pre - taken
            density, share = density_and_share(pre)
            act = (pre * share).astype(bf16)
            state_low = state.astype(bf16)
            res = dot_nt(act, state_low)
            slope = share + pre * density
            second_save[0, step] = state_low
            interleave(others, 1)
            res = res + state_b
            weighted = own_gain * res
            parts = dot_nn(jnp.concatenate([res, weighted], axis=0), state_low)
            base_act = dot_nn(own_base, state_low)
            interleave(others, 1)
            square = jnp.sum(res * res, axis=-1, keepdims=True)
            sum_gain = jnp.sum(weighted, axis=-1, keepdims=True)
            sum_base = jnp.sum(own_base * res, axis=-1, keepdims=True)
            sum_square = jnp.sum(weighted * res, axis=-1, keepdims=True)
            inverse = lax.rsqrt(square * (1.0 / HEAD_DIM) + inner_epsilon)
            scaled_mean = row_ref[2, at, :] + inverse * sum_gain * (1.0 / HEAD_DIM)
            along = inverse * (sum_base + inverse * sum_square) * (1.0 / HEAD_DIM)
            square_inverse = inverse * inverse
            along_half = along - square_inverse * level_ref[at, :]
            along_wide = jnp.concatenate([along_half, along_half], axis=1)
            normal = res * inverse
            back_res = inverse * (
                own_base + own_gain * normal - scaled_mean - normal * along_half[:, :HEAD_DIM]
            )
            back_low = back_res.astype(bf16)
            with_base = inverse * slope * base_act
            with_part = square_inverse * slope
            with_res = with_part * along_wide
            grad_full = with_base + (with_part * parts[MINI:] - with_res * parts[:MINI])
            grad = grad_full.astype(bf16)
            known_ref[at, :] = grad
            state = state - dot_tn(back_low, act)
            state_b = state_b - jnp.sum(back_res, axis=0, keepdims=True)
            slope_ref[at, :] = slope
            back_act = inverse * base_act + square_inverse * (
                parts[MINI:] - along_wide * parts[:MINI]
            )
            curve_ref[at, :] = back_act * density * (2.0 - pre * pre)
            act_ref[at, :] = act
            grad_pre_ref[at, :] = grad
            back_res_ref[at, :] = back_low
            norms_ref[at, :HEAD_DIM] = normal
            norms_ref[at, HEAD_DIM:] = jnp.broadcast_to(inverse, (MINI, HEAD_DIM))
        for _ in others:
            pass
        grad_all = known_ref[...]
        first_w[...] = first_w[...] - dot_tn(key, grad_all)
        first_b[...] = start_first_b - jnp.sum(grad_all.astype(f32), axis=0, keepdims=True)
        second_w[...] = state
        second_b[...] = state_b
        done_act[...] = act_ref[...]
        done_grad[...] = grad_all
        done_back[...] = back_res_ref[...]
        done_first[...] = first_low
        done_second[...] = start_low
        done_first_b[...] = start_first_b
        done_second_b[...] = start_b

    @pl.when(turn == 0)
    def _():
        for _ in ahead(0):
            pass
        chain(ahead(1))

    @pl.when((turn > 0) & (turn < devices))
    def _():
        chain(alternate(finish(), ahead(jnp.minimum(turn + 1, devices - 1))))

    @pl.when(turn == devices)
    def _():
        for _ in finish():
            pass


def backward_kernel(
    inner_part,
    feature_part,
    sequence_ref,
    packed_ref,
    rows_ref,
    head_grad_ref,
    next_act,
    next_grad,
    next_hidden,
    next_out_slope,
    next_norms,
    next_out_norms,
    next_first,
    next_second,
    now_act,
    now_slope,
    now_curve,
    now_second,
    last_grad,
    last_norms,
    last_first,
    gain_ref,
    bias_ref,
    back_ref,
    first_w,
    first_b,
    second_w,
    second_b,
    gain_sum,
    bias_sum,
    known_ref,
    vector_ref,
    grad_sum,
    to_wide,
    to_rows,
    to_spread,
    to_low,
    to_mix,
    to_state,
    to_sums,
    wide_ref,
    row_ref,
    spread_ref,
    low_ref,
    mix_ref,
    state_ref,
    sums_ref,
    end_known,
    end_rows,
    end_first,
):
    devices, chunk, _ = packed_ref.shape
    steps = chunk // MINI
    turn = pl.program_id(0)
    shard = back_ref.shape[1] - chunk
    gain = gain_ref[...]
    bias = bias_ref[...]
    square_gain = gain * gain
    rows, cols = token_grid(chunk)

    @pl.when(turn == 0)
    def _():
        for ref in (
            first_w,
            first_b,
            second_w,
            second_b,
            gain_sum,
            bias_sum,
            known_ref,
            grad_sum,
            end_known,
            end_rows,
            end_first,
        ):
            ref[...] = jnp.zeros_like(ref)

    def unpack(place):
        packed = packed_ref[place]
        query, key = two_parts(packed)
        miss = key.astype(f32) - packed[:, 2 * HEAD_DIM : 3 * HEAD_DIM].astype(f32) + bias
        return query, key, miss, rate_logit(packed)

    def rate_of(logit):
        return jax.nn.sigmoid(logit[:, :HEAD_DIM]) * rate_scale

    def prepare():
        query, key, miss, logit = unpack(jnp.maximum(devices - 1 - turn, 0))
        halves = []
        for index in range(head_grad_ref.shape[1]):
            values = head_grad_ref[0, index].astype(f32)
            halves += [values[:, :HEAD_DIM], values[:, HEAD_DIM:]]
        head_grad = jnp.concatenate(halves, axis=0)
        head_normal = next_out_norms[:, HEAD_DIM : 2 * HEAD_DIM]
        head_mean = mean_of(head_grad)
        head_tilt = mean_of(head_grad * head_normal)
        yield
        rate = rate_of(logit)
        normal = next_norms[:, :HEAD_DIM]
        rate_gain = rate * square_gain
        gain_normal = rate_gain * normal
        scaled = rate * (miss * gain) + gain_normal
        scaled_mean = mean_of(scaled)
        along = mean_of(scaled * normal)
        yield
        out_grad = next_out_norms[:, 3 * HEAD_DIM :] * (
            head_grad - head_mean - head_normal * head_tilt
        )
        out_normal = next_out_norms[:, :HEAD_DIM]
        normal_grad = out_grad * gain
        out_mean = mean_of(normal_grad)
        out_tilt = mean_of(normal_grad * out_normal)
        yield
        inverse = next_norms[:, HEAD_DIM:]
        back_res = (inverse * (scaled - scaled_mean - normal * along)).astype(bf16)
        gain_along = mean_of(gain_normal)
        gain_square = mean_of(gain_normal * normal)
        to_low[0] = back_res
        to_low[1] = key
        to_sums[2:3, :HEAD_DIM] = jnp.sum(out_grad * out_normal, axis=0, keepdims=True)
        to_sums[3:4, :HEAD_DIM] = jnp.sum(out_grad, axis=0, keepdims=True)
        yield
        res_grad = next_out_norms[:, 2 * HEAD_DIM : 3 * HEAD_DIM] * (
            normal_grad - out_mean - out_normal * out_tilt
        )
        to_sums[1:2, :HEAD_DIM] = jnp.sum(res_grad, axis=0, keepdims=True)
        res_grad_low = res_grad.astype(bf16)
        hidden_base = dot_nn(res_grad_low, next_second[0, 0])
        mix = dot_nt(res_grad_low, back_res)
        yield
        mix_t = dot_nt(back_res, res_grad_low)
        causal = cols <= rows
        later = rows <= cols
        second_grad = jnp.where(causal, -mix, 0.0)
        hidden_more = dot_nn(second_grad, next_act[...])
        yield
        second_grad_t = jnp.where(later, -mix_t, 0.0)
        to_rows[1] = normal
        to_rows[2] = rate_gain
        to_rows[3] = rate_gain - along
        to_rows[4] = gain_normal + scaled
        to_rows[5] = -(along + rate * row_mean(square_gain))
        yield
        for index, value in enumerate(
            (-(gain_along + scaled_mean), -(3.0 * along + gain_square), inverse * inverse)
        ):
            to_spread[index] = jnp.concatenate([value, value], axis=1)
        mix = dot_nt(next_act[...], next_hidden[...])
        yield
        query_pre_grad = (hidden_base + hidden_more) * next_out_slope[...]
        query_pre_low = query_pre_grad.astype(bf16)
        to_sums[0:1] = jnp.sum(query_pre_grad, axis=0, keepdims=True)
        first = dot_nt(query_pre_low, next_grad[...])
        yield
        second_mix_t = jnp.where(later, mix + 1.0, 0.0)
        to_rows[0] = -dot_nn(second_mix_t, res_grad_low)
        first_t = dot_nt(next_grad[...], query_pre_low)
        yield
        first_grad = jnp.where(causal, -first, 0.0)
        mix = dot_nt(key, query)
        query_grad = dot_nt(query_pre_low, next_first[0])
        query_more = dot_nn(first_grad, key)
        yield
        first_grad_t = jnp.where(later, -first_t, 0.0)
        to_rows[6] = dot_nn(first_grad_t, query)
        first_mix_t = jnp.where(later, mix + 1.0, 0.0).astype(bf16)
        yield
        to_rows[7] = out_grad + query_grad + query_more
        to_wide[1] = dot_nn(second_grad_t, next_hidden[...])
        yield
        to_wide[0] = -dot_nn(first_mix_t, query_pre_low)
        mix = dot_nt(key, key)
        yield
        to_mix[...] = jnp.where(cols // MINI > rows // MINI, mix + 1.0, 0.0).astype(bf16)
        to_state[0] = dot_tn(query, query_pre_low)
        yield
        to_state[1] = dot_tn(res_grad_low, next_hidden[...])

    def conclude():
        place = jnp.minimum(devices + 1 - turn, devices - 1)
        _, key, miss, logit = unpack(place)
        normal = last_norms[:, :HEAD_DIM]
        upon = end_rows[0]
        upon_mean = mean_of(upon)
        upon_tilt = mean_of(upon * normal)
        yield
        pre_grad = end_known[...]
        mix = dot_nt(last_grad[...], pre_grad)
        mix_t = dot_nt(pre_grad, last_grad[...])
        yield
        rate = rate_of(logit)
        scaled_grad = last_norms[:, HEAD_DIM:] * (upon - upon_mean - normal * upon_tilt)
        error_grad = scaled_grad * (rate * gain)
        rate_grad = mean_of(scaled_grad * (miss * gain + square_gain * normal))
        yield
        error = miss + normal * gain
        gain_sum[...] += jnp.sum(
            scaled_grad * rate * error + error_grad * normal, axis=0, keepdims=True
        )
        bias_sum[...] += jnp.sum(error_grad, axis=0, keepdims=True)
        from_grad = dot_nt(last_grad[...], end_first[...])
        yield
        far = rows // MINI < cols // MINI
        near = rows // MINI > cols // MINI
        cross = jnp.where(far, mix, 0.0) + jnp.where(near, mix_t, 0.0)
        from_pre = dot_nt(pre_grad, last_first[0])
        from_cross = dot_nn(cross, key)
        yield
        key_grad = end_rows[1] + error_grad - from_grad + from_pre - from_cross
        back_rate = rate_grad * float(HEAD_DIM) * rate * (1.0 - rate * (1.0 / rate_scale))
        lane = lax.broadcasted_iota(jnp.int32, (chunk, HEAD_DIM), 1)
        tail = jnp.where(lane == 0, back_rate, 0.0)
        packed = jnp.concatenate([end_rows[2], key_grad, -error_grad, tail], axis=1).astype(bf16)
        back_ref[place, :chunk] = packed
        yield
        count = 6
        size = grad_sum.shape[0] // count
        for index in range(count):
            at = slice(index * size, (index + 1) * size)
            grad_sum[at] = grad_sum[at] + dot_tn(rows_ref[0, 0, :, at], packed)
            yield

    def chain(following, previous):
        wide_ref[...] = to_wide[...]
        row_ref[...] = to_rows[...]
        spread_ref[...] = to_spread[...]
        low_ref[...] = to_low[...]
        mix_ref[...] = to_mix[...]
        state_ref[...] = to_state[...]
        sums_ref[...] = to_sums[...]
        first_next = first_w[...]
        first_next_low = first_next.astype(bf16)
        first_next_b = first_b[...]
        state = second_w[...]
        state_b = second_b[...]

        def base_of(step):
            at = slice(step * MINI, (step + 1) * MINI)
            return wide_ref[0, at, :] - dot_nn(low_ref[1, at, :], first_next_low) - first_next_b

        base = base_of(steps - 1)
        for step in reversed(range(steps)):
            at = slice(step * MINI, (step + 1) * MINI)
            grad = base
            if step + 1 < steps:
                grad = grad - taken
            state_low = state.astype(bf16)
            own_act = now_act[at, :]
            own_back = low_ref[0, at, :]
            back_base = row_ref[0, at, :] - dot_nt(own_act, state_low) - state_b
            own_low = now_second[0, step]
            slope = now_slope[at, :]
            back_act_grad = (grad * slope).astype(bf16)
            upon = dot_nt(back_act_grad, own_low)
            upon = back_base + upon
            own_normal, own_gain, own_grad, own_beta, own_alpha = (
                row_ref[index, at, :] for index in range(1, 6)
            )
            cross, cross_beta, square_inverse = (spread_ref[index, at, :] for index in range(3))
            main = dot_nn(upon * own_grad, own_low)
            act_base = wide_ref[1, at, :] - dot_nn(own_back, state_low)
            sides = dot_nn(jnp.concatenate([own_normal, own_gain, own_beta], axis=0), own_low)
            interleave(following, 2)
            interleave(previous, 1)
            alpha = row_mean(upon)
            beta = row_mean(upon * own_normal)
            gamma = row_mean(upon * own_gain)
            kappa = row_mean(upon * own_beta)
            level = alpha * own_alpha + beta * cross[:, :HEAD_DIM] + gamma
            tilt = alpha * cross + beta * cross_beta + kappa
            key_res_grad = square_inverse[:, :HEAD_DIM] * (
                upon * own_grad
                - alpha * own_gain
                - beta * own_beta
                - level
                - own_normal * tilt[:, :HEAD_DIM]
            )
            key_res_low = key_res_grad.astype(bf16)
            from_sides = (
                alpha * sides[MINI : 2 * MINI]
                + beta * sides[2 * MINI :]
                + jnp.concatenate([tilt, tilt], axis=1) * sides[:MINI]
            )
            factor = jnp.concatenate([square_inverse, square_inverse], axis=1) * slope
            known = act_base * slope + grad * now_curve[at, :] - factor * from_sides
            pre_grad = known + factor * main
            known_ref[at, :] = pre_grad.astype(bf16)
            if step > 0:
                taken = dot_nn(mix_ref[(step - 1) * MINI : step * MINI, :], known_ref[...])
                base = base_of(step - 1)
            state = state + dot_tn(
                jnp.concatenate([key_res_low, own_back], axis=0),
                jnp.concatenate([own_act, back_act_grad], axis=0),
            )
            state_b = state_b + jnp.sum(key_res_grad, axis=0, keepdims=True)
            row_ref[0, at, :] = upon
        for generator in (following, previous):
            for _ in generator:
                pass
        pre_grad_all = known_ref[...]
        first_w[...] = first_next + dot_tn(low_ref[1], pre_grad_all) + state_ref[0]
        first_b[...] = (
            first_next_b
            + jnp.sum(pre_grad_all.astype(f32), axis=0, keepdims=True)
            + sums_ref[0:1]
        )
        second_w[...] = state + state_ref[1]
        second_b[...] = state_b + sums_ref[1:2, :HEAD_DIM]
        gain_sum[...] += sums_ref[2:3, :HEAD_DIM]
        bias_sum[...] += sums_ref[3:4, :HEAD_DIM]
        end_known[...] = pre_grad_all
        end_rows[0] = row_ref[0]
        end_rows[1] = row_ref[6]
        end_rows[2] = row_ref[7]
        end_first[...] = first_next_low

    @pl.when(turn == 0)
    def _():
        for _ in prepare():
            pass

    @pl.when((turn > 0) & (turn <= devices))
    def _():
        chain(prepare(), conclude())

    @pl.when(turn == devices + 1)
    def _():
        for _ in conclude():
            pass
        vector_ref[...] = jnp.zeros_like(vector_ref)
        for index in range(devices):
            first = slice(index * inner_part, (index + 1) * inner_part)
            small = slice(index * feature_part, (index + 1) * feature_part)
            vector_ref[index : index + 1, :inner_part] = first_b[:, first]
            for number, source in enumerate((second_b, gain_sum, bias_sum)):
                start = inner_part + number * feature_part
                vector_ref[index : index + 1, start : start + feature_part] = source[:, small]
        columns = jnp.transpose(vector_ref[...]).astype(bf16)
        lanes = slice(MATRIX_LANE, MATRIX_LANE + inner_part)
        for index in range(devices):
            first = slice(index * inner_part, (index + 1) * inner_part)
            back_ref[index, :HEAD_DIM, lanes] = first_w[:, first].astype(bf16)
            back_ref[index, HEAD_DIM : 2 * HEAD_DIM, lanes] = second_w[:, first].astype(bf16)
            back_ref[index, :chunk, VECTOR_LANE : VECTOR_LANE + 1] = columns[:, index : index + 1]
            back_ref[index, chunk:] = grad_sum[index * shard : (index + 1) * shard].astype(bf16)


def whole_block(shape):
    return pl.BlockSpec(shape, lambda index, *_: (0,) * len(shape))


STATE_SHAPES = ((HEAD_DIM, INNER), (1, INNER), (HEAD_DIM, INNER), (1, HEAD_DIM))


def chain_forward(packed, inner_part, feature_part):
    blocks, chunk, _ = packed.shape
    length = blocks * chunk
    steps = chunk // MINI
    row = (1, HEAD_DIM)

    def forth(shape):
        return pl.BlockSpec(
            shape, lambda turn: (jnp.minimum(turn, blocks - 1),) + (0,) * (len(shape) - 1)
        )

    def behind(shape):
        return pl.BlockSpec(
            shape, lambda turn: (jnp.maximum(turn - 1, 0),) + (0,) * (len(shape) - 1)
        )

    def of_length(width, dtype):
        return jax.ShapeDtypeStruct((length, width), dtype)

    wide = (chunk, INNER)
    return pl.pallas_call(
        functools.partial(forward_kernel, inner_part, feature_part),
        grid=(blocks + 1,),
        in_specs=[whole_block(packed.shape)],
        out_specs=[behind((1, HEAD_DIM, chunk))]
        + [forth(wide)] * 4
        + [
            forth((chunk, 2 * HEAD_DIM)),
            forth((1, HEAD_DIM, INNER)),
            forth((1, steps, HEAD_DIM, INNER)),
        ]
        + [behind(wide)] * 3
        + [whole_block(row)] * 2,
        out_shape=[jax.ShapeDtypeStruct((blocks, HEAD_DIM, chunk), bf16)]
        + [of_length(INNER, dtype) for dtype in (bf16, bf16, f32, f32)]
        + [
            of_length(2 * HEAD_DIM, f32),
            jax.ShapeDtypeStruct((blocks, HEAD_DIM, INNER), bf16),
            jax.ShapeDtypeStruct((blocks, steps, HEAD_DIM, INNER), bf16),
        ]
        + [of_length(INNER, dtype) for dtype in (bf16, f32, f32)]
        + [jax.ShapeDtypeStruct(row, f32)] * 2,
        scratch_shapes=[pltpu.VMEM(shape, f32) for shape in STATE_SHAPES]
        + [
            pltpu.VMEM(wide, bf16),
            pltpu.VMEM((chunk, HEAD_DIM), bf16),
            pltpu.VMEM(wide, f32),
        ]
        + [
            pltpu.VMEM((3, chunk, HEAD_DIM), f32),
            pltpu.VMEM((chunk, 2 * HEAD_DIM), f32),
            pltpu.VMEM((chunk, chunk), bf16),
        ]
        * 2
        + [
            pltpu.VMEM(wide, bf16),
            pltpu.VMEM(wide, bf16),
            pltpu.VMEM((chunk, HEAD_DIM), bf16),
            pltpu.VMEM((HEAD_DIM, INNER), bf16),
            pltpu.VMEM((HEAD_DIM, INNER), bf16),
            pltpu.VMEM((1, INNER), f32),
            pltpu.VMEM(row, f32),
        ],
        compiler_params=pltpu.CompilerParams(
            dimension_semantics=("arbitrary",), vmem_limit_bytes=VMEM_BYTES
        ),
        cost_estimate=pl.CostEstimate(
            flops=CHAIN_FLOPS, transcendentals=0, bytes_accessed=16 * length * INNER
        ),
        name="chain_forward",
    )(packed)


def chain_backward(packed, rows, sequence, head_grad, saved, inner_part, feature_part):
    act, grad_pre, slope, curve, norms, first_save, second_save = saved[:7]
    hidden, out_slope, out_norms, gain, bias = saved[7:]
    blocks, chunk, _ = packed.shape
    width = rows.shape[-1]
    shard = width // blocks
    steps = chunk // MINI
    row = (1, HEAD_DIM)
    wide = (chunk, INNER)
    narrow = (chunk, 2 * HEAD_DIM)

    def at(shape, delay):
        def index_map(turn, _):
            place = jnp.clip(blocks - 1 - turn + delay, 0, blocks - 1)
            return (place,) + (0,) * (len(shape) - 1)

        return pl.BlockSpec(shape, index_map)

    def rows_map(turn, chosen):
        place = jnp.clip(blocks + 1 - turn, 0, blocks - 1)
        return (place // SEQS, (place + chosen[0]) % SEQS, 0, 0)

    state = (HEAD_DIM, INNER)
    carried = [
        pltpu.VMEM((2,) + wide, f32),
        pltpu.VMEM((8, chunk, HEAD_DIM), f32),
        pltpu.VMEM((3,) + narrow, f32),
        pltpu.VMEM((2, chunk, HEAD_DIM), bf16),
        pltpu.VMEM((chunk, chunk), bf16),
        pltpu.VMEM((2,) + state, f32),
        pltpu.VMEM((8, INNER), f32),
    ]
    return pl.pallas_call(
        functools.partial(backward_kernel, inner_part, feature_part),
        grid_spec=pltpu.PrefetchScalarGridSpec(
            num_scalar_prefetch=1,
            grid=(blocks + 2,),
            in_specs=[
                whole_block(packed.shape),
                pl.BlockSpec((1, 1, chunk, width), rows_map),
                at((1,) + head_grad.shape[1:], 0),
                at(wide, 0),
                at(wide, 0),
                at(wide, 0),
                at(wide, 0),
                at(narrow, 0),
                at(wide, 0),
                at((1,) + state, 0),
                at((1, 1) + state, 0),
                at(wide, 1),
                at(wide, 1),
                at(wide, 1),
                at((1, steps) + state, 1),
                at(wide, 2),
                at(narrow, 2),
                at((1,) + state, 2),
                whole_block(row),
                whole_block(row),
            ],
            out_specs=whole_block((blocks, chunk + shard, LANES)),
            scratch_shapes=[pltpu.VMEM(shape, f32) for shape in STATE_SHAPES + (row, row)]
            + [
                pltpu.VMEM(wide, bf16),
                pltpu.VMEM((chunk, 128), f32),
                pltpu.VMEM((width, LANES), f32),
            ]
            + carried
            + carried
            + [
                pltpu.VMEM(wide, bf16),
                pltpu.VMEM((3, chunk, HEAD_DIM), f32),
                pltpu.VMEM(state, bf16),
            ],
        ),
        out_shape=jax.ShapeDtypeStruct((blocks, chunk + shard, LANES), bf16),
        compiler_params=pltpu.CompilerParams(
            dimension_semantics=("arbitrary",), vmem_limit_bytes=VMEM_BYTES
        ),
        cost_estimate=pl.CostEstimate(
            flops=CHAIN_FLOPS, transcendentals=0, bytes_accessed=16 * blocks * chunk * INNER
        ),
        name="chain_backward",
    )(
        sequence,
        packed,
        rows,
        head_grad,
        act,
        grad_pre,
        hidden,
        out_slope,
        norms,
        out_norms,
        first_save,
        second_save,
        act,
        slope,
        curve,
        second_save,
        grad_pre,
        norms,
        first_save,
        gain,
        bias,
    )


def layer_norm_parts(values):
    centred = values - row_mean(values)
    inverse = lax.rsqrt(row_mean(centred * centred) + epsilon)
    return centred * inverse, inverse


def layer_norm_back(normal, inverse, scaling, grad):
    scaled = grad * scaling
    return inverse * (scaled - row_mean(scaled) - normal * row_mean(scaled * normal))


def start_kernel(
    head_count,
    rows_ref,
    weights_ref,
    gain_ref,
    inner_ref,
    packed_ref,
    normed_ref,
    matrix_ref,
):
    tensor_count = rows_ref.shape[0]
    seq_count, chunk, _ = normed_ref.shape
    rows = chunk // tensor_count
    matrix_ref[...] = jnp.zeros_like(matrix_ref)
    for head in range(head_count):
        first = head * 3 * HEAD_DIM
        rate = head_count * 3 * HEAD_DIM + head
        column = weights_ref[:, rate : rate + 1]
        matrix_ref[head, :, : 3 * HEAD_DIM] = weights_ref[:, first : first + 3 * HEAD_DIM]
        matrix_ref[head, :, RATE_LANE : RATE_LANE + 1] = column
        matrix_ref[head, :, RATE_LANE + 1 : RATE_LANE + 2] = column
    lane = lax.broadcasted_iota(jnp.int32, (chunk, LANES), 1)
    for sequence in range(seq_count):
        part = slice(sequence * rows, (sequence + 1) * rows)
        values = jnp.concatenate([rows_ref[index, part] for index in range(tensor_count)], axis=0)
        normal, _ = layer_norm_parts(values.astype(f32))
        normed = (normal * gain_ref[...]).astype(bf16)
        normed_ref[sequence] = normed
        for head in range(head_count):
            projected = dot_nn(normed, matrix_ref[head])
            rest = projected - projected.astype(bf16).astype(f32)
            projected = jnp.where(lane == RATE_LANE + 1, rest, projected).astype(bf16)
            packed_ref[head * seq_count + sequence] = jnp.where(
                lane >= VECTOR_LANE, inner_ref[head], projected
            )
    for index in range(head_count * seq_count, packed_ref.shape[0]):
        packed_ref[index] = jnp.zeros((chunk, LANES), bf16)


def feed_forward_kernel(
    heads_ref,
    rows_ref,
    weights_ref,
    out_ref,
    gain_ref,
    terms_ref,
    mixed_ref,
    normed_ref,
    back_ref,
    swiglu_ref,
    cot_ref,
):
    tensor_count, head_count, seq_count, _, chunk = heads_ref.shape
    ff_local = swiglu_ref.shape[1]
    rows = chunk // tensor_count
    total = seq_count * chunk
    for sequence in range(seq_count):
        part = slice(sequence * rows, (sequence + 1) * rows)
        other = slice((seq_count + sequence) * rows, (seq_count + sequence + 1) * rows)
        values = jnp.concatenate([rows_ref[index, part] for index in range(tensor_count)], axis=0)
        mixed = values.astype(f32)
        for index in range(tensor_count):
            heads = [heads_ref[index, head, sequence] for head in range(head_count)]
            heads = jnp.transpose(jnp.concatenate(heads, axis=0).astype(f32))
            mixed = mixed + dot_nt(heads, out_ref[index])
        for index in range(tensor_count):
            mixed_ref[index, sequence] = mixed[index * rows : (index + 1) * rows]
        normal, _ = layer_norm_parts(mixed)
        at = slice(sequence * chunk, (sequence + 1) * chunk)
        normed_ref[at] = (normal * gain_ref[...]).astype(bf16)
        for index in range(tensor_count):
            first = sequence * chunk + index * rows
            cot_ref[first : first + rows] = rows_ref[index, other]
    normed = normed_ref[...]
    cot = cot_ref[...]
    for first in range(0, ff_local, 256):
        at = slice(first, first + 256)
        beyond = slice(ff_local + first, ff_local + first + 256)
        gate = dot_nn(normed, weights_ref[:, at])
        up = dot_nn(normed, weights_ref[:, beyond])
        back = dot_nn(cot, weights_ref[:, 2 * ff_local + first : 2 * ff_local + first + 256])
        share = jax.nn.sigmoid(gate)
        silu = gate * share
        swiglu_ref[:, at] = (silu * up).astype(bf16)
        back_ref[:, at] = (back * up * (share * (1.0 + gate * (1.0 - share)))).astype(bf16)
        back_ref[:, beyond] = (back * silu).astype(bf16)
    ffn_term = dot_nt(back_ref[...], weights_ref[:, : 2 * ff_local]).astype(bf16)
    down_term = dot_nt(swiglu_ref[...], weights_ref[:, 2 * ff_local : 3 * ff_local]).astype(bf16)
    for sequence in range(seq_count):
        for index in range(tensor_count):
            first = sequence * chunk + index * rows
            terms_ref[index, sequence] = ffn_term[first : first + rows]
            terms_ref[index, seq_count + sequence] = down_term[first : first + rows]


def feed_forward_grad_kernel(normed_ref, back_ref, swiglu_ref, cot_ref, grads_ref):
    normed = jnp.transpose(normed_ref[...].astype(f32)).astype(bf16)
    cot = jnp.transpose(cot_ref[...].astype(f32)).astype(bf16)
    width = back_ref.shape[1]
    for first in range(0, width, 256):
        at = slice(first, first + 256)
        grads_ref[:, at] = dot_nn(normed, back_ref[:, at]).astype(bf16)
    for first in range(0, swiglu_ref.shape[1], 256):
        at = slice(width + first, width + first + 256)
        grads_ref[:, at] = dot_nn(cot, swiglu_ref[:, first : first + 256]).astype(bf16)


def head_back(grads_ref, out_ref, back_ref):
    tensor_count = out_ref.shape[0]
    seq_count, rows, _ = grads_ref.shape
    head_count = out_ref.shape[2] // HEAD_DIM
    for index in range(tensor_count):
        for sequence in range(seq_count):
            back = dot_nn(grads_ref[sequence], out_ref[index]).astype(bf16)
            for head in range(head_count):
                place = (head * seq_count + sequence) * tensor_count + index
                values = back[:, head * HEAD_DIM : (head + 1) * HEAD_DIM]
                back_ref[place, :, :HEAD_DIM] = values[: rows // 2]
                back_ref[place, :, HEAD_DIM:] = values[rows // 2 :]
    for place in range(head_count * seq_count * tensor_count, back_ref.shape[0]):
        back_ref[place] = jnp.zeros((rows // 2, 2 * HEAD_DIM), bf16)


def out_grad_kernel(grads_ref, heads_ref, out_grad_ref):
    head_count, seq_count, _, _ = heads_ref.shape
    devices, shard, _ = out_grad_ref.shape
    total = None
    for sequence in range(seq_count):
        heads = [heads_ref[head, sequence] for head in range(head_count)]
        grads = jnp.transpose(grads_ref[sequence].astype(f32))
        term = dot_nt(grads, jnp.concatenate(heads, axis=0))
        total = term if total is None else total + term
    for index in range(devices):
        out_grad_ref[index] = total[index * shard : (index + 1) * shard].astype(bf16)


def matrix_output_kernel(sums_ref, out_ref, weights_ref, gate_up_ref, down_ref, out_grad_ref, gain_ref):
    ff_local = down_ref.shape[1]
    sums = sums_ref[...].astype(f32)
    for index in range(2):
        gate_up_ref[:, index, :] = sums[:, index * ff_local : (index + 1) * ff_local]
    down_ref[...] = sums[:, 2 * ff_local :]
    total = out_ref[0].astype(f32)
    for index in range(1, out_ref.shape[0]):
        total = total + out_ref[index].astype(f32)
    out_grad_ref[...] = jnp.transpose(total)
    products = sums[:, : 2 * ff_local] * weights_ref[:, : 2 * ff_local].astype(f32)
    gain = jnp.sum(products, axis=-1, keepdims=True)
    gain_ref[...] = jnp.broadcast_to(gain, gain_ref.shape)


def feed_forward_back_kernel(
    rank_ref,
    terms_ref,
    mixed_ref,
    cot_ref,
    gain_ref,
    out_ref,
    back_ref,
    low_ref,
    result_ref,
    heads_ref,
):
    seq_count = mixed_ref.shape[1]
    for sequence in range(seq_count):
        grad = terms_ref[0, sequence].astype(f32)
        down = terms_ref[0, seq_count + sequence].astype(f32)
        for index in range(1, terms_ref.shape[0]):
            grad = grad + terms_ref[index, sequence].astype(f32)
            down = down + terms_ref[index, seq_count + sequence].astype(f32)
        mixed = mixed_ref[0, sequence]
        normal, inverse = layer_norm_parts(mixed)
        back = cot_ref[sequence].astype(f32)
        back = back + layer_norm_back(normal, inverse, gain_ref[...], grad)
        back_ref[sequence] = back
        low_ref[sequence] = back.astype(bf16)
        result_ref[sequence] = (mixed + down).astype(bf16)
    head_back(low_ref, out_ref, heads_ref)


def input_grad_kernel(terms_ref, tokens_ref, back_ref, gain_ref, grad_ref, gains_ref):
    seq_count, rows, _ = tokens_ref.shape
    for sequence in range(seq_count):
        at = slice(sequence * rows, (sequence + 1) * rows)
        total = terms_ref[0, at].astype(f32)
        for index in range(1, terms_ref.shape[0]):
            total = total + terms_ref[index, at].astype(f32)
        normal, inverse = layer_norm_parts(tokens_ref[sequence].astype(f32))
        total = layer_norm_back(normal, inverse, gain_ref[...], total)
        grad_ref[:, sequence, :] = back_ref[sequence] + total
    total = terms_ref[0, seq_count * rows :].astype(f32)
    for index in range(1, terms_ref.shape[0]):
        total = total + terms_ref[index, seq_count * rows :].astype(f32)
    width = gains_ref.shape[1]
    gains_ref[...] = (total[:2] + total[2:4])[:, :width]


def tail_kernel(
    received_ref,
    matrix_ref,
    own_ref,
    gain_two_ref,
    gains_ref,
    terms_ref,
    qkv_ref,
    small_ref,
    state_ref,
):
    head_count = matrix_ref.shape[0]
    shard = own_ref.shape[1]
    tensor_count, term_rows, width = terms_ref.shape
    chunk = received_ref.shape[1] - shard
    seq_count = (term_rows - 16) * tensor_count // chunk
    rows = chunk // tensor_count
    lane = lax.broadcasted_iota(jnp.int32, (chunk, LANES), 1)
    for sequence in range(seq_count):
        total = None
        for head in range(head_count):
            values = received_ref[head * seq_count + sequence, :chunk]
            values = jnp.where(lane <= RATE_LANE, values, jnp.zeros_like(values))
            term = dot_nt(values, matrix_ref[head])
            total = term if total is None else total + term
        for index in range(tensor_count):
            part = total[index * rows : (index + 1) * rows]
            terms_ref[index, sequence * rows : (sequence + 1) * rows] = part.astype(bf16)
    lane = lax.broadcasted_iota(jnp.int32, (shard, LANES), 1)
    column = lax.broadcasted_iota(jnp.int32, (shard, 128), 1)
    gain = None
    small = jnp.where(column == 1, gain_two_ref[...], 0.0)
    for head in range(head_count):
        grads = received_ref[head * seq_count, chunk:].astype(f32)
        state = received_ref[head * seq_count, :chunk, RATE_LANE:].astype(f32)
        for sequence in range(1, seq_count):
            grads = grads + received_ref[head * seq_count + sequence, chunk:].astype(f32)
            state = state + received_ref[
                head * seq_count + sequence, :chunk, RATE_LANE:
            ].astype(f32)
        state_ref[head] = state
        for index in range(3):
            at = slice(index * HEAD_DIM, (index + 1) * HEAD_DIM)
            qkv_ref[index, :, head * HEAD_DIM : (head + 1) * HEAD_DIM] = grads[:, at]
        products = jnp.where(lane <= RATE_LANE, grads * own_ref[head].astype(f32), 0.0)
        products = jnp.sum(products, axis=-1, keepdims=True)
        gain = products if gain is None else gain + products
        small = jnp.where(column == 2 + head, grads[:, RATE_LANE : RATE_LANE + 1], small)
    small = jnp.transpose(jnp.where(column == 0, gain, small))[: small_ref.shape[0]]
    small_ref[...] = small
    gain = small[:2] / gains_ref[...]
    high = gain.astype(bf16)
    low = (gain - high.astype(f32)).astype(bf16)
    block = jnp.concatenate([high.astype(f32), low.astype(f32), jnp.zeros((12, shard), f32)], axis=0)
    for index in range(tensor_count):
        first = seq_count * rows
        terms_ref[index, first:, :] = jnp.zeros((16, width), bf16)
        terms_ref[index, first:, :shard] = block.astype(bf16)


def whole_call(kernel, name, operands, results, vmem_bytes=GLUE_BYTES):
    def spec(shape):
        return pl.BlockSpec(shape, lambda: (0,) * len(shape))

    return pl.pallas_call(
        kernel,
        in_specs=[spec(operand.shape) for operand in operands],
        out_specs=[spec(result.shape) for result in results],
        out_shape=results,
        compiler_params=pltpu.CompilerParams(vmem_limit_bytes=vmem_bytes),
        name=name,
    )(*operands)


def dots(subscripts, left, right):
    return jnp.einsum(subscripts, left, right, preferred_element_type=f32)


def exchange(values, axis):
    return lax.all_to_all(values, axis, 0, 0, tiled=False)


def share_out(values, axis):
    count = lax.axis_size(axis)
    return exchange(jnp.broadcast_to(values[None], (count,) + values.shape), axis)


def ordered(*values):
    return lax.optimization_barrier(values)


def inner_block(matrix_one, matrix_two, vectors, rows):
    width = matrix_one.shape[-1]
    matrices = jnp.concatenate([matrix_one, matrix_two], axis=-2)
    column = jnp.concatenate(vectors, axis=-1)[..., None]
    lead = [(0, 0)] * (column.ndim - 2)
    column = jnp.pad(
        column,
        lead + [(0, rows - column.shape[-2]), (VECTOR_LANE, LANES - VECTOR_LANE - 1)],
    )
    matrices = jnp.pad(
        matrices,
        lead + [(0, rows - matrices.shape[-2]), (MATRIX_LANE, LANES - MATRIX_LANE - width)],
    )
    return column + matrices


def local(
    tokens,
    gain_attn,
    gain_ffn,
    w_qkv,
    w_rate,
    w_out,
    w_gate_up,
    w_down,
    w_one,
    b_one,
    w_two,
    b_two,
    norm_gain_inner,
    norm_bias_inner,
    cotangent,
):
    device_count = lax.axis_size(DP)
    tensor_count = lax.axis_size("tensor")
    local_rows, seq_count, width = tokens.shape
    row_count = local_rows * seq_count
    chunk = local_rows * tensor_count
    head_count = w_rate.shape[1]
    local_width = head_count * HEAD_DIM
    shard = w_qkv.shape[0]
    part = gain_attn.shape[0]
    ff_local = w_down.shape[0]
    chain_count = seq_count * head_count
    inner_part = w_one.shape[2]
    feature_part = b_two.shape[1]
    assert chain_count <= device_count and seq_count == SEQS
    assert chunk == 2 * HEAD_DIM and inner_part <= 32 and part <= shard
    rank = lax.axis_index("tensor")
    place = lax.axis_index(DP)

    own_tokens = tokens.transpose(1, 0, 2).reshape(row_count, width)
    own_cot = cotangent.transpose(1, 0, 2).reshape(row_count, width)
    row_full = share_out(jnp.concatenate([own_tokens, own_cot], axis=0), "tensor")
    head_columns = w_qkv.reshape(shard, 3, head_count, HEAD_DIM).transpose(0, 2, 1, 3)
    gain_columns = jnp.pad(jnp.stack([gain_attn, gain_ffn], axis=1), ((0, shard - part), (0, 0)))
    qkv_pack = jnp.concatenate(
        [head_columns.reshape(shard, 3 * local_width), w_rate, gain_columns], axis=1
    )
    qkv_half = lax.all_gather(qkv_pack, "inner", axis=0, tiled=True)
    qkv_full = lax.all_gather(qkv_half, "outer", axis=0, tiled=True)
    qkv_full, row_full = ordered(qkv_full, row_full)
    some_gains = qkv_full[:, 3 * local_width + head_count :]
    some_gains = some_gains.reshape(device_count, shard, 2)[:, :part].transpose(2, 0, 1)
    gains = lax.all_gather(some_gains.reshape(2, device_count * part), "tensor", axis=0)
    gains = gains.reshape(tensor_count, 2, device_count, part).transpose(1, 2, 0, 3)
    gains = gains.reshape(2, width).astype(f32)
    scale_attn, scale_ffn = gains[0:1], gains[1:2]

    ffn_pack = jnp.concatenate(
        [w_gate_up.reshape(shard, 2 * ff_local), w_down.T, w_out.T], axis=1
    )
    ffn_full = lax.all_gather(ffn_pack, DP, axis=0, tiled=True)
    own_out = ffn_full[:, 3 * ff_local :]

    inner = inner_block(
        w_one,
        w_two.transpose(0, 2, 1),
        [b_one, b_two, norm_gain_inner, norm_bias_inner],
        chunk,
    )
    shape = jax.ShapeDtypeStruct
    packed, normed_attn, head_matrix = whole_call(
        functools.partial(start_kernel, head_count),
        "projections",
        (row_full, qkv_full, scale_attn, inner),
        (
            shape((device_count, chunk, LANES), bf16),
            shape((seq_count, chunk, width), bf16),
            shape((head_count, width, LANES), bf16),
        ),
    )
    chain_in = exchange(packed, DP)

    side = lax.axis_index("inner")
    kept = lax.dynamic_index_in_dim(normed_attn, side, 0)
    given = lax.dynamic_index_in_dim(normed_attn, 1 - side, 0)
    taken = lax.ppermute(given, "inner", [(0, 1), (1, 0)])
    pair = jnp.concatenate([kept, taken], axis=0)
    chain_in, own_out, pair = ordered(chain_in, own_out, pair)
    chain_rows = lax.all_gather(pair, "outer", axis=0)
    out_full = lax.all_gather(own_out, "tensor", axis=0)

    forward_out = chain_forward(chain_in, inner_part, feature_part)
    saved = forward_out[1:]
    head_local = exchange(forward_out[0], DP)[:chain_count]
    head_local = head_local.reshape(head_count, seq_count, HEAD_DIM, chunk)
    head_rows = lax.all_gather(head_local, "tensor", axis=0, tiled=False)

    group_rows = seq_count * chunk
    terms, mixed, normed_ffn, back_gate_up, swiglu, group_cot = whole_call(
        feed_forward_kernel,
        "feed_forward",
        (head_rows, row_full, ffn_full, out_full, scale_ffn),
        (
            shape((tensor_count, 2 * seq_count, local_rows, width), bf16),
            shape((tensor_count, seq_count, local_rows, width), f32),
            shape((group_rows, width), bf16),
            shape((group_rows, 2 * ff_local), bf16),
            shape((group_rows, ff_local), bf16),
            shape((group_rows, width), bf16),
        ),
        VMEM_BYTES,
    )
    ffn_sums = exchange(terms, "tensor")
    (ffn_grads,) = whole_call(
        feed_forward_grad_kernel,
        "feed_forward_grads",
        (normed_ffn, back_gate_up, swiglu, group_cot),
        (shape((width, 3 * ff_local), bf16),),
        VMEM_BYTES,
    )
    ffn_grad_sums = lax.psum_scatter(ffn_grads, DP, scatter_dimension=0, tiled=True)
    ffn_sums, chain_rows, _ = ordered(ffn_sums, chain_rows, ffn_grads)
    own_shape = (seq_count, local_rows, width)
    own_cot = own_cot.reshape(own_shape)

    def fixed(operand):
        return pl.BlockSpec(operand.shape, lambda turn, _: (0,) * len(operand.shape))

    chosen_mixed = pl.BlockSpec((1,) + own_shape, lambda turn, chosen: (chosen[0], 0, 0, 0))
    own_block = pl.BlockSpec(own_shape, lambda turn, _: (0, 0, 0))
    head_shape = shape(
        (device_count * tensor_count, local_rows // 2, 2 * HEAD_DIM), bf16
    )
    back_mixed, back_low, result, back_head = pl.pallas_call(
        feed_forward_back_kernel,
        grid_spec=pltpu.PrefetchScalarGridSpec(
            num_scalar_prefetch=1,
            grid=(1,),
            in_specs=[
                fixed(ffn_sums),
                chosen_mixed,
                own_block,
                fixed(scale_ffn),
                fixed(out_full),
            ],
            out_specs=[own_block] * 3 + [fixed(head_shape)],
        ),
        out_shape=[shape(own_shape, dtype) for dtype in (f32, bf16, bf16)] + [head_shape],
        compiler_params=pltpu.CompilerParams(vmem_limit_bytes=VMEM_BYTES),
        name="feed_forward_back",
    )(jnp.reshape(rank, (1,)).astype(jnp.int32), ffn_sums, mixed, own_cot, scale_ffn, out_full)
    result = result.transpose(1, 0, 2)
    back_head, back_low = ordered(back_head, back_low)
    head_grad = exchange(back_head, DP + ("tensor",))
    head_grad = head_grad.reshape(device_count, tensor_count, local_rows // 2, 2 * HEAD_DIM)
    attn_grads = lax.all_gather(back_low, "tensor", axis=1, tiled=True)
    (out_terms,) = whole_call(
        out_grad_kernel,
        "out_grads",
        (attn_grads, head_local),
        (shape((device_count, shard, local_width), bf16),),
    )
    head_grad, out_terms = ordered(head_grad, out_terms)
    out_sums = exchange(out_terms, DP)

    chosen = jnp.reshape(side, (1,)).astype(jnp.int32)
    back_packed = chain_backward(
        chain_in, chain_rows, chosen, head_grad, saved, inner_part, feature_part
    )
    received = exchange(back_packed, DP)
    grad_gate_up, grad_down, grad_out, gain_two = whole_call(
        matrix_output_kernel,
        "matrix_outputs",
        (ffn_grad_sums, out_sums, ffn_pack),
        (
            shape((shard, 2, ff_local), f32),
            shape((shard, ff_local), f32),
            shape((local_width, shard), f32),
            shape((shard, 128), f32),
        ),
    )
    own_matrix = lax.dynamic_slice_in_dim(head_matrix, place * shard, shard, 1)
    own_gains = lax.dynamic_slice_in_dim(gains, place * shard, shard, 1)
    terms, grad_qkv, small, state_block = whole_call(
        tail_kernel,
        "tail",
        (received, head_matrix, own_matrix, gain_two, own_gains),
        (
            shape((tensor_count, row_count + 16, width), bf16),
            shape((3, shard, local_width), f32),
            shape((8, shard), f32),
            shape((head_count, chunk, LANES - RATE_LANE), f32),
        ),
    )
    input_grad, gain_sums = whole_call(
        input_grad_kernel,
        "input_grad",
        (exchange(terms, "tensor"), own_tokens.reshape(own_shape), back_mixed, scale_attn),
        (shape(tokens.shape, f32), shape((2, shard), f32)),
    )
    gain_sums = lax.dynamic_slice_in_dim(gain_sums, rank * part, part, 1)

    matrices = state_block[..., MATRIX_LANE - RATE_LANE :][..., :inner_part]
    grad_one = matrices[:, :HEAD_DIM]
    grad_two = matrices[:, HEAD_DIM : 2 * HEAD_DIM].transpose(0, 2, 1)
    columns = state_block[:, :, VECTOR_LANE - RATE_LANE]
    ends = [inner_part + index * feature_part for index in range(4)]
    grad_b_one = columns[:, : ends[0]]
    grad_b_two, grad_gain_inner, grad_bias_inner = (
        columns[:, ends[index] : ends[index + 1]] for index in range(3)
    )

    return (
        result,
        input_grad,
        gain_sums[0],
        gain_sums[1],
        grad_qkv.transpose(1, 0, 2),
        small[2 : 2 + head_count].T,
        grad_out,
        grad_gate_up,
        grad_down.T,
        grad_one,
        grad_b_one,
        grad_two,
        grad_b_two,
        grad_gain_inner,
        grad_bias_inner,
    )


def solution(mesh):
    devices = mesh.devices
    dp_count, tensor_count = mesh.shape["dp"], mesh.shape["tensor"]
    devices = devices.reshape(dp_count // SEQS, SEQS, tensor_count)
    split = jax.sharding.Mesh(devices, DP + ("tensor",))
    rows = P(DP + ("tensor",), None, None)
    gains = P(DP + ("tensor",))
    placed = (
        rows,
        gains,
        gains,
        P(DP, None, "tensor"),
        P(DP, "tensor"),
        P("tensor", DP),
        P(DP, None, "tensor"),
        P("tensor", DP),
        P("tensor", None, DP),
        P("tensor", DP),
        P("tensor", DP, None),
        P("tensor", DP),
        P("tensor", DP),
        P("tensor", DP),
    )
    return jax.shard_map(
        local,
        mesh=split,
        in_specs=placed + (rows,),
        out_specs=(rows,) + placed,
        check_vma=False,
    )
```

```python
import functools


import jax
import jax.numpy as jnp
from jax import lax
from jax.experimental import pallas as pl
from jax.experimental.pallas import tpu as pltpu
from jax.sharding import PartitionSpec as P

HEAD_DIM = 64
INNER = 256
MINI = 16
SEQS = 2
LANES = 256
RATE_LANE = 3 * HEAD_DIM
VECTOR_LANE = RATE_LANE + 2
MATRIX_LANE = LANES - 32
VMEM_BYTES = 56 * 1024 * 1024
DP = ("outer", "inner")
CHAIN_FLOPS = 27_000_000_000
GLUE_BYTES = 32 * 1024 * 1024

epsilon = 1e-05
inner_epsilon = 1e-06
inner_rate = 0.5
rate_scale = inner_rate / (MINI * HEAD_DIM)
root_half = 0.7071067811865476
normal_peak = 0.3989422804014327

f32 = jnp.float32
bf16 = jnp.bfloat16


def dot_nn(a, b):
    return lax.dot_general(
        a.astype(bf16), b.astype(bf16), (((1,), (0,)), ((), ())), preferred_element_type=f32
    )


def dot_nt(a, b):
    return lax.dot_general(
        a.astype(bf16), b.astype(bf16), (((1,), (1,)), ((), ())), preferred_element_type=f32
    )


def dot_tn(a, b):
    return lax.dot_general(
        a.astype(bf16), b.astype(bf16), (((0,), (0,)), ((), ())), preferred_element_type=f32
    )


def row_mean(values):
    return jnp.mean(values, axis=-1, keepdims=True)


def density_and_share(values):
    density = jnp.exp(-0.5 * values * values) * normal_peak
    share = 0.5 * (1.0 + lax.erf(values * root_half))
    return density, share


def token_grid(count):
    rows = lax.broadcasted_iota(jnp.int32, (count, count), 0)
    cols = lax.broadcasted_iota(jnp.int32, (count, count), 1)
    return rows, cols


def wide_mean(values):
    high = values.astype(bf16)
    low = (values - high.astype(f32)).astype(bf16)
    ones = jnp.full((values.shape[1], 128), 1.0 / values.shape[1], bf16)
    return dot_nn(high, ones) + dot_nn(low, ones)


def mean_of(values):
    return wide_mean(values)[:, :HEAD_DIM]


def two_parts(packed):
    return packed[:, :HEAD_DIM], packed[:, HEAD_DIM : 2 * HEAD_DIM]


def rate_logit(packed):
    source = lax.broadcasted_iota(jnp.int32, (2 * HEAD_DIM, 128), 0)
    spread = jnp.where((source >= HEAD_DIM) & (source < HEAD_DIM + 2), 1.0, 0.0)
    return dot_nn(packed[:, 2 * HEAD_DIM :], spread)


def alternate(*generators):
    left = list(generators)
    while left:
        for generator in list(left):
            if next(generator, generator) is generator:
                left.remove(generator)
            else:
                yield


def interleave(generator, count):
    for _ in range(count):
        if next(generator, generator) is generator:
            return


def forward_kernel(
    inner_part,
    feature_part,
    packed_ref,
    normed_ref,
    act_ref,
    grad_pre_ref,
    slope_ref,
    curve_ref,
    norms_ref,
    first_save,
    second_save,
    hidden_ref,
    out_slope_ref,
    out_norms_ref,
    gain_ref,
    bias_ref,
    first_w,
    first_b,
    second_w,
    second_b,
    known_ref,
    back_res_ref,
    pre_ref,
    to_rows,
    to_level,
    to_mix,
    row_ref,
    level_ref,
    mix_ref,
    done_act,
    done_grad,
    done_back,
    done_first,
    done_second,
    done_first_b,
    done_second_b,
):
    devices, chunk, _ = packed_ref.shape
    steps = chunk // MINI
    turn = pl.program_id(0)

    @pl.when(turn == 0)
    def _():
        for index in range(devices):
            block = packed_ref[index, :, LANES - 128 :].astype(f32)
            first = slice(index * inner_part, (index + 1) * inner_part)
            lanes = slice(MATRIX_LANE - LANES + 128, MATRIX_LANE - LANES + 128 + inner_part)
            first_w[:, first] = block[:HEAD_DIM, lanes]
            second_w[:, first] = block[HEAD_DIM : 2 * HEAD_DIM, lanes]
            at = VECTOR_LANE - LANES + 128
            vector = jnp.transpose(block)[at : at + 1]
            first_b[:, first] = vector[:, :inner_part]
            small = slice(index * feature_part, (index + 1) * feature_part)
            for number, target in enumerate((second_b, gain_ref, bias_ref)):
                start = inner_part + number * feature_part
                target[:, small] = vector[:, start : start + feature_part]
        known_ref[...] = jnp.zeros_like(known_ref)
        centred = second_w[...]
        second_w[...] = centred - jnp.mean(centred, axis=0, keepdims=True)
        second_b[...] = second_b[...] - row_mean(second_b[...])

    gain = gain_ref[...]
    bias = bias_ref[...]
    rows, cols = token_grid(chunk)

    def finish():
        query, key = two_parts(packed_ref[jnp.maximum(turn - 1, 0)])
        causal = cols <= rows
        mix = dot_nt(query, key)
        query_base = dot_nn(query, done_first[...])
        yield
        first_mix = jnp.where(causal, mix + 1.0, 0.0)
        taken = dot_nn(first_mix, done_grad[...])
        yield
        query_pre = query_base + done_first_b[...] - taken
        density, share = density_and_share(query_pre)
        hidden = (query_pre * share).astype(bf16)
        hidden_ref[...] = hidden
        out_slope_ref[...] = share + query_pre * density
        yield
        mix = dot_nt(hidden, done_act[...])
        res_base = dot_nt(hidden, done_second[...])
        yield
        second_mix = jnp.where(causal, mix + 1.0, 0.0)
        taken = dot_nn(second_mix, done_back[...])
        yield
        query_res = res_base + done_second_b[...] - taken
        square = mean_of(query_res * query_res)
        yield
        out_inverse = lax.rsqrt(square + inner_epsilon)
        out_normal = query_res * out_inverse
        outputs = query.astype(f32) + out_normal * gain + bias
        middle = mean_of(outputs)
        out_norms_ref[:, :HEAD_DIM] = out_normal
        out_norms_ref[:, 2 * HEAD_DIM : 3 * HEAD_DIM] = out_inverse
        yield
        centred = outputs - middle
        square = mean_of(centred * centred)
        yield
        head_inverse = lax.rsqrt(square + epsilon)
        head_normal = centred * head_inverse
        out_norms_ref[:, HEAD_DIM : 2 * HEAD_DIM] = head_normal
        out_norms_ref[:, 3 * HEAD_DIM :] = head_inverse
        normed_ref[0] = jnp.transpose(head_normal).astype(bf16)

    def ahead(place):
        packed = packed_ref[place]
        _, key = two_parts(packed)
        value = packed[:, 2 * HEAD_DIM : 3 * HEAD_DIM]
        logit = rate_logit(packed)
        mix = dot_nt(key, key)
        yield
        rate = jax.nn.sigmoid(logit) * rate_scale
        square_gain = gain * gain
        level_gain = rate * row_mean(square_gain)
        rate_base = rate[:, :HEAD_DIM] * (
            (key.astype(f32) - value.astype(f32) + bias) * gain
        )
        middle = mean_of(rate_base)
        to_rows[0] = rate_base
        to_rows[1] = rate[:, :HEAD_DIM] * square_gain - level_gain[:, :HEAD_DIM]
        to_level[...] = level_gain * inner_epsilon
        to_mix[...] = jnp.where(cols // MINI < rows // MINI, mix + 1.0, 0.0).astype(bf16)
        yield
        to_rows[2] = middle

    def chain(others):
        _, key = two_parts(packed_ref[jnp.minimum(turn, devices - 1)])
        row_ref[...] = to_rows[...]
        level_ref[...] = to_level[...]
        mix_ref[...] = to_mix[...]
        first_low = first_w[...].astype(bf16)
        first_save[0] = first_low
        start_first_b = first_b[...]
        start_b = second_b[...]
        pre_ref[...] = dot_nn(key, first_low) + start_first_b
        state = second_w[...]
        start_low = state.astype(bf16)
        state_b = start_b
        for step in range(steps):
            at = slice(step * MINI, (step + 1) * MINI)
            own_base = row_ref[0, at, :]
            own_gain = row_ref[1, at, :]
            pre = pre_ref[at, :]
            if step >= 1:
                taken = dot_nn(mix_ref[at, :], known_ref[...])
                pre = pre - taken
            density, share = density_and_share(pre)
            act = (pre * share).astype(bf16)
            state_low = state.astype(bf16)
            res = dot_nt(act, state_low)
            slope = share + pre * density
            second_save[0, step] = state_low
            interleave(others, 1)
            res = res + state_b
            weighted = own_gain * res
            parts = dot_nn(jnp.concatenate([res, weighted], axis=0), state_low)
            base_act = dot_nn(own_base, state_low)
            interleave(others, 1)
            square = jnp.sum(res * res, axis=-1, keepdims=True)
            sum_gain = jnp.sum(weighted, axis=-1, keepdims=True)
            sum_base = jnp.sum(own_base * res, axis=-1, keepdims=True)
            sum_square = jnp.sum(weighted * res, axis=-1, keepdims=True)
            inverse = lax.rsqrt(square * (1.0 / HEAD_DIM) + inner_epsilon)
            scaled_mean = row_ref[2, at, :] + inverse * sum_gain * (1.0 / HEAD_DIM)
            along = inverse * (sum_base + inverse * sum_square) * (1.0 / HEAD_DIM)
            square_inverse = inverse * inverse
            along_half = along - square_inverse * level_ref[at, :]
            along_wide = jnp.concatenate([along_half, along_half], axis=1)
            normal = res * inverse
            back_res = inverse * (
                own_base + own_gain * normal - scaled_mean - normal * along_half[:, :HEAD_DIM]
            )
            back_low = back_res.astype(bf16)
            with_base = inverse * slope * base_act
            with_part = square_inverse * slope
            with_res = with_part * along_wide
            grad_full = with_base + (with_part * parts[MINI:] - with_res * parts[:MINI])
            grad = grad_full.astype(bf16)
            known_ref[at, :] = grad
            state = state - dot_tn(back_low, act)
            state_b = state_b - jnp.sum(back_res, axis=0, keepdims=True)
            slope_ref[at, :] = slope
            back_act = inverse * base_act + square_inverse * (
                parts[MINI:] - along_wide * parts[:MINI]
            )
            curve_ref[at, :] = back_act * density * (2.0 - pre * pre)
            act_ref[at, :] = act
            grad_pre_ref[at, :] = grad
            back_res_ref[at, :] = back_low
            norms_ref[at, :HEAD_DIM] = normal
            norms_ref[at, HEAD_DIM:] = jnp.broadcast_to(inverse, (MINI, HEAD_DIM))
        for _ in others:
            pass
        grad_all = known_ref[...]
        first_w[...] = first_w[...] - dot_tn(key, grad_all)
        first_b[...] = start_first_b - jnp.sum(grad_all.astype(f32), axis=0, keepdims=True)
        second_w[...] = state
        second_b[...] = state_b
        done_act[...] = act_ref[...]
        done_grad[...] = grad_all
        done_back[...] = back_res_ref[...]
        done_first[...] = first_low
        done_second[...] = start_low
        done_first_b[...] = start_first_b
        done_second_b[...] = start_b

    @pl.when(turn == 0)
    def _():
        for _ in ahead(0):
            pass
        chain(ahead(1))

    @pl.when((turn > 0) & (turn < devices))
    def _():
        chain(alternate(finish(), ahead(jnp.minimum(turn + 1, devices - 1))))

    @pl.when(turn == devices)
    def _():
        for _ in finish():
            pass


def backward_kernel(
    inner_part,
    feature_part,
    sequence_ref,
    packed_ref,
    rows_ref,
    head_grad_ref,
    next_act,
    next_grad,
    next_hidden,
    next_out_slope,
    next_norms,
    next_out_norms,
    next_first,
    next_second,
    now_act,
    now_slope,
    now_curve,
    now_second,
    last_grad,
    last_norms,
    last_first,
    gain_ref,
    bias_ref,
    back_ref,
    first_w,
    first_b,
    second_w,
    second_b,
    gain_sum,
    bias_sum,
    known_ref,
    vector_ref,
    grad_sum,
    to_wide,
    to_rows,
    to_spread,
    to_low,
    to_mix,
    to_state,
    to_sums,
    wide_ref,
    row_ref,
    spread_ref,
    low_ref,
    mix_ref,
    state_ref,
    sums_ref,
    end_known,
    end_rows,
    end_first,
):
    devices, chunk, _ = packed_ref.shape
    steps = chunk // MINI
    turn = pl.program_id(0)
    shard = back_ref.shape[1] - chunk
    gain = gain_ref[...]
    bias = bias_ref[...]
    square_gain = gain * gain
    rows, cols = token_grid(chunk)

    @pl.when(turn == 0)
    def _():
        for ref in (
            first_w,
            first_b,
            second_w,
            second_b,
            gain_sum,
            bias_sum,
            known_ref,
            grad_sum,
            end_known,
            end_rows,
            end_first,
        ):
            ref[...] = jnp.zeros_like(ref)

    def unpack(place):
        packed = packed_ref[place]
        query, key = two_parts(packed)
        miss = key.astype(f32) - packed[:, 2 * HEAD_DIM : 3 * HEAD_DIM].astype(f32) + bias
        return query, key, miss, rate_logit(packed)

    def rate_of(logit):
        return jax.nn.sigmoid(logit[:, :HEAD_DIM]) * rate_scale

    def prepare():
        query, key, miss, logit = unpack(jnp.maximum(devices - 1 - turn, 0))
        halves = []
        for index in range(head_grad_ref.shape[1]):
            values = head_grad_ref[0, index].astype(f32)
            halves += [values[:, :HEAD_DIM], values[:, HEAD_DIM:]]
        head_grad = jnp.concatenate(halves, axis=0)
        head_normal = next_out_norms[:, HEAD_DIM : 2 * HEAD_DIM]
        head_mean = mean_of(head_grad)
        head_tilt = mean_of(head_grad * head_normal)
        yield
        rate = rate_of(logit)
        normal = next_norms[:, :HEAD_DIM]
        rate_gain = rate * square_gain
        gain_normal = rate_gain * normal
        scaled = rate * (miss * gain) + gain_normal
        scaled_mean = mean_of(scaled)
        along = mean_of(scaled * normal)
        yield
        out_grad = next_out_norms[:, 3 * HEAD_DIM :] * (
            head_grad - head_mean - head_normal * head_tilt
        )
        out_normal = next_out_norms[:, :HEAD_DIM]
        normal_grad = out_grad * gain
        out_mean = mean_of(normal_grad)
        out_tilt = mean_of(normal_grad * out_normal)
        yield
        inverse = next_norms[:, HEAD_DIM:]
        back_res = (inverse * (scaled - scaled_mean - normal * along)).astype(bf16)
        gain_along = mean_of(gain_normal)
        gain_square = mean_of(gain_normal * normal)
        to_low[0] = back_res
        to_low[1] = key
        to_sums[2:3, :HEAD_DIM] = jnp.sum(out_grad * out_normal, axis=0, keepdims=True)
        to_sums[3:4, :HEAD_DIM] = jnp.sum(out_grad, axis=0, keepdims=True)
        yield
        res_grad = next_out_norms[:, 2 * HEAD_DIM : 3 * HEAD_DIM] * (
            normal_grad - out_mean - out_normal * out_tilt
        )
        to_sums[1:2, :HEAD_DIM] = jnp.sum(res_grad, axis=0, keepdims=True)
        res_grad_low = res_grad.astype(bf16)
        hidden_base = dot_nn(res_grad_low, next_second[0, 0])
        mix = dot_nt(res_grad_low, back_res)
        yield
        mix_t = dot_nt(back_res, res_grad_low)
        causal = cols <= rows
        later = rows <= cols
        second_grad = jnp.where(causal, -mix, 0.0)
        hidden_more = dot_nn(second_grad, next_act[...])
        yield
        second_grad_t = jnp.where(later, -mix_t, 0.0)
        to_rows[1] = normal
        to_rows[2] = rate_gain
        to_rows[3] = rate_gain - along
        to_rows[4] = gain_normal + scaled
        to_rows[5] = -(along + rate * row_mean(square_gain))
        yield
        for index, value in enumerate(
            (-(gain_along + scaled_mean), -(3.0 * along + gain_square), inverse * inverse)
        ):
            to_spread[index] = jnp.concatenate([value, value], axis=1)
        mix = dot_nt(next_act[...], next_hidden[...])
        yield
        query_pre_grad = (hidden_base + hidden_more) * next_out_slope[...]
        query_pre_low = query_pre_grad.astype(bf16)
        to_sums[0:1] = jnp.sum(query_pre_grad, axis=0, keepdims=True)
        first = dot_nt(query_pre_low, next_grad[...])
        yield
        second_mix_t = jnp.where(later, mix + 1.0, 0.0)
        to_rows[0] = -dot_nn(second_mix_t, res_grad_low)
        first_t = dot_nt(next_grad[...], query_pre_low)
        yield
        first_grad = jnp.where(causal, -first, 0.0)
        mix = dot_nt(key, query)
        query_grad = dot_nt(query_pre_low, next_first[0])
        query_more = dot_nn(first_grad, key)
        yield
        first_grad_t = jnp.where(later, -first_t, 0.0)
        to_rows[6] = dot_nn(first_grad_t, query)
        first_mix_t = jnp.where(later, mix + 1.0, 0.0).astype(bf16)
        yield
        to_rows[7] = out_grad + query_grad + query_more
        to_wide[1] = dot_nn(second_grad_t, next_hidden[...])
        yield
        to_wide[0] = -dot_nn(first_mix_t, query_pre_low)
        mix = dot_nt(key, key)
        yield
        to_mix[...] = jnp.where(cols // MINI > rows // MINI, mix + 1.0, 0.0).astype(bf16)
        to_state[0] = dot_tn(query, query_pre_low)
        yield
        to_state[1] = dot_tn(res_grad_low, next_hidden[...])

    def conclude():
        place = jnp.minimum(devices + 1 - turn, devices - 1)
        _, key, miss, logit = unpack(place)
        normal = last_norms[:, :HEAD_DIM]
        upon = end_rows[0]
        upon_mean = mean_of(upon)
        upon_tilt = mean_of(upon * normal)
        yield
        pre_grad = end_known[...]
        mix = dot_nt(last_grad[...], pre_grad)
        mix_t = dot_nt(pre_grad, last_grad[...])
        yield
        rate = rate_of(logit)
        scaled_grad = last_norms[:, HEAD_DIM:] * (upon - upon_mean - normal * upon_tilt)
        error_grad = scaled_grad * (rate * gain)
        rate_grad = mean_of(scaled_grad * (miss * gain + square_gain * normal))
        yield
        error = miss + normal * gain
        gain_sum[...] += jnp.sum(
            scaled_grad * rate * error + error_grad * normal, axis=0, keepdims=True
        )
        bias_sum[...] += jnp.sum(error_grad, axis=0, keepdims=True)
        from_grad = dot_nt(last_grad[...], end_first[...])
        yield
        far = rows // MINI < cols // MINI
        near = rows // MINI > cols // MINI
        cross = jnp.where(far, mix, 0.0) + jnp.where(near, mix_t, 0.0)
        from_pre = dot_nt(pre_grad, last_first[0])
        from_cross = dot_nn(cross, key)
        yield
        key_grad = end_rows[1] + error_grad - from_grad + from_pre - from_cross
        back_rate = rate_grad * float(HEAD_DIM) * rate * (1.0 - rate * (1.0 / rate_scale))
        lane = lax.broadcasted_iota(jnp.int32, (chunk, HEAD_DIM), 1)
        tail = jnp.where(lane == 0, back_rate, 0.0)
        packed = jnp.concatenate([end_rows[2], key_grad, -error_grad, tail], axis=1).astype(bf16)
        back_ref[place, :chunk] = packed
        yield
        count = 6
        size = grad_sum.shape[0] // count
        for index in range(count):
            at = slice(index * size, (index + 1) * size)
            grad_sum[at] = grad_sum[at] + dot_tn(rows_ref[0, 0, :, at], packed)
            yield

    def chain(following, previous):
        wide_ref[...] = to_wide[...]
        row_ref[...] = to_rows[...]
        spread_ref[...] = to_spread[...]
        low_ref[...] = to_low[...]
        mix_ref[...] = to_mix[...]
        state_ref[...] = to_state[...]
        sums_ref[...] = to_sums[...]
        first_next = first_w[...]
        first_next_low = first_next.astype(bf16)
        first_next_b = first_b[...]
        state = second_w[...]
        state_b = second_b[...]

        def base_of(step):
            at = slice(step * MINI, (step + 1) * MINI)
            return wide_ref[0, at, :] - dot_nn(low_ref[1, at, :], first_next_low) - first_next_b

        base = base_of(steps - 1)
        for step in reversed(range(steps)):
            at = slice(step * MINI, (step + 1) * MINI)
            grad = base
            if step + 1 < steps:
                grad = grad - taken
            state_low = state.astype(bf16)
            own_act = now_act[at, :]
            own_back = low_ref[0, at, :]
            back_base = row_ref[0, at, :] - dot_nt(own_act, state_low) - state_b
            own_low = now_second[0, step]
            slope = now_slope[at, :]
            back_act_grad = (grad * slope).astype(bf16)
            upon = dot_nt(back_act_grad, own_low)
            upon = back_base + upon
            own_normal, own_gain, own_grad, own_beta, own_alpha = (
                row_ref[index, at, :] for index in range(1, 6)
            )
            cross, cross_beta, square_inverse = (spread_ref[index, at, :] for index in range(3))
            main = dot_nn(upon * own_grad, own_low)
            act_base = wide_ref[1, at, :] - dot_nn(own_back, state_low)
            sides = dot_nn(jnp.concatenate([own_normal, own_gain, own_beta], axis=0), own_low)
            interleave(following, 2)
            interleave(previous, 1)
            alpha = row_mean(upon)
            beta = row_mean(upon * own_normal)
            gamma = row_mean(upon * own_gain)
            kappa = row_mean(upon * own_beta)
            level = alpha * own_alpha + beta * cross[:, :HEAD_DIM] + gamma
            tilt = alpha * cross + beta * cross_beta + kappa
            key_res_grad = square_inverse[:, :HEAD_DIM] * (
                upon * own_grad
                - alpha * own_gain
                - beta * own_beta
                - level
                - own_normal * tilt[:, :HEAD_DIM]
            )
            key_res_low = key_res_grad.astype(bf16)
            from_sides = (
                alpha * sides[MINI : 2 * MINI]
                + beta * sides[2 * MINI :]
                + jnp.concatenate([tilt, tilt], axis=1) * sides[:MINI]
            )
            factor = jnp.concatenate([square_inverse, square_inverse], axis=1) * slope
            known = act_base * slope + grad * now_curve[at, :] - factor * from_sides
            pre_grad = known + factor * main
            known_ref[at, :] = pre_grad.astype(bf16)
            if step > 0:
                taken = dot_nn(mix_ref[(step - 1) * MINI : step * MINI, :], known_ref[...])
                base = base_of(step - 1)
            state = state + dot_tn(
                jnp.concatenate([key_res_low, own_back], axis=0),
                jnp.concatenate([own_act, back_act_grad], axis=0),
            )
            state_b = state_b + jnp.sum(key_res_grad, axis=0, keepdims=True)
            row_ref[0, at, :] = upon
        for generator in (following, previous):
            for _ in generator:
                pass
        pre_grad_all = known_ref[...]
        first_w[...] = first_next + dot_tn(low_ref[1], pre_grad_all) + state_ref[0]
        first_b[...] = (
            first_next_b
            + jnp.sum(pre_grad_all.astype(f32), axis=0, keepdims=True)
            + sums_ref[0:1]
        )
        second_w[...] = state + state_ref[1]
        second_b[...] = state_b + sums_ref[1:2, :HEAD_DIM]
        gain_sum[...] += sums_ref[2:3, :HEAD_DIM]
        bias_sum[...] += sums_ref[3:4, :HEAD_DIM]
        end_known[...] = pre_grad_all
        end_rows[0] = row_ref[0]
        end_rows[1] = row_ref[6]
        end_rows[2] = row_ref[7]
        end_first[...] = first_next_low

    @pl.when(turn == 0)
    def _():
        for _ in prepare():
            pass

    @pl.when((turn > 0) & (turn <= devices))
    def _():
        chain(prepare(), conclude())

    @pl.when(turn == devices + 1)
    def _():
        for _ in conclude():
            pass
        vector_ref[...] = jnp.zeros_like(vector_ref)
        for index in range(devices):
            first = slice(index * inner_part, (index + 1) * inner_part)
            small = slice(index * feature_part, (index + 1) * feature_part)
            vector_ref[index : index + 1, :inner_part] = first_b[:, first]
            for number, source in enumerate((second_b, gain_sum, bias_sum)):
                start = inner_part + number * feature_part
                vector_ref[index : index + 1, start : start + feature_part] = source[:, small]
        columns = jnp.transpose(vector_ref[...]).astype(bf16)
        lanes = slice(MATRIX_LANE, MATRIX_LANE + inner_part)
        for index in range(devices):
            first = slice(index * inner_part, (index + 1) * inner_part)
            back_ref[index, :HEAD_DIM, lanes] = first_w[:, first].astype(bf16)
            back_ref[index, HEAD_DIM : 2 * HEAD_DIM, lanes] = second_w[:, first].astype(bf16)
            back_ref[index, :chunk, VECTOR_LANE : VECTOR_LANE + 1] = columns[:, index : index + 1]
            back_ref[index, chunk:] = grad_sum[index * shard : (index + 1) * shard].astype(bf16)


def whole_block(shape):
    return pl.BlockSpec(shape, lambda index, *_: (0,) * len(shape))


STATE_SHAPES = ((HEAD_DIM, INNER), (1, INNER), (HEAD_DIM, INNER), (1, HEAD_DIM))


def chain_forward(packed, inner_part, feature_part):
    blocks, chunk, _ = packed.shape
    length = blocks * chunk
    steps = chunk // MINI
    row = (1, HEAD_DIM)

    def forth(shape):
        return pl.BlockSpec(
            shape, lambda turn: (jnp.minimum(turn, blocks - 1),) + (0,) * (len(shape) - 1)
        )

    def behind(shape):
        return pl.BlockSpec(
            shape, lambda turn: (jnp.maximum(turn - 1, 0),) + (0,) * (len(shape) - 1)
        )

    def of_length(width, dtype):
        return jax.ShapeDtypeStruct((length, width), dtype)

    wide = (chunk, INNER)
    return pl.pallas_call(
        functools.partial(forward_kernel, inner_part, feature_part),
        grid=(blocks + 1,),
        in_specs=[whole_block(packed.shape)],
        out_specs=[behind((1, HEAD_DIM, chunk))]
        + [forth(wide)] * 4
        + [
            forth((chunk, 2 * HEAD_DIM)),
            forth((1, HEAD_DIM, INNER)),
            forth((1, steps, HEAD_DIM, INNER)),
        ]
        + [behind(wide)] * 3
        + [whole_block(row)] * 2,
        out_shape=[jax.ShapeDtypeStruct((blocks, HEAD_DIM, chunk), bf16)]
        + [of_length(INNER, dtype) for dtype in (bf16, bf16, f32, f32)]
        + [
            of_length(2 * HEAD_DIM, f32),
            jax.ShapeDtypeStruct((blocks, HEAD_DIM, INNER), bf16),
            jax.ShapeDtypeStruct((blocks, steps, HEAD_DIM, INNER), bf16),
        ]
        + [of_length(INNER, dtype) for dtype in (bf16, f32, f32)]
        + [jax.ShapeDtypeStruct(row, f32)] * 2,
        scratch_shapes=[pltpu.VMEM(shape, f32) for shape in STATE_SHAPES]
        + [
            pltpu.VMEM(wide, bf16),
            pltpu.VMEM((chunk, HEAD_DIM), bf16),
            pltpu.VMEM(wide, f32),
        ]
        + [
            pltpu.VMEM((3, chunk, HEAD_DIM), f32),
            pltpu.VMEM((chunk, 2 * HEAD_DIM), f32),
            pltpu.VMEM((chunk, chunk), bf16),
        ]
        * 2
        + [
            pltpu.VMEM(wide, bf16),
            pltpu.VMEM(wide, bf16),
            pltpu.VMEM((chunk, HEAD_DIM), bf16),
            pltpu.VMEM((HEAD_DIM, INNER), bf16),
            pltpu.VMEM((HEAD_DIM, INNER), bf16),
            pltpu.VMEM((1, INNER), f32),
            pltpu.VMEM(row, f32),
        ],
        compiler_params=pltpu.CompilerParams(
            dimension_semantics=("arbitrary",), vmem_limit_bytes=VMEM_BYTES
        ),
        cost_estimate=pl.CostEstimate(
            flops=CHAIN_FLOPS, transcendentals=0, bytes_accessed=16 * length * INNER
        ),
        name="chain_forward",
    )(packed)


def chain_backward(packed, rows, sequence, head_grad, saved, inner_part, feature_part):
    act, grad_pre, slope, curve, norms, first_save, second_save = saved[:7]
    hidden, out_slope, out_norms, gain, bias = saved[7:]
    blocks, chunk, _ = packed.shape
    width = rows.shape[-1]
    shard = width // blocks
    steps = chunk // MINI
    row = (1, HEAD_DIM)
    wide = (chunk, INNER)
    narrow = (chunk, 2 * HEAD_DIM)

    def at(shape, delay):
        def index_map(turn, _):
            place = jnp.clip(blocks - 1 - turn + delay, 0, blocks - 1)
            return (place,) + (0,) * (len(shape) - 1)

        return pl.BlockSpec(shape, index_map)

    def rows_map(turn, chosen):
        place = jnp.clip(blocks + 1 - turn, 0, blocks - 1)
        return (place // SEQS, (place + chosen[0]) % SEQS, 0, 0)

    state = (HEAD_DIM, INNER)
    carried = [
        pltpu.VMEM((2,) + wide, f32),
        pltpu.VMEM((8, chunk, HEAD_DIM), f32),
        pltpu.VMEM((3,) + narrow, f32),
        pltpu.VMEM((2, chunk, HEAD_DIM), bf16),
        pltpu.VMEM((chunk, chunk), bf16),
        pltpu.VMEM((2,) + state, f32),
        pltpu.VMEM((8, INNER), f32),
    ]
    return pl.pallas_call(
        functools.partial(backward_kernel, inner_part, feature_part),
        grid_spec=pltpu.PrefetchScalarGridSpec(
            num_scalar_prefetch=1,
            grid=(blocks + 2,),
            in_specs=[
                whole_block(packed.shape),
                pl.BlockSpec((1, 1, chunk, width), rows_map),
                at((1,) + head_grad.shape[1:], 0),
                at(wide, 0),
                at(wide, 0),
                at(wide, 0),
                at(wide, 0),
                at(narrow, 0),
                at(wide, 0),
                at((1,) + state, 0),
                at((1, 1) + state, 0),
                at(wide, 1),
                at(wide, 1),
                at(wide, 1),
                at((1, steps) + state, 1),
                at(wide, 2),
                at(narrow, 2),
                at((1,) + state, 2),
                whole_block(row),
                whole_block(row),
            ],
            out_specs=whole_block((blocks, chunk + shard, LANES)),
            scratch_shapes=[pltpu.VMEM(shape, f32) for shape in STATE_SHAPES + (row, row)]
            + [
                pltpu.VMEM(wide, bf16),
                pltpu.VMEM((chunk, 128), f32),
                pltpu.VMEM((width, LANES), f32),
            ]
            + carried
            + carried
            + [
                pltpu.VMEM(wide, bf16),
                pltpu.VMEM((3, chunk, HEAD_DIM), f32),
                pltpu.VMEM(state, bf16),
            ],
        ),
        out_shape=jax.ShapeDtypeStruct((blocks, chunk + shard, LANES), bf16),
        compiler_params=pltpu.CompilerParams(
            dimension_semantics=("arbitrary",), vmem_limit_bytes=VMEM_BYTES
        ),
        cost_estimate=pl.CostEstimate(
            flops=CHAIN_FLOPS, transcendentals=0, bytes_accessed=16 * blocks * chunk * INNER
        ),
        name="chain_backward",
    )(
        sequence,
        packed,
        rows,
        head_grad,
        act,
        grad_pre,
        hidden,
        out_slope,
        norms,
        out_norms,
        first_save,
        second_save,
        act,
        slope,
        curve,
        second_save,
        grad_pre,
        norms,
        first_save,
        gain,
        bias,
    )


def layer_norm_parts(values):
    centred = values - row_mean(values)
    inverse = lax.rsqrt(row_mean(centred * centred) + epsilon)
    return centred * inverse, inverse


def layer_norm_back(normal, inverse, scaling, grad):
    scaled = grad * scaling
    return inverse * (scaled - row_mean(scaled) - normal * row_mean(scaled * normal))


def start_kernel(
    head_count,
    rows_ref,
    weights_ref,
    gain_ref,
    inner_ref,
    packed_ref,
    normed_ref,
    matrix_ref,
):
    tensor_count = rows_ref.shape[0]
    seq_count, chunk, _ = normed_ref.shape
    rows = chunk // tensor_count
    matrix_ref[...] = jnp.zeros_like(matrix_ref)
    for head in range(head_count):
        first = head * 3 * HEAD_DIM
        rate = head_count * 3 * HEAD_DIM + head
        column = weights_ref[:, rate : rate + 1]
        matrix_ref[head, :, : 3 * HEAD_DIM] = weights_ref[:, first : first + 3 * HEAD_DIM]
        matrix_ref[head, :, RATE_LANE : RATE_LANE + 1] = column
        matrix_ref[head, :, RATE_LANE + 1 : RATE_LANE + 2] = column
    lane = lax.broadcasted_iota(jnp.int32, (chunk, LANES), 1)
    for sequence in range(seq_count):
        part = slice(sequence * rows, (sequence + 1) * rows)
        values = jnp.concatenate([rows_ref[index, part] for index in range(tensor_count)], axis=0)
        normal, _ = layer_norm_parts(values.astype(f32))
        normed = (normal * gain_ref[...]).astype(bf16)
        normed_ref[sequence] = normed
        for head in range(head_count):
            projected = dot_nn(normed, matrix_ref[head])
            rest = projected - projected.astype(bf16).astype(f32)
            projected = jnp.where(lane == RATE_LANE + 1, rest, projected).astype(bf16)
            packed_ref[head * seq_count + sequence] = jnp.where(
                lane >= VECTOR_LANE, inner_ref[head], projected
            )
    for index in range(head_count * seq_count, packed_ref.shape[0]):
        packed_ref[index] = jnp.zeros((chunk, LANES), bf16)


def feed_forward_kernel(
    heads_ref,
    rows_ref,
    weights_ref,
    out_ref,
    gain_ref,
    terms_ref,
    mixed_ref,
    normed_ref,
    back_ref,
    swiglu_ref,
):
    tensor_count, head_count, seq_count, _, chunk = heads_ref.shape
    ff_local = swiglu_ref.shape[1]
    rows = chunk // tensor_count
    total = seq_count * chunk
    for sequence in range(seq_count):
        part = slice(sequence * rows, (sequence + 1) * rows)
        values = jnp.concatenate([rows_ref[index, part] for index in range(tensor_count)], axis=0)
        mixed = values.astype(f32)
        for index in range(tensor_count):
            heads = [heads_ref[index, head, sequence] for head in range(head_count)]
            heads = jnp.transpose(jnp.concatenate(heads, axis=0).astype(f32))
            mixed = mixed + dot_nt(heads, out_ref[index])
        for index in range(tensor_count):
            mixed_ref[index, sequence] = mixed[index * rows : (index + 1) * rows]
        normal, _ = layer_norm_parts(mixed)
        at = slice(sequence * chunk, (sequence + 1) * chunk)
        normed_ref[at] = (normal * gain_ref[...]).astype(bf16)
    normed = normed_ref[...]
    cot = cotangent_rows(rows_ref, seq_count, rows)
    for first in range(0, ff_local, 256):
        at = slice(first, first + 256)
        beyond = slice(ff_local + first, ff_local + first + 256)
        gate = dot_nn(normed, weights_ref[:, at])
        up = dot_nn(normed, weights_ref[:, beyond])
        back = dot_nn(cot, weights_ref[:, 2 * ff_local + first : 2 * ff_local + first + 256])
        share = jax.nn.sigmoid(gate)
        silu = gate * share
        swiglu_ref[:, at] = (silu * up).astype(bf16)
        back_ref[:, at] = (back * up * (share * (1.0 + gate * (1.0 - share)))).astype(bf16)
        back_ref[:, beyond] = (back * silu).astype(bf16)
    ffn_term = dot_nt(back_ref[...], weights_ref[:, : 2 * ff_local]).astype(bf16)
    down_term = dot_nt(swiglu_ref[...], weights_ref[:, 2 * ff_local : 3 * ff_local]).astype(bf16)
    for sequence in range(seq_count):
        for index in range(tensor_count):
            first = sequence * chunk + index * rows
            terms_ref[index, sequence] = ffn_term[first : first + rows]
            terms_ref[index, seq_count + sequence] = down_term[first : first + rows]


def cotangent_rows(rows_ref, seq_count, rows):
    count = rows_ref.shape[0]
    parts = [
        rows_ref[index, (seq_count + sequence) * rows : (seq_count + sequence + 1) * rows]
        for sequence in range(seq_count)
        for index in range(count)
    ]
    return jnp.concatenate(parts, axis=0)


def feed_forward_grad_kernel(normed_ref, back_ref, swiglu_ref, rows_ref, grads_ref):
    rows = normed_ref.shape[0] // (SEQS * rows_ref.shape[0])
    normed = jnp.transpose(normed_ref[...].astype(f32)).astype(bf16)
    cot = cotangent_rows(rows_ref, SEQS, rows)
    cot = jnp.transpose(cot.astype(f32)).astype(bf16)
    width = back_ref.shape[1]
    for first in range(0, width, 256):
        at = slice(first, first + 256)
        grads_ref[:, at] = dot_nn(normed, back_ref[:, at]).astype(bf16)
    for first in range(0, swiglu_ref.shape[1], 256):
        at = slice(width + first, width + first + 256)
        grads_ref[:, at] = dot_nn(cot, swiglu_ref[:, first : first + 256]).astype(bf16)


def head_back(grads_ref, out_ref, back_ref):
    tensor_count = out_ref.shape[0]
    seq_count, rows, _ = grads_ref.shape
    head_count = out_ref.shape[2] // HEAD_DIM
    for index in range(tensor_count):
        for sequence in range(seq_count):
            back = dot_nn(grads_ref[sequence], out_ref[index]).astype(bf16)
            for head in range(head_count):
                place = (head * seq_count + sequence) * tensor_count + index
                values = back[:, head * HEAD_DIM : (head + 1) * HEAD_DIM]
                back_ref[place, :, :HEAD_DIM] = values[: rows // 2]
                back_ref[place, :, HEAD_DIM:] = values[rows // 2 :]
    for place in range(head_count * seq_count * tensor_count, back_ref.shape[0]):
        back_ref[place] = jnp.zeros((rows // 2, 2 * HEAD_DIM), bf16)


def out_grad_kernel(grads_ref, heads_ref, out_grad_ref):
    head_count, seq_count, _, _ = heads_ref.shape
    devices, shard, _ = out_grad_ref.shape
    total = None
    for sequence in range(seq_count):
        heads = [heads_ref[head, sequence] for head in range(head_count)]
        grads = jnp.transpose(grads_ref[sequence].astype(f32))
        term = dot_nt(grads, jnp.concatenate(heads, axis=0))
        total = term if total is None else total + term
    for index in range(devices):
        out_grad_ref[index] = total[index * shard : (index + 1) * shard].astype(bf16)


def matrix_output_kernel(sums_ref, out_ref, weights_ref, gate_up_ref, down_ref, out_grad_ref, gain_ref):
    ff_local = down_ref.shape[1]
    sums = sums_ref[...].astype(f32)
    for index in range(2):
        gate_up_ref[:, index, :] = sums[:, index * ff_local : (index + 1) * ff_local]
    down_ref[...] = sums[:, 2 * ff_local :]
    total = out_ref[0].astype(f32)
    for index in range(1, out_ref.shape[0]):
        total = total + out_ref[index].astype(f32)
    out_grad_ref[...] = jnp.transpose(total)
    products = sums[:, : 2 * ff_local] * weights_ref[:, : 2 * ff_local].astype(f32)
    gain = jnp.sum(products, axis=-1, keepdims=True)
    gain_ref[...] = jnp.broadcast_to(gain, gain_ref.shape)


def feed_forward_back_kernel(
    rank_ref,
    terms_ref,
    mixed_ref,
    cot_ref,
    gain_ref,
    out_ref,
    back_ref,
    low_ref,
    result_ref,
    heads_ref,
):
    seq_count = mixed_ref.shape[1]
    for sequence in range(seq_count):
        grad = terms_ref[0, sequence].astype(f32)
        down = terms_ref[0, seq_count + sequence].astype(f32)
        for index in range(1, terms_ref.shape[0]):
            grad = grad + terms_ref[index, sequence].astype(f32)
            down = down + terms_ref[index, seq_count + sequence].astype(f32)
        mixed = mixed_ref[0, sequence]
        normal, inverse = layer_norm_parts(mixed)
        back = cot_ref[sequence].astype(f32)
        back = back + layer_norm_back(normal, inverse, gain_ref[...], grad)
        back_ref[sequence] = back
        low_ref[sequence] = back.astype(bf16)
        result_ref[sequence] = (mixed + down).astype(bf16)
    head_back(low_ref, out_ref, heads_ref)


def input_grad_kernel(terms_ref, tokens_ref, back_ref, gain_ref, grad_ref, gains_ref):
    seq_count, rows, _ = tokens_ref.shape
    for sequence in range(seq_count):
        at = slice(sequence * rows, (sequence + 1) * rows)
        total = terms_ref[0, at].astype(f32)
        for index in range(1, terms_ref.shape[0]):
            total = total + terms_ref[index, at].astype(f32)
        normal, inverse = layer_norm_parts(tokens_ref[sequence].astype(f32))
        total = layer_norm_back(normal, inverse, gain_ref[...], total)
        grad_ref[:, sequence, :] = back_ref[sequence] + total
    total = terms_ref[0, seq_count * rows :].astype(f32)
    for index in range(1, terms_ref.shape[0]):
        total = total + terms_ref[index, seq_count * rows :].astype(f32)
    width = gains_ref.shape[1]
    gains_ref[...] = (total[:2] + total[2:4])[:, :width]


def tail_kernel(
    received_ref,
    matrix_ref,
    own_ref,
    gain_two_ref,
    gains_ref,
    terms_ref,
    qkv_ref,
    small_ref,
    state_ref,
):
    head_count = matrix_ref.shape[0]
    shard = own_ref.shape[1]
    tensor_count, term_rows, width = terms_ref.shape
    chunk = received_ref.shape[1] - shard
    seq_count = (term_rows - 16) * tensor_count // chunk
    rows = chunk // tensor_count
    lane = lax.broadcasted_iota(jnp.int32, (chunk, LANES), 1)
    for sequence in range(seq_count):
        total = None
        for head in range(head_count):
            values = received_ref[head * seq_count + sequence, :chunk]
            values = jnp.where(lane <= RATE_LANE, values, jnp.zeros_like(values))
            term = dot_nt(values, matrix_ref[head])
            total = term if total is None else total + term
        for index in range(tensor_count):
            part = total[index * rows : (index + 1) * rows]
            terms_ref[index, sequence * rows : (sequence + 1) * rows] = part.astype(bf16)
    lane = lax.broadcasted_iota(jnp.int32, (shard, LANES), 1)
    column = lax.broadcasted_iota(jnp.int32, (shard, 128), 1)
    gain = None
    small = jnp.where(column == 1, gain_two_ref[...], 0.0)
    for head in range(head_count):
        grads = received_ref[head * seq_count, chunk:].astype(f32)
        state = received_ref[head * seq_count, :chunk, RATE_LANE:].astype(f32)
        for sequence in range(1, seq_count):
            grads = grads + received_ref[head * seq_count + sequence, chunk:].astype(f32)
            state = state + received_ref[
                head * seq_count + sequence, :chunk, RATE_LANE:
            ].astype(f32)
        state_ref[head] = state
        for index in range(3):
            at = slice(index * HEAD_DIM, (index + 1) * HEAD_DIM)
            qkv_ref[index, :, head * HEAD_DIM : (head + 1) * HEAD_DIM] = grads[:, at]
        products = jnp.where(lane <= RATE_LANE, grads * own_ref[head].astype(f32), 0.0)
        products = jnp.sum(products, axis=-1, keepdims=True)
        gain = products if gain is None else gain + products
        small = jnp.where(column == 2 + head, grads[:, RATE_LANE : RATE_LANE + 1], small)
    small = jnp.transpose(jnp.where(column == 0, gain, small))[: small_ref.shape[0]]
    small_ref[...] = small
    gain = small[:2] / gains_ref[...]
    high = gain.astype(bf16)
    low = (gain - high.astype(f32)).astype(bf16)
    block = jnp.concatenate([high.astype(f32), low.astype(f32), jnp.zeros((12, shard), f32)], axis=0)
    for index in range(tensor_count):
        first = seq_count * rows
        terms_ref[index, first:, :] = jnp.zeros((16, width), bf16)
        terms_ref[index, first:, :shard] = block.astype(bf16)


def whole_call(kernel, name, operands, results, vmem_bytes=GLUE_BYTES):
    def spec(shape):
        return pl.BlockSpec(shape, lambda: (0,) * len(shape))

    return pl.pallas_call(
        kernel,
        in_specs=[spec(operand.shape) for operand in operands],
        out_specs=[spec(result.shape) for result in results],
        out_shape=results,
        compiler_params=pltpu.CompilerParams(vmem_limit_bytes=vmem_bytes),
        name=name,
    )(*operands)


def dots(subscripts, left, right):
    return jnp.einsum(subscripts, left, right, preferred_element_type=f32)


def exchange(values, axis):
    return lax.all_to_all(values, axis, 0, 0, tiled=False)


def share_out(values, axis):
    count = lax.axis_size(axis)
    return exchange(jnp.broadcast_to(values[None], (count,) + values.shape), axis)


def ordered(*values):
    return lax.optimization_barrier(values)


def inner_block(matrix_one, matrix_two, vectors, rows):
    width = matrix_one.shape[-1]
    matrices = jnp.concatenate([matrix_one, matrix_two], axis=-2)
    column = jnp.concatenate(vectors, axis=-1)[..., None]
    lead = [(0, 0)] * (column.ndim - 2)
    column = jnp.pad(
        column,
        lead + [(0, rows - column.shape[-2]), (VECTOR_LANE, LANES - VECTOR_LANE - 1)],
    )
    matrices = jnp.pad(
        matrices,
        lead + [(0, rows - matrices.shape[-2]), (MATRIX_LANE, LANES - MATRIX_LANE - width)],
    )
    return column + matrices


def local(
    tokens,
    gain_attn,
    gain_ffn,
    w_qkv,
    w_rate,
    w_out,
    w_gate_up,
    w_down,
    w_one,
    b_one,
    w_two,
    b_two,
    norm_gain_inner,
    norm_bias_inner,
    cotangent,
):
    device_count = lax.axis_size(DP)
    tensor_count = lax.axis_size("tensor")
    local_rows, seq_count, width = tokens.shape
    row_count = local_rows * seq_count
    chunk = local_rows * tensor_count
    head_count = w_rate.shape[1]
    local_width = head_count * HEAD_DIM
    shard = w_qkv.shape[0]
    part = gain_attn.shape[0]
    ff_local = w_down.shape[0]
    chain_count = seq_count * head_count
    inner_part = w_one.shape[2]
    feature_part = b_two.shape[1]
    assert chain_count <= device_count and seq_count == SEQS
    assert chunk == 2 * HEAD_DIM and inner_part <= 32 and part <= shard
    rank = lax.axis_index("tensor")
    place = lax.axis_index(DP)

    own_tokens = tokens.transpose(1, 0, 2).reshape(row_count, width)
    own_cot = cotangent.transpose(1, 0, 2).reshape(row_count, width)
    row_full = share_out(jnp.concatenate([own_tokens, own_cot], axis=0), "tensor")
    head_columns = w_qkv.reshape(shard, 3, head_count, HEAD_DIM).transpose(0, 2, 1, 3)
    gain_columns = jnp.pad(jnp.stack([gain_attn, gain_ffn], axis=1), ((0, shard - part), (0, 0)))
    qkv_pack = jnp.concatenate(
        [head_columns.reshape(shard, 3 * local_width), w_rate, gain_columns], axis=1
    )
    qkv_half = lax.all_gather(qkv_pack, "inner", axis=0, tiled=True)
    qkv_full = lax.all_gather(qkv_half, "outer", axis=0, tiled=True)
    qkv_full, row_full = ordered(qkv_full, row_full)
    some_gains = qkv_full[:, 3 * local_width + head_count :]
    some_gains = some_gains.reshape(device_count, shard, 2)[:, :part].transpose(2, 0, 1)
    gains = lax.all_gather(some_gains.reshape(2, device_count * part), "tensor", axis=0)
    gains = gains.reshape(tensor_count, 2, device_count, part).transpose(1, 2, 0, 3)
    gains = gains.reshape(2, width).astype(f32)
    scale_attn, scale_ffn = gains[0:1], gains[1:2]

    ffn_pack = jnp.concatenate(
        [w_gate_up.reshape(shard, 2 * ff_local), w_down.T, w_out.T], axis=1
    )
    ffn_full = lax.all_gather(ffn_pack, DP, axis=0, tiled=True)
    own_out = ffn_full[:, 3 * ff_local :]

    inner = inner_block(
        w_one,
        w_two.transpose(0, 2, 1),
        [b_one, b_two, norm_gain_inner, norm_bias_inner],
        chunk,
    )
    shape = jax.ShapeDtypeStruct
    packed, normed_attn, head_matrix = whole_call(
        functools.partial(start_kernel, head_count),
        "projections",
        (row_full, qkv_full, scale_attn, inner),
        (
            shape((device_count, chunk, LANES), bf16),
            shape((seq_count, chunk, width), bf16),
            shape((head_count, width, LANES), bf16),
        ),
    )
    chain_in = exchange(packed, DP)

    side = lax.axis_index("inner")
    kept = lax.dynamic_index_in_dim(normed_attn, side, 0)
    given = lax.dynamic_index_in_dim(normed_attn, 1 - side, 0)
    taken = lax.ppermute(given, "inner", [(0, 1), (1, 0)])
    pair = jnp.concatenate([kept, taken], axis=0)
    chain_in, own_out, pair = ordered(chain_in, own_out, pair)
    chain_rows = lax.all_gather(pair, "outer", axis=0)
    out_full = lax.all_gather(own_out, "tensor", axis=0)

    forward_out = chain_forward(chain_in, inner_part, feature_part)
    saved = forward_out[1:]
    head_local = exchange(forward_out[0], DP)[:chain_count]
    head_local = head_local.reshape(head_count, seq_count, HEAD_DIM, chunk)
    head_rows = lax.all_gather(head_local, "tensor", axis=0, tiled=False)

    group_rows = seq_count * chunk
    terms, mixed, normed_ffn, back_gate_up, swiglu = whole_call(
        feed_forward_kernel,
        "feed_forward",
        (head_rows, row_full, ffn_full, out_full, scale_ffn),
        (
            shape((tensor_count, 2 * seq_count, local_rows, width), bf16),
            shape((tensor_count, seq_count, local_rows, width), f32),
            shape((group_rows, width), bf16),
            shape((group_rows, 2 * ff_local), bf16),
            shape((group_rows, ff_local), bf16),
        ),
        VMEM_BYTES,
    )
    ffn_sums = exchange(terms, "tensor")
    (ffn_grads,) = whole_call(
        feed_forward_grad_kernel,
        "feed_forward_grads",
        (normed_ffn, back_gate_up, swiglu, row_full),
        (shape((width, 3 * ff_local), bf16),),
        VMEM_BYTES,
    )
    ffn_grad_sums = lax.psum_scatter(ffn_grads, DP, scatter_dimension=0, tiled=True)
    ffn_sums, chain_rows, _ = ordered(ffn_sums, chain_rows, ffn_grads)
    own_shape = (seq_count, local_rows, width)
    own_cot = own_cot.reshape(own_shape)

    def fixed(operand):
        return pl.BlockSpec(operand.shape, lambda turn, _: (0,) * len(operand.shape))

    chosen_mixed = pl.BlockSpec((1,) + own_shape, lambda turn, chosen: (chosen[0], 0, 0, 0))
    own_block = pl.BlockSpec(own_shape, lambda turn, _: (0, 0, 0))
    head_shape = shape(
        (device_count * tensor_count, local_rows // 2, 2 * HEAD_DIM), bf16
    )
    back_mixed, back_low, result, back_head = pl.pallas_call(
        feed_forward_back_kernel,
        grid_spec=pltpu.PrefetchScalarGridSpec(
            num_scalar_prefetch=1,
            grid=(1,),
            in_specs=[
                fixed(ffn_sums),
                chosen_mixed,
                own_block,
                fixed(scale_ffn),
                fixed(out_full),
            ],
            out_specs=[own_block] * 3 + [fixed(head_shape)],
        ),
        out_shape=[shape(own_shape, dtype) for dtype in (f32, bf16, bf16)] + [head_shape],
        compiler_params=pltpu.CompilerParams(vmem_limit_bytes=VMEM_BYTES),
        name="feed_forward_back",
    )(jnp.reshape(rank, (1,)).astype(jnp.int32), ffn_sums, mixed, own_cot, scale_ffn, out_full)
    result = result.transpose(1, 0, 2)
    back_head, back_low = ordered(back_head, back_low)
    head_grad = exchange(back_head, DP + ("tensor",))
    head_grad = head_grad.reshape(device_count, tensor_count, local_rows // 2, 2 * HEAD_DIM)
    attn_grads = lax.all_gather(back_low, "tensor", axis=1, tiled=True)
    (out_terms,) = whole_call(
        out_grad_kernel,
        "out_grads",
        (attn_grads, head_local),
        (shape((device_count, shard, local_width), bf16),),
    )
    head_grad, out_terms = ordered(head_grad, out_terms)
    out_sums = exchange(out_terms, DP)

    chosen = jnp.reshape(side, (1,)).astype(jnp.int32)
    back_packed = chain_backward(
        chain_in, chain_rows, chosen, head_grad, saved, inner_part, feature_part
    )
    received = exchange(back_packed, DP)
    grad_gate_up, grad_down, grad_out, gain_two = whole_call(
        matrix_output_kernel,
        "matrix_outputs",
        (ffn_grad_sums, out_sums, ffn_pack),
        (
            shape((shard, 2, ff_local), f32),
            shape((shard, ff_local), f32),
            shape((local_width, shard), f32),
            shape((shard, 128), f32),
        ),
    )
    own_matrix = lax.dynamic_slice_in_dim(head_matrix, place * shard, shard, 1)
    own_gains = lax.dynamic_slice_in_dim(gains, place * shard, shard, 1)
    terms, grad_qkv, small, state_block = whole_call(
        tail_kernel,
        "tail",
        (received, head_matrix, own_matrix, gain_two, own_gains),
        (
            shape((tensor_count, row_count + 16, width), bf16),
            shape((3, shard, local_width), f32),
            shape((8, shard), f32),
            shape((head_count, chunk, LANES - RATE_LANE), f32),
        ),
    )
    input_grad, gain_sums = whole_call(
        input_grad_kernel,
        "input_grad",
        (exchange(terms, "tensor"), own_tokens.reshape(own_shape), back_mixed, scale_attn),
        (shape(tokens.shape, f32), shape((2, shard), f32)),
    )
    gain_sums = lax.dynamic_slice_in_dim(gain_sums, rank * part, part, 1)

    matrices = state_block[..., MATRIX_LANE - RATE_LANE :][..., :inner_part]
    grad_one = matrices[:, :HEAD_DIM]
    grad_two = matrices[:, HEAD_DIM : 2 * HEAD_DIM].transpose(0, 2, 1)
    columns = state_block[:, :, VECTOR_LANE - RATE_LANE]
    ends = [inner_part + index * feature_part for index in range(4)]
    grad_b_one = columns[:, : ends[0]]
    grad_b_two, grad_gain_inner, grad_bias_inner = (
        columns[:, ends[index] : ends[index + 1]] for index in range(3)
    )

    return (
        result,
        input_grad,
        gain_sums[0],
        gain_sums[1],
        grad_qkv.transpose(1, 0, 2),
        small[2 : 2 + head_count].T,
        grad_out,
        grad_gate_up,
        grad_down.T,
        grad_one,
        grad_b_one,
        grad_two,
        grad_b_two,
        grad_gain_inner,
        grad_bias_inner,
    )


def solution(mesh):
    devices = mesh.devices
    dp_count, tensor_count = mesh.shape["dp"], mesh.shape["tensor"]
    devices = devices.reshape(dp_count // SEQS, SEQS, tensor_count)
    split = jax.sharding.Mesh(devices, DP + ("tensor",))
    rows = P(DP + ("tensor",), None, None)
    gains = P(DP + ("tensor",))
    placed = (
        rows,
        gains,
        gains,
        P(DP, None, "tensor"),
        P(DP, "tensor"),
        P("tensor", DP),
        P(DP, None, "tensor"),
        P("tensor", DP),
        P("tensor", None, DP),
        P("tensor", DP),
        P("tensor", DP, None),
        P("tensor", DP),
        P("tensor", DP),
        P("tensor", DP),
    )
    return jax.shard_map(
        local,
        mesh=split,
        in_specs=placed + (rows,),
        out_specs=(rows,) + placed,
        check_vma=False,
    )
```
